32 devices in a mesh: dp: 8 (over z, y), tensor: 4 (over x, core).
Axes of the slice: x: 2, y: 2, z: 4, core: 2. Of those that a mesh axis runs over, the one named last changes fastest.
Arguments:
- patches: bfloat16 [8, 1536, 576], P('dp', 'tensor'), may hold values from -6 to 6
- view_counts: int32 [8], P('dp'), may hold values from 2 to 8, as said below
- splat_index: int32 [8, 4, 24576], P('dp', None, 'tensor'), may hold values from 0 to 98303, as said below
- splat_dist: int32 [8, 4, 24576], P('dp', None, 'tensor'), may hold values from 1 to 8
- alpha_label: int32 [8, 24576], P('dp', 'tensor'), may hold values from 0 to 2, as said below
- step_count: int32 [1], replicated, may hold values from 2 to 20
- row_master: float32 [4, 3145728], P('tensor', 'dp')
- row_first: float32 [4, 3145728], P('tensor', 'dp')
- row_second: float32 [4, 3145728], P('tensor', 'dp')
- row_ema: float32 [4, 3145728], P('tensor', 'dp')
- shared_master: float32 [1380352], P('dp')
- shared_first: float32 [1380352], P('dp')
- shared_second: float32 [1380352], P('dp')
- shared_ema: float32 [1380352], P('dp')
Outputs:
- grad_norm: float32 [1], replicated
- loss: float32 [1], replicated
- row_new: float32 [4, 3145728], P('tensor', 'dp')
- row_first_new: float32 [4, 3145728], P('tensor', 'dp')
- row_second_new: float32 [4, 3145728], P('tensor', 'dp')
- row_ema_new: float32 [4, 3145728], P('tensor', 'dp')
- row_copy: bfloat16 [4, 3145728], P('tensor', 'dp')
- shared_new: float32 [1380352], P('dp')
- shared_first_new: float32 [1380352], P('dp')
- shared_second_new: float32 [1380352], P('dp')
- shared_ema_new: float32 [1380352], P('dp')
- shared_copy: bfloat16 [1380352], P('dp')
The draws below stay inside these ranges and needn't reach their ends.
Inputs may be any that keep to these rules, and one draw needn't show every extreme that they name: Key slots from view_counts[s] * 192 on are padding views. `splat_index`: every entry of scene s names a Gaussian of that scene's real views: it is below view_counts[s] * 192 * 8 * 8. Every scene has at least one pixel whose alpha_label is below 2.
All inputs are finite; a program needn't handle non-finite values.
Results may differ from the reference program's by a relative error of at most 0.002.
The reference program's roundings to bfloat16 on the way count: a program that leaves them out, or rounds other values in their place, can miss the bound.
Values may be sent and summed in bfloat16 or wider, within the bound.
A program may use at most 128 MiB of HBM per device.

```python
import math
from functools import partial
import jax
import jax.numpy as jnp
from jax import lax

D = 1024
HEADS = 16
DH = 64
FF = 4096
PATCH = 8
MAXV = 8
KSPL = 4
VTOK = 192
SLOTS = 1536
PIN = 576
POUT = 768
RPIX = 24576
SCENES = 8
ROW_PARAMS = 3145728
SHARED_PARAMS = 1380352
N_TENSOR = 4


clip_norm = 0.005


def unit_noise(key, shape):
    return jnp.clip(jax.random.normal(key, shape, jnp.float32), -4.0, 4.0)


def scene_counts(key):
    drawn_counts = jax.random.randint(jax.random.fold_in(key, 11), (SCENES,), 2, MAXV + 1)
    fullest = jax.random.randint(jax.random.fold_in(key, 12), (), 0, SCENES)
    fewest = (fullest + 1 + jax.random.randint(jax.random.fold_in(key, 13), (), 0, SCENES - 1)) % SCENES
    return (drawn_counts.at[fullest].set(MAXV).at[fewest].set(2), fullest, fewest)


def draw_view_counts(key, part):
    counts_out, fullest, fewest = scene_counts(key)
    return counts_out


def draw_splat_index(key, part):
    counts_out, fullest, fewest = scene_counts(key)
    index_limit = counts_out * (VTOK * PATCH * PATCH)
    raw_index = jax.random.randint(jax.random.fold_in(key, 21), (SCENES, KSPL, RPIX), 0, 1 << 30)
    chosen = raw_index % index_limit[:, None, None]
    chosen = chosen.at[fullest, 0, 0].set(MAXV * VTOK * PATCH * PATCH - 1)
    return chosen.at[fewest, 0, 1].set(0)


def draw_alpha_label(key, part):
    labels = jax.random.randint(jax.random.fold_in(key, 31), (SCENES, RPIX), 0, 3)
    chosen_pixel = jax.random.randint(jax.random.fold_in(key, 32), (SCENES,), 0, RPIX)
    counted_label = jax.random.randint(jax.random.fold_in(key, 33), (SCENES,), 0, 2)
    marked = jnp.arange(RPIX)[None, :] == chosen_pixel[:, None]
    return jnp.where(marked, counted_label[:, None], labels)


def row_scale():
    local_width = D // N_TENSOR
    local_hidden = FF // N_TENSOR
    qkv_end = 3 * D * local_width
    out_end = qkv_end + local_width * D
    up_end = out_end + D * local_hidden
    column = jnp.arange(ROW_PARAMS)
    scale_row = jnp.where(column < qkv_end, 1.3 / math.sqrt(D), jnp.where(column < out_end, 4.0 / math.sqrt(D), jnp.where(column < up_end, 1.0 / math.sqrt(D), 1.0 / math.sqrt(FF))))
    return scale_row[None, :]


def shared_values(key):
    position = jnp.arange(SHARED_PARAMS)
    patch_end = PIN * D
    unpatch_end = patch_end + D * POUT
    noise_vals = unit_noise(key, (SHARED_PARAMS,))
    weight_part = jnp.where(position < patch_end, noise_vals / math.sqrt(PIN), noise_vals / math.sqrt(D))
    norm_row = (position - unpatch_end) // D
    norm_part = jnp.where(norm_row % 2 == 0, 1.0 + 0.1 * noise_vals, 0.2 * noise_vals)
    return jnp.where(position < unpatch_end, weight_part, norm_part)


def grad_size():
    return clip_norm / math.sqrt(N_TENSOR * ROW_PARAMS + SHARED_PARAMS)


def second_values(key, shape):
    level = jax.random.uniform(key, shape, jnp.float32, math.log(0.5), math.log(8.0))
    return 0.05 / 0.95 * grad_size() ** 2 * jnp.exp(level)


def draw_row_master(key, part):
    return row_scale() * unit_noise(jax.random.fold_in(key, 1), (N_TENSOR, ROW_PARAMS))


def draw_row_ema(key, part):
    return row_scale() * unit_noise(jax.random.fold_in(key, 2), (N_TENSOR, ROW_PARAMS))


def draw_row_first(key, part):
    return grad_size() / 9.0 * unit_noise(jax.random.fold_in(key, 3), (N_TENSOR, ROW_PARAMS))


def draw_row_second(key, part):
    return second_values(jax.random.fold_in(key, 4), (N_TENSOR, ROW_PARAMS))


def draw_shared_master(key, part):
    return shared_values(jax.random.fold_in(key, 5))


def draw_shared_ema(key, part):
    return shared_values(jax.random.fold_in(key, 6))


def draw_shared_first(key, part):
    return grad_size() / 9.0 * unit_noise(jax.random.fold_in(key, 7), (SHARED_PARAMS,))


def draw_shared_second(key, part):
    return second_values(jax.random.fold_in(key, 8), (SHARED_PARAMS,))


def plant(result, stream_key, low, high):
    index_at = [jax.random.randint(jax.random.fold_in(stream_key, axis), (), 0, length) for axis, length in enumerate(result.shape)]
    longest = result.shape.index(max(result.shape))
    beside = index_at[:longest] + [(index_at[longest] + 1) % result.shape[longest]] + index_at[longest + 1:]
    return result.at[tuple(index_at)].set(low).at[tuple(beside)].set(high)


def shard_levels(own_key, dims, pieces, smallest, high):
    loudness = 1.0
    for axis_at, parts in pieces:
        steps = jax.random.uniform(jax.random.fold_in(jax.random.fold_in(own_key, 6), axis_at), (parts,), jnp.float32, smallest / len(pieces), high / len(pieces))
        loudness = loudness * jnp.repeat(jnp.exp(steps), dims[axis_at] // parts).reshape((-1,) + (1,) * (len(dims) - 1 - axis_at))
    return loudness


def centred(own_key, shape, deviation, reach, split=(), dtype=jnp.bfloat16):
    level = shard_levels(own_key, shape, split, -0.22, 0.18) if split else 1.0
    drawn = jax.random.normal(own_key, shape, jnp.float32) * deviation * level
    return jnp.minimum(jnp.maximum(drawn, -reach), reach).astype(dtype)


def setup_inputs(seed: int = 0) -> dict:
    splits = jax.random.split(jax.random.key(seed), 15)
    patches = centred(splits[0], (SCENES, SLOTS, PIN), 1.0, 6.0, ((0, 8), (1, 4)))
    view_counts = draw_view_counts(jax.random.fold_in(splits[14], 71), 0)
    splat_index = draw_splat_index(jax.random.fold_in(splits[14], 71), 0)
    splat_dist = plant(jax.random.randint(splits[3], (SCENES, KSPL, RPIX), 1, 9), jax.random.fold_in(splits[3], 1), 1, 8).astype(jnp.int32)
    alpha_label = draw_alpha_label(jax.random.fold_in(splits[14], 71), 0)
    step_count = jax.random.randint(splits[5], (1,), 2, 21).astype(jnp.int32)
    row_master = draw_row_master(jax.random.fold_in(splits[14], 71), 0)
    row_first = draw_row_first(jax.random.fold_in(splits[14], 71), 0)
    row_second = draw_row_second(jax.random.fold_in(splits[14], 71), 0)
    row_ema = draw_row_ema(jax.random.fold_in(splits[14], 71), 0)
    shared_master = draw_shared_master(jax.random.fold_in(splits[14], 71), 0)
    shared_first = draw_shared_first(jax.random.fold_in(splits[14], 71), 0)
    shared_second = draw_shared_second(jax.random.fold_in(splits[14], 71), 0)
    shared_ema = draw_shared_ema(jax.random.fold_in(splits[14], 71), 0)
    return {"patches": patches, "view_counts": view_counts, "splat_index": splat_index, "splat_dist": splat_dist, "alpha_label": alpha_label, "step_count": step_count, "row_master": row_master, "row_first": row_first, "row_second": row_second, "row_ema": row_ema, "shared_master": shared_master, "shared_first": shared_first, "shared_second": shared_second, "shared_ema": shared_ema}


@jax.custom_vjp
def low(v):
    return lax.optimization_barrier(v.astype(jnp.bfloat16)).astype(jnp.float32)

@jax.custom_vjp
def low_back(v):
    return v

def low_keep(v):
    return (low(v), None)

def low_pass(kept, grad):
    return (grad,)

def back_keep(v):
    return (v, None)

def back_low(kept, grad):
    return (low(grad),)
low.defvjp(low_keep, low_pass)
low_back.defvjp(back_keep, back_low)
clip_norm = 0.005
beta_one = 0.9
beta_two = 0.95
adam_eps = 1e-08
decay_rate = 0.05
learn_rate = 0.03
ema_rate = 0.9
norm_eps = 1e-05
masked_score = -1e+30

def matmul(left_op, right_op):
    return jnp.dot(left_op, right_op, precision=lax.Precision.HIGHEST, preferred_element_type=jnp.float32)

def layer_norm(residual, gain_vec, bias_vec):
    centre = residual - lax.optimization_barrier(jnp.mean(residual, -1, keepdims=True))
    inverse = lax.rsqrt(lax.optimization_barrier(jnp.mean(centre * centre, -1, keepdims=True)) + norm_eps)
    return centre * inverse * gain_vec + bias_vec

def split_weights(row_flat, shared_flat):
    groups = row_flat.shape[0]
    local_width = D // groups
    local_hidden = FF // groups
    qkv_end = 3 * D * local_width
    out_end = qkv_end + local_width * D
    up_end = out_end + D * local_hidden
    qkv_proj = row_flat[:, :qkv_end].reshape(groups, D, 3, local_width).transpose(1, 2, 0, 3).reshape(D, 3 * D)
    out_proj = row_flat[:, qkv_end:out_end].reshape(D, D)
    up_proj = row_flat[:, out_end:up_end].reshape(groups, D, local_hidden).transpose(1, 0, 2).reshape(D, FF)
    down_proj = row_flat[:, up_end:].reshape(FF, D)
    patch_proj = shared_flat[:PIN * D].reshape(PIN, D)
    unpatch_proj = shared_flat[PIN * D:PIN * D + D * POUT].reshape(D, POUT)
    norm_params = shared_flat[PIN * D + D * POUT:].reshape(4, D)
    return (qkv_proj, out_proj, up_proj, down_proj, patch_proj, unpatch_proj, norm_params)

def one_head(head_in, key_valid):
    queries, keyset, values = head_in
    scores = low_back(matmul(queries, keyset.T) * DH ** (-0.5))
    scores = jnp.where(key_valid[None, :], scores, masked_score)
    weights = jax.nn.softmax(scores, -1)
    return matmul(low(weights), values)

def render_loss(gauss_table, splats, distance, valid_px, target):
    area = PATCH * PATCH
    opacity = jnp.take(gauss_table[:, :area].reshape(-1), splats)
    spread = jnp.take(gauss_table[:, area:2 * area].reshape(-1), splats)
    contrib = (0.02 + 0.96 * jax.nn.sigmoid(opacity)) * jnp.exp(-0.25 * distance * jax.nn.sigmoid(spread))
    keep_log = lax.optimization_barrier(jnp.sum(jnp.log1p(-contrib), 0))
    alpha_log = jnp.log(-jnp.expm1(keep_log))
    return jnp.sum(valid_px * -(target * alpha_log + (1.0 - target) * keep_log))

def scene_loss(weights, scene):
    qkv_proj, out_proj, up_proj, down_proj, patch_proj, unpatch_proj, norm_params = weights
    patch_rows, count_views, splats, distance, labels = scene
    length = patch_rows.shape[0]
    key_valid = jnp.arange(length) < count_views * VTOK
    embed = low_back(matmul(patch_rows, patch_proj))
    normed1 = low(layer_norm(embed, norm_params[0], norm_params[1]))
    qkv = low(low_back(matmul(normed1, qkv_proj)))
    queries = qkv[:, :D].reshape(length, HEADS, DH).transpose(1, 0, 2)
    keyset = qkv[:, D:2 * D].reshape(length, HEADS, DH).transpose(1, 0, 2)
    values = qkv[:, 2 * D:].reshape(length, HEADS, DH).transpose(1, 0, 2)
    heads_out = lax.map(jax.checkpoint(partial(one_head, key_valid=key_valid)), (queries, keyset, values))
    attended = low(low_back(heads_out.transpose(1, 0, 2).reshape(length, D)))
    resid1 = embed + low_back(matmul(attended, out_proj))
    normed2 = low(layer_norm(resid1, norm_params[2], norm_params[3]))
    upper = low_back(matmul(normed2, up_proj))
    active = low(jax.nn.gelu(upper, approximate=False))
    resid2 = resid1 + low_back(matmul(active, down_proj))
    gauss = low_back(matmul(low(resid2), unpatch_proj))
    valid_px = (labels < 2).astype(jnp.float32)
    target = (labels == 1).astype(jnp.float32)
    return render_loss(gauss[:, :2 * PATCH * PATCH], splats, distance, valid_px, target)

def adam_update(master, first_mom, second_mom, gradient, step_float):
    first_new = beta_one * first_mom + (1.0 - beta_one) * gradient
    second_new = beta_two * second_mom + (1.0 - beta_two) * gradient * gradient
    first_hat = first_new / (1.0 - jnp.power(beta_one, step_float))
    second_hat = second_new / (1.0 - jnp.power(beta_two, step_float))
    master_new = master - learn_rate * (first_hat / (jnp.sqrt(second_hat) + adam_eps) + decay_rate * master)
    return (master_new, first_new, second_new)

def reference(patches, view_counts, splat_index, splat_dist, alpha_label, step_count, row_master, row_first, row_second, row_ema, shared_master, shared_first, shared_second, shared_ema):
    scenes = (patches.astype(jnp.float32), view_counts, splat_index, splat_dist.astype(jnp.float32), alpha_label)

    def total_loss(row_flat, shared_flat):
        weights = split_weights(low(row_flat), low(shared_flat))

        def one_scene(carried, scene):
            return (carried + jax.checkpoint(scene_loss)(weights, scene), None)
        loss_sum, unused = lax.scan(one_scene, jnp.zeros((), jnp.float32), scenes)
        return loss_sum
    loss_sum, loss_back = jax.vjp(total_loss, row_master, shared_master)
    row_grad, shared_grad = loss_back(jnp.ones((), jnp.float32))
    pixels = jnp.sum((alpha_label < 2).astype(jnp.float32))
    norm_value = jnp.sqrt(jnp.sum(row_grad * row_grad) + jnp.sum(shared_grad * shared_grad)) / pixels
    factor = clip_norm / jnp.maximum(norm_value, clip_norm) / pixels
    step_float = step_count[0].astype(jnp.float32)
    row_new, row_first_new, row_second_new = adam_update(row_master, row_first, row_second, row_grad * factor, step_float)
    shared_new, shared_first_new, shared_second_new = adam_update(shared_master, shared_first, shared_second, shared_grad * factor, step_float)
    row_ema_new = ema_rate * row_ema + (1.0 - ema_rate) * row_new
    shared_ema_new = ema_rate * shared_ema + (1.0 - ema_rate) * shared_new
    return (norm_value.reshape(1), (loss_sum / pixels).reshape(1), row_new, row_first_new, row_second_new, row_ema_new, row_new.astype(jnp.bfloat16), shared_new, shared_first_new, shared_second_new, shared_ema_new, shared_new.astype(jnp.bfloat16))
```

```python
import functools
import math
from functools import partial

import jax
import jax.numpy as jnp
from jax import lax
from jax.experimental import pallas as pl
from jax.experimental.pallas import tpu as pltpu
from jax.sharding import PartitionSpec as P

MESH = pl.DeviceIdType.MESH
D = 1024
DH = 64
FF = 4096
PATCH = 8
VTOK = 192
PIN = 576
POUT = 768


clip_norm = 0.005
beta_one = 0.9
beta_two = 0.95
adam_eps = 1e-08
decay_rate = 0.05
learn_rate = 0.03
ema_rate = 0.9
norm_eps = 1e-05
masked_score = -1e30


def contract_rows(left_op, right_op):
    return lax.dot_general(
        left_op, right_op, (((0,), (0,)), ((), ())), preferred_element_type=jnp.float32
    )


def contract_last(left_op, right_op):
    return lax.dot_general(
        left_op, right_op, (((1,), (1,)), ((), ())), preferred_element_type=jnp.float32
    )


def layer_norm(residual, gain_vec, bias_vec):
    centre = residual - jnp.mean(residual, -1, keepdims=True)
    inverse = lax.rsqrt(jnp.mean(centre * centre, -1, keepdims=True) + norm_eps)
    scaled = centre * inverse
    return (scaled * gain_vec + bias_vec, scaled, inverse)


def norm_back(grad_out, scaled, inverse, gain_vec):
    grad_scaled = grad_out * gain_vec
    return inverse * (
        grad_scaled
        - jnp.mean(grad_scaled, -1, keepdims=True)
        - scaled * jnp.mean(grad_scaled * scaled, -1, keepdims=True)
    )


def score_block(q_part, keyset, key_valid):
    factor = q_part.shape[-1] ** (-0.5)
    scores = jnp.einsum("qhd,khd->hqk", q_part, keyset, preferred_element_type=jnp.float32) * factor
    return jnp.where(key_valid[None, None, :], scores, masked_score)


def attend_forward(queries, keyset, values, key_valid, block_rows):
    length = queries.shape[0]

    def one_block(q_part):
        scores = score_block(q_part, keyset, key_valid)
        top_score = jnp.max(scores, -1, keepdims=True)
        weights_exp = jnp.exp(scores - top_score)
        row_total = jnp.sum(weights_exp, -1, keepdims=True)
        weights_low = (weights_exp / row_total).astype(jnp.bfloat16)
        results = jnp.einsum(
            "hqk,khd->qhd", weights_low, values, preferred_element_type=jnp.float32
        )
        return (results, (top_score + jnp.log(row_total))[..., 0])

    q_blocks = queries.reshape(length // block_rows, block_rows, queries.shape[1], queries.shape[2])
    results, log_total = lax.map(one_block, q_blocks)
    return (results.reshape(length, queries.shape[1] * queries.shape[2]), log_total)


def attend_back(queries, keyset, values, key_valid, attended_grad, log_total, block_rows):
    length = queries.shape[0]
    factor = queries.shape[-1] ** (-0.5)

    def one_block(carried, inputs):
        grad_keys, grad_values = carried
        q_part, g_part, l_part = inputs
        scores = score_block(q_part, keyset, key_valid)
        weights = jnp.exp(scores - l_part[..., None])
        grad_weights = jnp.einsum(
            "qhd,khd->hqk", g_part, values, preferred_element_type=jnp.float32
        )
        centre = jnp.sum(weights * grad_weights, -1, keepdims=True)
        grad_scores = (weights * (grad_weights - centre)).astype(jnp.bfloat16)
        grad_query = (
            jnp.einsum("hqk,khd->qhd", grad_scores, keyset, preferred_element_type=jnp.float32)
            * factor
        )
        grad_keys = (
            grad_keys
            + jnp.einsum("hqk,qhd->khd", grad_scores, q_part, preferred_element_type=jnp.float32)
            * factor
        )
        grad_values = grad_values + jnp.einsum(
            "hqk,qhd->khd", weights.astype(jnp.bfloat16), g_part, preferred_element_type=jnp.float32
        )
        return ((grad_keys, grad_values), grad_query)

    block_shape = (length // block_rows, block_rows, queries.shape[1], queries.shape[2])
    zeros_kv = jnp.zeros(keyset.shape, jnp.float32)
    (grad_keys, grad_values), grad_query = lax.scan(
        one_block,
        (zeros_kv, zeros_kv),
        (queries.reshape(block_shape), attended_grad.reshape(block_shape), log_total),
    )
    return (
        grad_query.reshape(length, -1),
        grad_keys.reshape(length, -1),
        grad_values.reshape(length, -1),
    )


def layer_forward(embedded, weights, key_valid):
    qkv_proj, out_proj, up_proj, down_proj, norm_params = weights
    local_width = out_proj.shape[0]
    heads_here = local_width // DH
    normed1, scaled1, inverse1 = layer_norm(embedded, norm_params[0], norm_params[1])
    normed1_all = lax.all_gather(normed1.astype(jnp.bfloat16), "tensor", axis=0, tiled=True)
    length = normed1_all.shape[0]
    block_rows = min(512, length)
    qkv = jnp.dot(normed1_all, qkv_proj, preferred_element_type=jnp.float32).astype(jnp.bfloat16)
    queries = qkv[:, :local_width].reshape(length, heads_here, DH)
    keyset = qkv[:, local_width : 2 * local_width].reshape(length, heads_here, DH)
    values = qkv[:, 2 * local_width :].reshape(length, heads_here, DH)
    attended, log_total = attend_forward(queries, keyset, values, key_valid, block_rows)
    attended = attended.astype(jnp.bfloat16)
    resid1 = embedded + lax.psum_scatter(
        jnp.dot(attended, out_proj, preferred_element_type=jnp.float32),
        "tensor",
        scatter_dimension=0,
        tiled=True,
    )
    normed2, scaled2, inverse2 = layer_norm(resid1, norm_params[2], norm_params[3])
    normed2_all = lax.all_gather(normed2.astype(jnp.bfloat16), "tensor", axis=0, tiled=True)
    hidden_pre = jnp.dot(normed2_all, up_proj, preferred_element_type=jnp.float32)
    active = jax.nn.gelu(hidden_pre, approximate=False).astype(jnp.bfloat16)
    resid2 = resid1 + lax.psum_scatter(
        jnp.dot(active, down_proj, preferred_element_type=jnp.float32).astype(jnp.bfloat16),
        "tensor",
        scatter_dimension=0,
        tiled=True,
    ).astype(jnp.float32)
    saved_values = (
        scaled1,
        inverse1,
        normed1_all,
        queries,
        keyset,
        values,
        log_total,
        attended,
        scaled2,
        inverse2,
        normed2_all,
        hidden_pre,
        active,
    )
    return (resid2, saved_values)


def layer_backward(resid2_grad, weights, key_valid, saved_values):
    qkv_proj, out_proj, up_proj, down_proj, norm_params = weights
    (
        scaled1,
        inverse1,
        normed1_all,
        queries,
        keyset,
        values,
        log_total,
        attended,
        scaled2,
        inverse2,
        normed2_all,
        hidden_pre,
        active,
    ) = saved_values
    length = normed1_all.shape[0]
    block_rows = min(512, length)
    down_in = lax.all_gather(resid2_grad.astype(jnp.bfloat16), "tensor", axis=0, tiled=True)
    down_grad = contract_rows(active, down_in)
    active_grad = contract_last(down_in, down_proj)
    gelu_back = jax.vjp(partial(jax.nn.gelu, approximate=False), hidden_pre)[1]
    hidden_grad = gelu_back(active_grad)[0].astype(jnp.bfloat16)
    up_grad = contract_rows(normed2_all, hidden_grad)
    normed2_grad = lax.psum_scatter(
        contract_last(hidden_grad, up_proj).astype(jnp.bfloat16),
        "tensor",
        scatter_dimension=0,
        tiled=True,
    ).astype(jnp.float32)
    resid1_grad = resid2_grad + norm_back(normed2_grad, scaled2, inverse2, norm_params[2])
    branch_in = lax.all_gather(resid1_grad.astype(jnp.bfloat16), "tensor", axis=0, tiled=True)
    out_grad = contract_rows(attended, branch_in)
    attended_grad = contract_last(branch_in, out_proj).astype(jnp.bfloat16).reshape(queries.shape)
    grad_query, grad_key, grad_value = attend_back(
        queries, keyset, values, key_valid, attended_grad, log_total, block_rows
    )
    qkv_grad = jnp.concatenate([grad_query, grad_key, grad_value], 1).astype(jnp.bfloat16)
    qkv_weight_grad = contract_rows(normed1_all, qkv_grad)
    normed1_grad = lax.psum_scatter(
        contract_last(qkv_grad, qkv_proj).astype(jnp.bfloat16),
        "tensor",
        scatter_dimension=0,
        tiled=True,
    ).astype(jnp.float32)
    embed_grad = resid1_grad + norm_back(normed1_grad, scaled1, inverse1, norm_params[0])
    gain_grad = jnp.stack(
        [
            jnp.sum(normed1_grad * scaled1, 0),
            jnp.sum(normed1_grad, 0),
            jnp.sum(normed2_grad * scaled2, 0),
            jnp.sum(normed2_grad, 0),
        ]
    )
    return (embed_grad, (qkv_weight_grad, out_grad, up_grad, down_grad), gain_grad)


NT = (((1,), (1,)), ((), ()))
NN = (((1,), (0,)), ((), ()))

def render_kernel(area, wide, block, split, table_ref, splat_ref, dist_ref, label_ref, loss_ref, grad_ref, flip, picked, hot, spread_grad):
    tokens = table_ref.shape[0]
    groups = tokens // wide
    splats, pixels = splat_ref.shape
    for j in range(groups):
        flip[j * 2 * area : (j + 1) * 2 * area] = jnp.transpose(table_ref[j * wide : (j + 1) * wide].astype(jnp.float32)).astype(jnp.bfloat16)
    spread_grad[...] = jnp.zeros_like(spread_grad)
    wide_ids = lax.broadcasted_iota(jnp.int32, (wide, block), 0).astype(jnp.float32).astype(jnp.bfloat16)
    cell_ids = lax.broadcasted_iota(jnp.int32, (area, block), 0).astype(jnp.float32)
    cell_low = cell_ids.astype(jnp.bfloat16)
    one, nil = jnp.ones((wide, block), jnp.bfloat16), jnp.zeros((wide, block), jnp.bfloat16)

    def one_block(step, loss):
        here = pl.ds(pl.multiple_of(step * block, block), block)
        opacities, spreads, lows = [], [], []
        for k in range(splats):
            index = splat_ref[k : k + 1, here]
            token = index // area
            column = (token % wide).astype(jnp.float32).astype(jnp.bfloat16)
            group = (token // wide)
            cell = (index % area).astype(jnp.float32)
            match = jnp.where(wide_ids == column, one, nil)
            hot[k] = match
            picked[...] = lax.dot_general(flip[...], match, NN, preferred_element_type=jnp.float32)
            op_sum = jnp.zeros((area, block), jnp.float32)
            sp_sum = jnp.zeros((area, block), jnp.float32)
            for j in range(groups):
                same = cell_ids == jnp.where(group == j, cell, -1.0)
                op_sum += jnp.where(same, picked[j * 2 * area : j * 2 * area + area], 0.0)
                sp_sum += jnp.where(same, picked[j * 2 * area + area : (j + 1) * 2 * area], 0.0)
            opacities.append(jnp.sum(op_sum, 0, keepdims=True))
            spreads.append(jnp.sum(sp_sum, 0, keepdims=True))
            lows.append((group, cell))
        opacity, spread = jnp.concatenate(opacities, 0), jnp.concatenate(spreads, 0)
        distance = dist_ref[:, here].astype(jnp.float32)
        labels = label_ref[:, here]
        valid = jnp.where(labels < 2, 1.0, 0.0)
        target = jnp.where(labels == 1, 1.0, 0.0)
        op_sig, sp_sig = jax.nn.sigmoid(opacity), jax.nn.sigmoid(spread)
        fade = jnp.exp(-0.25 * distance * sp_sig)
        contrib = (0.02 + 0.96 * op_sig) * fade
        keep_log = jnp.sum(jnp.log1p(-contrib), 0, keepdims=True)
        keep = jnp.exp(keep_log)
        alpha = 1.0 - keep
        alpha_log = jnp.log(alpha)
        loss = loss - valid * (target * alpha_log + (1.0 - target) * keep_log)
        keep_grad = valid * (target * keep / alpha - (1.0 - target))
        contrib_grad = -keep_grad / (1.0 - contrib)
        op_grad = contrib_grad * (0.96 * op_sig * (1.0 - op_sig)) * fade
        sp_grad = contrib_grad * contrib * (-0.25 * distance * sp_sig * (1.0 - sp_sig))
        for k in range(splats):
            group, cell = lows[k]
            parts_op, parts_sp = op_grad[k : k + 1], sp_grad[k : k + 1]
            for part in range(split):
                low_op, low_sp = parts_op.astype(jnp.bfloat16), parts_sp.astype(jnp.bfloat16)
                parts_op, parts_sp = parts_op - low_op.astype(jnp.float32), parts_sp - low_sp.astype(jnp.float32)
                pieces = []
                for j in range(groups):
                    same = cell_low == jnp.where(group == j, cell, -1.0).astype(jnp.bfloat16)
                    pieces.append(jnp.where(same, low_op, jnp.bfloat16(0)))
                    pieces.append(jnp.where(same, low_sp, jnp.bfloat16(0)))
                weighted = jnp.concatenate(pieces, 0)
                spread_grad[...] += lax.dot_general(weighted, hot[k], NT, preferred_element_type=jnp.float32)
        return loss

    loss = lax.fori_loop(0, pixels // block, one_block, jnp.zeros((1, block), jnp.float32))
    loss_ref[...] = jnp.broadcast_to(jnp.sum(loss, 1, keepdims=True), loss_ref.shape)
    for j in range(groups):
        grad_ref[j * wide : (j + 1) * wide] = jnp.transpose(spread_grad[j * 2 * area : (j + 1) * 2 * area]).astype(grad_ref.dtype)

def render(table, splats, distance, labels, area, block=512, wide=256, split=2):
    tokens = table.shape[0]
    vm = pl.BlockSpec(memory_space=pltpu.VMEM)
    groups = tokens // wide
    return pl.pallas_call(
        functools.partial(render_kernel, area, wide, block, split),
        out_shape=(jax.ShapeDtypeStruct((8, 128), jnp.float32), jax.ShapeDtypeStruct(table.shape, jnp.bfloat16)),
        in_specs=[vm] * 4, out_specs=(vm, vm),
        scratch_shapes=[pltpu.VMEM((groups * 2 * area, wide), jnp.bfloat16), pltpu.VMEM((groups * 2 * area, block), jnp.float32),
            pltpu.VMEM((splats.shape[0], wide, block), jnp.bfloat16), pltpu.VMEM((groups * 2 * area, wide), jnp.float32)],
        compiler_params=pltpu.CompilerParams(vmem_limit_bytes=48 * 2**20),
    )(table, splats, distance, labels)


def owner_sum_kernel(lines, pieces, g_ref, o_ref, pair_out, pair_in, part, line_in, own_in, p_send, p_recv, l_send, up_recv, down_recv):
    me = lax.axis_index("dp")
    line, side = me // 2, lax.rem(me, 2)
    chunk = o_ref.shape[0]
    rows = chunk // pieces
    count = lines * pieces
    pair = {"dp": line * 2 + 1 - side}
    above = {"dp": lax.rem(line + 1, lines) * 2 + side}
    below = {"dp": lax.rem(line + lines - 1, lines) * 2 + side}
    has_below, has_above = line > 0, line < lines - 1

    def target(step):
        turn = lax.rem(step, lines)
        odd = lax.rem(turn, 2)
        return (1 - odd) * (lines - 1 - turn // 2) + odd * (turn // 2)

    def slot(step):
        return pl.ds(pl.multiple_of(step * rows, rows), rows)

    def here(step):
        return pl.ds(pl.multiple_of(step // lines * rows, rows), rows)

    def source(step, owner):
        return pl.ds(pl.multiple_of((target(step) * 2 + owner) * chunk + step // lines * rows, rows), rows)

    def copy(src, dst, send, recv, to):
        return pltpu.make_async_remote_copy(
            src_ref=src, dst_ref=dst, send_sem=send, recv_sem=recv, device_id=to, device_id_type=MESH
        )

    def pair_copy(step):
        return copy(pair_out.at[slot(step)], pair_in.at[slot(step)], p_send.at[step], p_recv.at[step], pair)

    def line_copy(step, to, recv):
        return copy(part.at[slot(step)], line_in.at[slot(step)], l_send.at[step], recv.at[step], to)

    def last_copy(step):
        return copy(part.at[slot(step)], own_in.at[here(step)], l_send.at[step], down_recv.at[step], below)

    barrier = pltpu.get_barrier_semaphore()
    pl.semaphore_signal(barrier, inc=1, device_id=pair, device_id_type=MESH)

    @pl.when(has_below)
    def _():
        pl.semaphore_signal(barrier, inc=1, device_id=below, device_id_type=MESH)

    @pl.when(has_above)
    def _():
        pl.semaphore_signal(barrier, inc=1, device_id=above, device_id_type=MESH)

    pl.semaphore_wait(barrier, 1 + jnp.minimum(line, 1) + jnp.minimum(lines - 1 - line, 1))

    @pl.loop(0, count)
    def _(step):
        pair_out[slot(step)] = g_ref[source(step, 1 - side)].astype(jnp.bfloat16)
        pair_copy(step).start()

    @pl.loop(0, count + lines - 1)
    def _(step):
        @pl.when(step < count)
        def _():
            pair_copy(step).wait_recv()
            part[slot(step)] = g_ref[source(step, side)].astype(jnp.float32) + pair_in[slot(step)].astype(jnp.float32)

        rising = step - line

        @pl.when((rising >= 0) & (rising < count) & (target(rising) > line))
        def _():
            @pl.when(has_below)
            def _():
                line_copy(rising, above, up_recv).wait_recv()
                part[slot(rising)] += line_in[slot(rising)]

            line_copy(rising, above, up_recv).start()

        falling = step - (lines - 1 - line)

        @pl.when((falling >= 0) & (falling < count) & (target(falling) < line))
        def _():
            @pl.when(has_above)
            def _():
                line_copy(falling, below, down_recv).wait_recv()
                part[slot(falling)] += line_in[slot(falling)]

            @pl.when(target(falling) == line - 1)
            def _():
                last_copy(falling).start()

            @pl.when(target(falling) < line - 1)
            def _():
                line_copy(falling, below, down_recv).start()

    @pl.loop(0, count)
    def _(step):
        pair_copy(step).wait_send()

        @pl.when(target(step) > line)
        def _():
            line_copy(step, above, up_recv).wait_send()

        @pl.when(target(step) < line)
        def _():
            line_copy(step, below, down_recv).wait_send()

        @pl.when(target(step) == line)
        def _():
            o_ref[here(step)] = part[slot(step)]

            @pl.when(has_below)
            def _():
                line_copy(step, above, up_recv).wait_recv()
                o_ref[here(step)] += line_in[slot(step)]

            @pl.when(has_above)
            def _():
                last_copy(step).wait_recv()
                o_ref[here(step)] += own_in[here(step)]


def owner_sum(grad, count_dp, collective_id, pieces):
    lines = count_dp // 2
    total, width = grad.shape
    chunk = total // count_dp
    half = (lines * chunk, width)
    vmem = pl.BlockSpec(memory_space=pltpu.VMEM)
    return pl.pallas_call(
        functools.partial(owner_sum_kernel, lines, pieces),
        out_shape=jax.ShapeDtypeStruct((chunk, width), jnp.float32),
        in_specs=[vmem],
        out_specs=vmem,
        scratch_shapes=[
            pltpu.VMEM(half, jnp.bfloat16),
            pltpu.VMEM(half, jnp.bfloat16),
            pltpu.VMEM(half, jnp.float32),
            pltpu.VMEM(half, jnp.float32),
            pltpu.VMEM((chunk, width), jnp.float32),
        ]
        + [pltpu.SemaphoreType.DMA((lines * pieces,))] * 5,
        compiler_params=pltpu.CompilerParams(
            collective_id=collective_id, has_side_effects=True, vmem_limit_bytes=62 * 2**20
        ),
    )(grad)


def total_kernel(mine_ref, sum_ref, slots, own_sem, send_sem, recv_sem):
    first, second = lax.axis_size("dp"), lax.axis_size("tensor")
    count = first * second
    me = lax.axis_index("dp") * second + lax.axis_index("tensor")

    def peer(step):
        other = lax.rem(me + step, count)
        return {"dp": other // second, "tensor": lax.rem(other, second)}

    barrier = pltpu.get_barrier_semaphore()

    @pl.loop(1, count)
    def _(step):
        pl.semaphore_signal(barrier, inc=1, device_id=peer(step), device_id_type=MESH)

    pl.semaphore_wait(barrier, count - 1)
    own = pltpu.make_async_copy(mine_ref, slots.at[me], own_sem)
    own.start()

    def send(step):
        return pltpu.make_async_remote_copy(
            src_ref=mine_ref,
            dst_ref=slots.at[me],
            send_sem=send_sem.at[step],
            recv_sem=recv_sem.at[step],
            device_id=peer(step),
            device_id_type=MESH,
        )

    @pl.loop(1, count)
    def _(step):
        send(step).start()

    @pl.loop(1, count)
    def _(step):
        send(step).wait()

    own.wait()
    sum_ref[...] = jnp.sum(slots[...], 0)


def total_over_all(mine, collective_id):
    count = lax.axis_size("dp") * lax.axis_size("tensor")
    vmem = pl.BlockSpec(memory_space=pltpu.VMEM)
    return pl.pallas_call(
        total_kernel,
        out_shape=jax.ShapeDtypeStruct(mine.shape, jnp.float32),
        in_specs=[vmem],
        out_specs=vmem,
        scratch_shapes=[
            pltpu.VMEM((count,) + mine.shape, jnp.float32),
            pltpu.SemaphoreType.DMA(()),
            pltpu.SemaphoreType.DMA((count,)),
            pltpu.SemaphoreType.DMA((count,)),
        ],
        compiler_params=pltpu.CompilerParams(collective_id=collective_id, has_side_effects=True),
    )(mine)


def pack_qkv(matrix, parts):
    rows, cols = matrix.shape
    first = matrix[:, :512].reshape(parts, 2, rows // parts // 2, 512).transpose(0, 2, 1, 3)
    second = matrix[:, 512:].reshape(parts, 4, rows // parts // 4, 256).transpose(0, 2, 1, 3)
    return jnp.concatenate([first.reshape(parts, -1, 1024), second.reshape(parts, -1, 1024)], 1).reshape(-1, 1024)


def unpack_qkv(packed, parts):
    rows = packed.shape[0] // parts
    packed = packed.reshape(parts, rows, 1024)
    cut = rows * 2 // 3
    first = packed[:, :cut].reshape(parts, cut, 2, 512).transpose(0, 2, 1, 3).reshape(-1, 512)
    second = packed[:, cut:].reshape(parts, rows - cut, 4, 256).transpose(0, 2, 1, 3).reshape(-1, 256)
    return jnp.concatenate([first, second], 1)


def by_lanes(flat, outer):
    size = flat.size // math.prod(outer)
    return flat.reshape(outer + ((size // 128, 128) if size % 128 == 0 else (size,)))


def pad_first(array, axis, unit):
    short = -array.shape[axis] % unit
    return jnp.pad(array, [(0, short if at == axis else 0) for at in range(array.ndim)])


def sum_to_owners(stack, count_dp):
    if count_dp == 8:
        return owner_sum(stack, count_dp, 1, 9)
    return lax.psum_scatter(stack, "dp", scatter_dimension=0, tiled=True)

def adam_update(master, first_mom, second_mom, gradient, step_float):
    first_new = beta_one * first_mom + (1.0 - beta_one) * gradient
    second_new = beta_two * second_mom + (1.0 - beta_two) * gradient * gradient
    first_hat = first_new / (1.0 - jnp.power(beta_one, step_float))
    second_hat = second_new / (1.0 - jnp.power(beta_two, step_float))
    master_new = master - learn_rate * (
        first_hat / (jnp.sqrt(second_hat) + adam_eps) + decay_rate * master
    )
    return (master_new, first_new, second_new)


def per_device(
    patches,
    view_counts,
    splat_index,
    splat_dist,
    alpha_label,
    step_count,
    row_master,
    row_first,
    row_second,
    row_ema,
    shared_master,
    shared_first,
    shared_second,
    shared_ema,
):
    groups = lax.axis_size("tensor")
    my_dp = lax.axis_index("dp")
    count_dp = lax.axis_size("dp")
    local_width = D // groups
    local_hidden = FF // groups
    qkv_parts = count_dp // 4
    share_rows = row_master.shape[1] // D
    own_row = row_master[0].astype(jnp.bfloat16)
    own_tiles = jnp.where(
        my_dp < qkv_parts,
        pack_qkv(own_row.reshape(-1, 3 * local_width), 1),
        own_row.reshape(share_rows, D),
    )
    row_weights = lax.all_gather(own_tiles, "dp", axis=0, tiled=True)
    own_flat = shared_master.astype(jnp.bfloat16)
    own_shared = by_lanes(own_flat, ())
    lead = own_shared.shape[0]
    own_shared = pad_first(own_shared, 0, 2048 // own_shared[0].size)
    shared_weights = lax.all_gather(own_shared, "dp", axis=0, tiled=False)[:, :lead].reshape(-1, 128)
    qkv_rows = 3 * local_width
    out_end = qkv_rows + local_width
    up_end = out_end + local_hidden
    patch_rows = PIN * D // 128
    unpatch_rows = D * POUT // 128
    weights = (
        unpack_qkv(row_weights[:qkv_rows], qkv_parts),
        row_weights[qkv_rows:out_end],
        row_weights[out_end:up_end],
        row_weights[up_end:],
        shared_weights[patch_rows + unpatch_rows :].reshape(4, D).astype(jnp.float32),
    )
    patch_proj = shared_weights[:patch_rows].reshape(PIN, D)
    used_cols = shared_weights[patch_rows : patch_rows + unpatch_rows].reshape(D, POUT // 128, 128)[:, 0]
    own_patches = patches[0]
    row_count = own_patches.shape[0]
    key_valid = jnp.arange(row_count * groups) < view_counts[0] * VTOK
    embedded = jnp.dot(own_patches, patch_proj, preferred_element_type=jnp.float32)
    resid2, saved_values = layer_forward(embedded, weights, key_valid)
    resid2_low = resid2.astype(jnp.bfloat16)
    gauss_table = lax.all_gather(
        jnp.dot(resid2_low, used_cols, preferred_element_type=jnp.float32).astype(jnp.bfloat16),
        "tensor",
        axis=0,
        tiled=True,
    )
    loss_tile, table_grad = render(gauss_table, splat_index[0], splat_dist[0], alpha_label, PATCH * PATCH)
    loss_part = loss_tile[0, 0]
    gauss_grad = lax.psum_scatter(table_grad, "tensor", scatter_dimension=0, tiled=True)
    unpatch_used = contract_rows(resid2_low, gauss_grad)
    resid2_grad = contract_last(gauss_grad, used_cols)
    embed_grad, weight_grad, gain_grad = layer_backward(
        resid2_grad, weights, key_valid, saved_values
    )
    patch_grad = contract_rows(own_patches, embed_grad.astype(jnp.bfloat16))
    unpatch_grad = jnp.concatenate(
        [unpatch_used, jnp.zeros((D, POUT - unpatch_used.shape[1]), jnp.float32)], 1
    )
    shared_grad = jnp.concatenate(
        [patch_grad.reshape(-1), unpatch_grad.reshape(-1), gain_grad.reshape(-1)]
    )
    split_grad = by_lanes(shared_grad, (count_dp, groups))
    lead = split_grad.shape[2]
    shared_stack = pad_first(split_grad, 2, 16 * D // split_grad[0, 0, 0].size).swapaxes(0, 1)
    shared_sum = lax.psum_scatter(shared_stack, "tensor", scatter_dimension=0, tiled=True)
    qkv_grad, out_grad, up_grad, down_grad = weight_grad
    row_stack = jnp.concatenate([pack_qkv(qkv_grad, qkv_parts), out_grad, up_grad, down_grad], 0)
    stack = jnp.concatenate(
        [row_stack.reshape(count_dp, share_rows, D), shared_sum.reshape(count_dp, -1, D)], 1
    ).reshape(-1, D)
    own_share = sum_to_owners(stack, count_dp)
    own_rows = own_share[:share_rows]
    row_share = jnp.where(my_dp < qkv_parts, unpack_qkv(own_rows, 1).reshape(-1), own_rows.reshape(-1))
    shared_part = own_share[share_rows:].reshape((-1,) + split_grad.shape[3:])[:lead]
    shared_share = lax.all_gather(shared_part, "tensor", axis=0, tiled=False).reshape(-1)
    own_squares = jnp.sum(row_share * row_share) + jnp.sum(shared_part * shared_part)
    pixel_part = jnp.sum((alpha_label < 2).astype(jnp.float32))
    scalars = jnp.stack([own_squares, loss_part, pixel_part]).reshape(3, 1)
    totals = total_over_all(jnp.pad(jnp.broadcast_to(scalars, (3, 128)), ((0, 5), (0, 0))), 2)
    square_total, loss_total, pixel_total = totals[0, 0], totals[1, 0], totals[2, 0]
    norm_value = jnp.sqrt(square_total) / pixel_total
    factor = clip_norm / jnp.maximum(norm_value, clip_norm) / pixel_total
    step_float = step_count[0].astype(jnp.float32)
    row_new, row_first_new, row_second_new = adam_update(
        row_master[0], row_first[0], row_second[0], row_share * factor, step_float
    )
    shared_new, shared_first_new, shared_second_new = adam_update(
        shared_master, shared_first, shared_second, shared_share * factor, step_float
    )
    row_ema_new = ema_rate * row_ema[0] + (1.0 - ema_rate) * row_new
    shared_ema_new = ema_rate * shared_ema + (1.0 - ema_rate) * shared_new
    return (
        norm_value.reshape(1),
        (loss_total / pixel_total).reshape(1),
        row_new[None],
        row_first_new[None],
        row_second_new[None],
        row_ema_new[None],
        row_new.astype(jnp.bfloat16)[None],
        shared_new,
        shared_first_new,
        shared_second_new,
        shared_ema_new,
        shared_new.astype(jnp.bfloat16),
    )


def solution(mesh):
    placed = (
        P("dp", "tensor", None),
        P("dp"),
        P("dp", None, "tensor"),
        P("dp", None, "tensor"),
        P("dp", "tensor"),
        P(),
        P("tensor", "dp"),
        P("tensor", "dp"),
        P("tensor", "dp"),
        P("tensor", "dp"),
        P("dp"),
        P("dp"),
        P("dp"),
        P("dp"),
    )
    return jax.shard_map(
        per_device,
        mesh=mesh,
        in_specs=placed,
        out_specs=(
            P(),
            P(),
            P("tensor", "dp"),
            P("tensor", "dp"),
            P("tensor", "dp"),
            P("tensor", "dp"),
            P("tensor", "dp"),
            P("dp"),
            P("dp"),
            P("dp"),
            P("dp"),
            P("dp"),
        ),
        check_vma=False,
    )
```

```python
import math
from functools import partial

import jax
import jax.numpy as jnp
from jax import lax
from jax.experimental import pallas as pl
from jax.experimental.pallas import tpu as pltpu
from jax.sharding import PartitionSpec as P

D = 1024
DH = 64
FF = 4096
PATCH = 8
VTOK = 192
PIN = 576
POUT = 768
VMEM = pl.BlockSpec(memory_space=pltpu.VMEM)
ROOT_HALF = 0.5**0.5
NORMAL_PEAK = (2.0 * math.pi) ** -0.5


clip_norm = 0.005
beta_one = 0.9
beta_two = 0.95
adam_eps = 1e-08
decay_rate = 0.05
learn_rate = 0.03
ema_rate = 0.9
norm_eps = 1e-05
masked_score = -1e30


MESH = pl.DeviceIdType.MESH
NN = (((1,), (0,)), ((), ()))
NT = (((1,), (1,)), ((), ()))
TN = (((0,), (0,)), ((), ()))
LOW = jnp.bfloat16
WIDE = jnp.float32
PIECES = 4
TILE = 256


def dot(left, right, dims=NN):
    return lax.dot_general(left, right, dims, preferred_element_type=WIDE)


def remote(src, dst, send, recv, to):
    return pltpu.make_async_remote_copy(
        src_ref=src, dst_ref=dst, send_sem=send, recv_sem=recv, device_id=to, device_id_type=MESH
    )


class Corner:
    def __init__(self):
        self.me = lax.axis_index("tensor")
        self.first, self.last = self.me // 2, lax.rem(self.me, 2)
        self.mate = self.first * 2 + 1 - self.last
        self.far = (1 - self.first) * 2 + self.last
        self.opposite = (1 - self.first) * 2 + 1 - self.last

    def block(self, step):
        return lax.rem(self.first + 1 - step // 2, 2) * 2 + lax.rem(self.last + 1 - lax.rem(step, 2), 2)

    def greet(self):
        barrier = pltpu.get_barrier_semaphore()
        for other in (self.mate, self.far):
            pl.semaphore_signal(barrier, inc=1, device_id={"tensor": other}, device_id_type=MESH)
        pl.semaphore_wait(barrier, 2)


class Gather:
    def __init__(self, corner, ref, pieces, sems):
        self.corner, self.ref, self.pieces, self.sems = corner, ref, pieces, sems
        self.size = ref.shape[0] // 4
        self.rows = self.size // pieces

    @staticmethod
    def scratch(pieces):
        return [pltpu.SemaphoreType.DMA((pieces,))] * 6

    def part(self, owner, piece):
        return pl.ds(pl.multiple_of(owner * self.size + piece * self.rows, self.rows), self.rows)

    def copy(self, owner, piece, kind, to):
        here = self.ref.at[self.part(owner, piece)]
        return remote(here, here, self.sems[2 * kind].at[piece], self.sems[2 * kind + 1].at[piece], {"tensor": to})

    def start(self, piece):
        self.copy(self.corner.me, piece, 1, self.corner.far).start()
        self.copy(self.corner.me, piece, 0, self.corner.mate).start()

    def relay(self, piece):
        self.copy(self.corner.far, piece, 1, self.corner.far).wait_recv()
        self.copy(self.corner.far, piece, 2, self.corner.mate).start()

    def finish(self):
        corner = self.corner
        for piece in range(self.pieces):
            self.copy(corner.mate, piece, 0, corner.mate).wait_recv()
            self.copy(corner.opposite, piece, 2, corner.mate).wait_recv()
            self.copy(corner.me, piece, 0, corner.mate).wait_send()
            self.copy(corner.me, piece, 1, corner.far).wait_send()
            self.copy(corner.far, piece, 2, corner.mate).wait_send()


class Scatter:
    def __init__(self, corner, pieces, mate_out, mate_in, far_out, far_in, mate_send, mate_recv, far_send, far_recv):
        self.corner, self.pieces = corner, pieces
        self.mate_out, self.mate_in, self.far_out, self.far_in = mate_out, mate_in, far_out, far_in
        self.sems = mate_send, mate_recv, far_send, far_recv
        self.rows = far_out.shape[0] // pieces

    @staticmethod
    def scratch(rows, width, pieces):
        return [
            pltpu.VMEM((2, rows, width), LOW),
            pltpu.VMEM((2, rows, width), LOW),
            pltpu.VMEM((rows, width), LOW),
            pltpu.VMEM((rows, width), LOW),
            pltpu.SemaphoreType.DMA((2, pieces)),
            pltpu.SemaphoreType.DMA((2, pieces)),
            pltpu.SemaphoreType.DMA((pieces,)),
            pltpu.SemaphoreType.DMA((pieces,)),
        ]

    def part(self, piece):
        return pl.ds(piece * self.rows, self.rows)

    def mate_copy(self, half, piece):
        part = self.part(piece)
        return remote(
            self.mate_out.at[half, part],
            self.mate_in.at[half, part],
            self.sems[0].at[half, piece],
            self.sems[1].at[half, piece],
            {"tensor": self.corner.mate},
        )

    def far_copy(self, piece):
        part = self.part(piece)
        return remote(
            self.far_out.at[part],
            self.far_in.at[part],
            self.sems[2].at[piece],
            self.sems[3].at[piece],
            {"tensor": self.corner.far},
        )

    def give(self, half, ref):
        for piece in range(self.pieces):
            part = self.part(piece)
            self.mate_out[half, part] = ref[part].astype(LOW)
            self.mate_copy(half, piece).start()

    def cross(self, ref):
        for piece in range(self.pieces):
            part = self.part(piece)
            self.mate_copy(0, piece).wait_recv()
            self.far_out[part] = (ref[part] + self.mate_in[0, part].astype(WIDE)).astype(LOW)
            self.far_copy(piece).start()

    def step(self, step, ref):
        @pl.when(step == 0)
        def _():
            self.give(0, ref)

        @pl.when(step == 1)
        def _():
            self.cross(ref)

        @pl.when(step == 2)
        def _():
            self.give(1, ref)

    def land(self, piece, ref):
        part = self.part(piece)
        self.mate_copy(1, piece).wait_recv()
        self.far_copy(piece).wait_recv()
        return ref[part] + self.mate_in[1, part].astype(WIDE) + self.far_in[part].astype(WIDE)

    def close(self):
        for piece in range(self.pieces):
            self.mate_copy(0, piece).wait_send()
            self.mate_copy(1, piece).wait_send()
            self.far_copy(piece).wait_send()


def standard(values):
    centre = values - jnp.mean(values, -1, keepdims=True)
    inverse = lax.rsqrt(jnp.mean(centre * centre, -1, keepdims=True) + norm_eps)
    return centre * inverse, inverse


def norm_back(grad_out, scaled, inverse, gain):
    grad_scaled = grad_out * gain
    return inverse * (
        grad_scaled
        - jnp.mean(grad_scaled, -1, keepdims=True)
        - scaled * jnp.mean(grad_scaled * scaled, -1, keepdims=True)
    )


def qkv_places(parts, rows, columns):
    share = rows // parts
    wide = columns * 2 // 3
    packed = share * columns // 1024
    for at in range(parts):
        for j in range(2):
            half = share // 2
            yield (at * packed, half, j * wide, wide, at * share + j * half, 0)
        for j in range(4):
            quarter = share // 4
            yield (at * packed + share // 2, quarter, j * (columns - wide), columns - wide, at * share + j * quarter, wide)


def unpack_into(full, packed, parts):
    for row, rows, col, cols, to_row, to_col in qkv_places(parts, full.shape[0], full.shape[1]):
        full[to_row : to_row + rows, to_col : to_col + cols] = packed[row : row + rows, col : col + cols]


def pack_from(packed, full, parts, base=0):
    for row, rows, col, cols, to_row, to_col in qkv_places(parts, full.shape[0], full.shape[1]):
        packed[base + row : base + row + rows, col : col + cols] = full[to_row : to_row + rows, to_col : to_col + cols]


def rows_of(block, size):
    return pl.ds(pl.multiple_of(block * size, size), size)


def column_loop(width, body):
    @pl.loop(0, width // TILE)
    def _(tile):
        body(pl.ds(pl.multiple_of(tile * TILE, TILE), TILE))


def attend_kernel(parts, q_rows, count_ref, patch_ref, proj_ref, norm_ref, packed_ref, out_ref,
                  embed_ref, normed1_ref, qkv_ref, attended_ref, log_ref, resid_ref, normed2_ref,
                  qkv_proj, term, *comm):
    corner = Corner()
    corner.greet()
    scatter = Scatter(corner, PIECES, *comm[:8])
    gather = Gather(corner, normed2_ref, PIECES, comm[8:])
    size, width = embed_ref.shape
    length = patch_ref.shape[0]
    local = attended_ref.shape[1]
    unpack_into(qkv_proj, packed_ref, parts)

    @pl.loop(0, 4)
    def _(block):
        here = rows_of(block, size)
        column_loop(width, lambda cols: term.__setitem__((slice(None), cols), dot(patch_ref[here], proj_ref[:, cols])))

        @pl.when(block == corner.me)
        def _():
            embed_ref[...] = term[...]

        scaled, inverse = standard(term[...])
        normed1_ref[here] = (scaled * norm_ref[0:1] + norm_ref[1:2]).astype(LOW)

        def columns(cols):
            qkv_ref[here, cols] = dot(normed1_ref[here], qkv_proj[:, cols]).astype(LOW)

        column_loop(3 * local, columns)

    valid = lax.broadcasted_iota(jnp.int32, (1, length), 1) < count_ref[0] * VTOK
    left = lax.broadcasted_iota(jnp.int32, (1, 2 * DH), 1) < DH
    factor = jnp.array(DH ** (-0.5), LOW)

    @pl.loop(0, length // q_rows)
    def _(turn):
        here = rows_of(turn, q_rows)
        for pair in range(local // (2 * DH)):
            lanes = slice(pair * 2 * DH, (pair + 1) * 2 * DH)
            queries = qkv_ref[here, lanes] * factor
            keyset = qkv_ref[:, local + pair * 2 * DH : local + (pair + 1) * 2 * DH]
            values = qkv_ref[:, 2 * local + pair * 2 * DH : 2 * local + (pair + 1) * 2 * DH]
            found = []
            for side in range(2):
                mine = left if side == 0 else ~left
                scores = dot(jnp.where(mine, queries, jnp.zeros_like(queries)), keyset, NT)
                scores = jnp.where(valid, scores, masked_score)
                top = jnp.max(scores, -1, keepdims=True)
                powers = jnp.exp(scores - top)
                total = jnp.sum(powers, -1, keepdims=True)
                log_ref[here, pair * 2 + side : pair * 2 + side + 1] = top + jnp.log(total)
                found.append(dot((powers * (1.0 / total)).astype(LOW), values))
            attended_ref[here, lanes] = jnp.where(left, found[0], found[1]).astype(LOW)

    @pl.loop(0, 4)
    def _(step):
        here = rows_of(corner.block(step), size)
        column_loop(width, lambda cols: term.__setitem__((slice(None), cols), dot(attended_ref[here], out_ref[:, cols])))
        scatter.step(step, term)

    for piece in range(PIECES):
        part = scatter.part(piece)
        resid = embed_ref[part] + scatter.land(piece, term)
        resid_ref[part] = resid
        scaled, inverse = standard(resid)
        normed2_ref[gather.part(corner.me, piece)] = (scaled * norm_ref[2:3] + norm_ref[3:4]).astype(LOW)
        gather.start(piece)
    for piece in range(PIECES):
        gather.relay(piece)
    gather.finish()
    scatter.close()


def attend(count, patches, patch_proj, norm, packed, out_proj, parts, collective_id):
    length, size = patches.shape[0], patches.shape[0] // 4
    width, local = patch_proj.shape[1], out_proj.shape[0]
    shape = jax.ShapeDtypeStruct
    return pl.pallas_call(
        partial(attend_kernel, parts, 256),
        out_shape=(
            shape((size, width), WIDE),
            shape((length, width), LOW),
            shape((length, 3 * local), LOW),
            shape((length, local), LOW),
            shape((length, local // DH), WIDE),
            shape((size, width), WIDE),
            shape((length, width), LOW),
        ),
        in_specs=[pl.BlockSpec(memory_space=pltpu.SMEM)] + [VMEM] * 5,
        out_specs=(VMEM,) * 7,
        scratch_shapes=[pltpu.VMEM((width, 3 * local), LOW), pltpu.VMEM((size, width), WIDE)]
        + Scatter.scratch(size, width, PIECES)
        + Gather.scratch(PIECES),
        compiler_params=pltpu.CompilerParams(
            collective_id=collective_id, has_side_effects=True, vmem_limit_bytes=62 * 2**20
        ),
    )(count, patches, patch_proj, norm, packed, out_proj)


def mlp_kernel(normed2_ref, up_ref, down_ref, resid1_ref, cols_ref, hidden_ref, active_ref, low_ref, table_ref, term, *comm):
    corner = Corner()
    corner.greet()
    scatter = Scatter(corner, PIECES, *comm[:8])
    gather = Gather(corner, table_ref, PIECES, comm[8:])
    size, width = resid1_ref.shape

    @pl.loop(0, 4)
    def _(step):
        here = rows_of(corner.block(step), size)

        def columns(cols):
            hidden = dot(normed2_ref[here], up_ref[:, cols])
            hidden_ref[here, cols] = hidden
            active_ref[here, cols] = (0.5 * hidden * (1.0 + lax.erf(hidden * ROOT_HALF))).astype(LOW)

        column_loop(up_ref.shape[1], columns)
        column_loop(width, lambda cols: term.__setitem__((slice(None), cols), dot(active_ref[here], down_ref[:, cols])))
        scatter.step(step, term)

    for piece in range(PIECES):
        part = scatter.part(piece)
        low_ref[part] = (resid1_ref[part] + scatter.land(piece, term)).astype(LOW)
        table_ref[gather.part(corner.me, piece)] = dot(low_ref[part], cols_ref[...]).astype(LOW)
        gather.start(piece)
    for piece in range(PIECES):
        gather.relay(piece)
    gather.finish()
    scatter.close()


def mlp(normed2, up_proj, down_proj, resid1, used_cols, collective_id):
    length, size, width = normed2.shape[0], resid1.shape[0], resid1.shape[1]
    hidden = up_proj.shape[1]
    shape = jax.ShapeDtypeStruct
    return pl.pallas_call(
        mlp_kernel,
        out_shape=(
            shape((length, hidden), WIDE),
            shape((length, hidden), LOW),
            shape((size, width), LOW),
            shape((length, used_cols.shape[1]), LOW),
        ),
        in_specs=[VMEM] * 5,
        out_specs=(VMEM,) * 4,
        scratch_shapes=[pltpu.VMEM((size, width), WIDE)]
        + Scatter.scratch(size, width, PIECES)
        + Gather.scratch(PIECES),
        compiler_params=pltpu.CompilerParams(
            collective_id=collective_id, has_side_effects=True, vmem_limit_bytes=62 * 2**20
        ),
    )(normed2, up_proj, down_proj, resid1, used_cols)


def mlp_back_kernel(table_ref, cols_ref, low_ref, active_ref, hidden_ref, normed2_ref, up_ref, down_ref, resid1_ref, norm_ref,
                    unpatch_ref, grad_ref, resid_grad_ref, branch_ref, gain_ref,
                    gauss, down_in, hidden_grad, term, tail, *comm):
    corner = Corner()
    corner.greet()
    small = Scatter(corner, 1, *comm[:8])
    spread = Gather(corner, gauss, 1, comm[8:14])
    scatter = Scatter(corner, PIECES, *comm[14:22])
    gather = Gather(corner, branch_ref, PIECES, comm[22:])
    size, width = resid1_ref.shape
    ff = up_ref.shape[1]

    def view(step):
        return table_ref.at[rows_of(corner.block(step), size)]

    tail[...] = view(0)[...].astype(WIDE)
    small.give(0, tail)
    tail[...] = view(1)[...].astype(WIDE)
    small.cross(tail)
    tail[...] = view(2)[...].astype(WIDE)
    small.give(1, tail)
    tail[...] = view(3)[...].astype(WIDE)
    own_gauss = small.land(0, tail).astype(LOW)
    gauss[spread.part(corner.me, 0)] = own_gauss
    spread.start(0)
    unpatch_ref[...] = dot(low_ref[...], own_gauss, TN)
    spread.relay(0)
    spread.finish()
    small.close()

    @pl.loop(0, 4)
    def _(step):
        here = rows_of(corner.block(step), size)
        term[...] = dot(gauss[here], cols_ref[...], NT)
        down_in[here] = term[...].astype(LOW)

        @pl.when(step == 3)
        def _():
            resid_grad_ref[...] = term[...]

        def columns(cols):
            active_grad = dot(down_in[here], down_ref[cols, :], NT)
            hidden = hidden_ref[here, cols]
            slope = 0.5 * (1.0 + lax.erf(hidden * ROOT_HALF)) + hidden * (jnp.exp(-0.5 * hidden * hidden) * NORMAL_PEAK)
            hidden_grad[here, cols] = (active_grad * slope).astype(LOW)

        column_loop(ff, columns)

        def back(cols):
            term[:, cols] = dot(hidden_grad[here], up_ref[cols, :], NT)

        column_loop(width, back)
        scatter.step(step, term)

    @pl.loop(0, width // TILE)
    def _(tile):
        cols = pl.ds(pl.multiple_of(tile * TILE, TILE), TILE)
        grad_ref[cols, :] = dot(normed2_ref[:, cols], hidden_grad[...], TN)

    @pl.loop(0, ff // TILE)
    def _(tile):
        cols = pl.ds(pl.multiple_of(tile * TILE, TILE), TILE)
        grad_ref[pl.ds(pl.multiple_of(width + tile * TILE, TILE), TILE), :] = dot(active_ref[:, cols], down_in[...], TN)

    gain_sum, bias_sum = jnp.zeros((1, width), WIDE), jnp.zeros((1, width), WIDE)
    for piece in range(PIECES):
        part = scatter.part(piece)
        grad = scatter.land(piece, term)
        scaled, inverse = standard(resid1_ref[part])
        total = resid_grad_ref[part] + norm_back(grad, scaled, inverse, norm_ref[2:3])
        resid_grad_ref[part] = total
        branch_ref[gather.part(corner.me, piece)] = total.astype(LOW)
        gather.start(piece)
        gain_sum += jnp.sum(grad * scaled, 0, keepdims=True)
        bias_sum += jnp.sum(grad, 0, keepdims=True)
    gain_ref[0:1] = gain_sum
    gain_ref[1:2] = bias_sum
    for piece in range(PIECES):
        gather.relay(piece)
    gather.finish()
    scatter.close()


def mlp_back(table_grad, used_cols, low, active, hidden, normed2, up_proj, down_proj, resid1, norm, collective_id):
    length, size, width = normed2.shape[0], resid1.shape[0], resid1.shape[1]
    ff, used = up_proj.shape[1], used_cols.shape[1]
    shape = jax.ShapeDtypeStruct
    return pl.pallas_call(
        mlp_back_kernel,
        out_shape=(
            shape((width, used), WIDE),
            shape((width + ff, width), WIDE),
            shape((size, width), WIDE),
            shape((length, width), LOW),
            shape((2, width), WIDE),
        ),
        in_specs=[VMEM] * 10,
        out_specs=(VMEM,) * 5,
        scratch_shapes=[
            pltpu.VMEM((length, used), LOW),
            pltpu.VMEM((length, width), LOW),
            pltpu.VMEM((length, ff), LOW),
            pltpu.VMEM((size, width), WIDE),
            pltpu.VMEM((size, used), WIDE),
        ]
        + Scatter.scratch(size, used, 1)
        + Gather.scratch(1)
        + Scatter.scratch(size, width, PIECES)
        + Gather.scratch(PIECES),
        compiler_params=pltpu.CompilerParams(
            collective_id=collective_id, has_side_effects=True, vmem_limit_bytes=63 * 2**20
        ),
    )(table_grad, used_cols, low, active, hidden, normed2, up_proj, down_proj, resid1, norm)


def attend_back_kernel(parts, q_rows, count_ref, branch_ref, out_ref, qkv_ref, log_ref, packed_ref, attended_ref, normed1_ref, embed_ref,
                       resid_grad_ref, norm_ref, patch_ref, grad_ref, patch_grad_ref, gain_ref,
                       qkv_proj, attended_grad, qkv_grad, key_grad, value_grad, full_grad, term, embed_grad, *comm):
    corner = Corner()
    corner.greet()
    scatter = Scatter(corner, PIECES, *comm)
    size, width = embed_ref.shape
    length, local = attended_ref.shape
    unpack_into(qkv_proj, packed_ref, parts)

    @pl.loop(0, 4)
    def _(block):
        here = rows_of(block, size)
        attended_grad[here] = dot(branch_ref[here], out_ref[...], NT).astype(LOW)

    key_grad[...] = jnp.zeros_like(key_grad)
    value_grad[...] = jnp.zeros_like(value_grad)
    valid = lax.broadcasted_iota(jnp.int32, (1, length), 1) < count_ref[0] * VTOK
    left = lax.broadcasted_iota(jnp.int32, (1, 2 * DH), 1) < DH
    factor = jnp.array(DH ** (-0.5), LOW)

    @pl.loop(0, length // q_rows)
    def _(turn):
        here = rows_of(turn, q_rows)
        for pair in range(local // (2 * DH)):
            lanes = slice(pair * 2 * DH, (pair + 1) * 2 * DH)
            queries = qkv_ref[here, lanes] * factor
            grads = attended_grad[here, lanes]
            keyset = qkv_ref[:, local + pair * 2 * DH : local + (pair + 1) * 2 * DH]
            values = qkv_ref[:, 2 * local + pair * 2 * DH : 2 * local + (pair + 1) * 2 * DH]
            found = []
            for side in range(2):
                mine = left if side == 0 else ~left
                own_query = jnp.where(mine, queries, jnp.zeros_like(queries))
                own_grad = jnp.where(mine, grads, jnp.zeros_like(grads))
                scores = jnp.where(valid, dot(own_query, keyset, NT), masked_score)
                probs = jnp.exp(scores - log_ref[here, pair * 2 + side : pair * 2 + side + 1])
                prob_grad = dot(own_grad, values, NT)
                value_grad[:, lanes] += dot(probs.astype(LOW), own_grad, TN)
                centre = jnp.sum(probs * prob_grad, -1, keepdims=True)
                score_grad = (probs * (prob_grad - centre)).astype(LOW)
                found.append(dot(score_grad, keyset))
                key_grad[:, lanes] += dot(score_grad, own_query, TN)
            qkv_grad[here, lanes] = (jnp.where(left, found[0], found[1]) * (DH ** (-0.5))).astype(LOW)

    qkv_grad[:, local : 2 * local] = key_grad[...].astype(LOW)
    qkv_grad[:, 2 * local :] = value_grad[...].astype(LOW)

    @pl.loop(0, 4)
    def _(step):
        here = rows_of(corner.block(step), size)

        def columns(cols):
            term[:, cols] = dot(qkv_grad[here], qkv_proj[cols, :], NT)

        column_loop(width, columns)
        scatter.step(step, term)

    grad_ref[grad_ref.shape[0] - local :, :] = dot(attended_ref[...], branch_ref[...], TN)

    @pl.loop(0, width // TILE)
    def _(tile):
        cols = pl.ds(pl.multiple_of(tile * TILE, TILE), TILE)
        full_grad[cols, :] = dot(normed1_ref[:, cols], qkv_grad[...], TN)

    pack_from(grad_ref, full_grad, parts)

    gain_sum, bias_sum = jnp.zeros((1, width), WIDE), jnp.zeros((1, width), WIDE)
    for piece in range(PIECES):
        part = scatter.part(piece)
        grad = scatter.land(piece, term)
        scaled, inverse = standard(embed_ref[part])
        embed_grad[part] = (resid_grad_ref[part] + norm_back(grad, scaled, inverse, norm_ref[0:1])).astype(LOW)
        gain_sum += jnp.sum(grad * scaled, 0, keepdims=True)
        bias_sum += jnp.sum(grad, 0, keepdims=True)
    gain_ref[0:1] = gain_sum
    gain_ref[1:2] = bias_sum
    patch_grad_ref[...] = dot(patch_ref[...], embed_grad[...], TN)
    scatter.close()


def attend_back(count, branch, out_proj, qkv, log_total, packed, attended, normed1, embed, resid_grad, norm, patches, parts, collective_id):
    length, local = attended.shape
    size, width = embed.shape
    shape = jax.ShapeDtypeStruct
    return pl.pallas_call(
        partial(attend_back_kernel, parts, 256),
        out_shape=(
            shape((4 * local, width), WIDE),
            shape((patches.shape[1], width), WIDE),
            shape((2, width), WIDE),
        ),
        in_specs=[pl.BlockSpec(memory_space=pltpu.SMEM)] + [VMEM] * 11,
        out_specs=(VMEM,) * 3,
        scratch_shapes=[
            pltpu.VMEM((width, 3 * local), LOW),
            pltpu.VMEM((length, local), LOW),
            pltpu.VMEM((length, 3 * local), LOW),
            pltpu.VMEM((length, local), WIDE),
            pltpu.VMEM((length, local), WIDE),
            pltpu.VMEM((width, 3 * local), WIDE),
            pltpu.VMEM((size, width), WIDE),
            pltpu.VMEM((size, width), LOW),
        ]
        + Scatter.scratch(size, width, PIECES),
        compiler_params=pltpu.CompilerParams(
            collective_id=collective_id, has_side_effects=True, vmem_limit_bytes=62 * 2**20
        ),
    )(count, branch, out_proj, qkv, log_total, packed, attended, normed1, embed, resid_grad, norm, patches)


def render_kernel(area, wide, block, split, table_ref, splat_ref, dist_ref, label_ref, loss_ref, grad_ref, flip, picked, hot, spread_grad):
    tokens = table_ref.shape[0]
    groups = tokens // wide
    splats, pixels = splat_ref.shape
    for j in range(groups):
        flip[j * 2 * area : (j + 1) * 2 * area] = jnp.transpose(table_ref[j * wide : (j + 1) * wide].astype(jnp.float32)).astype(jnp.bfloat16)
    spread_grad[...] = jnp.zeros_like(spread_grad)
    wide_ids = lax.broadcasted_iota(jnp.int32, (wide, block), 0).astype(jnp.float32).astype(jnp.bfloat16)
    cell_ids = lax.broadcasted_iota(jnp.int32, (area, block), 0).astype(jnp.float32)
    cell_low = cell_ids.astype(jnp.bfloat16)
    one, nil = jnp.ones((wide, block), jnp.bfloat16), jnp.zeros((wide, block), jnp.bfloat16)

    def one_block(step, loss):
        here = pl.ds(pl.multiple_of(step * block, block), block)
        opacities, spreads, lows = [], [], []
        for k in range(splats):
            index = splat_ref[k : k + 1, here]
            token = index // area
            column = (token % wide).astype(jnp.float32).astype(jnp.bfloat16)
            group = (token // wide)
            cell = (index % area).astype(jnp.float32)
            match = jnp.where(wide_ids == column, one, nil)
            hot[k] = match
            picked[...] = lax.dot_general(flip[...], match, NN, preferred_element_type=jnp.float32)
            op_sum = jnp.zeros((area, block), jnp.float32)
            sp_sum = jnp.zeros((area, block), jnp.float32)
            for j in range(groups):
                same = cell_ids == jnp.where(group == j, cell, -1.0)
                op_sum += jnp.where(same, picked[j * 2 * area : j * 2 * area + area], 0.0)
                sp_sum += jnp.where(same, picked[j * 2 * area + area : (j + 1) * 2 * area], 0.0)
            opacities.append(jnp.sum(op_sum, 0, keepdims=True))
            spreads.append(jnp.sum(sp_sum, 0, keepdims=True))
            lows.append((group, cell))
        opacity, spread = jnp.concatenate(opacities, 0), jnp.concatenate(spreads, 0)
        distance = dist_ref[:, here].astype(jnp.float32)
        labels = label_ref[:, here]
        valid = jnp.where(labels < 2, 1.0, 0.0)
        target = jnp.where(labels == 1, 1.0, 0.0)
        op_sig, sp_sig = jax.nn.sigmoid(opacity), jax.nn.sigmoid(spread)
        fade = jnp.exp(-0.25 * distance * sp_sig)
        contrib = (0.02 + 0.96 * op_sig) * fade
        keep_log = jnp.sum(jnp.log1p(-contrib), 0, keepdims=True)
        keep = jnp.exp(keep_log)
        alpha = 1.0 - keep
        alpha_log = jnp.log(alpha)
        loss = loss - valid * (target * alpha_log + (1.0 - target) * keep_log)
        keep_grad = valid * (target * keep / alpha - (1.0 - target))
        contrib_grad = -keep_grad / (1.0 - contrib)
        op_grad = contrib_grad * (0.96 * op_sig * (1.0 - op_sig)) * fade
        sp_grad = contrib_grad * contrib * (-0.25 * distance * sp_sig * (1.0 - sp_sig))
        for k in range(splats):
            group, cell = lows[k]
            parts_op, parts_sp = op_grad[k : k + 1], sp_grad[k : k + 1]
            for part in range(split):
                low_op, low_sp = parts_op.astype(jnp.bfloat16), parts_sp.astype(jnp.bfloat16)
                parts_op, parts_sp = parts_op - low_op.astype(jnp.float32), parts_sp - low_sp.astype(jnp.float32)
                pieces = []
                for j in range(groups):
                    same = cell_low == jnp.where(group == j, cell, -1.0).astype(jnp.bfloat16)
                    pieces.append(jnp.where(same, low_op, jnp.bfloat16(0)))
                    pieces.append(jnp.where(same, low_sp, jnp.bfloat16(0)))
                weighted = jnp.concatenate(pieces, 0)
                spread_grad[...] += lax.dot_general(weighted, hot[k], NT, preferred_element_type=jnp.float32)
        return loss

    loss = lax.fori_loop(0, pixels // block, one_block, jnp.zeros((1, block), jnp.float32))
    loss_ref[...] = jnp.broadcast_to(jnp.sum(loss, 1, keepdims=True), loss_ref.shape)
    for j in range(groups):
        grad_ref[j * wide : (j + 1) * wide] = jnp.transpose(spread_grad[j * 2 * area : (j + 1) * 2 * area]).astype(grad_ref.dtype)

def render(table, splats, distance, labels, area, block=512, wide=256, split=2):
    tokens = table.shape[0]
    vm = pl.BlockSpec(memory_space=pltpu.VMEM)
    groups = tokens // wide
    return pl.pallas_call(
        partial(render_kernel, area, wide, block, split),
        out_shape=(jax.ShapeDtypeStruct((8, 128), jnp.float32), jax.ShapeDtypeStruct(table.shape, jnp.bfloat16)),
        in_specs=[vm] * 4, out_specs=(vm, vm),
        scratch_shapes=[pltpu.VMEM((groups * 2 * area, wide), jnp.bfloat16), pltpu.VMEM((groups * 2 * area, block), jnp.float32),
            pltpu.VMEM((splats.shape[0], wide, block), jnp.bfloat16), pltpu.VMEM((groups * 2 * area, wide), jnp.float32)],
        compiler_params=pltpu.CompilerParams(vmem_limit_bytes=48 * 2**20),
    )(table, splats, distance, labels)


def owner_sum_kernel(lines, pieces, g_ref, o_ref, pair_out, pair_in, part, line_in, own_in, p_send, p_recv, l_send, up_recv, down_recv):
    me = lax.axis_index("dp")
    line, side = me // 2, lax.rem(me, 2)
    chunk = o_ref.shape[0]
    rows = chunk // pieces
    count = lines * pieces
    pair = {"dp": line * 2 + 1 - side}
    above = {"dp": lax.rem(line + 1, lines) * 2 + side}
    below = {"dp": lax.rem(line + lines - 1, lines) * 2 + side}
    has_below, has_above = line > 0, line < lines - 1

    def target(step):
        turn = lax.rem(step, lines)
        odd = lax.rem(turn, 2)
        return (1 - odd) * (lines - 1 - turn // 2) + odd * (turn // 2)

    def slot(step):
        return pl.ds(pl.multiple_of(step * rows, rows), rows)

    def here(step):
        return pl.ds(pl.multiple_of(step // lines * rows, rows), rows)

    def source(step, owner):
        return pl.ds(pl.multiple_of((target(step) * 2 + owner) * chunk + step // lines * rows, rows), rows)

    def copy(src, dst, send, recv, to):
        return pltpu.make_async_remote_copy(
            src_ref=src, dst_ref=dst, send_sem=send, recv_sem=recv, device_id=to, device_id_type=MESH
        )

    def pair_copy(step):
        return copy(pair_out.at[slot(step)], pair_in.at[slot(step)], p_send.at[step], p_recv.at[step], pair)

    def line_copy(step, to, recv):
        return copy(part.at[slot(step)], line_in.at[slot(step)], l_send.at[step], recv.at[step], to)

    def last_copy(step):
        return copy(part.at[slot(step)], own_in.at[here(step)], l_send.at[step], down_recv.at[step], below)

    barrier = pltpu.get_barrier_semaphore()
    pl.semaphore_signal(barrier, inc=1, device_id=pair, device_id_type=MESH)

    @pl.when(has_below)
    def _():
        pl.semaphore_signal(barrier, inc=1, device_id=below, device_id_type=MESH)

    @pl.when(has_above)
    def _():
        pl.semaphore_signal(barrier, inc=1, device_id=above, device_id_type=MESH)

    pl.semaphore_wait(barrier, 1 + jnp.minimum(line, 1) + jnp.minimum(lines - 1 - line, 1))

    @pl.loop(0, count)
    def _(step):
        pair_out[slot(step)] = g_ref[source(step, 1 - side)].astype(jnp.bfloat16)
        pair_copy(step).start()

    @pl.loop(0, count + lines - 1)
    def _(step):
        @pl.when(step < count)
        def _():
            pair_copy(step).wait_recv()
            part[slot(step)] = g_ref[source(step, side)].astype(jnp.float32) + pair_in[slot(step)].astype(jnp.float32)

        rising = step - line

        @pl.when((rising >= 0) & (rising < count) & (target(rising) > line))
        def _():
            @pl.when(has_below)
            def _():
                line_copy(rising, above, up_recv).wait_recv()
                part[slot(rising)] += line_in[slot(rising)]

            line_copy(rising, above, up_recv).start()

        falling = step - (lines - 1 - line)

        @pl.when((falling >= 0) & (falling < count) & (target(falling) < line))
        def _():
            @pl.when(has_above)
            def _():
                line_copy(falling, below, down_recv).wait_recv()
                part[slot(falling)] += line_in[slot(falling)]

            @pl.when(target(falling) == line - 1)
            def _():
                last_copy(falling).start()

            @pl.when(target(falling) < line - 1)
            def _():
                line_copy(falling, below, down_recv).start()

    @pl.loop(0, count)
    def _(step):
        pair_copy(step).wait_send()

        @pl.when(target(step) > line)
        def _():
            line_copy(step, above, up_recv).wait_send()

        @pl.when(target(step) < line)
        def _():
            line_copy(step, below, down_recv).wait_send()

        @pl.when(target(step) == line)
        def _():
            o_ref[here(step)] = part[slot(step)]

            @pl.when(has_below)
            def _():
                line_copy(step, above, up_recv).wait_recv()
                o_ref[here(step)] += line_in[slot(step)]

            @pl.when(has_above)
            def _():
                last_copy(step).wait_recv()
                o_ref[here(step)] += own_in[here(step)]


def owner_sum(grad, count_dp, collective_id, pieces):
    lines = count_dp // 2
    total, width = grad.shape
    chunk = total // count_dp
    half = (lines * chunk, width)
    vmem = pl.BlockSpec(memory_space=pltpu.VMEM)
    return pl.pallas_call(
        partial(owner_sum_kernel, lines, pieces),
        out_shape=jax.ShapeDtypeStruct((chunk, width), jnp.float32),
        in_specs=[vmem],
        out_specs=vmem,
        scratch_shapes=[
            pltpu.VMEM(half, jnp.bfloat16),
            pltpu.VMEM(half, jnp.bfloat16),
            pltpu.VMEM(half, jnp.float32),
            pltpu.VMEM(half, jnp.float32),
            pltpu.VMEM((chunk, width), jnp.float32),
        ]
        + [pltpu.SemaphoreType.DMA((lines * pieces,))] * 5,
        compiler_params=pltpu.CompilerParams(
            collective_id=collective_id, has_side_effects=True, vmem_limit_bytes=62 * 2**20
        ),
    )(grad)


def total_kernel(mine_ref, sum_ref, slots, own_sem, send_sem, recv_sem):
    first, second = lax.axis_size("dp"), lax.axis_size("tensor")
    count = first * second
    me = lax.axis_index("dp") * second + lax.axis_index("tensor")

    def peer(step):
        other = lax.rem(me + step, count)
        return {"dp": other // second, "tensor": lax.rem(other, second)}

    barrier = pltpu.get_barrier_semaphore()

    @pl.loop(1, count)
    def _(step):
        pl.semaphore_signal(barrier, inc=1, device_id=peer(step), device_id_type=MESH)

    pl.semaphore_wait(barrier, count - 1)
    own = pltpu.make_async_copy(mine_ref, slots.at[me], own_sem)
    own.start()

    def send(step):
        return pltpu.make_async_remote_copy(
            src_ref=mine_ref,
            dst_ref=slots.at[me],
            send_sem=send_sem.at[step],
            recv_sem=recv_sem.at[step],
            device_id=peer(step),
            device_id_type=MESH,
        )

    @pl.loop(1, count)
    def _(step):
        send(step).start()

    @pl.loop(1, count)
    def _(step):
        send(step).wait()

    own.wait()
    sum_ref[...] = jnp.sum(slots[...], 0)


def total_over_all(mine, collective_id):
    count = lax.axis_size("dp") * lax.axis_size("tensor")
    vmem = pl.BlockSpec(memory_space=pltpu.VMEM)
    return pl.pallas_call(
        total_kernel,
        out_shape=jax.ShapeDtypeStruct(mine.shape, jnp.float32),
        in_specs=[vmem],
        out_specs=vmem,
        scratch_shapes=[
            pltpu.VMEM((count,) + mine.shape, jnp.float32),
            pltpu.SemaphoreType.DMA(()),
            pltpu.SemaphoreType.DMA((count,)),
            pltpu.SemaphoreType.DMA((count,)),
        ],
        compiler_params=pltpu.CompilerParams(collective_id=collective_id, has_side_effects=True),
    )(mine)


def pack_qkv(matrix, parts):
    rows, cols = matrix.shape
    first = matrix[:, :512].reshape(parts, 2, rows // parts // 2, 512).transpose(0, 2, 1, 3)
    second = matrix[:, 512:].reshape(parts, 4, rows // parts // 4, 256).transpose(0, 2, 1, 3)
    return jnp.concatenate([first.reshape(parts, -1, 1024), second.reshape(parts, -1, 1024)], 1).reshape(-1, 1024)


def unpack_qkv(packed, parts):
    rows = packed.shape[0] // parts
    packed = packed.reshape(parts, rows, 1024)
    cut = rows * 2 // 3
    first = packed[:, :cut].reshape(parts, cut, 2, 512).transpose(0, 2, 1, 3).reshape(-1, 512)
    second = packed[:, cut:].reshape(parts, rows - cut, 4, 256).transpose(0, 2, 1, 3).reshape(-1, 256)
    return jnp.concatenate([first, second], 1)


def by_lanes(flat, outer):
    size = flat.size // math.prod(outer)
    return flat.reshape(outer + ((size // 128, 128) if size % 128 == 0 else (size,)))


def pad_first(array, axis, unit):
    short = -array.shape[axis] % unit
    return jnp.pad(array, [(0, short if at == axis else 0) for at in range(array.ndim)])


def sum_to_owners(stack, count_dp):
    if count_dp == 8:
        return owner_sum(stack, count_dp, 1, 9)
    return lax.psum_scatter(stack, "dp", scatter_dimension=0, tiled=True)

def adam_update(master, first_mom, second_mom, gradient, step_float):
    first_new = beta_one * first_mom + (1.0 - beta_one) * gradient
    second_new = beta_two * second_mom + (1.0 - beta_two) * gradient * gradient
    first_hat = first_new / (1.0 - jnp.power(beta_one, step_float))
    second_hat = second_new / (1.0 - jnp.power(beta_two, step_float))
    master_new = master - learn_rate * (
        first_hat / (jnp.sqrt(second_hat) + adam_eps) + decay_rate * master
    )
    return (master_new, first_new, second_new)


def per_device(
    patches,
    view_counts,
    splat_index,
    splat_dist,
    alpha_label,
    step_count,
    row_master,
    row_first,
    row_second,
    row_ema,
    shared_master,
    shared_first,
    shared_second,
    shared_ema,
):
    groups = lax.axis_size("tensor")
    my_dp = lax.axis_index("dp")
    count_dp = lax.axis_size("dp")
    local_width = D // groups
    local_hidden = FF // groups
    qkv_parts = count_dp // 4
    share_rows = row_master.shape[1] // D
    own_row = row_master[0].astype(jnp.bfloat16)
    own_tiles = jnp.where(
        my_dp < qkv_parts,
        pack_qkv(own_row.reshape(-1, 3 * local_width), 1),
        own_row.reshape(share_rows, D),
    )
    row_weights = lax.all_gather(own_tiles, "dp", axis=0, tiled=True)
    own_flat = shared_master.astype(jnp.bfloat16)
    own_shared = by_lanes(own_flat, ())
    lead = own_shared.shape[0]
    own_shared = pad_first(own_shared, 0, 2048 // own_shared[0].size)
    shared_weights = lax.all_gather(own_shared, "dp", axis=0, tiled=False)[:, :lead].reshape(-1, 128)
    qkv_rows = 3 * local_width
    out_end = qkv_rows + local_width
    up_end = out_end + local_hidden
    patch_rows = PIN * D // 128
    unpatch_rows = D * POUT // 128
    packed_qkv = row_weights[:qkv_rows]
    out_proj = row_weights[qkv_rows:out_end]
    up_proj = row_weights[out_end:up_end]
    down_proj = row_weights[up_end:]
    norm = shared_weights[patch_rows + unpatch_rows :].reshape(4, D).astype(jnp.float32)
    patch_proj = shared_weights[:patch_rows].reshape(PIN, D)
    used_cols = shared_weights[patch_rows : patch_rows + unpatch_rows].reshape(D, POUT // 128, 128)[:, 0]
    own_patches = patches[0]
    all_patches = lax.all_gather(own_patches, "tensor", axis=0, tiled=True)
    embed, normed1, qkv, attended, log_total, resid1, normed2 = attend(
        view_counts, all_patches, patch_proj, norm, packed_qkv, out_proj, qkv_parts, 3
    )
    hidden, active, resid2_low, gauss_table = mlp(normed2, up_proj, down_proj, resid1, used_cols, 4)
    loss_tile, table_grad = render(gauss_table, splat_index[0], splat_dist[0], alpha_label, PATCH * PATCH)
    loss_part = loss_tile[0, 0]
    unpatch_used, late_grad, resid_grad, branch, gain2_grad = mlp_back(
        table_grad, used_cols, resid2_low, active, hidden, normed2, up_proj, down_proj, resid1, norm, 5
    )
    early_grad, patch_grad, gain1_grad = attend_back(
        view_counts, branch, out_proj, qkv, log_total, packed_qkv, attended, normed1, embed, resid_grad, norm, own_patches, qkv_parts, 6
    )
    gain_grad = jnp.concatenate([gain1_grad, gain2_grad], 0)
    unpatch_grad = jnp.concatenate(
        [unpatch_used, jnp.zeros((D, POUT - unpatch_used.shape[1]), jnp.float32)], 1
    )
    shared_grad = jnp.concatenate(
        [patch_grad.reshape(-1), unpatch_grad.reshape(-1), gain_grad.reshape(-1)]
    )
    split_grad = by_lanes(shared_grad, (count_dp, groups))
    lead = split_grad.shape[2]
    shared_stack = pad_first(split_grad, 2, 16 * D // split_grad[0, 0, 0].size).swapaxes(0, 1)
    shared_sum = lax.psum_scatter(shared_stack, "tensor", scatter_dimension=0, tiled=True)
    row_stack = jnp.concatenate([early_grad, late_grad], 0)
    stack = jnp.concatenate(
        [row_stack.reshape(count_dp, share_rows, D), shared_sum.reshape(count_dp, -1, D)], 1
    ).reshape(-1, D)
    own_share = sum_to_owners(stack, count_dp)
    own_rows = own_share[:share_rows]
    row_share = jnp.where(my_dp < qkv_parts, unpack_qkv(own_rows, 1).reshape(-1), own_rows.reshape(-1))
    shared_part = own_share[share_rows:].reshape((-1,) + split_grad.shape[3:])[:lead]
    shared_share = lax.all_gather(shared_part, "tensor", axis=0, tiled=False).reshape(-1)
    own_squares = jnp.sum(row_share * row_share) + jnp.sum(shared_part * shared_part)
    pixel_part = jnp.sum((alpha_label < 2).astype(jnp.float32))
    scalars = jnp.stack([own_squares, loss_part, pixel_part]).reshape(3, 1)
    totals = total_over_all(jnp.pad(jnp.broadcast_to(scalars, (3, 128)), ((0, 5), (0, 0))), 2)
    square_total, loss_total, pixel_total = totals[0, 0], totals[1, 0], totals[2, 0]
    norm_value = jnp.sqrt(square_total) / pixel_total
    factor = clip_norm / jnp.maximum(norm_value, clip_norm) / pixel_total
    step_float = step_count[0].astype(jnp.float32)
    row_new, row_first_new, row_second_new = adam_update(
        row_master[0], row_first[0], row_second[0], row_share * factor, step_float
    )
    shared_new, shared_first_new, shared_second_new = adam_update(
        shared_master, shared_first, shared_second, shared_share * factor, step_float
    )
    row_ema_new = ema_rate * row_ema[0] + (1.0 - ema_rate) * row_new
    shared_ema_new = ema_rate * shared_ema + (1.0 - ema_rate) * shared_new
    return (
        norm_value.reshape(1),
        (loss_total / pixel_total).reshape(1),
        row_new[None],
        row_first_new[None],
        row_second_new[None],
        row_ema_new[None],
        row_new.astype(jnp.bfloat16)[None],
        shared_new,
        shared_first_new,
        shared_second_new,
        shared_ema_new,
        shared_new.astype(jnp.bfloat16),
    )


def solution(mesh):
    placed = (
        P("dp", "tensor", None),
        P("dp"),
        P("dp", None, "tensor"),
        P("dp", None, "tensor"),
        P("dp", "tensor"),
        P(),
        P("tensor", "dp"),
        P("tensor", "dp"),
        P("tensor", "dp"),
        P("tensor", "dp"),
        P("dp"),
        P("dp"),
        P("dp"),
        P("dp"),
    )
    return jax.shard_map(
        per_device,
        mesh=mesh,
        in_specs=placed,
        out_specs=(
            P(),
            P(),
            P("tensor", "dp"),
            P("tensor", "dp"),
            P("tensor", "dp"),
            P("tensor", "dp"),
            P("tensor", "dp"),
            P("dp"),
            P("dp"),
            P("dp"),
            P("dp"),
            P("dp"),
        ),
        check_vma=False,
    )
```

```python
import math
from functools import partial

import jax
import jax.numpy as jnp
from jax import lax
from jax.experimental import pallas as pl
from jax.experimental.pallas import tpu as pltpu
from jax.sharding import PartitionSpec as P

D = 1024
DH = 64
FF = 4096
PATCH = 8
VTOK = 192
PIN = 576
POUT = 768
VMEM = pl.BlockSpec(memory_space=pltpu.VMEM)
ROOT_HALF = 0.5**0.5
NORMAL_PEAK = (2.0 * math.pi) ** -0.5


clip_norm = 0.005
beta_one = 0.9
beta_two = 0.95
adam_eps = 1e-08
decay_rate = 0.05
learn_rate = 0.03
ema_rate = 0.9
norm_eps = 1e-05
masked_score = -1e30


MESH = pl.DeviceIdType.MESH
NN = (((1,), (0,)), ((), ()))
NT = (((1,), (1,)), ((), ()))
TN = (((0,), (0,)), ((), ()))
LOW = jnp.bfloat16
WIDE = jnp.float32
PIECES = 4
TILE = 256


def dot(left, right, dims=NN):
    return lax.dot_general(left, right, dims, preferred_element_type=WIDE)


def remote(src, dst, send, recv, to):
    return pltpu.make_async_remote_copy(
        src_ref=src, dst_ref=dst, send_sem=send, recv_sem=recv, device_id=to, device_id_type=MESH
    )


class Corner:
    def __init__(self):
        self.me = lax.axis_index("tensor")
        self.first, self.last = self.me // 2, lax.rem(self.me, 2)
        self.mate = self.first * 2 + 1 - self.last
        self.far = (1 - self.first) * 2 + self.last
        self.opposite = (1 - self.first) * 2 + 1 - self.last

    def block(self, step):
        return lax.rem(self.first + 1 - step // 2, 2) * 2 + lax.rem(self.last + 1 - lax.rem(step, 2), 2)

    def greet(self):
        barrier = pltpu.get_barrier_semaphore()
        for other in (self.mate, self.far):
            pl.semaphore_signal(barrier, inc=1, device_id={"tensor": other}, device_id_type=MESH)
        pl.semaphore_wait(barrier, 2)


class Gather:
    def __init__(self, corner, ref, pieces, sems):
        self.corner, self.ref, self.pieces, self.sems = corner, ref, pieces, sems
        self.size = ref.shape[0] // 4
        self.rows = self.size // pieces

    @staticmethod
    def scratch(pieces):
        return [pltpu.SemaphoreType.DMA((pieces,))] * 6

    def part(self, owner, piece):
        return pl.ds(pl.multiple_of(owner * self.size + piece * self.rows, self.rows), self.rows)

    def copy(self, owner, piece, kind, to):
        here = self.ref.at[self.part(owner, piece)]
        return remote(here, here, self.sems[2 * kind].at[piece], self.sems[2 * kind + 1].at[piece], {"tensor": to})

    def start(self, piece):
        self.copy(self.corner.me, piece, 1, self.corner.far).start()
        self.copy(self.corner.me, piece, 0, self.corner.mate).start()

    def relay(self, piece):
        self.copy(self.corner.far, piece, 1, self.corner.far).wait_recv()
        self.copy(self.corner.far, piece, 2, self.corner.mate).start()

    def finish(self):
        corner = self.corner
        for piece in range(self.pieces):
            self.copy(corner.mate, piece, 0, corner.mate).wait_recv()
            self.copy(corner.opposite, piece, 2, corner.mate).wait_recv()
            self.copy(corner.me, piece, 0, corner.mate).wait_send()
            self.copy(corner.me, piece, 1, corner.far).wait_send()
            self.copy(corner.far, piece, 2, corner.mate).wait_send()


class Scatter:
    def __init__(self, corner, pieces, mate_out, mate_in, far_out, far_in, mate_send, mate_recv, far_send, far_recv):
        self.corner, self.pieces = corner, pieces
        self.mate_out, self.mate_in, self.far_out, self.far_in = mate_out, mate_in, far_out, far_in
        self.sems = mate_send, mate_recv, far_send, far_recv
        self.rows = far_out.shape[0] // pieces

    @staticmethod
    def scratch(rows, width, pieces):
        return [
            pltpu.VMEM((2, rows, width), LOW),
            pltpu.VMEM((2, rows, width), LOW),
            pltpu.VMEM((rows, width), LOW),
            pltpu.VMEM((rows, width), LOW),
            pltpu.SemaphoreType.DMA((2, pieces)),
            pltpu.SemaphoreType.DMA((2, pieces)),
            pltpu.SemaphoreType.DMA((pieces,)),
            pltpu.SemaphoreType.DMA((pieces,)),
        ]

    def part(self, piece):
        return pl.ds(piece * self.rows, self.rows)

    def mate_copy(self, half, piece):
        part = self.part(piece)
        return remote(
            self.mate_out.at[half, part],
            self.mate_in.at[half, part],
            self.sems[0].at[half, piece],
            self.sems[1].at[half, piece],
            {"tensor": self.corner.mate},
        )

    def far_copy(self, piece):
        part = self.part(piece)
        return remote(
            self.far_out.at[part],
            self.far_in.at[part],
            self.sems[2].at[piece],
            self.sems[3].at[piece],
            {"tensor": self.corner.far},
        )

    def give(self, half, ref):
        for piece in range(self.pieces):
            part = self.part(piece)
            self.mate_out[half, part] = ref[part].astype(LOW)
            self.mate_copy(half, piece).start()

    def cross(self, ref):
        for piece in range(self.pieces):
            part = self.part(piece)
            self.mate_copy(0, piece).wait_recv()
            self.far_out[part] = (ref[part] + self.mate_in[0, part].astype(WIDE)).astype(LOW)
            self.far_copy(piece).start()

    def step(self, step, ref):
        @pl.when(step == 0)
        def _():
            self.give(0, ref)

        @pl.when(step == 1)
        def _():
            self.cross(ref)

        @pl.when(step == 2)
        def _():
            self.give(1, ref)

    def land(self, piece, ref):
        part = self.part(piece)
        self.mate_copy(1, piece).wait_recv()
        self.far_copy(piece).wait_recv()
        return ref[part] + self.mate_in[1, part].astype(WIDE) + self.far_in[part].astype(WIDE)

    def close(self):
        for piece in range(self.pieces):
            self.mate_copy(0, piece).wait_send()
            self.mate_copy(1, piece).wait_send()
            self.far_copy(piece).wait_send()


def standard(values):
    centre = values - jnp.mean(values, -1, keepdims=True)
    inverse = lax.rsqrt(jnp.mean(centre * centre, -1, keepdims=True) + norm_eps)
    return centre * inverse, inverse


def norm_back(grad_out, scaled, inverse, gain):
    grad_scaled = grad_out * gain
    return inverse * (
        grad_scaled
        - jnp.mean(grad_scaled, -1, keepdims=True)
        - scaled * jnp.mean(grad_scaled * scaled, -1, keepdims=True)
    )


def qkv_places(parts, rows, columns):
    share = rows // parts
    wide = columns * 2 // 3
    packed = share * columns // 1024
    for at in range(parts):
        for j in range(2):
            half = share // 2
            yield (at * packed, half, j * wide, wide, at * share + j * half, 0)
        for j in range(4):
            quarter = share // 4
            yield (at * packed + share // 2, quarter, j * (columns - wide), columns - wide, at * share + j * quarter, wide)


def unpack_into(full, packed, parts):
    for row, rows, col, cols, to_row, to_col in qkv_places(parts, full.shape[0], full.shape[1]):
        full[to_row : to_row + rows, to_col : to_col + cols] = packed[row : row + rows, col : col + cols]


def pack_from(packed, full, parts, base=0):
    for row, rows, col, cols, to_row, to_col in qkv_places(parts, full.shape[0], full.shape[1]):
        packed[base + row : base + row + rows, col : col + cols] = full[to_row : to_row + rows, to_col : to_col + cols]


def rows_of(block, size):
    return pl.ds(pl.multiple_of(block * size, size), size)


def column_loop(width, body):
    @pl.loop(0, width // TILE)
    def _(tile):
        body(pl.ds(pl.multiple_of(tile * TILE, TILE), TILE))


def attend_kernel(parts, q_rows, count_ref, patch_ref, proj_ref, norm_ref, packed_ref, out_ref, *rest):
    corner = Corner()
    corner.greet()
    attend_body(parts, q_rows, corner, None, count_ref, patch_ref, proj_ref, norm_ref, packed_ref, out_ref, *rest)


def attend_body(parts, q_rows, corner, progress, count_ref, patch_ref, proj_ref, norm_ref, packed_ref, out_ref,
                embed_ref, normed1_ref, qkv_ref, attended_ref, log_ref, resid_ref, normed2_ref,
                qkv_proj, term, *comm):
    progress = progress or (lambda *_: None)
    scatter = Scatter(corner, PIECES, *comm[:8])
    gather = Gather(corner, normed2_ref, PIECES, comm[8:])
    size, width = embed_ref.shape
    length = patch_ref.shape[0]
    local = attended_ref.shape[1]

    @pl.loop(0, 4)
    def _(block):
        here = rows_of(block, size)
        column_loop(width, lambda cols: term.__setitem__((slice(None), cols), dot(patch_ref[here], proj_ref[:, cols])))

        @pl.when(block == corner.me)
        def _():
            embed_ref[...] = term[...]

        scaled, inverse = standard(term[...])
        normed1_ref[here] = (scaled * norm_ref[0:1] + norm_ref[1:2]).astype(LOW)

    progress("weights")
    unpack_into(qkv_proj, packed_ref, parts)

    @pl.loop(0, 4)
    def _(block):
        here = rows_of(block, size)

        def columns(cols):
            qkv_ref[here, cols] = dot(normed1_ref[here], qkv_proj[:, cols]).astype(LOW)

        column_loop(3 * local, columns)

    valid = lax.broadcasted_iota(jnp.int32, (1, length), 1) < count_ref[0] * VTOK
    left = lax.broadcasted_iota(jnp.int32, (1, 2 * DH), 1) < DH
    factor = jnp.array(DH ** (-0.5), LOW)

    @pl.loop(0, length // q_rows)
    def _(turn):
        here = rows_of(turn, q_rows)
        for pair in range(local // (2 * DH)):
            lanes = slice(pair * 2 * DH, (pair + 1) * 2 * DH)
            queries = qkv_ref[here, lanes] * factor
            keyset = qkv_ref[:, local + pair * 2 * DH : local + (pair + 1) * 2 * DH]
            values = qkv_ref[:, 2 * local + pair * 2 * DH : 2 * local + (pair + 1) * 2 * DH]
            found = []
            for side in range(2):
                mine = left if side == 0 else ~left
                scores = dot(jnp.where(mine, queries, jnp.zeros_like(queries)), keyset, NT)
                scores = jnp.where(valid, scores, masked_score)
                top = jnp.max(scores, -1, keepdims=True)
                powers = jnp.exp(scores - top)
                total = jnp.sum(powers, -1, keepdims=True)
                log_ref[here, pair * 2 + side : pair * 2 + side + 1] = top + jnp.log(total)
                found.append(dot((powers * (1.0 / total)).astype(LOW), values))
            attended_ref[here, lanes] = jnp.where(left, found[0], found[1]).astype(LOW)
        progress("turn", turn)

    progress("out")

    @pl.loop(0, 4)
    def _(step):
        here = rows_of(corner.block(step), size)
        column_loop(width, lambda cols: term.__setitem__((slice(None), cols), dot(attended_ref[here], out_ref[:, cols])))
        scatter.step(step, term)

    for piece in range(PIECES):
        part = scatter.part(piece)
        resid = embed_ref[part] + scatter.land(piece, term)
        resid_ref[part] = resid
        scaled, inverse = standard(resid)
        normed2_ref[gather.part(corner.me, piece)] = (scaled * norm_ref[2:3] + norm_ref[3:4]).astype(LOW)
        gather.start(piece)
        progress("land", piece)
    for piece in range(PIECES):
        gather.relay(piece)
    gather.finish()
    scatter.close()


def attend(count, patches, patch_proj, norm, packed, out_proj, parts, collective_id):
    length, size = patches.shape[0], patches.shape[0] // 4
    width, local = patch_proj.shape[1], out_proj.shape[0]
    shape = jax.ShapeDtypeStruct
    return pl.pallas_call(
        partial(attend_kernel, parts, 256),
        out_shape=(
            shape((size, width), WIDE),
            shape((length, width), LOW),
            shape((length, 3 * local), LOW),
            shape((length, local), LOW),
            shape((length, local // DH), WIDE),
            shape((size, width), WIDE),
            shape((length, width), LOW),
        ),
        in_specs=[pl.BlockSpec(memory_space=pltpu.SMEM)] + [VMEM] * 5,
        out_specs=(VMEM,) * 7,
        scratch_shapes=[pltpu.VMEM((width, 3 * local), LOW), pltpu.VMEM((size, width), WIDE)]
        + Scatter.scratch(size, width, PIECES)
        + Gather.scratch(PIECES),
        compiler_params=pltpu.CompilerParams(
            collective_id=collective_id, has_side_effects=True, vmem_limit_bytes=62 * 2**20
        ),
    )(count, patches, patch_proj, norm, packed, out_proj)


class Lines:
    def __init__(self, lines):
        self.lines = lines
        self.me = lax.axis_index("dp")
        self.line, self.side = self.me // 2, lax.rem(self.me, 2)
        self.pair = {"dp": self.line * 2 + 1 - self.side}
        self.above = {"dp": lax.rem(self.line + 1, lines) * 2 + self.side}
        self.below = {"dp": lax.rem(self.line + lines - 1, lines) * 2 + self.side}
        self.has_below, self.has_above = self.line > 0, self.line < lines - 1

    def signal(self, barrier):
        pl.semaphore_signal(barrier, inc=1, device_id=self.pair, device_id_type=MESH)

        @pl.when(self.has_below)
        def _():
            pl.semaphore_signal(barrier, inc=1, device_id=self.below, device_id_type=MESH)

        @pl.when(self.has_above)
        def _():
            pl.semaphore_signal(barrier, inc=1, device_id=self.above, device_id_type=MESH)

        return 1 + jnp.minimum(self.line, 1) + jnp.minimum(self.lines - 1 - self.line, 1)


class LineGather:
    def __init__(self, spot, ref, base, chunk, pieces, late_own, sems):
        self.spot, self.ref, self.base, self.chunk, self.pieces, self.late_own = spot, ref, base, chunk, pieces, late_own
        self.sems = sems
        self.rows = chunk // pieces
        self.steps = (spot.lines - 1) * pieces

    @staticmethod
    def scratch(lines, pieces):
        return [pltpu.SemaphoreType.DMA((lines * pieces,))] * 6

    def copy(self, kind, line, side, piece, to):
        start = self.base + (line * 2 + side) * self.chunk + piece * self.rows
        here = self.ref.at[pl.ds(pl.multiple_of(start, 16), self.rows)]
        at = line * self.pieces + piece
        return remote(here, here, self.sems[2 * kind].at[at], self.sems[2 * kind + 1].at[at], to)

    def up(self, line, piece):
        return self.copy(0, line, self.spot.side, piece, self.spot.above)

    def down(self, line, piece):
        return self.copy(1, line, self.spot.side, piece, self.spot.below)

    def across(self, line, piece):
        return self.copy(2, line, self.spot.side, piece, self.spot.pair)

    def crossed(self, line, piece):
        return self.copy(2, line, 1 - self.spot.side, piece, self.spot.pair)

    def own(self, copy):
        @pl.loop(0, self.pieces)
        def _(piece):
            copy(self.spot.line, piece).start()

    def begin(self):
        spot = self.spot
        first = spot.line == 0 if self.late_own else spot.line >= 0

        @pl.when(first & spot.has_above)
        def _():
            self.own(self.up)

        @pl.when(spot.has_below)
        def _():
            self.own(self.down)

        @pl.when(first)
        def _():
            self.own(self.across)

    def step(self, at):
        spot = self.spot
        piece = lax.rem(at, self.pieces)

        @pl.when(at < spot.line * self.pieces)
        def _():
            line = at // self.pieces
            self.up(line, piece).wait_recv()

            @pl.when(spot.has_above)
            def _():
                self.up(line, piece).start()

            self.across(line, piece).start()

        if self.late_own:

            @pl.when((at == spot.line * self.pieces - 1) & spot.has_above)
            def _():
                self.own(self.up)

            @pl.when((at == self.pieces - 1) & spot.has_below)
            def _():
                self.own(self.across)

        @pl.when(at < (spot.lines - 1 - spot.line) * self.pieces)
        def _():
            line = spot.line + 1 + at // self.pieces
            self.down(line, piece).wait_recv()

            @pl.when(spot.has_below)
            def _():
                self.down(line, piece).start()

            self.across(line, piece).start()

    def wait_crossed(self, line, pieces=None):
        @pl.loop(0, pieces or self.pieces)
        def _(piece):
            self.crossed(line, piece).wait_recv()

    def close(self):
        spot = self.spot

        @pl.loop(0, spot.lines * self.pieces)
        def _(at):
            line, piece = at // self.pieces, lax.rem(at, self.pieces)
            self.across(line, piece).wait_send()

            @pl.when((line <= spot.line) & spot.has_above)
            def _():
                self.up(line, piece).wait_send()

            @pl.when((line >= spot.line) & spot.has_below)
            def _():
                self.down(line, piece).wait_send()


WINDOW = 48
FRONT = 80
PADDED = 1616
ROW_START = (0, 160, 336, 496)
USED_START = (None, None, None, 0, 128, 352, 576, 800)


def shared_offsets(me, quarter):
    chunk = SHARED_LANES
    rows = jnp.where(me == 0, 0, jnp.where(me == 1, 160, jnp.where(me == 2, 336, 496)))
    used = (me - 4) * 224 + 128
    return (
        FRONT + 8 * rows - me * chunk + 8 * WINDOW * quarter,
        FRONT + 8 * rows - me * chunk + 8 * 32 * quarter,
        FRONT + PATCH_LANES - me * chunk + 6 * 48 * quarter,
        FRONT + PATCH_LANES + 6 * used - me * chunk + 6 * 64 * quarter,
        FRONT + PATCH_LANES + 6 * D - me * chunk,
    )


def shared_walk(me, quarter, take, phases=range(5)):
    rows, last_rows, first_used, used, norm = shared_offsets(me, quarter)
    for j in range(8):
        if 0 in phases:
            take(me < 3, 0, WINDOW, j, rows + j, 8)
        if 1 in phases:
            take((me == 3) & (quarter < 3), 0, 32, j, last_rows + j, 8)
    if 2 in phases:
        for j in range(3):
            take((me == 3) & (quarter < 3), 32, 16, j, first_used + 6 * 16 * j, 6)
    if 3 in phases:
        for j in range(2):
            take(me > 3, 0, 32, j, used + 6 * 32 * j, 6)
    if 4 in phases:
        for j in range(8):
            take((me == 7) & (quarter == 0), 32, 8, j, norm + j, 8)


def window_pieces(kind, row):
    found = []
    if kind == 0:
        for me in range(3):
            at = row - ROW_START[me]
            if 0 <= at < 4 * WINDOW:
                found.append((me, at // WINDOW, at % WINDOW, None))
        at = row - ROW_START[3]
        if 0 <= at < 96:
            found.append((3, at // 32, at % 32, None))
    else:
        if row < 144:
            found.append((3, row // 48, 32, row % 48 // 16))
        for me in range(4, 8):
            at = row - USED_START[me]
            if 0 <= at < 256:
                found.append((me, at // 64, at % 32, at % 64 // 32))
    return found

SHARED_LANES = 1348
PATCH_LANES = PIN * D // 128
CHUNK_PIECES = 4


def forward_kernel(lines, q_rows, count_ref, row_ref, shared_ref, own_patch_ref,
                   weight_ref, used_ref, norm_ref,
                   embed_ref, normed1_ref, qkv_ref, attended_ref, log_ref, resid_ref, normed2_ref,
                   patches, proj, windows, *rest):
    body, extra = rest[:2 + 14], rest[2 + 14:]
    corner, spot = Corner(), Lines(lines)
    barrier = pltpu.get_barrier_semaphore()
    for other in (corner.mate, corner.far):
        pl.semaphore_signal(barrier, inc=1, device_id={"tensor": other}, device_id_type=MESH)
    pl.semaphore_wait(barrier, 2 + spot.signal(barrier))
    parts = lines // 2
    chunk = weight_ref.shape[0] // (2 * lines)
    size, inputs = own_patch_ref.shape
    window = LineGather(spot, windows, corner.me * (2 * lines * WINDOW), WINDOW, 1, False, extra[0:6])
    weights = LineGather(spot, weight_ref, 0, chunk, CHUNK_PIECES, True, extra[6:12])
    spread = Gather(corner, windows, 2, extra[12:18])
    given = Gather(corner, patches, 1, extra[18:24])

    patches[given.part(corner.me, 0)] = own_patch_ref[...]
    given.start(0)
    base = pl.multiple_of((corner.me * 2 * lines + spot.me) * WINDOW, 16)
    windows[pl.ds(base, WINDOW)] = jnp.zeros((WINDOW, windows.shape[1]), LOW)

    def take(condition, row, rows, j, start, stride):
        @pl.when(condition)
        def _():
            windows[pl.ds(pl.multiple_of(base + row, 16), rows), j * 128 : (j + 1) * 128] = shared_ref[
                pl.ds(start, rows, stride)
            ].astype(LOW)

    shared_walk(spot.me, corner.me, take)
    window.begin()
    own = pl.multiple_of(spot.me * chunk, 16)

    @pl.when(spot.me < parts)
    def _():
        for row, rows, col, cols, at, at_col in qkv_places(1, chunk * 4 // 3, D * 3 // 4):
            for j in range(cols // 128):
                weight_ref[pl.ds(pl.multiple_of(own + row, 16), rows), col + j * 128 : col + (j + 1) * 128] = row_ref[
                    pl.ds(6 * at + at_col // 128 + j, rows, 6)
                ].astype(LOW)

    @pl.when(spot.me >= parts)
    def _():
        for j in range(8):
            weight_ref[pl.ds(own, chunk), j * 128 : (j + 1) * 128] = row_ref[pl.ds(j, chunk, 8)].astype(LOW)

    weights.begin()
    for at in range(window.steps):
        window.step(at)
    for line in range(lines):
        window.wait_crossed(line)
    for piece in range(2):
        spread.start(piece)
    given.relay(0)
    for at in range(2):
        weights.step(at)
    spread.relay(0)
    weights.step(2)
    spread.relay(1)
    weights.step(3)
    given.finish()
    spread.finish()

    def source(me, quarter, row, rows, j):
        start = (quarter * 2 * lines + me) * WINDOW + row
        return windows[start : start + rows] if j is None else windows[start : start + rows, j * 128 : (j + 1) * 128]

    for row in range(0, proj.shape[0], 16):
        proj[row : row + 16] = sum(source(me, t, at, 16, j) for me, t, at, j in window_pieces(0, row))
    for row in range(0, used_ref.shape[0], 16):
        used_ref[row : row + 16] = sum(source(me, t, at, 16, j) for me, t, at, j in window_pieces(1, row))
    norm_ref[...] = source(2 * lines - 1, 0, 32, 8, None).astype(WIDE)

    def progress(place, at=None):
        if place == "weights":
            weights.wait_crossed(0)
        if place == "turn":
            @pl.when(at >= 2)
            def _():
                weights.step(at + 2)
        if place == "out":
            weights.wait_crossed(1)
        if place == "land":
            weights.step(8 + at)

    attend_body(parts, q_rows, corner, progress, count_ref, patches, proj, norm_ref,
                weight_ref.at[pl.ds(0, D * 3 // 4)], weight_ref.at[pl.ds(D * 3 // 4, D // 4)],
                embed_ref, normed1_ref, qkv_ref, attended_ref, log_ref, resid_ref, normed2_ref, *body)
    for line in range(2, lines):
        weights.wait_crossed(line)
    weights.close()
    window.close()


def forward(count, row_lanes, shared_lanes, own_patches, lines, collective_id):
    size, inputs = own_patches.shape
    length, width, local = 4 * size, D, D // 4
    shape = jax.ShapeDtypeStruct
    return pl.pallas_call(
        partial(forward_kernel, lines, 256),
        out_shape=(
            shape((3 * D, D), LOW),
            shape((D, 128), LOW),
            shape((8, D), WIDE),
            shape((size, width), WIDE),
            shape((length, width), LOW),
            shape((length, 3 * local), LOW),
            shape((length, local), LOW),
            shape((length, local // DH), WIDE),
            shape((size, width), WIDE),
            shape((length, width), LOW),
        ),
        in_specs=[pl.BlockSpec(memory_space=pltpu.SMEM)] + [VMEM] * 3,
        out_specs=(VMEM,) * 10,
        scratch_shapes=[
            pltpu.VMEM((length, inputs), LOW),
            pltpu.VMEM((inputs, width), LOW),
            pltpu.VMEM((8 * lines * WINDOW, width), LOW),
            pltpu.VMEM((width, 3 * local), LOW),
            pltpu.VMEM((size, width), WIDE),
        ]
        + Scatter.scratch(size, width, PIECES)
        + Gather.scratch(PIECES)
        + LineGather.scratch(lines, 1)
        + LineGather.scratch(lines, CHUNK_PIECES)
        + Gather.scratch(2)
        + Gather.scratch(1),
        compiler_params=pltpu.CompilerParams(
            collective_id=collective_id, has_side_effects=True, vmem_limit_bytes=63 * 2**20
        ),
    )(count, row_lanes, shared_lanes, own_patches)


def mlp_kernel(normed2_ref, up_ref, down_ref, resid1_ref, cols_ref, hidden_ref, active_ref, low_ref, table_ref, term, *comm):
    corner = Corner()
    corner.greet()
    scatter = Scatter(corner, PIECES, *comm[:8])
    gather = Gather(corner, table_ref, PIECES, comm[8:])
    size, width = resid1_ref.shape

    @pl.loop(0, 4)
    def _(step):
        here = rows_of(corner.block(step), size)

        def columns(cols):
            hidden = dot(normed2_ref[here], up_ref[:, cols])
            hidden_ref[here, cols] = hidden
            active_ref[here, cols] = (0.5 * hidden * (1.0 + lax.erf(hidden * ROOT_HALF))).astype(LOW)

        column_loop(up_ref.shape[1], columns)
        column_loop(width, lambda cols: term.__setitem__((slice(None), cols), dot(active_ref[here], down_ref[:, cols])))
        scatter.step(step, term)

    for piece in range(PIECES):
        part = scatter.part(piece)
        low_ref[part] = (resid1_ref[part] + scatter.land(piece, term)).astype(LOW)
        table_ref[gather.part(corner.me, piece)] = dot(low_ref[part], cols_ref[...]).astype(LOW)
        gather.start(piece)
    for piece in range(PIECES):
        gather.relay(piece)
    gather.finish()
    scatter.close()


def mlp(normed2, up_proj, down_proj, resid1, used_cols, collective_id):
    length, size, width = normed2.shape[0], resid1.shape[0], resid1.shape[1]
    hidden = up_proj.shape[1]
    shape = jax.ShapeDtypeStruct
    return pl.pallas_call(
        mlp_kernel,
        out_shape=(
            shape((length, hidden), WIDE),
            shape((length, hidden), LOW),
            shape((size, width), LOW),
            shape((length, used_cols.shape[1]), LOW),
        ),
        in_specs=[VMEM] * 5,
        out_specs=(VMEM,) * 4,
        scratch_shapes=[pltpu.VMEM((size, width), WIDE)]
        + Scatter.scratch(size, width, PIECES)
        + Gather.scratch(PIECES),
        compiler_params=pltpu.CompilerParams(
            collective_id=collective_id, has_side_effects=True, vmem_limit_bytes=62 * 2**20
        ),
    )(normed2, up_proj, down_proj, resid1, used_cols)


def mlp_back_kernel(table_ref, cols_ref, low_ref, active_ref, hidden_ref, normed2_ref, up_ref, down_ref, resid1_ref, norm_ref,
                    unpatch_ref, grad_ref, resid_grad_ref, branch_ref, gain_ref,
                    gauss, down_in, hidden_grad, term, tail, *comm):
    corner = Corner()
    corner.greet()
    small = Scatter(corner, 1, *comm[:8])
    spread = Gather(corner, gauss, 1, comm[8:14])
    scatter = Scatter(corner, PIECES, *comm[14:22])
    gather = Gather(corner, branch_ref, PIECES, comm[22:])
    size, width = resid1_ref.shape
    ff = up_ref.shape[1]

    def view(step):
        return table_ref.at[rows_of(corner.block(step), size)]

    tail[...] = view(0)[...].astype(WIDE)
    small.give(0, tail)
    tail[...] = view(1)[...].astype(WIDE)
    small.cross(tail)
    tail[...] = view(2)[...].astype(WIDE)
    small.give(1, tail)
    tail[...] = view(3)[...].astype(WIDE)
    own_gauss = small.land(0, tail).astype(LOW)
    gauss[spread.part(corner.me, 0)] = own_gauss
    spread.start(0)
    unpatch_ref[...] = dot(low_ref[...], own_gauss, TN)
    spread.relay(0)
    spread.finish()
    small.close()

    @pl.loop(0, 4)
    def _(step):
        here = rows_of(corner.block(step), size)
        term[...] = dot(gauss[here], cols_ref[...], NT)
        down_in[here] = term[...].astype(LOW)

        @pl.when(step == 3)
        def _():
            resid_grad_ref[...] = term[...]

        def columns(cols):
            active_grad = dot(down_in[here], down_ref[cols, :], NT)
            hidden = hidden_ref[here, cols]
            slope = 0.5 * (1.0 + lax.erf(hidden * ROOT_HALF)) + hidden * (jnp.exp(-0.5 * hidden * hidden) * NORMAL_PEAK)
            hidden_grad[here, cols] = (active_grad * slope).astype(LOW)

        column_loop(ff, columns)

        def back(cols):
            term[:, cols] = dot(hidden_grad[here], up_ref[cols, :], NT)

        column_loop(width, back)
        scatter.step(step, term)

    @pl.loop(0, width // TILE)
    def _(tile):
        cols = pl.ds(pl.multiple_of(tile * TILE, TILE), TILE)
        grad_ref[cols, :] = dot(normed2_ref[:, cols], hidden_grad[...], TN)

    @pl.loop(0, ff // TILE)
    def _(tile):
        cols = pl.ds(pl.multiple_of(tile * TILE, TILE), TILE)
        grad_ref[pl.ds(pl.multiple_of(width + tile * TILE, TILE), TILE), :] = dot(active_ref[:, cols], down_in[...], TN)

    gain_sum, bias_sum = jnp.zeros((1, width), WIDE), jnp.zeros((1, width), WIDE)
    for piece in range(PIECES):
        part = scatter.part(piece)
        grad = scatter.land(piece, term)
        scaled, inverse = standard(resid1_ref[part])
        total = resid_grad_ref[part] + norm_back(grad, scaled, inverse, norm_ref[2:3])
        resid_grad_ref[part] = total
        branch_ref[gather.part(corner.me, piece)] = total.astype(LOW)
        gather.start(piece)
        gain_sum += jnp.sum(grad * scaled, 0, keepdims=True)
        bias_sum += jnp.sum(grad, 0, keepdims=True)
    gain_ref[0:1] = gain_sum
    gain_ref[1:2] = bias_sum
    for piece in range(PIECES):
        gather.relay(piece)
    gather.finish()
    scatter.close()


def mlp_back(table_grad, used_cols, low, active, hidden, normed2, up_proj, down_proj, resid1, norm, collective_id):
    length, size, width = normed2.shape[0], resid1.shape[0], resid1.shape[1]
    ff, used = up_proj.shape[1], used_cols.shape[1]
    shape = jax.ShapeDtypeStruct
    return pl.pallas_call(
        mlp_back_kernel,
        out_shape=(
            shape((width, used), WIDE),
            shape((width + ff, width), WIDE),
            shape((size, width), WIDE),
            shape((length, width), LOW),
            shape((2, width), WIDE),
        ),
        in_specs=[VMEM] * 10,
        out_specs=(VMEM,) * 5,
        scratch_shapes=[
            pltpu.VMEM((length, used), LOW),
            pltpu.VMEM((length, width), LOW),
            pltpu.VMEM((length, ff), LOW),
            pltpu.VMEM((size, width), WIDE),
            pltpu.VMEM((size, used), WIDE),
        ]
        + Scatter.scratch(size, used, 1)
        + Gather.scratch(1)
        + Scatter.scratch(size, width, PIECES)
        + Gather.scratch(PIECES),
        compiler_params=pltpu.CompilerParams(
            collective_id=collective_id, has_side_effects=True, vmem_limit_bytes=63 * 2**20
        ),
    )(table_grad, used_cols, low, active, hidden, normed2, up_proj, down_proj, resid1, norm)


def attend_back_kernel(parts, q_rows, count_ref, branch_ref, out_ref, qkv_ref, log_ref, packed_ref, attended_ref, normed1_ref, embed_ref,
                       resid_grad_ref, norm_ref, patch_ref, grad_ref, patch_grad_ref, gain_ref,
                       qkv_proj, attended_grad, qkv_grad, key_grad, value_grad, full_grad, term, embed_grad, *comm):
    corner = Corner()
    corner.greet()
    scatter = Scatter(corner, PIECES, *comm)
    size, width = embed_ref.shape
    length, local = attended_ref.shape
    unpack_into(qkv_proj, packed_ref, parts)

    @pl.loop(0, 4)
    def _(block):
        here = rows_of(block, size)
        attended_grad[here] = dot(branch_ref[here], out_ref[...], NT).astype(LOW)

    key_grad[...] = jnp.zeros_like(key_grad)
    value_grad[...] = jnp.zeros_like(value_grad)
    valid = lax.broadcasted_iota(jnp.int32, (1, length), 1) < count_ref[0] * VTOK
    left = lax.broadcasted_iota(jnp.int32, (1, 2 * DH), 1) < DH
    factor = jnp.array(DH ** (-0.5), LOW)

    @pl.loop(0, length // q_rows)
    def _(turn):
        here = rows_of(turn, q_rows)
        for pair in range(local // (2 * DH)):
            lanes = slice(pair * 2 * DH, (pair + 1) * 2 * DH)
            queries = qkv_ref[here, lanes] * factor
            grads = attended_grad[here, lanes]
            keyset = qkv_ref[:, local + pair * 2 * DH : local + (pair + 1) * 2 * DH]
            values = qkv_ref[:, 2 * local + pair * 2 * DH : 2 * local + (pair + 1) * 2 * DH]
            found = []
            for side in range(2):
                mine = left if side == 0 else ~left
                own_query = jnp.where(mine, queries, jnp.zeros_like(queries))
                own_grad = jnp.where(mine, grads, jnp.zeros_like(grads))
                scores = jnp.where(valid, dot(own_query, keyset, NT), masked_score)
                probs = jnp.exp(scores - log_ref[here, pair * 2 + side : pair * 2 + side + 1])
                prob_grad = dot(own_grad, values, NT)
                value_grad[:, lanes] += dot(probs.astype(LOW), own_grad, TN)
                centre = jnp.sum(probs * prob_grad, -1, keepdims=True)
                score_grad = (probs * (prob_grad - centre)).astype(LOW)
                found.append(dot(score_grad, keyset))
                key_grad[:, lanes] += dot(score_grad, own_query, TN)
            qkv_grad[here, lanes] = (jnp.where(left, found[0], found[1]) * (DH ** (-0.5))).astype(LOW)

    qkv_grad[:, local : 2 * local] = key_grad[...].astype(LOW)
    qkv_grad[:, 2 * local :] = value_grad[...].astype(LOW)

    @pl.loop(0, 4)
    def _(step):
        here = rows_of(corner.block(step), size)

        def columns(cols):
            term[:, cols] = dot(qkv_grad[here], qkv_proj[cols, :], NT)

        column_loop(width, columns)
        scatter.step(step, term)

    grad_ref[grad_ref.shape[0] - local :, :] = dot(attended_ref[...], branch_ref[...], TN)

    @pl.loop(0, width // TILE)
    def _(tile):
        cols = pl.ds(pl.multiple_of(tile * TILE, TILE), TILE)
        full_grad[cols, :] = dot(normed1_ref[:, cols], qkv_grad[...], TN)

    pack_from(grad_ref, full_grad, parts)

    gain_sum, bias_sum = jnp.zeros((1, width), WIDE), jnp.zeros((1, width), WIDE)
    for piece in range(PIECES):
        part = scatter.part(piece)
        grad = scatter.land(piece, term)
        scaled, inverse = standard(embed_ref[part])
        embed_grad[part] = (resid_grad_ref[part] + norm_back(grad, scaled, inverse, norm_ref[0:1])).astype(LOW)
        gain_sum += jnp.sum(grad * scaled, 0, keepdims=True)
        bias_sum += jnp.sum(grad, 0, keepdims=True)
    gain_ref[0:1] = gain_sum
    gain_ref[1:2] = bias_sum
    patch_grad_ref[...] = dot(patch_ref[...], embed_grad[...], TN)
    scatter.close()


def attend_back(count, branch, out_proj, qkv, log_total, packed, attended, normed1, embed, resid_grad, norm, patches, parts, collective_id):
    length, local = attended.shape
    size, width = embed.shape
    shape = jax.ShapeDtypeStruct
    return pl.pallas_call(
        partial(attend_back_kernel, parts, 256),
        out_shape=(
            shape((4 * local, width), WIDE),
            shape((patches.shape[1], width), WIDE),
            shape((2, width), WIDE),
        ),
        in_specs=[pl.BlockSpec(memory_space=pltpu.SMEM)] + [VMEM] * 11,
        out_specs=(VMEM,) * 3,
        scratch_shapes=[
            pltpu.VMEM((width, 3 * local), LOW),
            pltpu.VMEM((length, local), LOW),
            pltpu.VMEM((length, 3 * local), LOW),
            pltpu.VMEM((length, local), WIDE),
            pltpu.VMEM((length, local), WIDE),
            pltpu.VMEM((width, 3 * local), WIDE),
            pltpu.VMEM((size, width), WIDE),
            pltpu.VMEM((size, width), LOW),
        ]
        + Scatter.scratch(size, width, PIECES),
        compiler_params=pltpu.CompilerParams(
            collective_id=collective_id, has_side_effects=True, vmem_limit_bytes=62 * 2**20
        ),
    )(count, branch, out_proj, qkv, log_total, packed, attended, normed1, embed, resid_grad, norm, patches)


def render_kernel(area, wide, block, split, table_ref, splat_ref, dist_ref, label_ref, loss_ref, grad_ref, flip, picked, hot, spread_grad):
    tokens = table_ref.shape[0]
    groups = tokens // wide
    splats, pixels = splat_ref.shape
    for j in range(groups):
        flip[j * 2 * area : (j + 1) * 2 * area] = jnp.transpose(table_ref[j * wide : (j + 1) * wide].astype(jnp.float32)).astype(jnp.bfloat16)
    spread_grad[...] = jnp.zeros_like(spread_grad)
    wide_ids = lax.broadcasted_iota(jnp.int32, (wide, block), 0).astype(jnp.float32).astype(jnp.bfloat16)
    cell_ids = lax.broadcasted_iota(jnp.int32, (area, block), 0).astype(jnp.float32)
    cell_low = cell_ids.astype(jnp.bfloat16)
    one, nil = jnp.ones((wide, block), jnp.bfloat16), jnp.zeros((wide, block), jnp.bfloat16)

    def one_block(step, loss):
        here = pl.ds(pl.multiple_of(step * block, block), block)
        opacities, spreads, lows = [], [], []
        for k in range(splats):
            index = splat_ref[k : k + 1, here]
            token = index // area
            column = (token % wide).astype(jnp.float32).astype(jnp.bfloat16)
            group = (token // wide)
            cell = (index % area).astype(jnp.float32)
            match = jnp.where(wide_ids == column, one, nil)
            hot[k] = match
            picked[...] = lax.dot_general(flip[...], match, NN, preferred_element_type=jnp.float32)
            op_sum = jnp.zeros((area, block), jnp.float32)
            sp_sum = jnp.zeros((area, block), jnp.float32)
            for j in range(groups):
                same = cell_ids == jnp.where(group == j, cell, -1.0)
                op_sum += jnp.where(same, picked[j * 2 * area : j * 2 * area + area], 0.0)
                sp_sum += jnp.where(same, picked[j * 2 * area + area : (j + 1) * 2 * area], 0.0)
            opacities.append(jnp.sum(op_sum, 0, keepdims=True))
            spreads.append(jnp.sum(sp_sum, 0, keepdims=True))
            lows.append((group, cell))
        opacity, spread = jnp.concatenate(opacities, 0), jnp.concatenate(spreads, 0)
        distance = dist_ref[:, here].astype(jnp.float32)
        labels = label_ref[:, here]
        valid = jnp.where(labels < 2, 1.0, 0.0)
        target = jnp.where(labels == 1, 1.0, 0.0)
        op_sig, sp_sig = jax.nn.sigmoid(opacity), jax.nn.sigmoid(spread)
        fade = jnp.exp(-0.25 * distance * sp_sig)
        contrib = (0.02 + 0.96 * op_sig) * fade
        keep_log = jnp.sum(jnp.log1p(-contrib), 0, keepdims=True)
        keep = jnp.exp(keep_log)
        alpha = 1.0 - keep
        alpha_log = jnp.log(alpha)
        loss = loss - valid * (target * alpha_log + (1.0 - target) * keep_log)
        keep_grad = valid * (target * keep / alpha - (1.0 - target))
        contrib_grad = -keep_grad / (1.0 - contrib)
        op_grad = contrib_grad * (0.96 * op_sig * (1.0 - op_sig)) * fade
        sp_grad = contrib_grad * contrib * (-0.25 * distance * sp_sig * (1.0 - sp_sig))
        for k in range(splats):
            group, cell = lows[k]
            parts_op, parts_sp = op_grad[k : k + 1], sp_grad[k : k + 1]
            for part in range(split):
                low_op, low_sp = parts_op.astype(jnp.bfloat16), parts_sp.astype(jnp.bfloat16)
                parts_op, parts_sp = parts_op - low_op.astype(jnp.float32), parts_sp - low_sp.astype(jnp.float32)
                pieces = []
                for j in range(groups):
                    same = cell_low == jnp.where(group == j, cell, -1.0).astype(jnp.bfloat16)
                    pieces.append(jnp.where(same, low_op, jnp.bfloat16(0)))
                    pieces.append(jnp.where(same, low_sp, jnp.bfloat16(0)))
                weighted = jnp.concatenate(pieces, 0)
                spread_grad[...] += lax.dot_general(weighted, hot[k], NT, preferred_element_type=jnp.float32)
        return loss

    loss = lax.fori_loop(0, pixels // block, one_block, jnp.zeros((1, block), jnp.float32))
    loss_ref[...] = jnp.broadcast_to(jnp.sum(loss, 1, keepdims=True), loss_ref.shape)
    for j in range(groups):
        grad_ref[j * wide : (j + 1) * wide] = jnp.transpose(spread_grad[j * 2 * area : (j + 1) * 2 * area]).astype(grad_ref.dtype)

def render(table, splats, distance, labels, area, block=512, wide=256, split=2):
    tokens = table.shape[0]
    vm = pl.BlockSpec(memory_space=pltpu.VMEM)
    groups = tokens // wide
    return pl.pallas_call(
        partial(render_kernel, area, wide, block, split),
        out_shape=(jax.ShapeDtypeStruct((8, 128), jnp.float32), jax.ShapeDtypeStruct(table.shape, jnp.bfloat16)),
        in_specs=[vm] * 4, out_specs=(vm, vm),
        scratch_shapes=[pltpu.VMEM((groups * 2 * area, wide), jnp.bfloat16), pltpu.VMEM((groups * 2 * area, block), jnp.float32),
            pltpu.VMEM((splats.shape[0], wide, block), jnp.bfloat16), pltpu.VMEM((groups * 2 * area, wide), jnp.float32)],
        compiler_params=pltpu.CompilerParams(vmem_limit_bytes=48 * 2**20),
    )(table, splats, distance, labels)


def owner_sum_kernel(lines, pieces, g_ref, o_ref, pair_out, pair_in, part, line_in, own_in, p_send, p_recv, l_send, up_recv, down_recv):
    me = lax.axis_index("dp")
    line, side = me // 2, lax.rem(me, 2)
    chunk = o_ref.shape[0]
    rows = chunk // pieces
    count = lines * pieces
    pair = {"dp": line * 2 + 1 - side}
    above = {"dp": lax.rem(line + 1, lines) * 2 + side}
    below = {"dp": lax.rem(line + lines - 1, lines) * 2 + side}
    has_below, has_above = line > 0, line < lines - 1

    def target(step):
        turn = lax.rem(step, lines)
        odd = lax.rem(turn, 2)
        return (1 - odd) * (lines - 1 - turn // 2) + odd * (turn // 2)

    def slot(step):
        return pl.ds(pl.multiple_of(step * rows, rows), rows)

    def here(step):
        return pl.ds(pl.multiple_of(step // lines * rows, rows), rows)

    def source(step, owner):
        return pl.ds(pl.multiple_of((target(step) * 2 + owner) * chunk + step // lines * rows, rows), rows)

    def copy(src, dst, send, recv, to):
        return pltpu.make_async_remote_copy(
            src_ref=src, dst_ref=dst, send_sem=send, recv_sem=recv, device_id=to, device_id_type=MESH
        )

    def pair_copy(step):
        return copy(pair_out.at[slot(step)], pair_in.at[slot(step)], p_send.at[step], p_recv.at[step], pair)

    def line_copy(step, to, recv):
        return copy(part.at[slot(step)], line_in.at[slot(step)], l_send.at[step], recv.at[step], to)

    def last_copy(step):
        return copy(part.at[slot(step)], own_in.at[here(step)], l_send.at[step], down_recv.at[step], below)

    barrier = pltpu.get_barrier_semaphore()
    pl.semaphore_signal(barrier, inc=1, device_id=pair, device_id_type=MESH)

    @pl.when(has_below)
    def _():
        pl.semaphore_signal(barrier, inc=1, device_id=below, device_id_type=MESH)

    @pl.when(has_above)
    def _():
        pl.semaphore_signal(barrier, inc=1, device_id=above, device_id_type=MESH)

    pl.semaphore_wait(barrier, 1 + jnp.minimum(line, 1) + jnp.minimum(lines - 1 - line, 1))

    @pl.loop(0, count)
    def _(step):
        pair_out[slot(step)] = g_ref[source(step, 1 - side)].astype(jnp.bfloat16)
        pair_copy(step).start()

    @pl.loop(0, count + lines - 1)
    def _(step):
        @pl.when(step < count)
        def _():
            pair_copy(step).wait_recv()
            part[slot(step)] = g_ref[source(step, side)].astype(jnp.float32) + pair_in[slot(step)].astype(jnp.float32)

        rising = step - line

        @pl.when((rising >= 0) & (rising < count) & (target(rising) > line))
        def _():
            @pl.when(has_below)
            def _():
                line_copy(rising, above, up_recv).wait_recv()
                part[slot(rising)] += line_in[slot(rising)]

            line_copy(rising, above, up_recv).start()

        falling = step - (lines - 1 - line)

        @pl.when((falling >= 0) & (falling < count) & (target(falling) < line))
        def _():
            @pl.when(has_above)
            def _():
                line_copy(falling, below, down_recv).wait_recv()
                part[slot(falling)] += line_in[slot(falling)]

            @pl.when(target(falling) == line - 1)
            def _():
                last_copy(falling).start()

            @pl.when(target(falling) < line - 1)
            def _():
                line_copy(falling, below, down_recv).start()

    @pl.loop(0, count)
    def _(step):
        pair_copy(step).wait_send()

        @pl.when(target(step) > line)
        def _():
            line_copy(step, above, up_recv).wait_send()

        @pl.when(target(step) < line)
        def _():
            line_copy(step, below, down_recv).wait_send()

        @pl.when(target(step) == line)
        def _():
            o_ref[here(step)] = part[slot(step)]

            @pl.when(has_below)
            def _():
                line_copy(step, above, up_recv).wait_recv()
                o_ref[here(step)] += line_in[slot(step)]

            @pl.when(has_above)
            def _():
                last_copy(step).wait_recv()
                o_ref[here(step)] += own_in[here(step)]


def owner_sum(grad, count_dp, collective_id, pieces):
    lines = count_dp // 2
    total, width = grad.shape
    chunk = total // count_dp
    half = (lines * chunk, width)
    vmem = pl.BlockSpec(memory_space=pltpu.VMEM)
    return pl.pallas_call(
        partial(owner_sum_kernel, lines, pieces),
        out_shape=jax.ShapeDtypeStruct((chunk, width), jnp.float32),
        in_specs=[vmem],
        out_specs=vmem,
        scratch_shapes=[
            pltpu.VMEM(half, jnp.bfloat16),
            pltpu.VMEM(half, jnp.bfloat16),
            pltpu.VMEM(half, jnp.float32),
            pltpu.VMEM(half, jnp.float32),
            pltpu.VMEM((chunk, width), jnp.float32),
        ]
        + [pltpu.SemaphoreType.DMA((lines * pieces,))] * 5,
        compiler_params=pltpu.CompilerParams(
            collective_id=collective_id, has_side_effects=True, vmem_limit_bytes=62 * 2**20
        ),
    )(grad)


def total_kernel(mine_ref, sum_ref, slots, own_sem, send_sem, recv_sem):
    first, second = lax.axis_size("dp"), lax.axis_size("tensor")
    count = first * second
    me = lax.axis_index("dp") * second + lax.axis_index("tensor")

    def peer(step):
        other = lax.rem(me + step, count)
        return {"dp": other // second, "tensor": lax.rem(other, second)}

    barrier = pltpu.get_barrier_semaphore()

    @pl.loop(1, count)
    def _(step):
        pl.semaphore_signal(barrier, inc=1, device_id=peer(step), device_id_type=MESH)

    pl.semaphore_wait(barrier, count - 1)
    own = pltpu.make_async_copy(mine_ref, slots.at[me], own_sem)
    own.start()

    def send(step):
        return pltpu.make_async_remote_copy(
            src_ref=mine_ref,
            dst_ref=slots.at[me],
            send_sem=send_sem.at[step],
            recv_sem=recv_sem.at[step],
            device_id=peer(step),
            device_id_type=MESH,
        )

    @pl.loop(1, count)
    def _(step):
        send(step).start()

    @pl.loop(1, count)
    def _(step):
        send(step).wait()

    own.wait()
    sum_ref[...] = jnp.sum(slots[...], 0)


def total_over_all(mine, collective_id):
    count = lax.axis_size("dp") * lax.axis_size("tensor")
    vmem = pl.BlockSpec(memory_space=pltpu.VMEM)
    return pl.pallas_call(
        total_kernel,
        out_shape=jax.ShapeDtypeStruct(mine.shape, jnp.float32),
        in_specs=[vmem],
        out_specs=vmem,
        scratch_shapes=[
            pltpu.VMEM((count,) + mine.shape, jnp.float32),
            pltpu.SemaphoreType.DMA(()),
            pltpu.SemaphoreType.DMA((count,)),
            pltpu.SemaphoreType.DMA((count,)),
        ],
        compiler_params=pltpu.CompilerParams(collective_id=collective_id, has_side_effects=True),
    )(mine)


def pack_qkv(matrix, parts):
    rows, cols = matrix.shape
    first = matrix[:, :512].reshape(parts, 2, rows // parts // 2, 512).transpose(0, 2, 1, 3)
    second = matrix[:, 512:].reshape(parts, 4, rows // parts // 4, 256).transpose(0, 2, 1, 3)
    return jnp.concatenate([first.reshape(parts, -1, 1024), second.reshape(parts, -1, 1024)], 1).reshape(-1, 1024)


def unpack_qkv(packed, parts):
    rows = packed.shape[0] // parts
    packed = packed.reshape(parts, rows, 1024)
    cut = rows * 2 // 3
    first = packed[:, :cut].reshape(parts, cut, 2, 512).transpose(0, 2, 1, 3).reshape(-1, 512)
    second = packed[:, cut:].reshape(parts, rows - cut, 4, 256).transpose(0, 2, 1, 3).reshape(-1, 256)
    return jnp.concatenate([first, second], 1)


def by_lanes(flat, outer):
    size = flat.size // math.prod(outer)
    return flat.reshape(outer + ((size // 128, 128) if size % 128 == 0 else (size,)))


def pad_first(array, axis, unit):
    short = -array.shape[axis] % unit
    return jnp.pad(array, [(0, short if at == axis else 0) for at in range(array.ndim)])


def sum_to_owners(stack, count_dp):
    if count_dp == 8:
        return owner_sum(stack, count_dp, 1, 9)
    return lax.psum_scatter(stack, "dp", scatter_dimension=0, tiled=True)

def adam_update(master, first_mom, second_mom, gradient, step_float):
    first_new = beta_one * first_mom + (1.0 - beta_one) * gradient
    second_new = beta_two * second_mom + (1.0 - beta_two) * gradient * gradient
    first_hat = first_new / (1.0 - jnp.power(beta_one, step_float))
    second_hat = second_new / (1.0 - jnp.power(beta_two, step_float))
    master_new = master - learn_rate * (
        first_hat / (jnp.sqrt(second_hat) + adam_eps) + decay_rate * master
    )
    return (master_new, first_new, second_new)


def per_device(
    patches,
    view_counts,
    splat_index,
    splat_dist,
    alpha_label,
    step_count,
    row_master,
    row_first,
    row_second,
    row_ema,
    shared_master,
    shared_first,
    shared_second,
    shared_ema,
):
    groups = lax.axis_size("tensor")
    my_dp = lax.axis_index("dp")
    count_dp = lax.axis_size("dp")
    local_width = D // groups
    local_hidden = FF // groups
    qkv_parts = count_dp // 4
    share_rows = row_master.shape[1] // D
    own_patches = patches[0]
    if count_dp == 8:
        shared_lanes = jnp.pad(
            shared_master.reshape(SHARED_LANES, 128), ((FRONT, PADDED - FRONT - SHARED_LANES), (0, 0))
        )
        weights, used_cols, norm, embed, normed1, qkv, attended, log_total, resid1, normed2 = forward(
            view_counts, row_master.reshape(-1, 128), shared_lanes, own_patches, count_dp // 2, 7
        )
        packed_qkv, out_proj, up_proj, down_proj = jnp.split(weights, (3 * local_width, D, D + local_hidden))
    else:
        own_row = row_master[0].astype(jnp.bfloat16)
        own_tiles = jnp.where(
            my_dp < qkv_parts,
            pack_qkv(own_row.reshape(-1, 3 * local_width), 1),
            own_row.reshape(share_rows, D),
        )
        weights = lax.all_gather(own_tiles, "dp", axis=0, tiled=True)
        own_flat = shared_master.astype(jnp.bfloat16)
        own_shared = by_lanes(own_flat, ())
        lead = own_shared.shape[0]
        own_shared = pad_first(own_shared, 0, 2048 // own_shared[0].size)
        shared_weights = lax.all_gather(own_shared, "dp", axis=0, tiled=False)[:, :lead].reshape(-1, 128)
        qkv_rows = 3 * local_width
        out_end = qkv_rows + local_width
        up_end = out_end + local_hidden
        patch_rows = PIN * D // 128
        unpatch_rows = D * POUT // 128
        packed_qkv = weights[:qkv_rows]
        out_proj = weights[qkv_rows:out_end]
        up_proj = weights[out_end:up_end]
        down_proj = weights[up_end:]
        norm = shared_weights[patch_rows + unpatch_rows :].reshape(4, D).astype(jnp.float32)
        patch_proj = shared_weights[:patch_rows].reshape(PIN, D)
        used_cols = shared_weights[patch_rows : patch_rows + unpatch_rows].reshape(D, POUT // 128, 128)[:, 0]
        all_patches = lax.all_gather(own_patches, "tensor", axis=0, tiled=True)
        embed, normed1, qkv, attended, log_total, resid1, normed2 = attend(
            view_counts, all_patches, patch_proj, norm, packed_qkv, out_proj, qkv_parts, 3
        )
    hidden, active, resid2_low, gauss_table = mlp(normed2, up_proj, down_proj, resid1, used_cols, 4)
    loss_tile, table_grad = render(gauss_table, splat_index[0], splat_dist[0], alpha_label, PATCH * PATCH)
    loss_part = loss_tile[0, 0]
    unpatch_used, late_grad, resid_grad, branch, gain2_grad = mlp_back(
        table_grad, used_cols, resid2_low, active, hidden, normed2, up_proj, down_proj, resid1, norm, 5
    )
    early_grad, patch_grad, gain1_grad = attend_back(
        view_counts, branch, out_proj, qkv, log_total, packed_qkv, attended, normed1, embed, resid_grad, norm, own_patches, qkv_parts, 6
    )
    gain_grad = jnp.concatenate([gain1_grad, gain2_grad], 0)
    unpatch_grad = jnp.concatenate(
        [unpatch_used, jnp.zeros((D, POUT - unpatch_used.shape[1]), jnp.float32)], 1
    )
    shared_grad = jnp.concatenate(
        [patch_grad.reshape(-1), unpatch_grad.reshape(-1), gain_grad.reshape(-1)]
    )
    split_grad = by_lanes(shared_grad, (count_dp, groups))
    lead = split_grad.shape[2]
    shared_stack = pad_first(split_grad, 2, 16 * D // split_grad[0, 0, 0].size).swapaxes(0, 1)
    shared_sum = lax.psum_scatter(shared_stack, "tensor", scatter_dimension=0, tiled=True)
    row_stack = jnp.concatenate([early_grad, late_grad], 0)
    stack = jnp.concatenate(
        [row_stack.reshape(count_dp, share_rows, D), shared_sum.reshape(count_dp, -1, D)], 1
    ).reshape(-1, D)
    own_share = sum_to_owners(stack, count_dp)
    own_rows = own_share[:share_rows]
    row_share = jnp.where(my_dp < qkv_parts, unpack_qkv(own_rows, 1).reshape(-1), own_rows.reshape(-1))
    shared_part = own_share[share_rows:].reshape((-1,) + split_grad.shape[3:])[:lead]
    shared_share = lax.all_gather(shared_part, "tensor", axis=0, tiled=False).reshape(-1)
    own_squares = jnp.sum(row_share * row_share) + jnp.sum(shared_part * shared_part)
    pixel_part = jnp.sum((alpha_label < 2).astype(jnp.float32))
    scalars = jnp.stack([own_squares, loss_part, pixel_part]).reshape(3, 1)
    totals = total_over_all(jnp.pad(jnp.broadcast_to(scalars, (3, 128)), ((0, 5), (0, 0))), 2)
    square_total, loss_total, pixel_total = totals[0, 0], totals[1, 0], totals[2, 0]
    norm_value = jnp.sqrt(square_total) / pixel_total
    factor = clip_norm / jnp.maximum(norm_value, clip_norm) / pixel_total
    step_float = step_count[0].astype(jnp.float32)
    row_new, row_first_new, row_second_new = adam_update(
        row_master[0], row_first[0], row_second[0], row_share * factor, step_float
    )
    shared_new, shared_first_new, shared_second_new = adam_update(
        shared_master, shared_first, shared_second, shared_share * factor, step_float
    )
    row_ema_new = ema_rate * row_ema[0] + (1.0 - ema_rate) * row_new
    shared_ema_new = ema_rate * shared_ema + (1.0 - ema_rate) * shared_new
    return (
        norm_value.reshape(1),
        (loss_total / pixel_total).reshape(1),
        row_new[None],
        row_first_new[None],
        row_second_new[None],
        row_ema_new[None],
        row_new.astype(jnp.bfloat16)[None],
        shared_new,
        shared_first_new,
        shared_second_new,
        shared_ema_new,
        shared_new.astype(jnp.bfloat16),
    )


def solution(mesh):
    placed = (
        P("dp", "tensor", None),
        P("dp"),
        P("dp", None, "tensor"),
        P("dp", None, "tensor"),
        P("dp", "tensor"),
        P(),
        P("tensor", "dp"),
        P("tensor", "dp"),
        P("tensor", "dp"),
        P("tensor", "dp"),
        P("dp"),
        P("dp"),
        P("dp"),
        P("dp"),
    )
    return jax.shard_map(
        per_device,
        mesh=mesh,
        in_specs=placed,
        out_specs=(
            P(),
            P(),
            P("tensor", "dp"),
            P("tensor", "dp"),
            P("tensor", "dp"),
            P("tensor", "dp"),
            P("tensor", "dp"),
            P("dp"),
            P("dp"),
            P("dp"),
            P("dp"),
            P("dp"),
        ),
        check_vma=False,
    )
```

```python
import math
from functools import partial

import jax
import jax.numpy as jnp
from jax import lax
from jax.experimental import pallas as pl
from jax.experimental.pallas import tpu as pltpu
from jax.sharding import PartitionSpec as P

D = 1024
DH = 64
FF = 4096
PATCH = 8
VTOK = 192
PIN = 576
POUT = 768
VMEM = pl.BlockSpec(memory_space=pltpu.VMEM)
ROOT_HALF = 0.5**0.5
NORMAL_PEAK = (2.0 * math.pi) ** -0.5


clip_norm = 0.005
beta_one = 0.9
beta_two = 0.95
adam_eps = 1e-08
decay_rate = 0.05
learn_rate = 0.03
ema_rate = 0.9
norm_eps = 1e-05
masked_score = -1e30


MESH = pl.DeviceIdType.MESH
NN = (((1,), (0,)), ((), ()))
NT = (((1,), (1,)), ((), ()))
TN = (((0,), (0,)), ((), ()))
LOW = jnp.bfloat16
WIDE = jnp.float32
PIECES = 4
TILE = 256


def dot(left, right, dims=NN):
    return lax.dot_general(left, right, dims, preferred_element_type=WIDE)


def remote(src, dst, send, recv, to):
    return pltpu.make_async_remote_copy(
        src_ref=src, dst_ref=dst, send_sem=send, recv_sem=recv, device_id=to, device_id_type=MESH
    )


class Corner:
    def __init__(self):
        self.me = lax.axis_index("tensor")
        self.first, self.last = self.me // 2, lax.rem(self.me, 2)
        self.mate = self.first * 2 + 1 - self.last
        self.far = (1 - self.first) * 2 + self.last
        self.opposite = (1 - self.first) * 2 + 1 - self.last

    def block(self, step):
        return lax.rem(self.first + 1 - step // 2, 2) * 2 + lax.rem(self.last + 1 - lax.rem(step, 2), 2)

    def greet(self):
        barrier = pltpu.get_barrier_semaphore()
        for other in (self.mate, self.far):
            pl.semaphore_signal(barrier, inc=1, device_id={"tensor": other}, device_id_type=MESH)
        pl.semaphore_wait(barrier, 2)


class Gather:
    def __init__(self, corner, ref, pieces, sems):
        self.corner, self.ref, self.pieces, self.sems = corner, ref, pieces, sems
        self.size = ref.shape[0] // 4
        self.rows = self.size // pieces

    @staticmethod
    def scratch(pieces):
        return [pltpu.SemaphoreType.DMA((pieces,))] * 6

    def part(self, owner, piece):
        return pl.ds(pl.multiple_of(owner * self.size + piece * self.rows, self.rows), self.rows)

    def copy(self, owner, piece, kind, to):
        here = self.ref.at[self.part(owner, piece)]
        return remote(here, here, self.sems[2 * kind].at[piece], self.sems[2 * kind + 1].at[piece], {"tensor": to})

    def start(self, piece):
        self.copy(self.corner.me, piece, 1, self.corner.far).start()
        self.copy(self.corner.me, piece, 0, self.corner.mate).start()

    def relay(self, piece):
        self.copy(self.corner.far, piece, 1, self.corner.far).wait_recv()
        self.copy(self.corner.far, piece, 2, self.corner.mate).start()

    def finish(self):
        corner = self.corner
        for piece in range(self.pieces):
            self.copy(corner.mate, piece, 0, corner.mate).wait_recv()
            self.copy(corner.opposite, piece, 2, corner.mate).wait_recv()
            self.copy(corner.me, piece, 0, corner.mate).wait_send()
            self.copy(corner.me, piece, 1, corner.far).wait_send()
            self.copy(corner.far, piece, 2, corner.mate).wait_send()


class Scatter:
    def __init__(self, corner, pieces, mate_out, mate_in, far_out, far_in, mate_send, mate_recv, far_send, far_recv):
        self.corner, self.pieces = corner, pieces
        self.mate_out, self.mate_in, self.far_out, self.far_in = mate_out, mate_in, far_out, far_in
        self.sems = mate_send, mate_recv, far_send, far_recv
        self.rows = far_out.shape[0] // pieces

    @staticmethod
    def scratch(rows, width, pieces):
        return [
            pltpu.VMEM((2, rows, width), LOW),
            pltpu.VMEM((2, rows, width), LOW),
            pltpu.VMEM((rows, width), LOW),
            pltpu.VMEM((rows, width), LOW),
            pltpu.SemaphoreType.DMA((2, pieces)),
            pltpu.SemaphoreType.DMA((2, pieces)),
            pltpu.SemaphoreType.DMA((pieces,)),
            pltpu.SemaphoreType.DMA((pieces,)),
        ]

    def part(self, piece):
        return pl.ds(piece * self.rows, self.rows)

    def mate_copy(self, half, piece):
        part = self.part(piece)
        return remote(
            self.mate_out.at[half, part],
            self.mate_in.at[half, part],
            self.sems[0].at[half, piece],
            self.sems[1].at[half, piece],
            {"tensor": self.corner.mate},
        )

    def far_copy(self, piece):
        part = self.part(piece)
        return remote(
            self.far_out.at[part],
            self.far_in.at[part],
            self.sems[2].at[piece],
            self.sems[3].at[piece],
            {"tensor": self.corner.far},
        )

    def give(self, half, ref):
        for piece in range(self.pieces):
            part = self.part(piece)
            self.mate_out[half, part] = ref[part].astype(LOW)
            self.mate_copy(half, piece).start()

    def cross(self, ref):
        for piece in range(self.pieces):
            part = self.part(piece)
            self.mate_copy(0, piece).wait_recv()
            self.far_out[part] = (ref[part] + self.mate_in[0, part].astype(WIDE)).astype(LOW)
            self.far_copy(piece).start()

    def step(self, step, ref):
        @pl.when(step == 0)
        def _():
            self.give(0, ref)

        @pl.when(step == 1)
        def _():
            self.cross(ref)

        @pl.when(step == 2)
        def _():
            self.give(1, ref)

    def land(self, piece, ref):
        part = self.part(piece)
        self.mate_copy(1, piece).wait_recv()
        self.far_copy(piece).wait_recv()
        return ref[part] + self.mate_in[1, part].astype(WIDE) + self.far_in[part].astype(WIDE)

    def close(self):
        for piece in range(self.pieces):
            self.mate_copy(0, piece).wait_send()
            self.mate_copy(1, piece).wait_send()
            self.far_copy(piece).wait_send()


def standard(values):
    centre = values - jnp.mean(values, -1, keepdims=True)
    inverse = lax.rsqrt(jnp.mean(centre * centre, -1, keepdims=True) + norm_eps)
    return centre * inverse, inverse


def norm_back(grad_out, scaled, inverse, gain):
    grad_scaled = grad_out * gain
    return inverse * (
        grad_scaled
        - jnp.mean(grad_scaled, -1, keepdims=True)
        - scaled * jnp.mean(grad_scaled * scaled, -1, keepdims=True)
    )


def qkv_places(parts, rows, columns):
    share = rows // parts
    wide = columns * 2 // 3
    packed = share * columns // 1024
    for at in range(parts):
        for j in range(2):
            half = share // 2
            yield (at * packed, half, j * wide, wide, at * share + j * half, 0)
        for j in range(4):
            quarter = share // 4
            yield (at * packed + share // 2, quarter, j * (columns - wide), columns - wide, at * share + j * quarter, wide)


def unpack_into(full, packed, parts):
    for row, rows, col, cols, to_row, to_col in qkv_places(parts, full.shape[0], full.shape[1]):
        full[to_row : to_row + rows, to_col : to_col + cols] = packed[row : row + rows, col : col + cols]


def pack_from(packed, full, parts, base=0):
    for row, rows, col, cols, to_row, to_col in qkv_places(parts, full.shape[0], full.shape[1]):
        packed[base + row : base + row + rows, col : col + cols] = full[to_row : to_row + rows, to_col : to_col + cols]


def rows_of(block, size):
    return pl.ds(pl.multiple_of(block * size, size), size)


def column_loop(width, body):
    @pl.loop(0, width // TILE)
    def _(tile):
        body(pl.ds(pl.multiple_of(tile * TILE, TILE), TILE))


def attend_kernel(parts, q_rows, count_ref, patch_ref, proj_ref, norm_ref, packed_ref, out_ref, *rest):
    corner = Corner()
    corner.greet()
    attend_body(parts, q_rows, corner, None, count_ref, patch_ref, proj_ref, norm_ref, packed_ref, out_ref, *rest)


def attend_body(parts, q_rows, corner, progress, count_ref, patch_ref, proj_ref, norm_ref, packed_ref, out_ref,
                embed_ref, normed1_ref, qkv_ref, attended_ref, log_ref, resid_ref, normed2_ref,
                qkv_proj, term, *comm):
    progress = progress or (lambda *_: None)
    scatter = Scatter(corner, PIECES, *comm[:8])
    gather = Gather(corner, normed2_ref, PIECES, comm[8:])
    size, width = embed_ref.shape
    length = patch_ref.shape[0]
    local = attended_ref.shape[1]

    @pl.loop(0, 4)
    def _(block):
        here = rows_of(block, size)
        column_loop(width, lambda cols: term.__setitem__((slice(None), cols), dot(patch_ref[here], proj_ref[:, cols])))

        @pl.when(block == corner.me)
        def _():
            embed_ref[...] = term[...]

        scaled, inverse = standard(term[...])
        normed1_ref[here] = (scaled * norm_ref[0:1] + norm_ref[1:2]).astype(LOW)

    progress("weights")
    unpack_into(qkv_proj, packed_ref, parts)

    @pl.loop(0, 4)
    def _(block):
        here = rows_of(block, size)

        def columns(cols):
            qkv_ref[here, cols] = dot(normed1_ref[here], qkv_proj[:, cols]).astype(LOW)

        column_loop(3 * local, columns)

    valid = lax.broadcasted_iota(jnp.int32, (1, length), 1) < count_ref[0] * VTOK
    left = lax.broadcasted_iota(jnp.int32, (1, 2 * DH), 1) < DH
    factor = jnp.array(DH ** (-0.5), LOW)

    @pl.loop(0, length // q_rows)
    def _(turn):
        here = rows_of(turn, q_rows)
        for pair in range(local // (2 * DH)):
            lanes = slice(pair * 2 * DH, (pair + 1) * 2 * DH)
            queries = qkv_ref[here, lanes] * factor
            keyset = qkv_ref[:, local + pair * 2 * DH : local + (pair + 1) * 2 * DH]
            values = qkv_ref[:, 2 * local + pair * 2 * DH : 2 * local + (pair + 1) * 2 * DH]
            found = []
            for side in range(2):
                mine = left if side == 0 else ~left
                scores = dot(jnp.where(mine, queries, jnp.zeros_like(queries)), keyset, NT)
                scores = jnp.where(valid, scores, masked_score)
                top = jnp.max(scores, -1, keepdims=True)
                powers = jnp.exp(scores - top)
                total = jnp.sum(powers, -1, keepdims=True)
                log_ref[here, pair * 2 + side : pair * 2 + side + 1] = top + jnp.log(total)
                found.append(dot((powers * (1.0 / total)).astype(LOW), values))
            attended_ref[here, lanes] = jnp.where(left, found[0], found[1]).astype(LOW)
        progress("turn", turn)

    progress("out")

    @pl.loop(0, 4)
    def _(step):
        here = rows_of(corner.block(step), size)
        column_loop(width, lambda cols: term.__setitem__((slice(None), cols), dot(attended_ref[here], out_ref[:, cols])))
        scatter.step(step, term)

    for piece in range(PIECES):
        part = scatter.part(piece)
        resid = embed_ref[part] + scatter.land(piece, term)
        resid_ref[part] = resid
        scaled, inverse = standard(resid)
        normed2_ref[gather.part(corner.me, piece)] = (scaled * norm_ref[2:3] + norm_ref[3:4]).astype(LOW)
        gather.start(piece)
        progress("land", piece)
    for piece in range(PIECES):
        gather.relay(piece)
    gather.finish()
    scatter.close()


def attend(count, patches, patch_proj, norm, packed, out_proj, parts, collective_id):
    length, size = patches.shape[0], patches.shape[0] // 4
    width, local = patch_proj.shape[1], out_proj.shape[0]
    shape = jax.ShapeDtypeStruct
    return pl.pallas_call(
        partial(attend_kernel, parts, 256),
        out_shape=(
            shape((size, width), WIDE),
            shape((length, width), LOW),
            shape((length, 3 * local), LOW),
            shape((length, local), LOW),
            shape((length, local // DH), WIDE),
            shape((size, width), WIDE),
            shape((length, width), LOW),
        ),
        in_specs=[pl.BlockSpec(memory_space=pltpu.SMEM)] + [VMEM] * 5,
        out_specs=(VMEM,) * 7,
        scratch_shapes=[pltpu.VMEM((width, 3 * local), LOW), pltpu.VMEM((size, width), WIDE)]
        + Scatter.scratch(size, width, PIECES)
        + Gather.scratch(PIECES),
        compiler_params=pltpu.CompilerParams(
            collective_id=collective_id, has_side_effects=True, vmem_limit_bytes=62 * 2**20
        ),
    )(count, patches, patch_proj, norm, packed, out_proj)


class Lines:
    def __init__(self, lines):
        self.lines = lines
        self.me = lax.axis_index("dp")
        self.line, self.side = self.me // 2, lax.rem(self.me, 2)
        self.pair = {"dp": self.line * 2 + 1 - self.side}
        self.above = {"dp": lax.rem(self.line + 1, lines) * 2 + self.side}
        self.below = {"dp": lax.rem(self.line + lines - 1, lines) * 2 + self.side}
        self.has_below, self.has_above = self.line > 0, self.line < lines - 1

    def signal(self, barrier):
        pl.semaphore_signal(barrier, inc=1, device_id=self.pair, device_id_type=MESH)

        @pl.when(self.has_below)
        def _():
            pl.semaphore_signal(barrier, inc=1, device_id=self.below, device_id_type=MESH)

        @pl.when(self.has_above)
        def _():
            pl.semaphore_signal(barrier, inc=1, device_id=self.above, device_id_type=MESH)

        return 1 + jnp.minimum(self.line, 1) + jnp.minimum(self.lines - 1 - self.line, 1)


class LineGather:
    def __init__(self, spot, ref, base, chunk, pieces, late_own, sems):
        self.spot, self.ref, self.base, self.chunk, self.pieces, self.late_own = spot, ref, base, chunk, pieces, late_own
        self.sems = sems
        self.rows = chunk // pieces
        self.steps = (spot.lines - 1) * pieces

    @staticmethod
    def scratch(lines, pieces):
        return [pltpu.SemaphoreType.DMA((lines * pieces,))] * 6

    def copy(self, kind, line, side, piece, to):
        start = self.base + (line * 2 + side) * self.chunk + piece * self.rows
        here = self.ref.at[pl.ds(pl.multiple_of(start, 16), self.rows)]
        at = line * self.pieces + piece
        return remote(here, here, self.sems[2 * kind].at[at], self.sems[2 * kind + 1].at[at], to)

    def up(self, line, piece):
        return self.copy(0, line, self.spot.side, piece, self.spot.above)

    def down(self, line, piece):
        return self.copy(1, line, self.spot.side, piece, self.spot.below)

    def across(self, line, piece):
        return self.copy(2, line, self.spot.side, piece, self.spot.pair)

    def crossed(self, line, piece):
        return self.copy(2, line, 1 - self.spot.side, piece, self.spot.pair)

    def own(self, copy):
        @pl.loop(0, self.pieces)
        def _(piece):
            copy(self.spot.line, piece).start()

    def begin(self):
        spot = self.spot
        first = spot.line == 0 if self.late_own else spot.line >= 0

        @pl.when(first & spot.has_above)
        def _():
            self.own(self.up)

        @pl.when(spot.has_below)
        def _():
            self.own(self.down)

        @pl.when(first)
        def _():
            self.own(self.across)

    def step(self, at):
        spot = self.spot
        piece = lax.rem(at, self.pieces)

        @pl.when(at < spot.line * self.pieces)
        def _():
            line = at // self.pieces
            self.up(line, piece).wait_recv()

            @pl.when(spot.has_above)
            def _():
                self.up(line, piece).start()

            self.across(line, piece).start()

        if self.late_own:

            @pl.when((at == spot.line * self.pieces - 1) & spot.has_above)
            def _():
                self.own(self.up)

            @pl.when((at == self.pieces - 1) & spot.has_below)
            def _():
                self.own(self.across)

        @pl.when(at < (spot.lines - 1 - spot.line) * self.pieces)
        def _():
            line = spot.line + 1 + at // self.pieces
            self.down(line, piece).wait_recv()

            @pl.when(spot.has_below)
            def _():
                self.down(line, piece).start()

            self.across(line, piece).start()

    def wait_crossed(self, line, pieces=None):
        @pl.loop(0, pieces or self.pieces)
        def _(piece):
            self.crossed(line, piece).wait_recv()

    def close(self):
        spot = self.spot

        @pl.loop(0, spot.lines * self.pieces)
        def _(at):
            line, piece = at // self.pieces, lax.rem(at, self.pieces)
            self.across(line, piece).wait_send()

            @pl.when((line <= spot.line) & spot.has_above)
            def _():
                self.up(line, piece).wait_send()

            @pl.when((line >= spot.line) & spot.has_below)
            def _():
                self.down(line, piece).wait_send()


WINDOW = 48
FRONT = 80
PADDED = 1616
ROW_START = (0, 160, 336, 496)
USED_START = (None, None, None, 0, 128, 352, 576, 800)


def shared_offsets(me, quarter):
    chunk = SHARED_LANES
    rows = jnp.where(me == 0, 0, jnp.where(me == 1, 160, jnp.where(me == 2, 336, 496)))
    used = (me - 4) * 224 + 128
    return (
        FRONT + 8 * rows - me * chunk + 8 * WINDOW * quarter,
        FRONT + 8 * rows - me * chunk + 8 * 32 * quarter,
        FRONT + PATCH_LANES - me * chunk + 6 * 48 * quarter,
        FRONT + PATCH_LANES + 6 * used - me * chunk + 6 * 64 * quarter,
        FRONT + PATCH_LANES + 6 * D - me * chunk,
    )


def shared_walk(me, quarter, take, phases=range(5)):
    rows, last_rows, first_used, used, norm = shared_offsets(me, quarter)
    for j in range(8):
        if 0 in phases:
            take(me < 3, 0, WINDOW, j, rows + j, 8)
        if 1 in phases:
            take((me == 3) & (quarter < 3), 0, 32, j, last_rows + j, 8)
    if 2 in phases:
        for j in range(3):
            take((me == 3) & (quarter < 3), 32, 16, j, first_used + 6 * 16 * j, 6)
    if 3 in phases:
        for j in range(2):
            take(me > 3, 0, 32, j, used + 6 * 32 * j, 6)
    if 4 in phases:
        for j in range(8):
            take((me == 7) & (quarter == 0), 32, 8, j, norm + j, 8)


def window_pieces(kind, row):
    found = []
    if kind == 0:
        for me in range(3):
            at = row - ROW_START[me]
            if 0 <= at < 4 * WINDOW:
                found.append((me, at // WINDOW, at % WINDOW, None))
        at = row - ROW_START[3]
        if 0 <= at < 96:
            found.append((3, at // 32, at % 32, None))
    else:
        if row < 144:
            found.append((3, row // 48, 32, row % 48 // 16))
        for me in range(4, 8):
            at = row - USED_START[me]
            if 0 <= at < 256:
                found.append((me, at // 64, at % 32, at % 64 // 32))
    return found

SHARED_LANES = 1348
PATCH_LANES = PIN * D // 128
CHUNK_PIECES = 4


def forward_kernel(lines, q_rows, count_ref, row_ref, shared_ref, own_patch_ref,
                   weight_ref, used_ref, norm_ref,
                   embed_ref, normed1_ref, qkv_ref, attended_ref, log_ref, resid_ref, normed2_ref,
                   patches, proj, windows, *rest):
    body, extra = rest[:2 + 14], rest[2 + 14:]
    corner, spot = Corner(), Lines(lines)
    barrier = pltpu.get_barrier_semaphore()
    for other in (corner.mate, corner.far):
        pl.semaphore_signal(barrier, inc=1, device_id={"tensor": other}, device_id_type=MESH)
    pl.semaphore_wait(barrier, 2 + spot.signal(barrier))
    parts = lines // 2
    chunk = weight_ref.shape[0] // (2 * lines)
    size, inputs = own_patch_ref.shape
    window = LineGather(spot, windows, corner.me * (2 * lines * WINDOW), WINDOW, 1, False, extra[0:6])
    weights = LineGather(spot, weight_ref, 0, chunk, CHUNK_PIECES, True, extra[6:12])
    spread = Gather(corner, windows, 2, extra[12:18])
    given = Gather(corner, patches, 1, extra[18:24])

    patches[given.part(corner.me, 0)] = own_patch_ref[...]
    given.start(0)
    base = pl.multiple_of((corner.me * 2 * lines + spot.me) * WINDOW, 16)
    windows[pl.ds(base, WINDOW)] = jnp.zeros((WINDOW, windows.shape[1]), LOW)

    def take(condition, row, rows, j, start, stride):
        @pl.when(condition)
        def _():
            windows[pl.ds(pl.multiple_of(base + row, 16), rows), j * 128 : (j + 1) * 128] = shared_ref[
                pl.ds(start, rows, stride)
            ].astype(LOW)

    shared_walk(spot.me, corner.me, take)
    window.begin()
    own = pl.multiple_of(spot.me * chunk, 16)

    @pl.when(spot.me < parts)
    def _():
        for row, rows, col, cols, at, at_col in qkv_places(1, chunk * 4 // 3, D * 3 // 4):
            for j in range(cols // 128):
                weight_ref[pl.ds(pl.multiple_of(own + row, 16), rows), col + j * 128 : col + (j + 1) * 128] = row_ref[
                    pl.ds(6 * at + at_col // 128 + j, rows, 6)
                ].astype(LOW)

    @pl.when(spot.me >= parts)
    def _():
        for j in range(8):
            weight_ref[pl.ds(own, chunk), j * 128 : (j + 1) * 128] = row_ref[pl.ds(j, chunk, 8)].astype(LOW)

    weights.begin()
    for at in range(window.steps):
        window.step(at)
    for line in range(lines):
        window.wait_crossed(line)
    for piece in range(2):
        spread.start(piece)
    given.relay(0)
    for at in range(2):
        weights.step(at)
    spread.relay(0)
    weights.step(2)
    spread.relay(1)
    weights.step(3)
    given.finish()
    spread.finish()

    def source(me, quarter, row, rows, j):
        start = (quarter * 2 * lines + me) * WINDOW + row
        return windows[start : start + rows] if j is None else windows[start : start + rows, j * 128 : (j + 1) * 128]

    for row in range(0, proj.shape[0], 16):
        proj[row : row + 16] = sum(source(me, t, at, 16, j) for me, t, at, j in window_pieces(0, row))
    for row in range(0, used_ref.shape[0], 16):
        used_ref[row : row + 16] = sum(source(me, t, at, 16, j) for me, t, at, j in window_pieces(1, row))
    norm_ref[...] = source(2 * lines - 1, 0, 32, 8, None).astype(WIDE)

    def progress(place, at=None):
        if place == "weights":
            weights.wait_crossed(0)
        if place == "turn":
            @pl.when(at >= 2)
            def _():
                weights.step(at + 2)
        if place == "out":
            weights.wait_crossed(1)
        if place == "land":
            weights.step(8 + at)

    attend_body(parts, q_rows, corner, progress, count_ref, patches, proj, norm_ref,
                weight_ref.at[pl.ds(0, D * 3 // 4)], weight_ref.at[pl.ds(D * 3 // 4, D // 4)],
                embed_ref, normed1_ref, qkv_ref, attended_ref, log_ref, resid_ref, normed2_ref, *body)
    for line in range(2, lines):
        weights.wait_crossed(line)
    weights.close()
    window.close()


def forward(count, row_lanes, shared_lanes, own_patches, lines, collective_id):
    size, inputs = own_patches.shape
    length, width, local = 4 * size, D, D // 4
    shape = jax.ShapeDtypeStruct
    return pl.pallas_call(
        partial(forward_kernel, lines, 256),
        out_shape=(
            shape((3 * D, D), LOW),
            shape((D, 128), LOW),
            shape((8, D), WIDE),
            shape((size, width), WIDE),
            shape((length, width), LOW),
            shape((length, 3 * local), LOW),
            shape((length, local), LOW),
            shape((length, local // DH), WIDE),
            shape((size, width), WIDE),
            shape((length, width), LOW),
        ),
        in_specs=[pl.BlockSpec(memory_space=pltpu.SMEM)] + [VMEM] * 3,
        out_specs=(VMEM,) * 10,
        scratch_shapes=[
            pltpu.VMEM((length, inputs), LOW),
            pltpu.VMEM((inputs, width), LOW),
            pltpu.VMEM((8 * lines * WINDOW, width), LOW),
            pltpu.VMEM((width, 3 * local), LOW),
            pltpu.VMEM((size, width), WIDE),
        ]
        + Scatter.scratch(size, width, PIECES)
        + Gather.scratch(PIECES)
        + LineGather.scratch(lines, 1)
        + LineGather.scratch(lines, CHUNK_PIECES)
        + Gather.scratch(2)
        + Gather.scratch(1),
        compiler_params=pltpu.CompilerParams(
            collective_id=collective_id, has_side_effects=True, vmem_limit_bytes=63 * 2**20
        ),
    )(count, row_lanes, shared_lanes, own_patches)


def mlp_kernel(normed2_ref, up_ref, down_ref, resid1_ref, cols_ref, hidden_ref, active_ref, low_ref, table_ref, term, *comm):
    corner = Corner()
    corner.greet()
    scatter = Scatter(corner, PIECES, *comm[:8])
    gather = Gather(corner, table_ref, PIECES, comm[8:])
    size, width = resid1_ref.shape

    @pl.loop(0, 4)
    def _(step):
        here = rows_of(corner.block(step), size)

        def columns(cols):
            hidden = dot(normed2_ref[here], up_ref[:, cols])
            hidden_ref[here, cols] = hidden
            active_ref[here, cols] = (0.5 * hidden * (1.0 + lax.erf(hidden * ROOT_HALF))).astype(LOW)

        column_loop(up_ref.shape[1], columns)
        column_loop(width, lambda cols: term.__setitem__((slice(None), cols), dot(active_ref[here], down_ref[:, cols])))
        scatter.step(step, term)

    for piece in range(PIECES):
        part = scatter.part(piece)
        low_ref[part] = (resid1_ref[part] + scatter.land(piece, term)).astype(LOW)
        table_ref[gather.part(corner.me, piece)] = dot(low_ref[part], cols_ref[...]).astype(LOW)
        gather.start(piece)
    for piece in range(PIECES):
        gather.relay(piece)
    gather.finish()
    scatter.close()


def mlp(normed2, up_proj, down_proj, resid1, used_cols, collective_id):
    length, size, width = normed2.shape[0], resid1.shape[0], resid1.shape[1]
    hidden = up_proj.shape[1]
    shape = jax.ShapeDtypeStruct
    return pl.pallas_call(
        mlp_kernel,
        out_shape=(
            shape((length, hidden), WIDE),
            shape((length, hidden), LOW),
            shape((size, width), LOW),
            shape((length, used_cols.shape[1]), LOW),
        ),
        in_specs=[VMEM] * 5,
        out_specs=(VMEM,) * 4,
        scratch_shapes=[pltpu.VMEM((size, width), WIDE)]
        + Scatter.scratch(size, width, PIECES)
        + Gather.scratch(PIECES),
        compiler_params=pltpu.CompilerParams(
            collective_id=collective_id, has_side_effects=True, vmem_limit_bytes=62 * 2**20
        ),
    )(normed2, up_proj, down_proj, resid1, used_cols)


def mlp_back_kernel(table_ref, cols_ref, low_ref, active_ref, hidden_ref, normed2_ref, up_ref, down_ref, resid1_ref, norm_ref,
                    unpatch_ref, grad_ref, resid_grad_ref, branch_ref, gain_ref,
                    gauss, down_in, hidden_grad, term, tail, *comm):
    corner = Corner()
    corner.greet()
    small = Scatter(corner, 1, *comm[:8])
    spread = Gather(corner, gauss, 1, comm[8:14])
    scatter = Scatter(corner, PIECES, *comm[14:22])
    gather = Gather(corner, branch_ref, PIECES, comm[22:])
    size, width = resid1_ref.shape
    ff = up_ref.shape[1]

    def view(step):
        return table_ref.at[rows_of(corner.block(step), size)]

    tail[...] = view(0)[...].astype(WIDE)
    small.give(0, tail)
    tail[...] = view(1)[...].astype(WIDE)
    small.cross(tail)
    tail[...] = view(2)[...].astype(WIDE)
    small.give(1, tail)
    tail[...] = view(3)[...].astype(WIDE)
    own_gauss = small.land(0, tail).astype(LOW)
    gauss[spread.part(corner.me, 0)] = own_gauss
    spread.start(0)
    unpatch_ref[...] = dot(low_ref[...], own_gauss, TN)
    spread.relay(0)
    spread.finish()
    small.close()

    @pl.loop(0, 4)
    def _(step):
        here = rows_of(corner.block(step), size)
        term[...] = dot(gauss[here], cols_ref[...], NT)
        down_in[here] = term[...].astype(LOW)

        @pl.when(step == 3)
        def _():
            resid_grad_ref[...] = term[...]

        def columns(cols):
            active_grad = dot(down_in[here], down_ref[cols, :], NT)
            hidden = hidden_ref[here, cols]
            slope = 0.5 * (1.0 + lax.erf(hidden * ROOT_HALF)) + hidden * (jnp.exp(-0.5 * hidden * hidden) * NORMAL_PEAK)
            hidden_grad[here, cols] = (active_grad * slope).astype(LOW)

        column_loop(ff, columns)

        def back(cols):
            term[:, cols] = dot(hidden_grad[here], up_ref[cols, :], NT)

        column_loop(width, back)
        scatter.step(step, term)

    @pl.loop(0, width // TILE)
    def _(tile):
        cols = pl.ds(pl.multiple_of(tile * TILE, TILE), TILE)
        grad_ref[cols, :] = dot(normed2_ref[:, cols], hidden_grad[...], TN)

    @pl.loop(0, ff // TILE)
    def _(tile):
        cols = pl.ds(pl.multiple_of(tile * TILE, TILE), TILE)
        grad_ref[pl.ds(pl.multiple_of(width + tile * TILE, TILE), TILE), :] = dot(active_ref[:, cols], down_in[...], TN)

    gain_sum, bias_sum = jnp.zeros((1, width), WIDE), jnp.zeros((1, width), WIDE)
    for piece in range(PIECES):
        part = scatter.part(piece)
        grad = scatter.land(piece, term)
        scaled, inverse = standard(resid1_ref[part])
        total = resid_grad_ref[part] + norm_back(grad, scaled, inverse, norm_ref[2:3])
        resid_grad_ref[part] = total
        branch_ref[gather.part(corner.me, piece)] = total.astype(LOW)
        gather.start(piece)
        gain_sum += jnp.sum(grad * scaled, 0, keepdims=True)
        bias_sum += jnp.sum(grad, 0, keepdims=True)
    gain_ref[0:1] = gain_sum
    gain_ref[1:2] = bias_sum
    for piece in range(PIECES):
        gather.relay(piece)
    gather.finish()
    scatter.close()


def mlp_back(table_grad, used_cols, low, active, hidden, normed2, up_proj, down_proj, resid1, norm, collective_id):
    length, size, width = normed2.shape[0], resid1.shape[0], resid1.shape[1]
    ff, used = up_proj.shape[1], used_cols.shape[1]
    shape = jax.ShapeDtypeStruct
    return pl.pallas_call(
        mlp_back_kernel,
        out_shape=(
            shape((width, used), WIDE),
            shape((width + ff, width), WIDE),
            shape((size, width), WIDE),
            shape((length, width), LOW),
            shape((2, width), WIDE),
        ),
        in_specs=[VMEM] * 10,
        out_specs=(VMEM,) * 5,
        scratch_shapes=[
            pltpu.VMEM((length, used), LOW),
            pltpu.VMEM((length, width), LOW),
            pltpu.VMEM((length, ff), LOW),
            pltpu.VMEM((size, width), WIDE),
            pltpu.VMEM((size, used), WIDE),
        ]
        + Scatter.scratch(size, used, 1)
        + Gather.scratch(1)
        + Scatter.scratch(size, width, PIECES)
        + Gather.scratch(PIECES),
        compiler_params=pltpu.CompilerParams(
            collective_id=collective_id, has_side_effects=True, vmem_limit_bytes=63 * 2**20
        ),
    )(table_grad, used_cols, low, active, hidden, normed2, up_proj, down_proj, resid1, norm)


def attend_back_kernel(parts, q_rows, count_ref, branch_ref, out_ref, qkv_ref, log_ref, packed_ref, attended_ref, normed1_ref, embed_ref,
                       resid_grad_ref, norm_ref, patch_ref, grad_ref, patch_grad_ref, gain_ref,
                       qkv_proj, attended_grad, qkv_grad, key_grad, value_grad, full_grad, term, embed_grad, *comm):
    corner = Corner()
    corner.greet()
    scatter = Scatter(corner, PIECES, *comm)
    size, width = embed_ref.shape
    length, local = attended_ref.shape
    unpack_into(qkv_proj, packed_ref, parts)

    @pl.loop(0, 4)
    def _(block):
        here = rows_of(block, size)
        attended_grad[here] = dot(branch_ref[here], out_ref[...], NT).astype(LOW)

    key_grad[...] = jnp.zeros_like(key_grad)
    value_grad[...] = jnp.zeros_like(value_grad)
    valid = lax.broadcasted_iota(jnp.int32, (1, length), 1) < count_ref[0] * VTOK
    left = lax.broadcasted_iota(jnp.int32, (1, 2 * DH), 1) < DH
    factor = jnp.array(DH ** (-0.5), LOW)

    @pl.loop(0, length // q_rows)
    def _(turn):
        here = rows_of(turn, q_rows)
        for pair in range(local // (2 * DH)):
            lanes = slice(pair * 2 * DH, (pair + 1) * 2 * DH)
            queries = qkv_ref[here, lanes] * factor
            grads = attended_grad[here, lanes]
            keyset = qkv_ref[:, local + pair * 2 * DH : local + (pair + 1) * 2 * DH]
            values = qkv_ref[:, 2 * local + pair * 2 * DH : 2 * local + (pair + 1) * 2 * DH]
            found = []
            for side in range(2):
                mine = left if side == 0 else ~left
                own_query = jnp.where(mine, queries, jnp.zeros_like(queries))
                own_grad = jnp.where(mine, grads, jnp.zeros_like(grads))
                scores = jnp.where(valid, dot(own_query, keyset, NT), masked_score)
                probs = jnp.exp(scores - log_ref[here, pair * 2 + side : pair * 2 + side + 1])
                prob_grad = dot(own_grad, values, NT)
                value_grad[:, lanes] += dot(probs.astype(LOW), own_grad, TN)
                centre = jnp.sum(probs * prob_grad, -1, keepdims=True)
                score_grad = (probs * (prob_grad - centre)).astype(LOW)
                found.append(dot(score_grad, keyset))
                key_grad[:, lanes] += dot(score_grad, own_query, TN)
            qkv_grad[here, lanes] = (jnp.where(left, found[0], found[1]) * (DH ** (-0.5))).astype(LOW)

    qkv_grad[:, local : 2 * local] = key_grad[...].astype(LOW)
    qkv_grad[:, 2 * local :] = value_grad[...].astype(LOW)

    @pl.loop(0, 4)
    def _(step):
        here = rows_of(corner.block(step), size)

        def columns(cols):
            term[:, cols] = dot(qkv_grad[here], qkv_proj[cols, :], NT)

        column_loop(width, columns)
        scatter.step(step, term)

    grad_ref[grad_ref.shape[0] - local :, :] = dot(attended_ref[...], branch_ref[...], TN)

    @pl.loop(0, width // TILE)
    def _(tile):
        cols = pl.ds(pl.multiple_of(tile * TILE, TILE), TILE)
        full_grad[cols, :] = dot(normed1_ref[:, cols], qkv_grad[...], TN)

    pack_from(grad_ref, full_grad, parts)

    gain_sum, bias_sum = jnp.zeros((1, width), WIDE), jnp.zeros((1, width), WIDE)
    for piece in range(PIECES):
        part = scatter.part(piece)
        grad = scatter.land(piece, term)
        scaled, inverse = standard(embed_ref[part])
        embed_grad[part] = (resid_grad_ref[part] + norm_back(grad, scaled, inverse, norm_ref[0:1])).astype(LOW)
        gain_sum += jnp.sum(grad * scaled, 0, keepdims=True)
        bias_sum += jnp.sum(grad, 0, keepdims=True)
    gain_ref[0:1] = gain_sum
    gain_ref[1:2] = bias_sum
    patch_grad_ref[...] = dot(patch_ref[...], embed_grad[...], TN)
    scatter.close()


def attend_back(count, branch, out_proj, qkv, log_total, packed, attended, normed1, embed, resid_grad, norm, patches, parts, collective_id):
    length, local = attended.shape
    size, width = embed.shape
    shape = jax.ShapeDtypeStruct
    return pl.pallas_call(
        partial(attend_back_kernel, parts, 256),
        out_shape=(
            shape((4 * local, width), WIDE),
            shape((patches.shape[1], width), WIDE),
            shape((2, width), WIDE),
        ),
        in_specs=[pl.BlockSpec(memory_space=pltpu.SMEM)] + [VMEM] * 11,
        out_specs=(VMEM,) * 3,
        scratch_shapes=[
            pltpu.VMEM((width, 3 * local), LOW),
            pltpu.VMEM((length, local), LOW),
            pltpu.VMEM((length, 3 * local), LOW),
            pltpu.VMEM((length, local), WIDE),
            pltpu.VMEM((length, local), WIDE),
            pltpu.VMEM((width, 3 * local), WIDE),
            pltpu.VMEM((size, width), WIDE),
            pltpu.VMEM((size, width), LOW),
        ]
        + Scatter.scratch(size, width, PIECES),
        compiler_params=pltpu.CompilerParams(
            collective_id=collective_id, has_side_effects=True, vmem_limit_bytes=62 * 2**20
        ),
    )(count, branch, out_proj, qkv, log_total, packed, attended, normed1, embed, resid_grad, norm, patches)


class LineSum:
    def __init__(self, spot, pieces, low, source, buffers, sems):
        self.spot, self.pieces, self.low, self.source = spot, pieces, low, source
        self.pair_out, self.pair_in, self.part, self.line_in, self.low_out, self.low_in = buffers
        self.p_send, self.p_recv, self.l_send, self.up_recv, self.down_recv = sems
        self.count = spot.lines * pieces
        self.rows = self.part.shape[0] // self.count

    @staticmethod
    def scratch(lines, rows, pieces, width, low):
        half = (lines * rows, width)
        kept = half if low else (rows, width)
        kind = LOW if low else WIDE
        return [
            pltpu.VMEM(half, LOW),
            pltpu.VMEM(half, LOW),
            pltpu.VMEM(half, WIDE),
            pltpu.VMEM(half, WIDE),
            pltpu.VMEM(half if low else (16, 128), LOW),
            pltpu.VMEM(kept, kind),
        ] + [pltpu.SemaphoreType.DMA((lines * pieces,))] * 5

    def target(self, step):
        turn = lax.rem(step, self.spot.lines)
        odd = lax.rem(turn, 2)
        return (1 - odd) * (self.spot.lines - 1 - turn // 2) + odd * (turn // 2)

    def slot(self, step):
        return pl.ds(pl.multiple_of(step * self.rows, 16), self.rows)

    def pair_copy(self, step):
        slot = self.slot(step)
        return remote(self.pair_out.at[slot], self.pair_in.at[slot], self.p_send.at[step], self.p_recv.at[step], self.spot.pair)

    def line_copy(self, step, to, recv):
        slot = self.slot(step)
        return remote(self.part.at[slot], self.line_in.at[slot], self.l_send.at[step], recv.at[step], to)

    def low_copy(self, step, to, recv):
        slot = self.slot(step)
        return remote(self.low_out.at[slot], self.low_in.at[slot], self.l_send.at[step], recv.at[step], to)

    def last_copy(self, step):
        here = pl.ds(pl.multiple_of(step // self.spot.lines * self.rows, 16), self.rows)
        return remote(self.part.at[self.slot(step)], self.low_in.at[here], self.l_send.at[step], self.down_recv.at[step], self.spot.below)

    def begin(self, step):
        self.pair_out[self.slot(step)] = self.source(self.target(step), 1 - self.spot.side, step // self.spot.lines).astype(LOW)
        self.pair_copy(step).start()

    def add(self, step, low):
        slot = self.slot(step)
        self.part[slot] += self.low_in[slot].astype(WIDE) if low else self.line_in[slot]

    def travel(self, step, rising):
        spot, slot = self.spot, self.slot(step)
        to, recv = (spot.above, self.up_recv) if rising else (spot.below, self.down_recv)
        last = spot.lines - 1
        from_end = spot.line == (1 if rising else last - 1)
        at_end = spot.line == (0 if rising else last)
        target = self.target(step)
        if self.low:

            @pl.when(at_end)
            def _():
                self.low_out[slot] = self.part[slot].astype(LOW)
                self.low_copy(step, to, recv).start()

            @pl.when(from_end)
            def _():
                self.low_copy(step, to, recv).wait_recv()
                self.add(step, True)

            @pl.when(jnp.logical_not(at_end | from_end))
            def _():
                self.line_copy(step, to, recv).wait_recv()
                self.add(step, False)

            @pl.when(jnp.logical_not(at_end))
            def _():
                self.line_copy(step, to, recv).start()
        else:

            @pl.when(jnp.logical_not(at_end))
            def _():
                self.line_copy(step, to, recv).wait_recv()
                self.add(step, False)

            if rising:
                self.line_copy(step, to, recv).start()
            else:

                @pl.when(target == spot.line - 1)
                def _():
                    self.last_copy(step).start()

                @pl.when(target < spot.line - 1)
                def _():
                    self.line_copy(step, to, recv).start()

    def advance(self, step):
        spot = self.spot

        @pl.when(step < self.count)
        def _():
            slot = self.slot(step)
            self.pair_copy(step).wait_recv()
            own = self.source(self.target(step), spot.side, step // spot.lines)
            self.part[slot] = own + self.pair_in[slot].astype(WIDE)

        rising = step - spot.line

        @pl.when((rising >= 0) & (rising < self.count) & (self.target(rising) > spot.line))
        def _():
            self.travel(rising, True)

        falling = step - (spot.lines - 1 - spot.line)

        @pl.when((falling >= 0) & (falling < self.count) & (self.target(falling) < spot.line))
        def _():
            self.travel(falling, False)

    def close(self, step, give):
        spot, slot = self.spot, self.slot(step)
        target = self.target(step)
        last = spot.lines - 1
        self.pair_copy(step).wait_send()

        @pl.when(target > spot.line)
        def _():
            if self.low:

                @pl.when(spot.line == 0)
                def _():
                    self.low_copy(step, spot.above, self.up_recv).wait_send()

                @pl.when(spot.line > 0)
                def _():
                    self.line_copy(step, spot.above, self.up_recv).wait_send()
            else:
                self.line_copy(step, spot.above, self.up_recv).wait_send()

        @pl.when(target < spot.line)
        def _():
            if self.low:

                @pl.when(spot.line == last)
                def _():
                    self.low_copy(step, spot.below, self.down_recv).wait_send()

                @pl.when(spot.line < last)
                def _():
                    self.line_copy(step, spot.below, self.down_recv).wait_send()
            else:
                self.line_copy(step, spot.below, self.down_recv).wait_send()

        @pl.when(target == spot.line)
        def _():
            if self.low:

                @pl.when(spot.line == 1)
                def _():
                    self.low_copy(step, spot.above, self.up_recv).wait_recv()
                    self.add(step, True)

                @pl.when(spot.line > 1)
                def _():
                    self.line_copy(step, spot.above, self.up_recv).wait_recv()
                    self.add(step, False)

                @pl.when(spot.line == last - 1)
                def _():
                    self.low_copy(step, spot.below, self.down_recv).wait_recv()
                    self.add(step, True)

                @pl.when(spot.line < last - 1)
                def _():
                    self.line_copy(step, spot.below, self.down_recv).wait_recv()
                    self.add(step, False)
            else:

                @pl.when(spot.has_below)
                def _():
                    self.line_copy(step, spot.above, self.up_recv).wait_recv()
                    self.add(step, False)

                @pl.when(spot.has_above)
                def _():
                    self.last_copy(step).wait_recv()
                    here = pl.ds(pl.multiple_of(step // spot.lines * self.rows, 16), self.rows)
                    self.part[slot] += self.low_in[here]

            give(step // spot.lines, self.part[slot])


SUM_PIECES = 6


def share_kernel(lines, early_ref, late_ref, patch_ref, used_ref, gain_ref, loss_ref, label_ref,
                 row_ref, shared_ref, total_ref,
                 term, windows, mine, slots, rows_out, *comm):
    corner, spot = Corner(), Lines(lines)
    pairs, width = 2 * lines, early_ref.shape[1]
    quarters = 4
    count = pairs * quarters
    me = spot.me * quarters + corner.me
    barrier = pltpu.get_barrier_semaphore()

    def peer(step):
        other = lax.rem(me + step, count)
        return {"dp": other // quarters, "tensor": lax.rem(other, quarters)}

    @pl.loop(1, count)
    def _(step):
        pl.semaphore_signal(barrier, inc=1, device_id=peer(step), device_id_type=MESH)

    pl.semaphore_wait(barrier, count - 1)
    chunk = (early_ref.shape[0] + late_ref.shape[0]) // pairs
    rows = chunk // SUM_PIECES
    edge = early_ref.shape[0]

    def weight_term(line, side, piece):
        start = (line * 2 + side) * chunk + piece * rows
        inside = start < edge
        first = early_ref[pl.ds(pl.multiple_of(jnp.where(inside, start, 0), 8), rows)]
        second = late_ref[pl.ds(pl.multiple_of(jnp.where(inside, 0, start - edge), 8), rows)]
        return jnp.where(inside, first, second)

    def shared_term(line, side, piece):
        return mine[pl.ds(pl.multiple_of((line * 2 + side) * WINDOW, 16), WINDOW)]

    weights = LineSum(spot, SUM_PIECES, True, weight_term, comm[0:6], comm[6:11])
    shared = LineSum(spot, 1, False, shared_term, comm[11:17], comm[17:22])
    scatter = Scatter(corner, PIECES, *comm[22:30])
    gather = Gather(corner, windows, 1, comm[30:36])
    own_sem, send_sem, recv_sem = comm[36:39]

    @pl.loop(0, weights.count)
    def _(step):
        weights.begin(step)

    @pl.loop(0, 4)
    def _(step):
        block = corner.block(step)
        term[...] = jnp.zeros_like(term)

        def rows_at(start, size):
            return pl.ds(pl.multiple_of(start, 16), size)

        for owner in range(3):
            at = owner * WINDOW
            term[at : at + WINDOW] = patch_ref[rows_at(ROW_START[owner] + block * WINDOW, WINDOW)]

        @pl.when(block < 3)
        def _():
            at = 3 * WINDOW
            term[at : at + 16] = patch_ref[rows_at(ROW_START[3] + block * 32, 16)]

            @pl.when(block < 2)
            def _():
                term[at + 16 : at + 32] = patch_ref[rows_at(ROW_START[3] + block * 32 + 16, 16)]

            for j in range(3):
                term[at + 32 : at + 48, j * 128 : (j + 1) * 128] = used_ref[rows_at(block * 48 + 16 * j, 16)]

        for owner in range(4, 8):
            at = owner * WINDOW
            for j in range(2):

                @pl.when((block < 3) | (owner < 7) | (j < 1))
                def _():
                    term[at : at + 32, j * 128 : (j + 1) * 128] = used_ref[rows_at(USED_START[owner] + block * 64 + 32 * j, 32)]

        @pl.when(block == 0)
        def _():
            term[7 * WINDOW + 32 : 7 * WINDOW + 40] = gain_ref[...]

        scatter.step(step, term)

    @pl.loop(0, 8)
    def _(step):
        weights.advance(step)

    for piece in range(PIECES):
        mine[scatter.part(piece)] = scatter.land(piece, term)
    for step in range(lines):
        shared.begin(step)

    @pl.loop(8, weights.count + lines - 1)
    def _(step):
        weights.advance(step)

    for step in range(2 * lines - 1):
        shared.advance(step)

    def keep_window(piece, value):
        windows[gather.part(corner.me, 0)] = value

    @pl.loop(0, lines)
    def _(step):
        shared.close(step, keep_window)

    gather.start(0)

    def keep_rows(piece, value):
        rows_out[pl.ds(pl.multiple_of(piece * rows, rows), rows)] = value

    @pl.loop(0, weights.count)
    def _(step):
        weights.close(step, keep_rows)

    gather.relay(0)

    @pl.when(spot.me < lines // 2)
    def _():
        for row, height, col, cols, at, at_col in qkv_places(1, chunk * 4 // 3, width * 3 // 4):
            for j in range(cols // 128):
                row_ref[pl.ds(6 * at + at_col // 128 + j, height, 6)] = rows_out[
                    row : row + height, col + j * 128 : col + (j + 1) * 128
                ]

    @pl.when(spot.me >= lines // 2)
    def _():
        for j in range(8):
            row_ref[pl.ds(j, chunk, 8)] = rows_out[:, j * 128 : (j + 1) * 128]

    squares = jnp.sum(rows_out[...] * rows_out[...], 0, keepdims=True)
    gather.finish()
    shared_ref[...] = jnp.zeros_like(shared_ref)
    for phase in range(5):
        for quarter in range(4):

            def take(condition, row, height, j, start, stride):
                @pl.when(condition)
                def _():
                    at = quarter * WINDOW + row
                    shared_ref[pl.ds(start, height, stride)] = windows[at : at + height, j * 128 : (j + 1) * 128]

            shared_walk(spot.me, quarter, take, (phase,))
    kept = shared_ref[FRONT : FRONT + PADDED - FRONT]
    place = lax.broadcasted_iota(jnp.int32, kept.shape, 0)
    kept = jnp.where((place < SHARED_LANES) & (corner.me == 0), kept, 0.0)
    square = jnp.sum(jnp.sum(squares, 1, keepdims=True)) + jnp.sum(kept * kept)
    counted = jnp.sum(jnp.where(label_ref[...] < 2, 1.0, 0.0))
    line = lax.broadcasted_iota(jnp.int32, total_ref.shape, 0)
    slots[me] = jnp.where(line == 0, square, jnp.where(line == 1, loss_ref[...], jnp.where(line == 2, counted, 0.0)))

    def send(step):
        return remote(slots.at[me], slots.at[me], send_sem.at[step], recv_sem.at[step], peer(step))

    def arrive(step):
        source = lax.rem(me - step + count, count)
        return remote(slots.at[source], slots.at[source], send_sem.at[step], recv_sem.at[step], peer(step))

    @pl.loop(1, count)
    def _(step):
        send(step).start()

    @pl.loop(1, count)
    def _(step):
        arrive(step).wait_recv()

    total_ref[...] = jnp.sum(slots[...], 0)

    @pl.loop(1, count)
    def _(step):
        send(step).wait_send()

    scatter.close()


def share(early, late, patch_grad, used_grad, gains, loss_tile, labels, lines, collective_id):
    width = early.shape[1]
    chunk = (early.shape[0] + late.shape[0]) // (2 * lines)
    count = 8 * lines
    shape = jax.ShapeDtypeStruct
    return pl.pallas_call(
        partial(share_kernel, lines),
        out_shape=(shape((chunk * width // 128, 128), WIDE), shape((PADDED, 128), WIDE), shape((8, 128), WIDE)),
        in_specs=[VMEM] * 7,
        out_specs=(VMEM,) * 3,
        scratch_shapes=[
            pltpu.VMEM((2 * lines * WINDOW, width), WIDE),
            pltpu.VMEM((4 * WINDOW, width), WIDE),
            pltpu.VMEM((2 * lines * WINDOW, width), WIDE),
            pltpu.VMEM((count, 8, 128), WIDE),
            pltpu.VMEM((chunk, width), WIDE),
        ]
        + LineSum.scratch(lines, chunk, SUM_PIECES, width, True)
        + LineSum.scratch(lines, WINDOW, 1, width, False)
        + Scatter.scratch(2 * lines * WINDOW, width, PIECES)
        + Gather.scratch(1)
        + [
            pltpu.SemaphoreType.DMA(()),
            pltpu.SemaphoreType.DMA((count,)),
            pltpu.SemaphoreType.DMA((count,)),
        ],
        compiler_params=pltpu.CompilerParams(
            collective_id=collective_id, has_side_effects=True, vmem_limit_bytes=63 * 2**20
        ),
    )(early, late, patch_grad, used_grad, gains, loss_tile, labels)


def render_kernel(area, wide, block, split, table_ref, splat_ref, dist_ref, label_ref, loss_ref, grad_ref, flip, picked, hot, spread_grad):
    tokens = table_ref.shape[0]
    groups = tokens // wide
    splats, pixels = splat_ref.shape
    for j in range(groups):
        flip[j * 2 * area : (j + 1) * 2 * area] = jnp.transpose(table_ref[j * wide : (j + 1) * wide].astype(jnp.float32)).astype(jnp.bfloat16)
    spread_grad[...] = jnp.zeros_like(spread_grad)
    wide_ids = lax.broadcasted_iota(jnp.int32, (wide, block), 0).astype(jnp.float32).astype(jnp.bfloat16)
    cell_ids = lax.broadcasted_iota(jnp.int32, (area, block), 0).astype(jnp.float32)
    cell_low = cell_ids.astype(jnp.bfloat16)
    one, nil = jnp.ones((wide, block), jnp.bfloat16), jnp.zeros((wide, block), jnp.bfloat16)

    def one_block(step, loss):
        here = pl.ds(pl.multiple_of(step * block, block), block)
        opacities, spreads, lows = [], [], []
        for k in range(splats):
            index = splat_ref[k : k + 1, here]
            token = index // area
            column = (token % wide).astype(jnp.float32).astype(jnp.bfloat16)
            group = (token // wide)
            cell = (index % area).astype(jnp.float32)
            match = jnp.where(wide_ids == column, one, nil)
            hot[k] = match
            picked[...] = lax.dot_general(flip[...], match, NN, preferred_element_type=jnp.float32)
            op_sum = jnp.zeros((area, block), jnp.float32)
            sp_sum = jnp.zeros((area, block), jnp.float32)
            for j in range(groups):
                same = cell_ids == jnp.where(group == j, cell, -1.0)
                op_sum += jnp.where(same, picked[j * 2 * area : j * 2 * area + area], 0.0)
                sp_sum += jnp.where(same, picked[j * 2 * area + area : (j + 1) * 2 * area], 0.0)
            opacities.append(jnp.sum(op_sum, 0, keepdims=True))
            spreads.append(jnp.sum(sp_sum, 0, keepdims=True))
            lows.append((group, cell))
        opacity, spread = jnp.concatenate(opacities, 0), jnp.concatenate(spreads, 0)
        distance = dist_ref[:, here].astype(jnp.float32)
        labels = label_ref[:, here]
        valid = jnp.where(labels < 2, 1.0, 0.0)
        target = jnp.where(labels == 1, 1.0, 0.0)
        op_sig, sp_sig = jax.nn.sigmoid(opacity), jax.nn.sigmoid(spread)
        fade = jnp.exp(-0.25 * distance * sp_sig)
        contrib = (0.02 + 0.96 * op_sig) * fade
        keep_log = jnp.sum(jnp.log1p(-contrib), 0, keepdims=True)
        keep = jnp.exp(keep_log)
        alpha = 1.0 - keep
        alpha_log = jnp.log(alpha)
        loss = loss - valid * (target * alpha_log + (1.0 - target) * keep_log)
        keep_grad = valid * (target * keep / alpha - (1.0 - target))
        contrib_grad = -keep_grad / (1.0 - contrib)
        op_grad = contrib_grad * (0.96 * op_sig * (1.0 - op_sig)) * fade
        sp_grad = contrib_grad * contrib * (-0.25 * distance * sp_sig * (1.0 - sp_sig))
        for k in range(splats):
            group, cell = lows[k]
            parts_op, parts_sp = op_grad[k : k + 1], sp_grad[k : k + 1]
            for part in range(split):
                low_op, low_sp = parts_op.astype(jnp.bfloat16), parts_sp.astype(jnp.bfloat16)
                parts_op, parts_sp = parts_op - low_op.astype(jnp.float32), parts_sp - low_sp.astype(jnp.float32)
                pieces = []
                for j in range(groups):
                    same = cell_low == jnp.where(group == j, cell, -1.0).astype(jnp.bfloat16)
                    pieces.append(jnp.where(same, low_op, jnp.bfloat16(0)))
                    pieces.append(jnp.where(same, low_sp, jnp.bfloat16(0)))
                weighted = jnp.concatenate(pieces, 0)
                spread_grad[...] += lax.dot_general(weighted, hot[k], NT, preferred_element_type=jnp.float32)
        return loss

    loss = lax.fori_loop(0, pixels // block, one_block, jnp.zeros((1, block), jnp.float32))
    loss_ref[...] = jnp.broadcast_to(jnp.sum(loss, 1, keepdims=True), loss_ref.shape)
    for j in range(groups):
        grad_ref[j * wide : (j + 1) * wide] = jnp.transpose(spread_grad[j * 2 * area : (j + 1) * 2 * area]).astype(grad_ref.dtype)

def render(table, splats, distance, labels, area, block=512, wide=256, split=2):
    tokens = table.shape[0]
    vm = pl.BlockSpec(memory_space=pltpu.VMEM)
    groups = tokens // wide
    return pl.pallas_call(
        partial(render_kernel, area, wide, block, split),
        out_shape=(jax.ShapeDtypeStruct((8, 128), jnp.float32), jax.ShapeDtypeStruct(table.shape, jnp.bfloat16)),
        in_specs=[vm] * 4, out_specs=(vm, vm),
        scratch_shapes=[pltpu.VMEM((groups * 2 * area, wide), jnp.bfloat16), pltpu.VMEM((groups * 2 * area, block), jnp.float32),
            pltpu.VMEM((splats.shape[0], wide, block), jnp.bfloat16), pltpu.VMEM((groups * 2 * area, wide), jnp.float32)],
        compiler_params=pltpu.CompilerParams(vmem_limit_bytes=48 * 2**20),
    )(table, splats, distance, labels)


def owner_sum_kernel(lines, pieces, g_ref, o_ref, pair_out, pair_in, part, line_in, own_in, p_send, p_recv, l_send, up_recv, down_recv):
    me = lax.axis_index("dp")
    line, side = me // 2, lax.rem(me, 2)
    chunk = o_ref.shape[0]
    rows = chunk // pieces
    count = lines * pieces
    pair = {"dp": line * 2 + 1 - side}
    above = {"dp": lax.rem(line + 1, lines) * 2 + side}
    below = {"dp": lax.rem(line + lines - 1, lines) * 2 + side}
    has_below, has_above = line > 0, line < lines - 1

    def target(step):
        turn = lax.rem(step, lines)
        odd = lax.rem(turn, 2)
        return (1 - odd) * (lines - 1 - turn // 2) + odd * (turn // 2)

    def slot(step):
        return pl.ds(pl.multiple_of(step * rows, rows), rows)

    def here(step):
        return pl.ds(pl.multiple_of(step // lines * rows, rows), rows)

    def source(step, owner):
        return pl.ds(pl.multiple_of((target(step) * 2 + owner) * chunk + step // lines * rows, rows), rows)

    def copy(src, dst, send, recv, to):
        return pltpu.make_async_remote_copy(
            src_ref=src, dst_ref=dst, send_sem=send, recv_sem=recv, device_id=to, device_id_type=MESH
        )

    def pair_copy(step):
        return copy(pair_out.at[slot(step)], pair_in.at[slot(step)], p_send.at[step], p_recv.at[step], pair)

    def line_copy(step, to, recv):
        return copy(part.at[slot(step)], line_in.at[slot(step)], l_send.at[step], recv.at[step], to)

    def last_copy(step):
        return copy(part.at[slot(step)], own_in.at[here(step)], l_send.at[step], down_recv.at[step], below)

    barrier = pltpu.get_barrier_semaphore()
    pl.semaphore_signal(barrier, inc=1, device_id=pair, device_id_type=MESH)

    @pl.when(has_below)
    def _():
        pl.semaphore_signal(barrier, inc=1, device_id=below, device_id_type=MESH)

    @pl.when(has_above)
    def _():
        pl.semaphore_signal(barrier, inc=1, device_id=above, device_id_type=MESH)

    pl.semaphore_wait(barrier, 1 + jnp.minimum(line, 1) + jnp.minimum(lines - 1 - line, 1))

    @pl.loop(0, count)
    def _(step):
        pair_out[slot(step)] = g_ref[source(step, 1 - side)].astype(jnp.bfloat16)
        pair_copy(step).start()

    @pl.loop(0, count + lines - 1)
    def _(step):
        @pl.when(step < count)
        def _():
            pair_copy(step).wait_recv()
            part[slot(step)] = g_ref[source(step, side)].astype(jnp.float32) + pair_in[slot(step)].astype(jnp.float32)

        rising = step - line

        @pl.when((rising >= 0) & (rising < count) & (target(rising) > line))
        def _():
            @pl.when(has_below)
            def _():
                line_copy(rising, above, up_recv).wait_recv()
                part[slot(rising)] += line_in[slot(rising)]

            line_copy(rising, above, up_recv).start()

        falling = step - (lines - 1 - line)

        @pl.when((falling >= 0) & (falling < count) & (target(falling) < line))
        def _():
            @pl.when(has_above)
            def _():
                line_copy(falling, below, down_recv).wait_recv()
                part[slot(falling)] += line_in[slot(falling)]

            @pl.when(target(falling) == line - 1)
            def _():
                last_copy(falling).start()

            @pl.when(target(falling) < line - 1)
            def _():
                line_copy(falling, below, down_recv).start()

    @pl.loop(0, count)
    def _(step):
        pair_copy(step).wait_send()

        @pl.when(target(step) > line)
        def _():
            line_copy(step, above, up_recv).wait_send()

        @pl.when(target(step) < line)
        def _():
            line_copy(step, below, down_recv).wait_send()

        @pl.when(target(step) == line)
        def _():
            o_ref[here(step)] = part[slot(step)]

            @pl.when(has_below)
            def _():
                line_copy(step, above, up_recv).wait_recv()
                o_ref[here(step)] += line_in[slot(step)]

            @pl.when(has_above)
            def _():
                last_copy(step).wait_recv()
                o_ref[here(step)] += own_in[here(step)]


def owner_sum(grad, count_dp, collective_id, pieces):
    lines = count_dp // 2
    total, width = grad.shape
    chunk = total // count_dp
    half = (lines * chunk, width)
    vmem = pl.BlockSpec(memory_space=pltpu.VMEM)
    return pl.pallas_call(
        partial(owner_sum_kernel, lines, pieces),
        out_shape=jax.ShapeDtypeStruct((chunk, width), jnp.float32),
        in_specs=[vmem],
        out_specs=vmem,
        scratch_shapes=[
            pltpu.VMEM(half, jnp.bfloat16),
            pltpu.VMEM(half, jnp.bfloat16),
            pltpu.VMEM(half, jnp.float32),
            pltpu.VMEM(half, jnp.float32),
            pltpu.VMEM((chunk, width), jnp.float32),
        ]
        + [pltpu.SemaphoreType.DMA((lines * pieces,))] * 5,
        compiler_params=pltpu.CompilerParams(
            collective_id=collective_id, has_side_effects=True, vmem_limit_bytes=62 * 2**20
        ),
    )(grad)


def total_kernel(mine_ref, sum_ref, slots, own_sem, send_sem, recv_sem):
    first, second = lax.axis_size("dp"), lax.axis_size("tensor")
    count = first * second
    me = lax.axis_index("dp") * second + lax.axis_index("tensor")

    def peer(step):
        other = lax.rem(me + step, count)
        return {"dp": other // second, "tensor": lax.rem(other, second)}

    barrier = pltpu.get_barrier_semaphore()

    @pl.loop(1, count)
    def _(step):
        pl.semaphore_signal(barrier, inc=1, device_id=peer(step), device_id_type=MESH)

    pl.semaphore_wait(barrier, count - 1)
    own = pltpu.make_async_copy(mine_ref, slots.at[me], own_sem)
    own.start()

    def send(step):
        return pltpu.make_async_remote_copy(
            src_ref=mine_ref,
            dst_ref=slots.at[me],
            send_sem=send_sem.at[step],
            recv_sem=recv_sem.at[step],
            device_id=peer(step),
            device_id_type=MESH,
        )

    @pl.loop(1, count)
    def _(step):
        send(step).start()

    @pl.loop(1, count)
    def _(step):
        send(step).wait()

    own.wait()
    sum_ref[...] = jnp.sum(slots[...], 0)


def total_over_all(mine, collective_id):
    count = lax.axis_size("dp") * lax.axis_size("tensor")
    vmem = pl.BlockSpec(memory_space=pltpu.VMEM)
    return pl.pallas_call(
        total_kernel,
        out_shape=jax.ShapeDtypeStruct(mine.shape, jnp.float32),
        in_specs=[vmem],
        out_specs=vmem,
        scratch_shapes=[
            pltpu.VMEM((count,) + mine.shape, jnp.float32),
            pltpu.SemaphoreType.DMA(()),
            pltpu.SemaphoreType.DMA((count,)),
            pltpu.SemaphoreType.DMA((count,)),
        ],
        compiler_params=pltpu.CompilerParams(collective_id=collective_id, has_side_effects=True),
    )(mine)


def pack_qkv(matrix, parts):
    rows, cols = matrix.shape
    first = matrix[:, :512].reshape(parts, 2, rows // parts // 2, 512).transpose(0, 2, 1, 3)
    second = matrix[:, 512:].reshape(parts, 4, rows // parts // 4, 256).transpose(0, 2, 1, 3)
    return jnp.concatenate([first.reshape(parts, -1, 1024), second.reshape(parts, -1, 1024)], 1).reshape(-1, 1024)


def unpack_qkv(packed, parts):
    rows = packed.shape[0] // parts
    packed = packed.reshape(parts, rows, 1024)
    cut = rows * 2 // 3
    first = packed[:, :cut].reshape(parts, cut, 2, 512).transpose(0, 2, 1, 3).reshape(-1, 512)
    second = packed[:, cut:].reshape(parts, rows - cut, 4, 256).transpose(0, 2, 1, 3).reshape(-1, 256)
    return jnp.concatenate([first, second], 1)


def by_lanes(flat, outer):
    size = flat.size // math.prod(outer)
    return flat.reshape(outer + ((size // 128, 128) if size % 128 == 0 else (size,)))


def pad_first(array, axis, unit):
    short = -array.shape[axis] % unit
    return jnp.pad(array, [(0, short if at == axis else 0) for at in range(array.ndim)])


def sum_to_owners(stack, count_dp):
    if count_dp == 8:
        return owner_sum(stack, count_dp, 1, 9)
    return lax.psum_scatter(stack, "dp", scatter_dimension=0, tiled=True)

def adam_update(master, first_mom, second_mom, gradient, step_float):
    first_new = beta_one * first_mom + (1.0 - beta_one) * gradient
    second_new = beta_two * second_mom + (1.0 - beta_two) * gradient * gradient
    first_hat = first_new / (1.0 - jnp.power(beta_one, step_float))
    second_hat = second_new / (1.0 - jnp.power(beta_two, step_float))
    master_new = master - learn_rate * (
        first_hat / (jnp.sqrt(second_hat) + adam_eps) + decay_rate * master
    )
    return (master_new, first_new, second_new)


def adam_kernel(total_ref, count_ref, *refs):
    norm_value = jnp.sqrt(total_ref[0, 0:1]) / total_ref[2, 0:1]
    factor = clip_norm / jnp.maximum(norm_value, clip_norm) / total_ref[2, 0:1]
    step_float = jnp.full((1, 1), count_ref[0], jnp.int32).astype(WIDE)
    grad, master, first, second, ema = (ref[...] for ref in refs[:5])
    new, first_new, second_new = adam_update(master, first, second, grad * factor.reshape(1, 1), step_float)
    for ref, value in zip(refs[5:], (new, first_new, second_new, ema_rate * ema + (1.0 - ema_rate) * new, new.astype(LOW))):
        ref[...] = value


def adam(totals, step_count, grad, master, first, second, ema, block):
    size = master.shape[1]
    spec = pl.BlockSpec((1, block), lambda at: (0, at))
    return pl.pallas_call(
        adam_kernel,
        grid=(size // block,),
        out_shape=tuple(jax.ShapeDtypeStruct(master.shape, kind) for kind in (WIDE,) * 4 + (LOW,)),
        in_specs=[pl.BlockSpec((8, 128), lambda at: (0, 0)), pl.BlockSpec(memory_space=pltpu.SMEM)] + [spec] * 5,
        out_specs=(spec,) * 5,
    )(totals, step_count, grad, master, first, second, ema)


def per_device(
    patches,
    view_counts,
    splat_index,
    splat_dist,
    alpha_label,
    step_count,
    row_master,
    row_first,
    row_second,
    row_ema,
    shared_master,
    shared_first,
    shared_second,
    shared_ema,
):
    groups = lax.axis_size("tensor")
    my_dp = lax.axis_index("dp")
    count_dp = lax.axis_size("dp")
    local_width = D // groups
    local_hidden = FF // groups
    qkv_parts = count_dp // 4
    share_rows = row_master.shape[1] // D
    own_patches = patches[0]
    if count_dp == 8:
        shared_lanes = jnp.pad(
            shared_master.reshape(SHARED_LANES, 128), ((FRONT, PADDED - FRONT - SHARED_LANES), (0, 0))
        )
        weights, used_cols, norm, embed, normed1, qkv, attended, log_total, resid1, normed2 = forward(
            view_counts, row_master.reshape(-1, 128), shared_lanes, own_patches, count_dp // 2, 7
        )
        packed_qkv, out_proj, up_proj, down_proj = jnp.split(weights, (3 * local_width, D, D + local_hidden))
    else:
        own_row = row_master[0].astype(jnp.bfloat16)
        own_tiles = jnp.where(
            my_dp < qkv_parts,
            pack_qkv(own_row.reshape(-1, 3 * local_width), 1),
            own_row.reshape(share_rows, D),
        )
        weights = lax.all_gather(own_tiles, "dp", axis=0, tiled=True)
        own_flat = shared_master.astype(jnp.bfloat16)
        own_shared = by_lanes(own_flat, ())
        lead = own_shared.shape[0]
        own_shared = pad_first(own_shared, 0, 2048 // own_shared[0].size)
        shared_weights = lax.all_gather(own_shared, "dp", axis=0, tiled=False)[:, :lead].reshape(-1, 128)
        qkv_rows = 3 * local_width
        out_end = qkv_rows + local_width
        up_end = out_end + local_hidden
        patch_rows = PIN * D // 128
        unpatch_rows = D * POUT // 128
        packed_qkv = weights[:qkv_rows]
        out_proj = weights[qkv_rows:out_end]
        up_proj = weights[out_end:up_end]
        down_proj = weights[up_end:]
        norm = shared_weights[patch_rows + unpatch_rows :].reshape(4, D).astype(jnp.float32)
        patch_proj = shared_weights[:patch_rows].reshape(PIN, D)
        used_cols = shared_weights[patch_rows : patch_rows + unpatch_rows].reshape(D, POUT // 128, 128)[:, 0]
        all_patches = lax.all_gather(own_patches, "tensor", axis=0, tiled=True)
        embed, normed1, qkv, attended, log_total, resid1, normed2 = attend(
            view_counts, all_patches, patch_proj, norm, packed_qkv, out_proj, qkv_parts, 3
        )
    hidden, active, resid2_low, gauss_table = mlp(normed2, up_proj, down_proj, resid1, used_cols, 4)
    loss_tile, table_grad = render(gauss_table, splat_index[0], splat_dist[0], alpha_label, PATCH * PATCH)
    loss_part = loss_tile[0, 0]
    unpatch_used, late_grad, resid_grad, branch, gain2_grad = mlp_back(
        table_grad, used_cols, resid2_low, active, hidden, normed2, up_proj, down_proj, resid1, norm, 5
    )
    early_grad, patch_grad, gain1_grad = attend_back(
        view_counts, branch, out_proj, qkv, log_total, packed_qkv, attended, normed1, embed, resid_grad, norm, own_patches, qkv_parts, 6
    )
    gain_grad = jnp.concatenate([gain1_grad, gain2_grad], 0)
    if count_dp == 8:
        gains = jnp.pad(gain_grad, ((0, 4), (0, 0)))
        row_lanes, shared_kept, totals = share(
            early_grad, late_grad, patch_grad, unpatch_used, gains, loss_tile, alpha_label, count_dp // 2, 8
        )
        row_share = row_lanes.reshape(-1)
        shared_share = shared_kept[FRONT : FRONT + SHARED_LANES].reshape(-1)
    else:
        unpatch_grad = jnp.concatenate(
            [unpatch_used, jnp.zeros((D, POUT - unpatch_used.shape[1]), jnp.float32)], 1
        )
        shared_grad = jnp.concatenate(
            [patch_grad.reshape(-1), unpatch_grad.reshape(-1), gain_grad.reshape(-1)]
        )
        split_grad = by_lanes(shared_grad, (count_dp, groups))
        lead = split_grad.shape[2]
        shared_stack = pad_first(split_grad, 2, 16 * D // split_grad[0, 0, 0].size).swapaxes(0, 1)
        shared_sum = lax.psum_scatter(shared_stack, "tensor", scatter_dimension=0, tiled=True)
        row_stack = jnp.concatenate([early_grad, late_grad], 0)
        stack = jnp.concatenate(
            [row_stack.reshape(count_dp, share_rows, D), shared_sum.reshape(count_dp, -1, D)], 1
        ).reshape(-1, D)
        own_share = sum_to_owners(stack, count_dp)
        own_rows = own_share[:share_rows]
        row_share = jnp.where(my_dp < qkv_parts, unpack_qkv(own_rows, 1).reshape(-1), own_rows.reshape(-1))
        shared_part = own_share[share_rows:].reshape((-1,) + split_grad.shape[3:])[:lead]
        shared_share = lax.all_gather(shared_part, "tensor", axis=0, tiled=False).reshape(-1)
        own_squares = jnp.sum(row_share * row_share) + jnp.sum(shared_part * shared_part)
        pixel_part = jnp.sum((alpha_label < 2).astype(jnp.float32))
        scalars = jnp.stack([own_squares, loss_part, pixel_part]).reshape(3, 1)
        totals = total_over_all(jnp.pad(jnp.broadcast_to(scalars, (3, 128)), ((0, 5), (0, 0))), 2)
    square_total, loss_total, pixel_total = totals[0, 0], totals[1, 0], totals[2, 0]
    norm_value = jnp.sqrt(square_total) / pixel_total
    factor = clip_norm / jnp.maximum(norm_value, clip_norm) / pixel_total
    step_float = step_count[0].astype(jnp.float32)
    row_new, row_first_new, row_second_new, row_ema_new, row_copy = adam(
        totals, step_count, row_share[None], row_master, row_first, row_second, row_ema, row_master.shape[1] // 6
    )
    shared_new, shared_first_new, shared_second_new = adam_update(
        shared_master, shared_first, shared_second, shared_share * factor, step_float
    )
    shared_ema_new = ema_rate * shared_ema + (1.0 - ema_rate) * shared_new
    return (
        norm_value.reshape(1),
        (loss_total / pixel_total).reshape(1),
        row_new,
        row_first_new,
        row_second_new,
        row_ema_new,
        row_copy,
        shared_new,
        shared_first_new,
        shared_second_new,
        shared_ema_new,
        shared_new.astype(jnp.bfloat16),
    )


def solution(mesh):
    placed = (
        P("dp", "tensor", None),
        P("dp"),
        P("dp", None, "tensor"),
        P("dp", None, "tensor"),
        P("dp", "tensor"),
        P(),
        P("tensor", "dp"),
        P("tensor", "dp"),
        P("tensor", "dp"),
        P("tensor", "dp"),
        P("dp"),
        P("dp"),
        P("dp"),
        P("dp"),
    )
    return jax.shard_map(
        per_device,
        mesh=mesh,
        in_specs=placed,
        out_specs=(
            P(),
            P(),
            P("tensor", "dp"),
            P("tensor", "dp"),
            P("tensor", "dp"),
            P("tensor", "dp"),
            P("tensor", "dp"),
            P("dp"),
            P("dp"),
            P("dp"),
            P("dp"),
            P("dp"),
        ),
        check_vma=False,
    )
```

```python
import math
from functools import partial

import jax
import jax.numpy as jnp
from jax import lax
from jax.experimental import pallas as pl
from jax.experimental.pallas import tpu as pltpu
from jax.sharding import PartitionSpec as P

D = 1024
DH = 64
FF = 4096
PATCH = 8
VTOK = 192
PIN = 576
POUT = 768
VMEM = pl.BlockSpec(memory_space=pltpu.VMEM)
HBM = pl.BlockSpec(memory_space=pl.ANY)
ROOT_HALF = 0.5**0.5
NORMAL_PEAK = (2.0 * math.pi) ** -0.5


clip_norm = 0.005
beta_one = 0.9
beta_two = 0.95
adam_eps = 1e-08
decay_rate = 0.05
learn_rate = 0.03
ema_rate = 0.9
norm_eps = 1e-05
masked_score = -1e30


MESH = pl.DeviceIdType.MESH
NN = (((1,), (0,)), ((), ()))
NT = (((1,), (1,)), ((), ()))
TN = (((0,), (0,)), ((), ()))
LOW = jnp.bfloat16
WIDE = jnp.float32
PIECES = 4
TILE = 256


def dot(left, right, dims=NN):
    return lax.dot_general(left, right, dims, preferred_element_type=WIDE)


def remote(src, dst, send, recv, to):
    return pltpu.make_async_remote_copy(
        src_ref=src, dst_ref=dst, send_sem=send, recv_sem=recv, device_id=to, device_id_type=MESH
    )


class Corner:
    def __init__(self):
        self.me = lax.axis_index("tensor")
        self.first, self.last = self.me // 2, lax.rem(self.me, 2)
        self.mate = self.first * 2 + 1 - self.last
        self.far = (1 - self.first) * 2 + self.last
        self.opposite = (1 - self.first) * 2 + 1 - self.last

    def block(self, step):
        return lax.rem(self.first + 1 - step // 2, 2) * 2 + lax.rem(self.last + 1 - lax.rem(step, 2), 2)

    def greet(self):
        barrier = pltpu.get_barrier_semaphore()
        for other in (self.mate, self.far):
            pl.semaphore_signal(barrier, inc=1, device_id={"tensor": other}, device_id_type=MESH)
        pl.semaphore_wait(barrier, 2)


class Gather:
    def __init__(self, corner, ref, pieces, sems, short=None):
        self.corner, self.ref, self.pieces, self.sems, self.short = corner, ref, pieces, sems, short
        self.size = ref.shape[0] // 4
        self.rows = self.size // pieces

    @staticmethod
    def scratch(pieces):
        return [pltpu.SemaphoreType.DMA((pieces,))] * 6

    def part(self, owner, piece, rows=None):
        return pl.ds(pl.multiple_of(owner * self.size + piece * self.rows, self.rows), rows or self.rows)

    def run(self, act, owner, piece, kind, to):
        def go(rows):
            here = self.ref.at[self.part(owner, piece, rows)]
            sems = self.sems[2 * kind].at[piece], self.sems[2 * kind + 1].at[piece]
            getattr(remote(here, here, *sems, {"tensor": to}), act)()

        by_half(self.short, piece < self.pieces // 2, self.rows, go)

    def start(self, piece):
        self.run("start", self.corner.me, piece, 1, self.corner.far)
        self.run("start", self.corner.me, piece, 0, self.corner.mate)

    def relay(self, piece):
        self.run("wait_recv", self.corner.far, piece, 1, self.corner.far)
        self.run("start", self.corner.far, piece, 2, self.corner.mate)

    def finish(self):
        corner = self.corner
        for piece in range(self.pieces):
            self.run("wait_recv", corner.mate, piece, 0, corner.mate)
            self.run("wait_recv", corner.opposite, piece, 2, corner.mate)
            self.run("wait_send", corner.me, piece, 0, corner.mate)
            self.run("wait_send", corner.me, piece, 1, corner.far)
            self.run("wait_send", corner.far, piece, 2, corner.mate)


def by_half(short, first, rows, go):
    if short is None:
        go(rows)
    elif isinstance(first, bool):
        go(rows if first else short)
    else:
        pl.when(first)(lambda: go(rows))
        pl.when(jnp.logical_not(first))(lambda: go(short))


class Scatter:
    def __init__(self, corner, pieces, mate_out, mate_in, far_out, far_in, mate_send, mate_recv, far_send, far_recv):
        self.corner, self.pieces = corner, pieces
        self.mate_out, self.mate_in, self.far_out, self.far_in = mate_out, mate_in, far_out, far_in
        self.sems = mate_send, mate_recv, far_send, far_recv
        self.rows = far_out.shape[0] // pieces

    @staticmethod
    def scratch(rows, width, pieces):
        return [
            pltpu.VMEM((2, rows, width), LOW),
            pltpu.VMEM((2, rows, width), LOW),
            pltpu.VMEM((rows, width), LOW),
            pltpu.VMEM((rows, width), LOW),
            pltpu.SemaphoreType.DMA((2, pieces)),
            pltpu.SemaphoreType.DMA((2, pieces)),
            pltpu.SemaphoreType.DMA((pieces,)),
            pltpu.SemaphoreType.DMA((pieces,)),
        ]

    def part(self, piece):
        return pl.ds(piece * self.rows, self.rows)

    def mate_copy(self, half, piece):
        part = self.part(piece)
        return remote(
            self.mate_out.at[half, part],
            self.mate_in.at[half, part],
            self.sems[0].at[half, piece],
            self.sems[1].at[half, piece],
            {"tensor": self.corner.mate},
        )

    def far_copy(self, piece):
        part = self.part(piece)
        return remote(
            self.far_out.at[part],
            self.far_in.at[part],
            self.sems[2].at[piece],
            self.sems[3].at[piece],
            {"tensor": self.corner.far},
        )

    def give(self, half, ref):
        for piece in range(self.pieces):
            part = self.part(piece)
            self.mate_out[half, part] = ref[part].astype(LOW)
            self.mate_copy(half, piece).start()

    def cross(self, ref):
        for piece in range(self.pieces):
            part = self.part(piece)
            self.mate_copy(0, piece).wait_recv()
            self.far_out[part] = (ref[part] + self.mate_in[0, part].astype(WIDE)).astype(LOW)
            self.far_copy(piece).start()

    def step(self, step, ref):
        @pl.when(step == 0)
        def _():
            self.give(0, ref)

        @pl.when(step == 1)
        def _():
            self.cross(ref)

        @pl.when(step == 2)
        def _():
            self.give(1, ref)

    def land(self, piece, ref):
        part = self.part(piece)
        self.mate_copy(1, piece).wait_recv()
        self.far_copy(piece).wait_recv()
        return ref[part] + self.mate_in[1, part].astype(WIDE) + self.far_in[part].astype(WIDE)

    def close(self):
        for piece in range(self.pieces):
            self.mate_copy(0, piece).wait_send()
            self.mate_copy(1, piece).wait_send()
            self.far_copy(piece).wait_send()


def standard(values):
    centre = values - jnp.mean(values, -1, keepdims=True)
    inverse = lax.rsqrt(jnp.mean(centre * centre, -1, keepdims=True) + norm_eps)
    return centre * inverse, inverse


def norm_back(grad_out, scaled, inverse, gain):
    grad_scaled = grad_out * gain
    return inverse * (
        grad_scaled
        - jnp.mean(grad_scaled, -1, keepdims=True)
        - scaled * jnp.mean(grad_scaled * scaled, -1, keepdims=True)
    )


def qkv_places(parts, rows, columns):
    share = rows // parts
    wide = columns * 2 // 3
    packed = share * columns // 1024
    for at in range(parts):
        for j in range(2):
            half = share // 2
            yield (at * packed, half, j * wide, wide, at * share + j * half, 0)
        for j in range(4):
            quarter = share // 4
            yield (at * packed + share // 2, quarter, j * (columns - wide), columns - wide, at * share + j * quarter, wide)


def unpack_into(full, packed, parts):
    for row, rows, col, cols, to_row, to_col in qkv_places(parts, full.shape[0], full.shape[1]):
        full[to_row : to_row + rows, to_col : to_col + cols] = packed[row : row + rows, col : col + cols]


def pack_from(packed, full, parts, base=0):
    for row, rows, col, cols, to_row, to_col in qkv_places(parts, full.shape[0], full.shape[1]):
        packed[base + row : base + row + rows, col : col + cols] = full[to_row : to_row + rows, to_col : to_col + cols]


def rows_of(block, size):
    return pl.ds(pl.multiple_of(block * size, size), size)


def column_loop(width, body):
    @pl.loop(0, width // TILE)
    def _(tile):
        body(pl.ds(pl.multiple_of(tile * TILE, TILE), TILE))


def attend_kernel(parts, q_rows, count_ref, patch_ref, proj_ref, norm_ref, weight_ref, *rest):
    corner = Corner()
    corner.greet()
    attend_body(parts, q_rows, corner, None, count_ref, patch_ref, proj_ref, norm_ref, weight_ref, *rest)


def attend_body(parts, q_rows, corner, progress, count_ref, patch_ref, proj_ref, norm_ref, weight_ref,
                embed_ref, normed1_ref, qkv_ref, attended_ref, log_ref, resid_ref, normed2_ref,
                qkv_proj, term, held, held_sem, *comm):
    progress = progress or (lambda *_: None)
    scatter = Scatter(corner, PIECES, *comm[:8])
    gather = Gather(corner, normed2_ref, PIECES, comm[8:])
    packed_rows = held.shape[0] * 3 // 4
    packed_ref, out_ref = held.at[pl.ds(0, packed_rows)], held.at[pl.ds(packed_rows, held.shape[0] - packed_rows)]

    def hold(start, target, at):
        copy = pltpu.make_async_copy(weight_ref.at[pl.ds(start, target.shape[0])], target, held_sem.at[at])
        copy.start()
        copy.wait()

    size, width = embed_ref.shape
    length = patch_ref.shape[0]
    local = attended_ref.shape[1]

    @pl.loop(0, 4)
    def _(block):
        here = rows_of(block, size)
        column_loop(width, lambda cols: term.__setitem__((slice(None), cols), dot(patch_ref[here], proj_ref[:, cols])))

        @pl.when(block == corner.me)
        def _():
            embed_ref[...] = term[...]

        scaled, inverse = standard(term[...])
        normed1_ref[here] = (scaled * norm_ref[0:1] + norm_ref[1:2]).astype(LOW)
        progress("embed", block)

    progress("weights")
    hold(0, packed_ref, 0)
    unpack_into(qkv_proj, packed_ref, parts)

    @pl.loop(0, 4)
    def _(block):
        here = rows_of(block, size)

        def columns(cols):
            qkv_ref[here, cols] = dot(normed1_ref[here], qkv_proj[:, cols]).astype(LOW)

        column_loop(3 * local, columns)

    valid = lax.broadcasted_iota(jnp.int32, (1, length), 1) < count_ref[0] * VTOK
    left = lax.broadcasted_iota(jnp.int32, (1, 2 * DH), 1) < DH
    factor = jnp.array(DH ** (-0.5), LOW)

    @pl.loop(0, length // q_rows)
    def _(turn):
        here = rows_of(turn, q_rows)
        for pair in range(local // (2 * DH)):
            lanes = slice(pair * 2 * DH, (pair + 1) * 2 * DH)
            queries = qkv_ref[here, lanes] * factor
            keyset = qkv_ref[:, local + pair * 2 * DH : local + (pair + 1) * 2 * DH]
            values = qkv_ref[:, 2 * local + pair * 2 * DH : 2 * local + (pair + 1) * 2 * DH]
            found = []
            for side in range(2):
                mine = left if side == 0 else ~left
                scores = dot(jnp.where(mine, queries, jnp.zeros_like(queries)), keyset, NT)
                scores = jnp.where(valid, scores, masked_score)
                top = jnp.max(scores, -1, keepdims=True)
                powers = jnp.exp(scores - top)
                total = jnp.sum(powers, -1, keepdims=True)
                log_ref[here, pair * 2 + side : pair * 2 + side + 1] = top + jnp.log(total)
                found.append(dot((powers * (1.0 / total)).astype(LOW), values))
            attended_ref[here, lanes] = jnp.where(left, found[0], found[1]).astype(LOW)
        progress("turn", turn)

    progress("out")
    hold(packed_rows, out_ref, 1)

    @pl.loop(0, 4)
    def _(step):
        here = rows_of(corner.block(step), size)
        column_loop(width, lambda cols: term.__setitem__((slice(None), cols), dot(attended_ref[here], out_ref[:, cols])))
        scatter.step(step, term)
        progress("give", step)

    for piece in range(PIECES):
        part = scatter.part(piece)
        resid = embed_ref[part] + scatter.land(piece, term)
        resid_ref[part] = resid
        scaled, inverse = standard(resid)
        normed2_ref[gather.part(corner.me, piece)] = (scaled * norm_ref[2:3] + norm_ref[3:4]).astype(LOW)
        gather.start(piece)
        progress("land", piece)
    for piece in range(PIECES):
        gather.relay(piece)
    gather.finish()
    scatter.close()


def attend(count, patches, patch_proj, norm, weights, parts, collective_id):
    length, size = patches.shape[0], patches.shape[0] // 4
    width, local = patch_proj.shape[1], patch_proj.shape[1] // 4
    shape = jax.ShapeDtypeStruct
    return pl.pallas_call(
        partial(attend_kernel, parts, 256),
        out_shape=(
            shape((size, width), WIDE),
            shape((length, width), LOW),
            shape((length, 3 * local), LOW),
            shape((length, local), LOW),
            shape((length, local // DH), WIDE),
            shape((size, width), WIDE),
            shape((length, width), LOW),
        ),
        in_specs=[pl.BlockSpec(memory_space=pltpu.SMEM)] + [VMEM] * 3 + [HBM],
        out_specs=(VMEM,) * 7,
        scratch_shapes=[
            pltpu.VMEM((width, 3 * local), LOW),
            pltpu.VMEM((size, width), WIDE),
            pltpu.VMEM((4 * local, width), LOW),
            pltpu.SemaphoreType.DMA((2,)),
        ]
        + Scatter.scratch(size, width, PIECES)
        + Gather.scratch(PIECES),
        compiler_params=pltpu.CompilerParams(
            collective_id=collective_id, has_side_effects=True, vmem_limit_bytes=62 * 2**20
        ),
    )(count, patches, patch_proj, norm, weights)


class Lines:
    def __init__(self, lines):
        self.lines = lines
        self.me = lax.axis_index("dp")
        self.line, self.side = self.me // 2, lax.rem(self.me, 2)
        self.pair = {"dp": self.line * 2 + 1 - self.side}
        self.above = {"dp": lax.rem(self.line + 1, lines) * 2 + self.side}
        self.below = {"dp": lax.rem(self.line + lines - 1, lines) * 2 + self.side}
        self.has_below, self.has_above = self.line > 0, self.line < lines - 1

    def signal(self, barrier):
        pl.semaphore_signal(barrier, inc=1, device_id=self.pair, device_id_type=MESH)

        @pl.when(self.has_below)
        def _():
            pl.semaphore_signal(barrier, inc=1, device_id=self.below, device_id_type=MESH)

        @pl.when(self.has_above)
        def _():
            pl.semaphore_signal(barrier, inc=1, device_id=self.above, device_id_type=MESH)

        return 1 + jnp.minimum(self.line, 1) + jnp.minimum(self.lines - 1 - self.line, 1)


class LineGather:
    def __init__(self, spot, ref, base, chunk, pieces, late_own, sems, short=None):
        self.spot, self.ref, self.base, self.chunk, self.pieces, self.late_own = spot, ref, base, chunk, pieces, late_own
        self.sems, self.short = sems, short
        self.rows = chunk // pieces
        self.steps = (spot.lines - 1) * pieces

    @staticmethod
    def scratch(lines, pieces):
        return [pltpu.SemaphoreType.DMA((lines * pieces,))] * 6

    def run(self, act, kind, line, piece, crossed=False):
        spot = self.spot
        side = 1 - spot.side if crossed else spot.side
        to = (spot.above, spot.below, spot.pair)[kind]

        def go(rows):
            start = self.base + (line * 2 + side) * self.chunk + piece * self.rows
            here = self.ref.at[pl.ds(pl.multiple_of(start, 16), rows)]
            at = line * self.pieces + piece
            getattr(remote(here, here, self.sems[2 * kind].at[at], self.sems[2 * kind + 1].at[at], to), act)()

        by_half(self.short, line < spot.lines // 2, self.rows, go)

    def own(self, kind, first=0, last=None):
        @pl.loop(first, self.pieces if last is None else last)
        def _(piece):
            self.run("start", kind, self.spot.line, piece)

    def early(self):
        return jnp.where(self.spot.line == 0, self.pieces, jnp.minimum(self.spot.line, self.pieces - 1))

    def begin(self):
        spot = self.spot
        if self.late_own:

            @pl.when(spot.line == 0)
            def _():
                self.own(0)

            return

        @pl.when(spot.has_above)
        def _():
            self.own(0)

        @pl.when(spot.has_below)
        def _():
            self.own(1)

        self.own(2)

    def follow(self):
        @pl.when(self.spot.has_below)
        def _():
            self.own(1)

        self.own(2, 0, self.early())

    def step(self, at):
        spot = self.spot
        piece = lax.rem(at, self.pieces)

        @pl.when(at < spot.line * self.pieces)
        def _():
            line = at // self.pieces
            self.run("wait_recv", 0, line, piece)

            @pl.when(spot.has_above)
            def _():
                self.run("start", 0, line, piece)

            self.run("start", 2, line, piece)

        if self.late_own:

            @pl.when((at == spot.line * self.pieces - 1) & spot.has_above)
            def _():
                self.own(0)

            @pl.when((at == self.pieces - 1) & spot.has_below)
            def _():
                self.own(2, self.early())

        @pl.when(at < (spot.lines - 1 - spot.line) * self.pieces)
        def _():
            line = spot.line + 1 + at // self.pieces
            self.run("wait_recv", 1, line, piece)

            @pl.when(spot.has_below)
            def _():
                self.run("start", 1, line, piece)

            self.run("start", 2, line, piece)

    def wait_crossed(self, line):
        @pl.loop(0, self.pieces)
        def _(piece):
            self.run("wait_recv", 2, line, piece, True)

    def close(self):
        spot = self.spot

        @pl.loop(0, spot.lines * self.pieces)
        def _(at):
            line, piece = at // self.pieces, lax.rem(at, self.pieces)
            self.run("wait_send", 2, line, piece)

            @pl.when((line <= spot.line) & spot.has_above)
            def _():
                self.run("wait_send", 0, line, piece)

            @pl.when((line >= spot.line) & spot.has_below)
            def _():
                self.run("wait_send", 1, line, piece)


WINDOW = 48
SHORT = 16
FRONT = 80
PADDED = 1616
ROW_START = (0, 160, 336, 496)
USED_START = (None, None, None, 0, 128, 352, 576, 800)


def shared_offsets(me, quarter):
    chunk = SHARED_LANES
    rows = jnp.where(me == 0, 0, jnp.where(me == 1, 160, jnp.where(me == 2, 336, 496)))
    used = (me - 4) * 224 + 128
    return (
        FRONT + 8 * rows - me * chunk + 8 * WINDOW * quarter,
        FRONT + 8 * rows - me * chunk + 8 * 32 * quarter,
        FRONT + PATCH_LANES - me * chunk + 6 * 48 * quarter,
        FRONT + PATCH_LANES + 6 * used - me * chunk + 6 * 64 * quarter,
        FRONT + PATCH_LANES + 6 * D - me * chunk,
    )


def shared_walk(me, quarter, take, phases=range(5)):
    rows, last_rows, first_used, used, norm = shared_offsets(me, quarter)
    for j in range(8):
        if 0 in phases:
            take(me < 3, 0, WINDOW, j, rows + j, 8)
        if 1 in phases:
            take((me == 3) & (quarter < 3), 0, 32, j, last_rows + j, 8)
    if 2 in phases:
        for j in range(3):
            take((me == 3) & (quarter < 3), 32, 16, j, first_used + 6 * 16 * j, 6)
    if 3 in phases:
        for j in range(4):
            take(me > 3, 0, SHORT, j, used + 6 * SHORT * j, 6)
    if 4 in phases:
        for j in range(4):
            take((me == 7) & (quarter == 0), 0, SHORT, 4 + j, norm + j, 4)


def window_pieces(kind, row):
    found = []
    if kind == 0:
        for me in range(3):
            at = row - ROW_START[me]
            if 0 <= at < 4 * WINDOW:
                found.append((me, at // WINDOW, at % WINDOW, None))
        at = row - ROW_START[3]
        if 0 <= at < 96:
            found.append((3, at // 32, at % 32, None))
    else:
        if row < 144:
            found.append((3, row // 48, 32, row % 48 // 16))
        for me in range(4, 8):
            at = row - USED_START[me]
            if 0 <= at < 256:
                found.append((me, at // 64, 0, at % 64 // 16))
    return found

SHARED_LANES = 1348
PATCH_LANES = PIN * D // 128
CHUNK_PIECES = 4


def forward_kernel(lines, q_rows, count_ref, row_ref, shared_ref, own_patch_ref,
                   weight_ref, used_ref, norm_ref,
                   embed_ref, normed1_ref, qkv_ref, attended_ref, log_ref, resid_ref, normed2_ref,
                   patches, proj, windows, own_chunk, own_sem, *rest):
    body, extra = rest[:4 + 14], rest[4 + 14:]
    corner, spot = Corner(), Lines(lines)
    barrier = pltpu.get_barrier_semaphore()
    for other in (corner.mate, corner.far):
        pl.semaphore_signal(barrier, inc=1, device_id={"tensor": other}, device_id_type=MESH)
    pl.semaphore_wait(barrier, 2 + spot.signal(barrier))
    parts = lines // 2
    chunk = weight_ref.shape[0] // (2 * lines)
    size, inputs = own_patch_ref.shape
    window = LineGather(spot, windows, corner.me * (2 * lines * WINDOW), WINDOW, 1, False, extra[0:6], SHORT)
    weights = LineGather(spot, weight_ref, 0, chunk, CHUNK_PIECES, True, extra[6:12])
    spread = Gather(corner, windows, 2 * lines, extra[12:18], SHORT)
    given = Gather(corner, patches, 1, extra[18:24])

    patches[given.part(corner.me, 0)] = own_patch_ref[...]
    given.start(0)
    base = pl.multiple_of((corner.me * 2 * lines + spot.me) * WINDOW, 16)
    windows[pl.ds(base, WINDOW)] = jnp.zeros((WINDOW, windows.shape[1]), LOW)

    def take(condition, row, rows, j, start, stride):
        @pl.when(condition)
        def _():
            windows[pl.ds(pl.multiple_of(base + row, 16), rows), j * 128 : (j + 1) * 128] = shared_ref[
                pl.ds(start, rows, stride)
            ].astype(LOW)

    shared_walk(spot.me, corner.me, take)
    window.begin()
    spread.start(spot.me)
    own = pl.multiple_of(spot.me * chunk, 16)

    @pl.when(spot.me < parts)
    def _():
        for row, rows, col, cols, at, at_col in qkv_places(1, chunk * 4 // 3, D * 3 // 4):
            for j in range(cols // 128):
                own_chunk[row : row + rows, col + j * 128 : col + (j + 1) * 128] = row_ref[
                    pl.ds(6 * at + at_col // 128 + j, rows, 6)
                ].astype(LOW)

    @pl.when(spot.me >= parts)
    def _():
        for j in range(8):
            own_chunk[:, j * 128 : (j + 1) * 128] = row_ref[pl.ds(j, chunk, 8)].astype(LOW)

    kept = pltpu.make_async_copy(own_chunk, weight_ref.at[pl.ds(own, chunk)], own_sem)
    kept.start()
    kept.wait()
    weights.begin()

    def passed(stage, act):
        if stage == 0:
            act(spot.me, None)
            act(spot.line * 2 + 1 - spot.side, spot.line)
            return
        for near in (True, False):
            for there, line in (
                (stage - 1 < spot.line, stage - 1),
                (stage - 1 < lines - 1 - spot.line, spot.line + stage),
            ):

                @pl.when(there)
                def _():
                    act(line * 2 + (spot.side if near else 1 - spot.side), None if near else line)

    def send_on(owner, line):
        if line is not None:
            window.wait_crossed(line)
        spread.start(owner)

    def relay_on(owner, line):
        spread.relay(owner)

    window.wait_crossed(spot.line)
    spread.start(spot.line * 2 + 1 - spot.side)
    window.step(0)
    passed(1, send_on)
    window.step(1)
    passed(2, send_on)
    window.step(2)
    weights.follow()
    weights.step(0)
    passed(3, send_on)
    weights.step(1)
    given.relay(0)
    passed(0, relay_on)
    weights.step(2)
    passed(1, relay_on)
    weights.step(3)
    passed(2, relay_on)
    passed(3, relay_on)
    spread.finish()
    given.finish()

    def source(me, quarter, row, rows, j):
        start = (quarter * 2 * lines + me) * WINDOW + row
        return windows[start : start + rows] if j is None else windows[start : start + rows, j * 128 : (j + 1) * 128]

    for row in range(0, proj.shape[0], 16):
        proj[row : row + 16] = sum(source(me, t, at, 16, j) for me, t, at, j in window_pieces(0, row))
    for row in range(0, used_ref.shape[0], 16):
        used_ref[row : row + 16] = sum(source(me, t, at, 16, j) for me, t, at, j in window_pieces(1, row))
    ends = source(2 * lines - 1, 0, 0, SHORT, None)[:, D // 2 :].astype(WIDE)
    norm_ref[...] = jnp.zeros_like(norm_ref)
    for row in range(8):
        norm_ref[row // 2 : row // 2 + 1, row % 2 * D // 2 : (row % 2 + 1) * D // 2] = ends[row : row + 1]

    def progress(place, at=None):
        if place == "embed":

            @pl.when(at == 2)
            def _():
                weights.step(4)

        if place == "weights":
            weights.step(5)
            weights.wait_crossed(0)
        if place == "turn":

            @pl.when(lax.rem(at, 2) == 1)
            def _():
                weights.step(6 + at // 2)

        if place == "give":

            @pl.when(at < 3)
            def _():
                weights.step(9 + at)

        if place == "out":
            weights.wait_crossed(1)

    attend_body(parts, q_rows, corner, progress, count_ref, patches, proj, norm_ref,
                weight_ref, embed_ref, normed1_ref, qkv_ref, attended_ref, log_ref, resid_ref, normed2_ref, *body)
    for line in range(2, lines):
        weights.wait_crossed(line)
    weights.close()
    window.close()


def forward(count, row_lanes, shared_lanes, own_patches, lines, collective_id):
    size, inputs = own_patches.shape
    length, width, local = 4 * size, D, D // 4
    shape = jax.ShapeDtypeStruct
    return pl.pallas_call(
        partial(forward_kernel, lines, 256),
        out_shape=(
            shape((3 * D, D), LOW),
            shape((D, 128), LOW),
            shape((8, D), WIDE),
            shape((size, width), WIDE),
            shape((length, width), LOW),
            shape((length, 3 * local), LOW),
            shape((length, local), LOW),
            shape((length, local // DH), WIDE),
            shape((size, width), WIDE),
            shape((length, width), LOW),
        ),
        in_specs=[pl.BlockSpec(memory_space=pltpu.SMEM)] + [VMEM] * 3,
        out_specs=(HBM,) + (VMEM,) * 9,
        scratch_shapes=[
            pltpu.VMEM((length, inputs), LOW),
            pltpu.VMEM((inputs, width), LOW),
            pltpu.VMEM((8 * lines * WINDOW, width), LOW),
            pltpu.VMEM((3 * D // (2 * lines), width), LOW),
            pltpu.SemaphoreType.DMA(()),
            pltpu.VMEM((width, 3 * local), LOW),
            pltpu.VMEM((size, width), WIDE),
            pltpu.VMEM((4 * local, width), LOW),
            pltpu.SemaphoreType.DMA((2,)),
        ]
        + Scatter.scratch(size, width, PIECES)
        + Gather.scratch(PIECES)
        + LineGather.scratch(lines, 1)
        + LineGather.scratch(lines, CHUNK_PIECES)
        + Gather.scratch(2 * lines)
        + Gather.scratch(1),
        compiler_params=pltpu.CompilerParams(
            collective_id=collective_id, has_side_effects=True, vmem_limit_bytes=63 * 2**20
        ),
    )(count, row_lanes, shared_lanes, own_patches)


class Moves:
    def __init__(self, sems, *pairs):
        self.copies = [pltpu.make_async_copy(src, dst, sems.at[at]) for at, (src, dst) in enumerate(pairs)]

    def start(self, *which):
        for at in which or range(len(self.copies)):
            self.copies[at].start()

    def wait(self, *which):
        for at in which or range(len(self.copies)):
            self.copies[at].wait()


def mlp_kernel(normed2_ref, weight_ref, resid1_ref, cols_ref, hidden_out, active_out, low_ref, table_ref,
               term, up_ref, down_ref, hidden_ref, active_ref, load_sem, hidden_sem, active_sem, *comm):
    first, ff = up_ref.shape[0], down_ref.shape[0]
    loads = Moves(load_sem, (weight_ref.at[pl.ds(first, first)], up_ref), (weight_ref.at[pl.ds(2 * first, ff)], down_ref))
    loads.start()
    corner = Corner()
    corner.greet()
    scatter = Scatter(corner, PIECES, *comm[:8])
    gather = Gather(corner, table_ref, PIECES, comm[8:])
    size, width = resid1_ref.shape
    loads.wait()

    def stores(step):
        here = rows_of(corner.block(step), size)
        return (
            pltpu.make_async_copy(hidden_ref.at[here], hidden_out.at[here], hidden_sem.at[step]),
            pltpu.make_async_copy(active_ref.at[here], active_out.at[here], active_sem.at[step]),
        )

    @pl.loop(0, 4)
    def _(step):
        here = rows_of(corner.block(step), size)

        def columns(cols):
            hidden = dot(normed2_ref[here], up_ref[:, cols])
            hidden_ref[here, cols] = hidden
            active_ref[here, cols] = (0.5 * hidden * (1.0 + lax.erf(hidden * ROOT_HALF))).astype(LOW)

        column_loop(up_ref.shape[1], columns)
        for copy in stores(step):
            copy.start()
        column_loop(width, lambda cols: term.__setitem__((slice(None), cols), dot(active_ref[here], down_ref[:, cols])))
        scatter.step(step, term)

    for piece in range(PIECES):
        part = scatter.part(piece)
        low_ref[part] = (resid1_ref[part] + scatter.land(piece, term)).astype(LOW)
        table_ref[gather.part(corner.me, piece)] = dot(low_ref[part], cols_ref[...]).astype(LOW)
        gather.start(piece)
    for piece in range(PIECES):
        gather.relay(piece)
    gather.finish()
    scatter.close()
    for step in range(4):
        for copy in stores(step):
            copy.wait()


def mlp(normed2, weights, resid1, used_cols, collective_id):
    length, size, width = normed2.shape[0], resid1.shape[0], resid1.shape[1]
    hidden = FF // 4
    shape = jax.ShapeDtypeStruct
    return pl.pallas_call(
        mlp_kernel,
        out_shape=(
            shape((length, hidden), WIDE),
            shape((length, hidden), LOW),
            shape((size, width), LOW),
            shape((length, used_cols.shape[1]), LOW),
        ),
        in_specs=[VMEM, HBM, VMEM, VMEM],
        out_specs=(HBM, HBM, VMEM, VMEM),
        scratch_shapes=[
            pltpu.VMEM((size, width), WIDE),
            pltpu.VMEM((width, hidden), LOW),
            pltpu.VMEM((hidden, width), LOW),
            pltpu.VMEM((length, hidden), WIDE),
            pltpu.VMEM((length, hidden), LOW),
            pltpu.SemaphoreType.DMA((2,)),
            pltpu.SemaphoreType.DMA((4,)),
            pltpu.SemaphoreType.DMA((4,)),
        ]
        + Scatter.scratch(size, width, PIECES)
        + Gather.scratch(PIECES),
        compiler_params=pltpu.CompilerParams(
            collective_id=collective_id, has_side_effects=True, vmem_limit_bytes=62 * 2**20
        ),
    )(normed2, weights, resid1, used_cols)


def mlp_back_kernel(table_ref, cols_ref, low_ref, active_in, hidden_in, normed2_in, weight_ref, resid1_ref, norm_ref,
                    unpatch_ref, grad_out, resid_grad_ref, branch_ref, gain_ref,
                    gauss, down_in, hidden_grad, term, tail, active_ref, hidden_ref, normed2_ref, up_ref, down_ref, grad_ref,
                    load_sem, store_sem, *comm):
    first = up_ref.shape[0]
    loads = Moves(
        load_sem,
        (weight_ref.at[pl.ds(2 * first, down_ref.shape[0])], down_ref),
        (hidden_in, hidden_ref),
        (weight_ref.at[pl.ds(first, first)], up_ref),
        (normed2_in, normed2_ref),
        (active_in, active_ref),
    )
    loads.start()
    corner = Corner()
    corner.greet()
    small = Scatter(corner, 1, *comm[:8])
    spread = Gather(corner, gauss, 1, comm[8:14])
    scatter = Scatter(corner, PIECES, *comm[14:22])
    gather = Gather(corner, branch_ref, PIECES, comm[22:])
    size, width = resid1_ref.shape
    ff = up_ref.shape[1]

    def view(step):
        return table_ref.at[rows_of(corner.block(step), size)]

    tail[...] = view(0)[...].astype(WIDE)
    small.give(0, tail)
    tail[...] = view(1)[...].astype(WIDE)
    small.cross(tail)
    tail[...] = view(2)[...].astype(WIDE)
    small.give(1, tail)
    tail[...] = view(3)[...].astype(WIDE)
    own_gauss = small.land(0, tail).astype(LOW)
    gauss[spread.part(corner.me, 0)] = own_gauss
    spread.start(0)
    unpatch_ref[...] = dot(low_ref[...], own_gauss, TN)
    spread.relay(0)
    spread.finish()
    small.close()
    loads.wait(0, 1, 2)

    @pl.loop(0, 4)
    def _(step):
        here = rows_of(corner.block(step), size)
        term[...] = dot(gauss[here], cols_ref[...], NT)
        down_in[here] = term[...].astype(LOW)

        @pl.when(step == 3)
        def _():
            resid_grad_ref[...] = term[...]

        def columns(cols):
            active_grad = dot(down_in[here], down_ref[cols, :], NT)
            hidden = hidden_ref[here, cols]
            slope = 0.5 * (1.0 + lax.erf(hidden * ROOT_HALF)) + hidden * (jnp.exp(-0.5 * hidden * hidden) * NORMAL_PEAK)
            hidden_grad[here, cols] = (active_grad * slope).astype(LOW)

        column_loop(ff, columns)

        def back(cols):
            term[:, cols] = dot(hidden_grad[here], up_ref[cols, :], NT)

        column_loop(width, back)
        scatter.step(step, term)

    def store(tile):
        part = pl.ds(pl.multiple_of(tile * TILE, TILE), TILE)
        return pltpu.make_async_copy(grad_ref.at[part], grad_out.at[part], store_sem.at[tile])

    loads.wait(3, 4)

    @pl.loop(0, width // TILE)
    def _(tile):
        cols = pl.ds(pl.multiple_of(tile * TILE, TILE), TILE)
        grad_ref[cols, :] = dot(normed2_ref[:, cols], hidden_grad[...], TN)
        store(tile).start()

    @pl.loop(0, ff // TILE)
    def _(tile):
        cols = pl.ds(pl.multiple_of(tile * TILE, TILE), TILE)
        grad_ref[pl.ds(pl.multiple_of(width + tile * TILE, TILE), TILE), :] = dot(active_ref[:, cols], down_in[...], TN)
        store(width // TILE + tile).start()

    gain_sum, bias_sum = jnp.zeros((1, width), WIDE), jnp.zeros((1, width), WIDE)
    for piece in range(PIECES):
        part = scatter.part(piece)
        grad = scatter.land(piece, term)
        scaled, inverse = standard(resid1_ref[part])
        total = resid_grad_ref[part] + norm_back(grad, scaled, inverse, norm_ref[2:3])
        resid_grad_ref[part] = total
        branch_ref[gather.part(corner.me, piece)] = total.astype(LOW)
        gather.start(piece)
        gain_sum += jnp.sum(grad * scaled, 0, keepdims=True)
        bias_sum += jnp.sum(grad, 0, keepdims=True)
    gain_ref[0:1] = gain_sum
    gain_ref[1:2] = bias_sum
    for piece in range(PIECES):
        gather.relay(piece)
    gather.finish()
    scatter.close()

    @pl.loop(0, (width + ff) // TILE)
    def _(tile):
        store(tile).wait()


def mlp_back(table_grad, used_cols, low, active, hidden, normed2, weights, resid1, norm, collective_id):
    length, size, width = normed2.shape[0], resid1.shape[0], resid1.shape[1]
    ff, used = hidden.shape[1], used_cols.shape[1]
    shape = jax.ShapeDtypeStruct
    return pl.pallas_call(
        mlp_back_kernel,
        out_shape=(
            shape((width, used), WIDE),
            shape((width + ff, width), WIDE),
            shape((size, width), WIDE),
            shape((length, width), LOW),
            shape((2, width), WIDE),
        ),
        in_specs=[VMEM] * 3 + [HBM] * 4 + [VMEM] * 2,
        out_specs=(VMEM, HBM, VMEM, VMEM, VMEM),
        scratch_shapes=[
            pltpu.VMEM((length, used), LOW),
            pltpu.VMEM((length, width), LOW),
            pltpu.VMEM((length, ff), LOW),
            pltpu.VMEM((size, width), WIDE),
            pltpu.VMEM((size, used), WIDE),
            pltpu.VMEM((length, ff), LOW),
            pltpu.VMEM((length, ff), WIDE),
            pltpu.VMEM((length, width), LOW),
            pltpu.VMEM((width, ff), LOW),
            pltpu.VMEM((ff, width), LOW),
            pltpu.VMEM((width + ff, width), WIDE),
            pltpu.SemaphoreType.DMA((5,)),
            pltpu.SemaphoreType.DMA(((width + ff) // TILE,)),
        ]
        + Scatter.scratch(size, used, 1)
        + Gather.scratch(1)
        + Scatter.scratch(size, width, PIECES)
        + Gather.scratch(PIECES),
        compiler_params=pltpu.CompilerParams(
            collective_id=collective_id, has_side_effects=True, vmem_limit_bytes=63 * 2**20
        ),
    )(table_grad, used_cols, low, active, hidden, normed2, weights, resid1, norm)


def attend_back_kernel(parts, q_rows, count_ref, branch_ref, weight_ref, qkv_ref, log_ref, attended_ref, normed1_in, embed_ref,
                       resid_grad_ref, norm_ref, patch_ref, grad_ref, patch_grad_ref, gain_ref,
                       qkv_proj, attended_grad, qkv_grad, key_grad, value_grad, full_grad, term, embed_grad,
                       held, normed1_ref, load_sem, *comm):
    loads = Moves(load_sem, (weight_ref.at[pl.ds(0, held.shape[0])], held), (normed1_in, normed1_ref))
    loads.start()
    corner = Corner()
    corner.greet()
    scatter = Scatter(corner, PIECES, *comm)
    size, width = embed_ref.shape
    length, local = attended_ref.shape
    packed_ref, out_ref = held.at[pl.ds(0, 3 * local)], held.at[pl.ds(3 * local, local)]
    loads.wait(0)
    unpack_into(qkv_proj, packed_ref, parts)

    @pl.loop(0, 4)
    def _(block):
        here = rows_of(block, size)
        attended_grad[here] = dot(branch_ref[here], out_ref[...], NT).astype(LOW)

    key_grad[...] = jnp.zeros_like(key_grad)
    value_grad[...] = jnp.zeros_like(value_grad)
    valid = lax.broadcasted_iota(jnp.int32, (1, length), 1) < count_ref[0] * VTOK
    left = lax.broadcasted_iota(jnp.int32, (1, 2 * DH), 1) < DH
    factor = jnp.array(DH ** (-0.5), LOW)

    @pl.loop(0, length // q_rows)
    def _(turn):
        here = rows_of(turn, q_rows)
        for pair in range(local // (2 * DH)):
            lanes = slice(pair * 2 * DH, (pair + 1) * 2 * DH)
            queries = qkv_ref[here, lanes] * factor
            grads = attended_grad[here, lanes]
            keyset = qkv_ref[:, local + pair * 2 * DH : local + (pair + 1) * 2 * DH]
            values = qkv_ref[:, 2 * local + pair * 2 * DH : 2 * local + (pair + 1) * 2 * DH]
            found = []
            for side in range(2):
                mine = left if side == 0 else ~left
                own_query = jnp.where(mine, queries, jnp.zeros_like(queries))
                own_grad = jnp.where(mine, grads, jnp.zeros_like(grads))
                scores = jnp.where(valid, dot(own_query, keyset, NT), masked_score)
                probs = jnp.exp(scores - log_ref[here, pair * 2 + side : pair * 2 + side + 1])
                prob_grad = dot(own_grad, values, NT)
                value_grad[:, lanes] += dot(probs.astype(LOW), own_grad, TN)
                centre = jnp.sum(probs * prob_grad, -1, keepdims=True)
                score_grad = (probs * (prob_grad - centre)).astype(LOW)
                found.append(dot(score_grad, keyset))
                key_grad[:, lanes] += dot(score_grad, own_query, TN)
            qkv_grad[here, lanes] = (jnp.where(left, found[0], found[1]) * (DH ** (-0.5))).astype(LOW)

    qkv_grad[:, local : 2 * local] = key_grad[...].astype(LOW)
    qkv_grad[:, 2 * local :] = value_grad[...].astype(LOW)

    @pl.loop(0, 4)
    def _(step):
        here = rows_of(corner.block(step), size)

        def columns(cols):
            term[:, cols] = dot(qkv_grad[here], qkv_proj[cols, :], NT)

        column_loop(width, columns)
        scatter.step(step, term)

    grad_ref[grad_ref.shape[0] - local :, :] = dot(attended_ref[...], branch_ref[...], TN)
    loads.wait(1)

    @pl.loop(0, width // TILE)
    def _(tile):
        cols = pl.ds(pl.multiple_of(tile * TILE, TILE), TILE)
        full_grad[cols, :] = dot(normed1_ref[:, cols], qkv_grad[...], TN)

    pack_from(grad_ref, full_grad, parts)

    gain_sum, bias_sum = jnp.zeros((1, width), WIDE), jnp.zeros((1, width), WIDE)
    for piece in range(PIECES):
        part = scatter.part(piece)
        grad = scatter.land(piece, term)
        scaled, inverse = standard(embed_ref[part])
        embed_grad[part] = (resid_grad_ref[part] + norm_back(grad, scaled, inverse, norm_ref[0:1])).astype(LOW)
        gain_sum += jnp.sum(grad * scaled, 0, keepdims=True)
        bias_sum += jnp.sum(grad, 0, keepdims=True)
    gain_ref[0:1] = gain_sum
    gain_ref[1:2] = bias_sum
    patch_grad_ref[...] = dot(patch_ref[...], embed_grad[...], TN)
    scatter.close()


def attend_back(count, branch, weights, qkv, log_total, attended, normed1, embed, resid_grad, norm, patches, parts, collective_id):
    length, local = attended.shape
    size, width = embed.shape
    shape = jax.ShapeDtypeStruct
    return pl.pallas_call(
        partial(attend_back_kernel, parts, 256),
        out_shape=(
            shape((4 * local, width), WIDE),
            shape((patches.shape[1], width), WIDE),
            shape((2, width), WIDE),
        ),
        in_specs=[pl.BlockSpec(memory_space=pltpu.SMEM), VMEM, HBM] + [VMEM] * 3 + [HBM] + [VMEM] * 4,
        out_specs=(VMEM,) * 3,
        scratch_shapes=[
            pltpu.VMEM((width, 3 * local), LOW),
            pltpu.VMEM((length, local), LOW),
            pltpu.VMEM((length, 3 * local), LOW),
            pltpu.VMEM((length, local), WIDE),
            pltpu.VMEM((length, local), WIDE),
            pltpu.VMEM((width, 3 * local), WIDE),
            pltpu.VMEM((size, width), WIDE),
            pltpu.VMEM((size, width), LOW),
            pltpu.VMEM((4 * local, width), LOW),
            pltpu.VMEM((length, width), LOW),
            pltpu.SemaphoreType.DMA((2,)),
        ]
        + Scatter.scratch(size, width, PIECES),
        compiler_params=pltpu.CompilerParams(
            collective_id=collective_id, has_side_effects=True, vmem_limit_bytes=62 * 2**20
        ),
    )(count, branch, weights, qkv, log_total, attended, normed1, embed, resid_grad, norm, patches)


class LineSum:
    def __init__(self, spot, pieces, low, source, buffers, sems):
        self.spot, self.pieces, self.low, self.source = spot, pieces, low, source
        self.pair_out, self.pair_in, self.part, self.line_in, self.low_out, self.low_in = buffers
        self.p_send, self.p_recv, self.l_send, self.up_recv, self.down_recv = sems
        self.count = spot.lines * pieces
        self.rows = self.part.shape[0] // self.count

    @staticmethod
    def scratch(lines, rows, pieces, width, low):
        half = (lines * rows, width)
        kept = half if low else (rows, width)
        kind = LOW if low else WIDE
        return [
            pltpu.VMEM(half, LOW),
            pltpu.VMEM(half, LOW),
            pltpu.VMEM(half, WIDE),
            pltpu.VMEM(half, WIDE),
            pltpu.VMEM(half if low else (16, 128), LOW),
            pltpu.VMEM(kept, kind),
        ] + [pltpu.SemaphoreType.DMA((lines * pieces,))] * 5

    def target(self, step):
        turn = lax.rem(step, self.spot.lines)
        odd = lax.rem(turn, 2)
        return (1 - odd) * (self.spot.lines - 1 - turn // 2) + odd * (turn // 2)

    def slot(self, step):
        return pl.ds(pl.multiple_of(step * self.rows, 16), self.rows)

    def pair_copy(self, step):
        slot = self.slot(step)
        return remote(self.pair_out.at[slot], self.pair_in.at[slot], self.p_send.at[step], self.p_recv.at[step], self.spot.pair)

    def line_copy(self, step, to, recv):
        slot = self.slot(step)
        return remote(self.part.at[slot], self.line_in.at[slot], self.l_send.at[step], recv.at[step], to)

    def low_copy(self, step, to, recv):
        slot = self.slot(step)
        return remote(self.low_out.at[slot], self.low_in.at[slot], self.l_send.at[step], recv.at[step], to)

    def last_copy(self, step):
        here = pl.ds(pl.multiple_of(step // self.spot.lines * self.rows, 16), self.rows)
        return remote(self.part.at[self.slot(step)], self.low_in.at[here], self.l_send.at[step], self.down_recv.at[step], self.spot.below)

    def begin(self, step):
        self.pair_out[self.slot(step)] = self.source(self.target(step), 1 - self.spot.side, step // self.spot.lines).astype(LOW)
        self.pair_copy(step).start()

    def add(self, step, low):
        slot = self.slot(step)
        self.part[slot] += self.low_in[slot].astype(WIDE) if low else self.line_in[slot]

    def travel(self, step, rising):
        spot, slot = self.spot, self.slot(step)
        to, recv = (spot.above, self.up_recv) if rising else (spot.below, self.down_recv)
        last = spot.lines - 1
        from_end = spot.line == (1 if rising else last - 1)
        at_end = spot.line == (0 if rising else last)
        target = self.target(step)
        if self.low:

            @pl.when(at_end)
            def _():
                self.low_out[slot] = self.part[slot].astype(LOW)
                self.low_copy(step, to, recv).start()

            @pl.when(from_end)
            def _():
                self.low_copy(step, to, recv).wait_recv()
                self.add(step, True)

            @pl.when(jnp.logical_not(at_end | from_end))
            def _():
                self.line_copy(step, to, recv).wait_recv()
                self.add(step, False)

            @pl.when(jnp.logical_not(at_end))
            def _():
                self.line_copy(step, to, recv).start()
        else:

            @pl.when(jnp.logical_not(at_end))
            def _():
                self.line_copy(step, to, recv).wait_recv()
                self.add(step, False)

            if rising:
                self.line_copy(step, to, recv).start()
            else:

                @pl.when(target == spot.line - 1)
                def _():
                    self.last_copy(step).start()

                @pl.when(target < spot.line - 1)
                def _():
                    self.line_copy(step, to, recv).start()

    def advance(self, step):
        spot = self.spot

        @pl.when(step < self.count)
        def _():
            slot = self.slot(step)
            self.pair_copy(step).wait_recv()
            own = self.source(self.target(step), spot.side, step // spot.lines)
            self.part[slot] = own + self.pair_in[slot].astype(WIDE)

        rising = step - spot.line

        @pl.when((rising >= 0) & (rising < self.count) & (self.target(rising) > spot.line))
        def _():
            self.travel(rising, True)

        falling = step - (spot.lines - 1 - spot.line)

        @pl.when((falling >= 0) & (falling < self.count) & (self.target(falling) < spot.line))
        def _():
            self.travel(falling, False)

    def close(self, step, give):
        spot, slot = self.spot, self.slot(step)
        target = self.target(step)
        last = spot.lines - 1
        self.pair_copy(step).wait_send()

        @pl.when(target > spot.line)
        def _():
            if self.low:

                @pl.when(spot.line == 0)
                def _():
                    self.low_copy(step, spot.above, self.up_recv).wait_send()

                @pl.when(spot.line > 0)
                def _():
                    self.line_copy(step, spot.above, self.up_recv).wait_send()
            else:
                self.line_copy(step, spot.above, self.up_recv).wait_send()

        @pl.when(target < spot.line)
        def _():
            if self.low:

                @pl.when(spot.line == last)
                def _():
                    self.low_copy(step, spot.below, self.down_recv).wait_send()

                @pl.when(spot.line < last)
                def _():
                    self.line_copy(step, spot.below, self.down_recv).wait_send()
            else:
                self.line_copy(step, spot.below, self.down_recv).wait_send()

        @pl.when(target == spot.line)
        def _():
            if self.low:

                @pl.when(spot.line == 1)
                def _():
                    self.low_copy(step, spot.above, self.up_recv).wait_recv()
                    self.add(step, True)

                @pl.when(spot.line > 1)
                def _():
                    self.line_copy(step, spot.above, self.up_recv).wait_recv()
                    self.add(step, False)

                @pl.when(spot.line == last - 1)
                def _():
                    self.low_copy(step, spot.below, self.down_recv).wait_recv()
                    self.add(step, True)

                @pl.when(spot.line < last - 1)
                def _():
                    self.line_copy(step, spot.below, self.down_recv).wait_recv()
                    self.add(step, False)
            else:

                @pl.when(spot.has_below)
                def _():
                    self.line_copy(step, spot.above, self.up_recv).wait_recv()
                    self.add(step, False)

                @pl.when(spot.has_above)
                def _():
                    self.last_copy(step).wait_recv()
                    here = pl.ds(pl.multiple_of(step // spot.lines * self.rows, 16), self.rows)
                    self.part[slot] += self.low_in[here]

            give(step // spot.lines, self.part[slot])


SUM_PIECES = 6


def share_kernel(lines, early_ref, late_ref, patch_ref, used_ref, gain_ref, loss_ref, label_ref,
                 row_ref, shared_ref, total_ref,
                 term, windows, mine, slots, rows_out, *comm):
    corner, spot = Corner(), Lines(lines)
    pairs, width = 2 * lines, early_ref.shape[1]
    quarters = 4
    count = pairs * quarters
    me = spot.me * quarters + corner.me
    barrier = pltpu.get_barrier_semaphore()

    def peer(step):
        other = lax.rem(me + step, count)
        return {"dp": other // quarters, "tensor": lax.rem(other, quarters)}

    @pl.loop(1, count)
    def _(step):
        pl.semaphore_signal(barrier, inc=1, device_id=peer(step), device_id_type=MESH)

    pl.semaphore_wait(barrier, count - 1)
    chunk = (early_ref.shape[0] + late_ref.shape[0]) // pairs
    rows = chunk // SUM_PIECES
    edge = early_ref.shape[0]

    def weight_term(line, side, piece):
        start = (line * 2 + side) * chunk + piece * rows
        inside = start < edge
        first = early_ref[pl.ds(pl.multiple_of(jnp.where(inside, start, 0), 8), rows)]
        second = late_ref[pl.ds(pl.multiple_of(jnp.where(inside, 0, start - edge), 8), rows)]
        return jnp.where(inside, first, second)

    def shared_term(line, side, piece):
        return mine[pl.ds(pl.multiple_of((line * 2 + side) * WINDOW, 16), WINDOW)]

    weights = LineSum(spot, SUM_PIECES, True, weight_term, comm[0:6], comm[6:11])
    shared = LineSum(spot, 1, False, shared_term, comm[11:17], comm[17:22])
    scatter = Scatter(corner, PIECES, *comm[22:30])
    gather = Gather(corner, windows, 1, comm[30:36])
    own_sem, send_sem, recv_sem = comm[36:39]

    @pl.loop(0, weights.count)
    def _(step):
        weights.begin(step)

    @pl.loop(0, 4)
    def _(step):
        block = corner.block(step)
        term[...] = jnp.zeros_like(term)

        def rows_at(start, size):
            return pl.ds(pl.multiple_of(start, 16), size)

        for owner in range(3):
            at = owner * WINDOW
            term[at : at + WINDOW] = patch_ref[rows_at(ROW_START[owner] + block * WINDOW, WINDOW)]

        @pl.when(block < 3)
        def _():
            at = 3 * WINDOW
            term[at : at + 16] = patch_ref[rows_at(ROW_START[3] + block * 32, 16)]

            @pl.when(block < 2)
            def _():
                term[at + 16 : at + 32] = patch_ref[rows_at(ROW_START[3] + block * 32 + 16, 16)]

            for j in range(3):
                term[at + 32 : at + 48, j * 128 : (j + 1) * 128] = used_ref[rows_at(block * 48 + 16 * j, 16)]

        for owner in range(4, 8):
            at = owner * WINDOW
            for j in range(4):

                @pl.when((block < 3) | (owner < 7) | (j < 2))
                def _():
                    term[at : at + SHORT, j * 128 : (j + 1) * 128] = used_ref[
                        rows_at(USED_START[owner] + block * 64 + SHORT * j, SHORT)
                    ]

        @pl.when(block == 0)
        def _():
            for row in range(8):
                at = 7 * WINDOW + row
                term[at : at + 1, width // 2 :] = gain_ref[row // 2 : row // 2 + 1, row % 2 * width // 2 : (row % 2 + 1) * width // 2]

        scatter.step(step, term)

    @pl.loop(0, 8)
    def _(step):
        weights.advance(step)

    for piece in range(PIECES):
        mine[scatter.part(piece)] = scatter.land(piece, term)
    for step in range(lines):
        shared.begin(step)

    @pl.loop(8, weights.count + lines - 1)
    def _(step):
        weights.advance(step)

    for step in range(2 * lines - 1):
        shared.advance(step)

    def keep_window(piece, value):
        windows[gather.part(corner.me, 0)] = value

    @pl.loop(0, lines)
    def _(step):
        shared.close(step, keep_window)

    gather.start(0)

    def keep_rows(piece, value):
        rows_out[pl.ds(pl.multiple_of(piece * rows, rows), rows)] = value

    @pl.loop(0, weights.count)
    def _(step):
        weights.close(step, keep_rows)

    gather.relay(0)

    @pl.when(spot.me < lines // 2)
    def _():
        for row, height, col, cols, at, at_col in qkv_places(1, chunk * 4 // 3, width * 3 // 4):
            for j in range(cols // 128):
                row_ref[pl.ds(6 * at + at_col // 128 + j, height, 6)] = rows_out[
                    row : row + height, col + j * 128 : col + (j + 1) * 128
                ]

    @pl.when(spot.me >= lines // 2)
    def _():
        for j in range(8):
            row_ref[pl.ds(j, chunk, 8)] = rows_out[:, j * 128 : (j + 1) * 128]

    squares = jnp.sum(rows_out[...] * rows_out[...], 0, keepdims=True)
    gather.finish()
    shared_ref[...] = jnp.zeros_like(shared_ref)
    for phase in range(5):
        for quarter in range(4):

            def take(condition, row, height, j, start, stride):
                @pl.when(condition)
                def _():
                    at = quarter * WINDOW + row
                    shared_ref[pl.ds(start, height, stride)] = windows[at : at + height, j * 128 : (j + 1) * 128]

            shared_walk(spot.me, quarter, take, (phase,))
    kept = shared_ref[FRONT : FRONT + PADDED - FRONT]
    place = lax.broadcasted_iota(jnp.int32, kept.shape, 0)
    kept = jnp.where((place < SHARED_LANES) & (corner.me == 0), kept, 0.0)
    square = jnp.sum(jnp.sum(squares, 1, keepdims=True)) + jnp.sum(kept * kept)
    counted = jnp.sum(jnp.where(label_ref[...] < 2, 1.0, 0.0))
    line = lax.broadcasted_iota(jnp.int32, total_ref.shape, 0)
    slots[me] = jnp.where(line == 0, square, jnp.where(line == 1, loss_ref[...], jnp.where(line == 2, counted, 0.0)))

    def send(step):
        return remote(slots.at[me], slots.at[me], send_sem.at[step], recv_sem.at[step], peer(step))

    def arrive(step):
        source = lax.rem(me - step + count, count)
        return remote(slots.at[source], slots.at[source], send_sem.at[step], recv_sem.at[step], peer(step))

    @pl.loop(1, count)
    def _(step):
        send(step).start()

    @pl.loop(1, count)
    def _(step):
        arrive(step).wait_recv()

    total_ref[...] = jnp.sum(slots[...], 0)

    @pl.loop(1, count)
    def _(step):
        send(step).wait_send()

    scatter.close()


def share(early, late, patch_grad, used_grad, gains, loss_tile, labels, lines, collective_id):
    width = early.shape[1]
    chunk = (early.shape[0] + late.shape[0]) // (2 * lines)
    count = 8 * lines
    shape = jax.ShapeDtypeStruct
    return pl.pallas_call(
        partial(share_kernel, lines),
        out_shape=(shape((chunk * width // 128, 128), WIDE), shape((PADDED, 128), WIDE), shape((8, 128), WIDE)),
        in_specs=[VMEM] * 7,
        out_specs=(VMEM,) * 3,
        scratch_shapes=[
            pltpu.VMEM((2 * lines * WINDOW, width), WIDE),
            pltpu.VMEM((4 * WINDOW, width), WIDE),
            pltpu.VMEM((2 * lines * WINDOW, width), WIDE),
            pltpu.VMEM((count, 8, 128), WIDE),
            pltpu.VMEM((chunk, width), WIDE),
        ]
        + LineSum.scratch(lines, chunk, SUM_PIECES, width, True)
        + LineSum.scratch(lines, WINDOW, 1, width, False)
        + Scatter.scratch(2 * lines * WINDOW, width, PIECES)
        + Gather.scratch(1)
        + [
            pltpu.SemaphoreType.DMA(()),
            pltpu.SemaphoreType.DMA((count,)),
            pltpu.SemaphoreType.DMA((count,)),
        ],
        compiler_params=pltpu.CompilerParams(
            collective_id=collective_id, has_side_effects=True, vmem_limit_bytes=63 * 2**20
        ),
    )(early, late, patch_grad, used_grad, gains, loss_tile, labels)


def render_kernel(area, wide, block, split, table_ref, splat_ref, dist_ref, label_ref, loss_ref, grad_ref, flip, picked, hot, spread_grad):
    tokens = table_ref.shape[0]
    groups = tokens // wide
    splats, pixels = splat_ref.shape
    for j in range(groups):
        flip[j * 2 * area : (j + 1) * 2 * area] = jnp.transpose(table_ref[j * wide : (j + 1) * wide].astype(jnp.float32)).astype(jnp.bfloat16)
    spread_grad[...] = jnp.zeros_like(spread_grad)
    wide_ids = lax.broadcasted_iota(jnp.int32, (wide, block), 0).astype(jnp.float32).astype(jnp.bfloat16)
    cell_ids = lax.broadcasted_iota(jnp.int32, (area, block), 0).astype(jnp.float32)
    cell_low = cell_ids.astype(jnp.bfloat16)
    one, nil = jnp.ones((wide, block), jnp.bfloat16), jnp.zeros((wide, block), jnp.bfloat16)

    def one_block(step, loss):
        here = pl.ds(pl.multiple_of(step * block, block), block)
        opacities, spreads, lows = [], [], []
        for k in range(splats):
            index = splat_ref[k : k + 1, here]
            token = index // area
            column = (token % wide).astype(jnp.float32).astype(jnp.bfloat16)
            group = (token // wide)
            cell = (index % area).astype(jnp.float32)
            match = jnp.where(wide_ids == column, one, nil)
            hot[k] = match
            picked[...] = lax.dot_general(flip[...], match, NN, preferred_element_type=jnp.float32)
            op_sum = jnp.zeros((area, block), jnp.float32)
            sp_sum = jnp.zeros((area, block), jnp.float32)
            for j in range(groups):
                same = cell_ids == jnp.where(group == j, cell, -1.0)
                op_sum += jnp.where(same, picked[j * 2 * area : j * 2 * area + area], 0.0)
                sp_sum += jnp.where(same, picked[j * 2 * area + area : (j + 1) * 2 * area], 0.0)
            opacities.append(jnp.sum(op_sum, 0, keepdims=True))
            spreads.append(jnp.sum(sp_sum, 0, keepdims=True))
            lows.append((group, cell))
        opacity, spread = jnp.concatenate(opacities, 0), jnp.concatenate(spreads, 0)
        distance = dist_ref[:, here].astype(jnp.float32)
        labels = label_ref[:, here]
        valid = jnp.where(labels < 2, 1.0, 0.0)
        target = jnp.where(labels == 1, 1.0, 0.0)
        op_sig, sp_sig = jax.nn.sigmoid(opacity), jax.nn.sigmoid(spread)
        fade = jnp.exp(-0.25 * distance * sp_sig)
        contrib = (0.02 + 0.96 * op_sig) * fade
        keep_log = jnp.sum(jnp.log1p(-contrib), 0, keepdims=True)
        keep = jnp.exp(keep_log)
        alpha = 1.0 - keep
        alpha_log = jnp.log(alpha)
        loss = loss - valid * (target * alpha_log + (1.0 - target) * keep_log)
        keep_grad = valid * (target * keep / alpha - (1.0 - target))
        contrib_grad = -keep_grad / (1.0 - contrib)
        op_grad = contrib_grad * (0.96 * op_sig * (1.0 - op_sig)) * fade
        sp_grad = contrib_grad * contrib * (-0.25 * distance * sp_sig * (1.0 - sp_sig))
        for k in range(splats):
            group, cell = lows[k]
            parts_op, parts_sp = op_grad[k : k + 1], sp_grad[k : k + 1]
            for part in range(split):
                low_op, low_sp = parts_op.astype(jnp.bfloat16), parts_sp.astype(jnp.bfloat16)
                parts_op, parts_sp = parts_op - low_op.astype(jnp.float32), parts_sp - low_sp.astype(jnp.float32)
                pieces = []
                for j in range(groups):
                    same = cell_low == jnp.where(group == j, cell, -1.0).astype(jnp.bfloat16)
                    pieces.append(jnp.where(same, low_op, jnp.bfloat16(0)))
                    pieces.append(jnp.where(same, low_sp, jnp.bfloat16(0)))
                weighted = jnp.concatenate(pieces, 0)
                spread_grad[...] += lax.dot_general(weighted, hot[k], NT, preferred_element_type=jnp.float32)
        return loss

    loss = lax.fori_loop(0, pixels // block, one_block, jnp.zeros((1, block), jnp.float32))
    loss_ref[...] = jnp.broadcast_to(jnp.sum(loss, 1, keepdims=True), loss_ref.shape)
    for j in range(groups):
        grad_ref[j * wide : (j + 1) * wide] = jnp.transpose(spread_grad[j * 2 * area : (j + 1) * 2 * area]).astype(grad_ref.dtype)

def render(table, splats, distance, labels, area, block=512, wide=256, split=2):
    tokens = table.shape[0]
    vm = pl.BlockSpec(memory_space=pltpu.VMEM)
    groups = tokens // wide
    return pl.pallas_call(
        partial(render_kernel, area, wide, block, split),
        out_shape=(jax.ShapeDtypeStruct((8, 128), jnp.float32), jax.ShapeDtypeStruct(table.shape, jnp.bfloat16)),
        in_specs=[vm] * 4, out_specs=(vm, vm),
        scratch_shapes=[pltpu.VMEM((groups * 2 * area, wide), jnp.bfloat16), pltpu.VMEM((groups * 2 * area, block), jnp.float32),
            pltpu.VMEM((splats.shape[0], wide, block), jnp.bfloat16), pltpu.VMEM((groups * 2 * area, wide), jnp.float32)],
        compiler_params=pltpu.CompilerParams(vmem_limit_bytes=48 * 2**20),
    )(table, splats, distance, labels)


def owner_sum_kernel(lines, pieces, g_ref, o_ref, pair_out, pair_in, part, line_in, own_in, p_send, p_recv, l_send, up_recv, down_recv):
    me = lax.axis_index("dp")
    line, side = me // 2, lax.rem(me, 2)
    chunk = o_ref.shape[0]
    rows = chunk // pieces
    count = lines * pieces
    pair = {"dp": line * 2 + 1 - side}
    above = {"dp": lax.rem(line + 1, lines) * 2 + side}
    below = {"dp": lax.rem(line + lines - 1, lines) * 2 + side}
    has_below, has_above = line > 0, line < lines - 1

    def target(step):
        turn = lax.rem(step, lines)
        odd = lax.rem(turn, 2)
        return (1 - odd) * (lines - 1 - turn // 2) + odd * (turn // 2)

    def slot(step):
        return pl.ds(pl.multiple_of(step * rows, rows), rows)

    def here(step):
        return pl.ds(pl.multiple_of(step // lines * rows, rows), rows)

    def source(step, owner):
        return pl.ds(pl.multiple_of((target(step) * 2 + owner) * chunk + step // lines * rows, rows), rows)

    def copy(src, dst, send, recv, to):
        return pltpu.make_async_remote_copy(
            src_ref=src, dst_ref=dst, send_sem=send, recv_sem=recv, device_id=to, device_id_type=MESH
        )

    def pair_copy(step):
        return copy(pair_out.at[slot(step)], pair_in.at[slot(step)], p_send.at[step], p_recv.at[step], pair)

    def line_copy(step, to, recv):
        return copy(part.at[slot(step)], line_in.at[slot(step)], l_send.at[step], recv.at[step], to)

    def last_copy(step):
        return copy(part.at[slot(step)], own_in.at[here(step)], l_send.at[step], down_recv.at[step], below)

    barrier = pltpu.get_barrier_semaphore()
    pl.semaphore_signal(barrier, inc=1, device_id=pair, device_id_type=MESH)

    @pl.when(has_below)
    def _():
        pl.semaphore_signal(barrier, inc=1, device_id=below, device_id_type=MESH)

    @pl.when(has_above)
    def _():
        pl.semaphore_signal(barrier, inc=1, device_id=above, device_id_type=MESH)

    pl.semaphore_wait(barrier, 1 + jnp.minimum(line, 1) + jnp.minimum(lines - 1 - line, 1))

    @pl.loop(0, count)
    def _(step):
        pair_out[slot(step)] = g_ref[source(step, 1 - side)].astype(jnp.bfloat16)
        pair_copy(step).start()

    @pl.loop(0, count + lines - 1)
    def _(step):
        @pl.when(step < count)
        def _():
            pair_copy(step).wait_recv()
            part[slot(step)] = g_ref[source(step, side)].astype(jnp.float32) + pair_in[slot(step)].astype(jnp.float32)

        rising = step - line

        @pl.when((rising >= 0) & (rising < count) & (target(rising) > line))
        def _():
            @pl.when(has_below)
            def _():
                line_copy(rising, above, up_recv).wait_recv()
                part[slot(rising)] += line_in[slot(rising)]

            line_copy(rising, above, up_recv).start()

        falling = step - (lines - 1 - line)

        @pl.when((falling >= 0) & (falling < count) & (target(falling) < line))
        def _():
            @pl.when(has_above)
            def _():
                line_copy(falling, below, down_recv).wait_recv()
                part[slot(falling)] += line_in[slot(falling)]

            @pl.when(target(falling) == line - 1)
            def _():
                last_copy(falling).start()

            @pl.when(target(falling) < line - 1)
            def _():
                line_copy(falling, below, down_recv).start()

    @pl.loop(0, count)
    def _(step):
        pair_copy(step).wait_send()

        @pl.when(target(step) > line)
        def _():
            line_copy(step, above, up_recv).wait_send()

        @pl.when(target(step) < line)
        def _():
            line_copy(step, below, down_recv).wait_send()

        @pl.when(target(step) == line)
        def _():
            o_ref[here(step)] = part[slot(step)]

            @pl.when(has_below)
            def _():
                line_copy(step, above, up_recv).wait_recv()
                o_ref[here(step)] += line_in[slot(step)]

            @pl.when(has_above)
            def _():
                last_copy(step).wait_recv()
                o_ref[here(step)] += own_in[here(step)]


def owner_sum(grad, count_dp, collective_id, pieces):
    lines = count_dp // 2
    total, width = grad.shape
    chunk = total // count_dp
    half = (lines * chunk, width)
    vmem = pl.BlockSpec(memory_space=pltpu.VMEM)
    return pl.pallas_call(
        partial(owner_sum_kernel, lines, pieces),
        out_shape=jax.ShapeDtypeStruct((chunk, width), jnp.float32),
        in_specs=[vmem],
        out_specs=vmem,
        scratch_shapes=[
            pltpu.VMEM(half, jnp.bfloat16),
            pltpu.VMEM(half, jnp.bfloat16),
            pltpu.VMEM(half, jnp.float32),
            pltpu.VMEM(half, jnp.float32),
            pltpu.VMEM((chunk, width), jnp.float32),
        ]
        + [pltpu.SemaphoreType.DMA((lines * pieces,))] * 5,
        compiler_params=pltpu.CompilerParams(
            collective_id=collective_id, has_side_effects=True, vmem_limit_bytes=62 * 2**20
        ),
    )(grad)


def total_kernel(mine_ref, sum_ref, slots, own_sem, send_sem, recv_sem):
    first, second = lax.axis_size("dp"), lax.axis_size("tensor")
    count = first * second
    me = lax.axis_index("dp") * second + lax.axis_index("tensor")

    def peer(step):
        other = lax.rem(me + step, count)
        return {"dp": other // second, "tensor": lax.rem(other, second)}

    barrier = pltpu.get_barrier_semaphore()

    @pl.loop(1, count)
    def _(step):
        pl.semaphore_signal(barrier, inc=1, device_id=peer(step), device_id_type=MESH)

    pl.semaphore_wait(barrier, count - 1)
    own = pltpu.make_async_copy(mine_ref, slots.at[me], own_sem)
    own.start()

    def send(step):
        return pltpu.make_async_remote_copy(
            src_ref=mine_ref,
            dst_ref=slots.at[me],
            send_sem=send_sem.at[step],
            recv_sem=recv_sem.at[step],
            device_id=peer(step),
            device_id_type=MESH,
        )

    @pl.loop(1, count)
    def _(step):
        send(step).start()

    @pl.loop(1, count)
    def _(step):
        send(step).wait()

    own.wait()
    sum_ref[...] = jnp.sum(slots[...], 0)


def total_over_all(mine, collective_id):
    count = lax.axis_size("dp") * lax.axis_size("tensor")
    vmem = pl.BlockSpec(memory_space=pltpu.VMEM)
    return pl.pallas_call(
        total_kernel,
        out_shape=jax.ShapeDtypeStruct(mine.shape, jnp.float32),
        in_specs=[vmem],
        out_specs=vmem,
        scratch_shapes=[
            pltpu.VMEM((count,) + mine.shape, jnp.float32),
            pltpu.SemaphoreType.DMA(()),
            pltpu.SemaphoreType.DMA((count,)),
            pltpu.SemaphoreType.DMA((count,)),
        ],
        compiler_params=pltpu.CompilerParams(collective_id=collective_id, has_side_effects=True),
    )(mine)


def pack_qkv(matrix, parts):
    rows, cols = matrix.shape
    first = matrix[:, :512].reshape(parts, 2, rows // parts // 2, 512).transpose(0, 2, 1, 3)
    second = matrix[:, 512:].reshape(parts, 4, rows // parts // 4, 256).transpose(0, 2, 1, 3)
    return jnp.concatenate([first.reshape(parts, -1, 1024), second.reshape(parts, -1, 1024)], 1).reshape(-1, 1024)


def unpack_qkv(packed, parts):
    rows = packed.shape[0] // parts
    packed = packed.reshape(parts, rows, 1024)
    cut = rows * 2 // 3
    first = packed[:, :cut].reshape(parts, cut, 2, 512).transpose(0, 2, 1, 3).reshape(-1, 512)
    second = packed[:, cut:].reshape(parts, rows - cut, 4, 256).transpose(0, 2, 1, 3).reshape(-1, 256)
    return jnp.concatenate([first, second], 1)


def by_lanes(flat, outer):
    size = flat.size // math.prod(outer)
    return flat.reshape(outer + ((size // 128, 128) if size % 128 == 0 else (size,)))


def pad_first(array, axis, unit):
    short = -array.shape[axis] % unit
    return jnp.pad(array, [(0, short if at == axis else 0) for at in range(array.ndim)])


def sum_to_owners(stack, count_dp):
    if count_dp == 8:
        return owner_sum(stack, count_dp, 1, 9)
    return lax.psum_scatter(stack, "dp", scatter_dimension=0, tiled=True)

def adam_update(master, first_mom, second_mom, gradient, step_float):
    first_new = beta_one * first_mom + (1.0 - beta_one) * gradient
    second_new = beta_two * second_mom + (1.0 - beta_two) * gradient * gradient
    first_hat = first_new / (1.0 - jnp.power(beta_one, step_float))
    second_hat = second_new / (1.0 - jnp.power(beta_two, step_float))
    master_new = master - learn_rate * (
        first_hat / (jnp.sqrt(second_hat) + adam_eps) + decay_rate * master
    )
    return (master_new, first_new, second_new)


def adam_kernel(total_ref, count_ref, *refs):
    norm_value = jnp.sqrt(total_ref[0, 0:1]) / total_ref[2, 0:1]
    factor = clip_norm / jnp.maximum(norm_value, clip_norm) / total_ref[2, 0:1]
    step_float = jnp.full((1, 1), count_ref[0], jnp.int32).astype(WIDE)
    grad, master, first, second, ema = (ref[...] for ref in refs[:5])
    new, first_new, second_new = adam_update(master, first, second, grad * factor.reshape(1, 1), step_float)
    for ref, value in zip(refs[5:], (new, first_new, second_new, ema_rate * ema + (1.0 - ema_rate) * new, new.astype(LOW))):
        ref[...] = value


def adam(totals, step_count, grad, master, first, second, ema, block):
    size = master.shape[1]
    spec = pl.BlockSpec((1, block), lambda at: (0, at))
    return pl.pallas_call(
        adam_kernel,
        grid=(size // block,),
        out_shape=tuple(jax.ShapeDtypeStruct(master.shape, kind) for kind in (WIDE,) * 4 + (LOW,)),
        in_specs=[pl.BlockSpec((8, 128), lambda at: (0, 0)), pl.BlockSpec(memory_space=pltpu.SMEM)] + [spec] * 5,
        out_specs=(spec,) * 5,
    )(totals, step_count, grad, master, first, second, ema)


def per_device(
    patches,
    view_counts,
    splat_index,
    splat_dist,
    alpha_label,
    step_count,
    row_master,
    row_first,
    row_second,
    row_ema,
    shared_master,
    shared_first,
    shared_second,
    shared_ema,
):
    groups = lax.axis_size("tensor")
    my_dp = lax.axis_index("dp")
    count_dp = lax.axis_size("dp")
    local_width = D // groups
    qkv_parts = count_dp // 4
    share_rows = row_master.shape[1] // D
    own_patches = patches[0]
    if count_dp == 8:
        shared_lanes = jnp.pad(
            shared_master.reshape(SHARED_LANES, 128), ((FRONT, PADDED - FRONT - SHARED_LANES), (0, 0))
        )
        weights, used_cols, norm, embed, normed1, qkv, attended, log_total, resid1, normed2 = forward(
            view_counts, row_master.reshape(-1, 128), shared_lanes, own_patches, count_dp // 2, 7
        )
    else:
        own_row = row_master[0].astype(jnp.bfloat16)
        own_tiles = jnp.where(
            my_dp < qkv_parts,
            pack_qkv(own_row.reshape(-1, 3 * local_width), 1),
            own_row.reshape(share_rows, D),
        )
        weights = lax.all_gather(own_tiles, "dp", axis=0, tiled=True)
        own_flat = shared_master.astype(jnp.bfloat16)
        own_shared = by_lanes(own_flat, ())
        lead = own_shared.shape[0]
        own_shared = pad_first(own_shared, 0, 2048 // own_shared[0].size)
        shared_weights = lax.all_gather(own_shared, "dp", axis=0, tiled=False)[:, :lead].reshape(-1, 128)
        patch_rows = PIN * D // 128
        unpatch_rows = D * POUT // 128
        norm = shared_weights[patch_rows + unpatch_rows :].reshape(4, D).astype(jnp.float32)
        patch_proj = shared_weights[:patch_rows].reshape(PIN, D)
        used_cols = shared_weights[patch_rows : patch_rows + unpatch_rows].reshape(D, POUT // 128, 128)[:, 0]
        all_patches = lax.all_gather(own_patches, "tensor", axis=0, tiled=True)
        embed, normed1, qkv, attended, log_total, resid1, normed2 = attend(
            view_counts, all_patches, patch_proj, norm, weights, qkv_parts, 3
        )
    hidden, active, resid2_low, gauss_table = mlp(normed2, weights, resid1, used_cols, 4)
    loss_tile, table_grad = render(gauss_table, splat_index[0], splat_dist[0], alpha_label, PATCH * PATCH)
    loss_part = loss_tile[0, 0]
    unpatch_used, late_grad, resid_grad, branch, gain2_grad = mlp_back(
        table_grad, used_cols, resid2_low, active, hidden, normed2, weights, resid1, norm, 5
    )
    early_grad, patch_grad, gain1_grad = attend_back(
        view_counts, branch, weights, qkv, log_total, attended, normed1, embed, resid_grad, norm, own_patches, qkv_parts, 6
    )
    gain_grad = jnp.concatenate([gain1_grad, gain2_grad], 0)
    if count_dp == 8:
        gains = jnp.pad(gain_grad, ((0, 4), (0, 0)))
        row_lanes, shared_kept, totals = share(
            early_grad, late_grad, patch_grad, unpatch_used, gains, loss_tile, alpha_label, count_dp // 2, 8
        )
        row_share = row_lanes.reshape(-1)
        shared_share = shared_kept[FRONT : FRONT + SHARED_LANES].reshape(-1)
    else:
        unpatch_grad = jnp.concatenate(
            [unpatch_used, jnp.zeros((D, POUT - unpatch_used.shape[1]), jnp.float32)], 1
        )
        shared_grad = jnp.concatenate(
            [patch_grad.reshape(-1), unpatch_grad.reshape(-1), gain_grad.reshape(-1)]
        )
        split_grad = by_lanes(shared_grad, (count_dp, groups))
        lead = split_grad.shape[2]
        shared_stack = pad_first(split_grad, 2, 16 * D // split_grad[0, 0, 0].size).swapaxes(0, 1)
        shared_sum = lax.psum_scatter(shared_stack, "tensor", scatter_dimension=0, tiled=True)
        row_stack = jnp.concatenate([early_grad, late_grad], 0)
        stack = jnp.concatenate(
            [row_stack.reshape(count_dp, share_rows, D), shared_sum.reshape(count_dp, -1, D)], 1
        ).reshape(-1, D)
        own_share = sum_to_owners(stack, count_dp)
        own_rows = own_share[:share_rows]
        row_share = jnp.where(my_dp < qkv_parts, unpack_qkv(own_rows, 1).reshape(-1), own_rows.reshape(-1))
        shared_part = own_share[share_rows:].reshape((-1,) + split_grad.shape[3:])[:lead]
        shared_share = lax.all_gather(shared_part, "tensor", axis=0, tiled=False).reshape(-1)
        own_squares = jnp.sum(row_share * row_share) + jnp.sum(shared_part * shared_part)
        pixel_part = jnp.sum((alpha_label < 2).astype(jnp.float32))
        scalars = jnp.stack([own_squares, loss_part, pixel_part]).reshape(3, 1)
        totals = total_over_all(jnp.pad(jnp.broadcast_to(scalars, (3, 128)), ((0, 5), (0, 0))), 2)
    square_total, loss_total, pixel_total = totals[0, 0], totals[1, 0], totals[2, 0]
    norm_value = jnp.sqrt(square_total) / pixel_total
    factor = clip_norm / jnp.maximum(norm_value, clip_norm) / pixel_total
    step_float = step_count[0].astype(jnp.float32)
    row_new, row_first_new, row_second_new, row_ema_new, row_copy = adam(
        totals, step_count, row_share[None], row_master, row_first, row_second, row_ema, row_master.shape[1] // 6
    )
    shared_new, shared_first_new, shared_second_new = adam_update(
        shared_master, shared_first, shared_second, shared_share * factor, step_float
    )
    shared_ema_new = ema_rate * shared_ema + (1.0 - ema_rate) * shared_new
    return (
        norm_value.reshape(1),
        (loss_total / pixel_total).reshape(1),
        row_new,
        row_first_new,
        row_second_new,
        row_ema_new,
        row_copy,
        shared_new,
        shared_first_new,
        shared_second_new,
        shared_ema_new,
        shared_new.astype(jnp.bfloat16),
    )


def solution(mesh):
    placed = (
        P("dp", "tensor", None),
        P("dp"),
        P("dp", None, "tensor"),
        P("dp", None, "tensor"),
        P("dp", "tensor"),
        P(),
        P("tensor", "dp"),
        P("tensor", "dp"),
        P("tensor", "dp"),
        P("tensor", "dp"),
        P("dp"),
        P("dp"),
        P("dp"),
        P("dp"),
    )
    return jax.shard_map(
        per_device,
        mesh=mesh,
        in_specs=placed,
        out_specs=(
            P(),
            P(),
            P("tensor", "dp"),
            P("tensor", "dp"),
            P("tensor", "dp"),
            P("tensor", "dp"),
            P("tensor", "dp"),
            P("dp"),
            P("dp"),
            P("dp"),
            P("dp"),
            P("dp"),
        ),
        check_vma=False,
    )
```

```python
import math
from functools import partial

import jax
import jax.numpy as jnp
from jax import lax
from jax.experimental import pallas as pl
from jax.experimental.pallas import tpu as pltpu
from jax.sharding import PartitionSpec as P

D = 1024
DH = 64
FF = 4096
PATCH = 8
VTOK = 192
PIN = 576
POUT = 768
VMEM = pl.BlockSpec(memory_space=pltpu.VMEM)
HBM = pl.BlockSpec(memory_space=pl.ANY)
ROOT_HALF = 0.5**0.5
NORMAL_PEAK = (2.0 * math.pi) ** -0.5


clip_norm = 0.005
beta_one = 0.9
beta_two = 0.95
adam_eps = 1e-08
decay_rate = 0.05
learn_rate = 0.03
ema_rate = 0.9
norm_eps = 1e-05
masked_score = -1e30


MESH = pl.DeviceIdType.MESH
NN = (((1,), (0,)), ((), ()))
NT = (((1,), (1,)), ((), ()))
TN = (((0,), (0,)), ((), ()))
LOW = jnp.bfloat16
WIDE = jnp.float32
PIECES = 4
TILE = 256


def dot(left, right, dims=NN):
    return lax.dot_general(left, right, dims, preferred_element_type=WIDE)


def remote(src, dst, send, recv, to):
    return pltpu.make_async_remote_copy(
        src_ref=src, dst_ref=dst, send_sem=send, recv_sem=recv, device_id=to, device_id_type=MESH
    )


class Corner:
    def __init__(self):
        self.me = lax.axis_index("tensor")
        self.first, self.last = self.me // 2, lax.rem(self.me, 2)
        self.mate = self.first * 2 + 1 - self.last
        self.far = (1 - self.first) * 2 + self.last
        self.opposite = (1 - self.first) * 2 + 1 - self.last

    def block(self, step):
        return lax.rem(self.first + 1 - step // 2, 2) * 2 + lax.rem(self.last + 1 - lax.rem(step, 2), 2)

    def greet(self):
        barrier = pltpu.get_barrier_semaphore()
        for other in (self.mate, self.far):
            pl.semaphore_signal(barrier, inc=1, device_id={"tensor": other}, device_id_type=MESH)
        pl.semaphore_wait(barrier, 2)


class Gather:
    def __init__(self, corner, ref, pieces, sems, short=None):
        self.corner, self.ref, self.pieces, self.sems, self.short = corner, ref, pieces, sems, short
        self.size = ref.shape[0] // 4
        self.rows = self.size // pieces

    @staticmethod
    def scratch(pieces):
        return [pltpu.SemaphoreType.DMA((pieces,))] * 6

    def part(self, owner, piece, rows=None):
        return pl.ds(pl.multiple_of(owner * self.size + piece * self.rows, self.rows), rows or self.rows)

    def run(self, act, owner, piece, kind, to):
        def go(rows):
            here = self.ref.at[self.part(owner, piece, rows)]
            sems = self.sems[2 * kind].at[piece], self.sems[2 * kind + 1].at[piece]
            getattr(remote(here, here, *sems, {"tensor": to}), act)()

        by_half(self.short, piece < self.pieces // 2, self.rows, go)

    def start(self, piece):
        self.run("start", self.corner.me, piece, 1, self.corner.far)
        self.run("start", self.corner.me, piece, 0, self.corner.mate)

    def relay(self, piece):
        self.run("wait_recv", self.corner.far, piece, 1, self.corner.far)
        self.run("start", self.corner.far, piece, 2, self.corner.mate)

    def finish(self):
        corner = self.corner
        for piece in range(self.pieces):
            self.run("wait_recv", corner.mate, piece, 0, corner.mate)
            self.run("wait_recv", corner.opposite, piece, 2, corner.mate)
            self.run("wait_send", corner.me, piece, 0, corner.mate)
            self.run("wait_send", corner.me, piece, 1, corner.far)
            self.run("wait_send", corner.far, piece, 2, corner.mate)


def by_half(short, first, rows, go):
    if short is None:
        go(rows)
    elif isinstance(first, bool):
        go(rows if first else short)
    else:
        pl.when(first)(lambda: go(rows))
        pl.when(jnp.logical_not(first))(lambda: go(short))


class Scatter:
    def __init__(self, corner, pieces, mate_out, mate_in, far_out, far_in, mate_send, mate_recv, far_send, far_recv):
        self.corner, self.pieces = corner, pieces
        self.mate_out, self.mate_in, self.far_out, self.far_in = mate_out, mate_in, far_out, far_in
        self.sems = mate_send, mate_recv, far_send, far_recv
        self.rows = far_out.shape[0] // pieces

    @staticmethod
    def scratch(rows, width, pieces):
        return [
            pltpu.VMEM((2, rows, width), LOW),
            pltpu.VMEM((2, rows, width), LOW),
            pltpu.VMEM((rows, width), LOW),
            pltpu.VMEM((rows, width), LOW),
            pltpu.SemaphoreType.DMA((2, pieces)),
            pltpu.SemaphoreType.DMA((2, pieces)),
            pltpu.SemaphoreType.DMA((pieces,)),
            pltpu.SemaphoreType.DMA((pieces,)),
        ]

    def part(self, piece):
        return pl.ds(piece * self.rows, self.rows)

    def mate_copy(self, half, piece):
        part = self.part(piece)
        return remote(
            self.mate_out.at[half, part],
            self.mate_in.at[half, part],
            self.sems[0].at[half, piece],
            self.sems[1].at[half, piece],
            {"tensor": self.corner.mate},
        )

    def far_copy(self, piece):
        part = self.part(piece)
        return remote(
            self.far_out.at[part],
            self.far_in.at[part],
            self.sems[2].at[piece],
            self.sems[3].at[piece],
            {"tensor": self.corner.far},
        )

    def give(self, half, ref):
        for piece in range(self.pieces):
            part = self.part(piece)
            self.mate_out[half, part] = ref[part].astype(LOW)
            self.mate_copy(half, piece).start()

    def cross(self, ref):
        for piece in range(self.pieces):
            part = self.part(piece)
            self.mate_copy(0, piece).wait_recv()
            self.far_out[part] = (ref[part] + self.mate_in[0, part].astype(WIDE)).astype(LOW)
            self.far_copy(piece).start()

    def step(self, step, ref):
        @pl.when(step == 0)
        def _():
            self.give(0, ref)

        @pl.when(step == 1)
        def _():
            self.cross(ref)

        @pl.when(step == 2)
        def _():
            self.give(1, ref)

    def land(self, piece, ref):
        part = self.part(piece)
        self.mate_copy(1, piece).wait_recv()
        self.far_copy(piece).wait_recv()
        return ref[part] + self.mate_in[1, part].astype(WIDE) + self.far_in[part].astype(WIDE)

    def close(self):
        for piece in range(self.pieces):
            self.mate_copy(0, piece).wait_send()
            self.mate_copy(1, piece).wait_send()
            self.far_copy(piece).wait_send()


def standard(values):
    centre = values - jnp.mean(values, -1, keepdims=True)
    inverse = lax.rsqrt(jnp.mean(centre * centre, -1, keepdims=True) + norm_eps)
    return centre * inverse, inverse


def norm_back(grad_out, scaled, inverse, gain):
    grad_scaled = grad_out * gain
    return inverse * (
        grad_scaled
        - jnp.mean(grad_scaled, -1, keepdims=True)
        - scaled * jnp.mean(grad_scaled * scaled, -1, keepdims=True)
    )


def qkv_places(parts, rows, columns):
    share = rows // parts
    wide = columns * 2 // 3
    packed = share * columns // 1024
    for at in range(parts):
        for j in range(2):
            half = share // 2
            yield (at * packed, half, j * wide, wide, at * share + j * half, 0)
        for j in range(4):
            quarter = share // 4
            yield (at * packed + share // 2, quarter, j * (columns - wide), columns - wide, at * share + j * quarter, wide)


def unpack_into(full, packed, parts):
    for row, rows, col, cols, to_row, to_col in qkv_places(parts, full.shape[0], full.shape[1]):
        full[to_row : to_row + rows, to_col : to_col + cols] = packed[row : row + rows, col : col + cols]


def pack_from(packed, full, parts, base=0):
    for row, rows, col, cols, to_row, to_col in qkv_places(parts, full.shape[0], full.shape[1]):
        packed[base + row : base + row + rows, col : col + cols] = full[to_row : to_row + rows, to_col : to_col + cols]


def rows_of(block, size):
    return pl.ds(pl.multiple_of(block * size, size), size)


def column_loop(width, body):
    @pl.loop(0, width // TILE)
    def _(tile):
        body(pl.ds(pl.multiple_of(tile * TILE, TILE), TILE))


def attend_kernel(parts, q_rows, count_ref, patch_ref, proj_ref, norm_ref, weight_ref, *rest):
    corner = Corner()
    corner.greet()
    attend_body(parts, q_rows, corner, None, count_ref, patch_ref, proj_ref, norm_ref, weight_ref, *rest)


def attend_body(parts, q_rows, corner, progress, count_ref, patch_ref, proj_ref, norm_ref, weight_ref,
                embed_ref, normed1_ref, qkv_ref, attended_ref, log_ref, resid_ref, normed2_ref,
                qkv_proj, term, held, held_sem, *comm):
    progress = progress or (lambda *_: None)
    scatter = Scatter(corner, PIECES, *comm[:8])
    gather = Gather(corner, normed2_ref, PIECES, comm[8:])
    packed_rows = held.shape[0] * 3 // 4
    packed_ref, out_ref = held.at[pl.ds(0, packed_rows)], held.at[pl.ds(packed_rows, held.shape[0] - packed_rows)]

    def hold(start, target, at):
        copy = pltpu.make_async_copy(weight_ref.at[pl.ds(start, target.shape[0])], target, held_sem.at[at])
        copy.start()
        copy.wait()

    size, width = embed_ref.shape
    length = patch_ref.shape[0]
    local = attended_ref.shape[1]

    @pl.loop(0, 4)
    def _(block):
        here = rows_of(block, size)
        column_loop(width, lambda cols: term.__setitem__((slice(None), cols), dot(patch_ref[here], proj_ref[:, cols])))

        @pl.when(block == corner.me)
        def _():
            embed_ref[...] = term[...]

        scaled, inverse = standard(term[...])
        normed1_ref[here] = (scaled * norm_ref[0:1] + norm_ref[1:2]).astype(LOW)
        progress("embed", block)

    progress("weights")
    hold(0, packed_ref, 0)
    unpack_into(qkv_proj, packed_ref, parts)

    @pl.loop(0, 4)
    def _(block):
        here = rows_of(block, size)

        def columns(cols):
            qkv_ref[here, cols] = dot(normed1_ref[here], qkv_proj[:, cols]).astype(LOW)

        column_loop(3 * local, columns)

    valid = lax.broadcasted_iota(jnp.int32, (1, length), 1) < count_ref[0] * VTOK
    left = lax.broadcasted_iota(jnp.int32, (1, 2 * DH), 1) < DH
    factor = jnp.array(DH ** (-0.5), LOW)

    @pl.loop(0, length // q_rows)
    def _(turn):
        here = rows_of(turn, q_rows)
        for pair in range(local // (2 * DH)):
            lanes = slice(pair * 2 * DH, (pair + 1) * 2 * DH)
            queries = qkv_ref[here, lanes] * factor
            keyset = qkv_ref[:, local + pair * 2 * DH : local + (pair + 1) * 2 * DH]
            values = qkv_ref[:, 2 * local + pair * 2 * DH : 2 * local + (pair + 1) * 2 * DH]
            found = []
            for side in range(2):
                mine = left if side == 0 else ~left
                scores = dot(jnp.where(mine, queries, jnp.zeros_like(queries)), keyset, NT)
                scores = jnp.where(valid, scores, masked_score)
                top = jnp.max(scores, -1, keepdims=True)
                powers = jnp.exp(scores - top)
                total = jnp.sum(powers, -1, keepdims=True)
                log_ref[here, pair * 2 + side : pair * 2 + side + 1] = top + jnp.log(total)
                found.append(dot((powers * (1.0 / total)).astype(LOW), values))
            attended_ref[here, lanes] = jnp.where(left, found[0], found[1]).astype(LOW)
        progress("turn", turn)

    progress("out")
    hold(packed_rows, out_ref, 1)

    @pl.loop(0, 4)
    def _(step):
        here = rows_of(corner.block(step), size)
        column_loop(width, lambda cols: term.__setitem__((slice(None), cols), dot(attended_ref[here], out_ref[:, cols])))
        scatter.step(step, term)
        progress("give", step)

    for piece in range(PIECES):
        part = scatter.part(piece)
        resid = embed_ref[part] + scatter.land(piece, term)
        resid_ref[part] = resid
        scaled, inverse = standard(resid)
        normed2_ref[gather.part(corner.me, piece)] = (scaled * norm_ref[2:3] + norm_ref[3:4]).astype(LOW)
        gather.start(piece)
        progress("land", piece)
    for piece in range(PIECES):
        gather.relay(piece)
    gather.finish()
    scatter.close()


def attend(count, patches, patch_proj, norm, weights, parts, collective_id):
    length, size = patches.shape[0], patches.shape[0] // 4
    width, local = patch_proj.shape[1], patch_proj.shape[1] // 4
    shape = jax.ShapeDtypeStruct
    return pl.pallas_call(
        partial(attend_kernel, parts, 256),
        out_shape=(
            shape((size, width), WIDE),
            shape((length, width), LOW),
            shape((length, 3 * local), LOW),
            shape((length, local), LOW),
            shape((length, local // DH), WIDE),
            shape((size, width), WIDE),
            shape((length, width), LOW),
        ),
        in_specs=[pl.BlockSpec(memory_space=pltpu.SMEM)] + [VMEM] * 3 + [HBM],
        out_specs=(VMEM,) * 7,
        scratch_shapes=[
            pltpu.VMEM((width, 3 * local), LOW),
            pltpu.VMEM((size, width), WIDE),
            pltpu.VMEM((4 * local, width), LOW),
            pltpu.SemaphoreType.DMA((2,)),
        ]
        + Scatter.scratch(size, width, PIECES)
        + Gather.scratch(PIECES),
        compiler_params=pltpu.CompilerParams(
            collective_id=collective_id, has_side_effects=True, vmem_limit_bytes=62 * 2**20
        ),
    )(count, patches, patch_proj, norm, weights)


class Lines:
    def __init__(self, lines):
        self.lines = lines
        self.me = lax.axis_index("dp")
        self.line, self.side = self.me // 2, lax.rem(self.me, 2)
        self.pair = {"dp": self.line * 2 + 1 - self.side}
        self.above = {"dp": lax.rem(self.line + 1, lines) * 2 + self.side}
        self.below = {"dp": lax.rem(self.line + lines - 1, lines) * 2 + self.side}
        self.has_below, self.has_above = self.line > 0, self.line < lines - 1

    def signal(self, barrier):
        pl.semaphore_signal(barrier, inc=1, device_id=self.pair, device_id_type=MESH)

        @pl.when(self.has_below)
        def _():
            pl.semaphore_signal(barrier, inc=1, device_id=self.below, device_id_type=MESH)

        @pl.when(self.has_above)
        def _():
            pl.semaphore_signal(barrier, inc=1, device_id=self.above, device_id_type=MESH)

        return 1 + jnp.minimum(self.line, 1) + jnp.minimum(self.lines - 1 - self.line, 1)


class LineGather:
    def __init__(self, spot, ref, base, chunk, pieces, late_own, sems, short=None):
        self.spot, self.ref, self.base, self.chunk, self.pieces, self.late_own = spot, ref, base, chunk, pieces, late_own
        self.sems, self.short = sems, short
        self.rows = chunk // pieces
        self.steps = (spot.lines - 1) * pieces

    @staticmethod
    def scratch(lines, pieces):
        return [pltpu.SemaphoreType.DMA((lines * pieces,))] * 6

    def run(self, act, kind, line, piece, crossed=False):
        spot = self.spot
        side = 1 - spot.side if crossed else spot.side
        to = (spot.above, spot.below, spot.pair)[kind]

        def go(rows):
            start = self.base + (line * 2 + side) * self.chunk + piece * self.rows
            here = self.ref.at[pl.ds(pl.multiple_of(start, 16), rows)]
            at = line * self.pieces + piece
            getattr(remote(here, here, self.sems[2 * kind].at[at], self.sems[2 * kind + 1].at[at], to), act)()

        by_half(self.short, line < spot.lines // 2, self.rows, go)

    def own(self, kind, first=0, last=None):
        @pl.loop(first, self.pieces if last is None else last)
        def _(piece):
            self.run("start", kind, self.spot.line, piece)

    def early(self):
        return jnp.where(self.spot.line == 0, self.pieces, jnp.minimum(self.spot.line, self.pieces - 1))

    def begin(self):
        spot = self.spot
        if self.late_own:

            @pl.when(spot.line == 0)
            def _():
                self.own(0)

            return

        @pl.when(spot.has_above)
        def _():
            self.own(0)

        @pl.when(spot.has_below)
        def _():
            self.own(1)

        self.own(2)

    def follow(self):
        @pl.when(self.spot.has_below)
        def _():
            self.own(1)

        self.own(2, 0, self.early())

    def step(self, at):
        spot = self.spot
        piece = lax.rem(at, self.pieces)

        @pl.when(at < spot.line * self.pieces)
        def _():
            line = at // self.pieces
            self.run("wait_recv", 0, line, piece)

            @pl.when(spot.has_above)
            def _():
                self.run("start", 0, line, piece)

            self.run("start", 2, line, piece)

        if self.late_own:

            @pl.when((at == spot.line * self.pieces - 1) & spot.has_above)
            def _():
                self.own(0)

            @pl.when((at == self.pieces - 1) & spot.has_below)
            def _():
                self.own(2, self.early())

        @pl.when(at < (spot.lines - 1 - spot.line) * self.pieces)
        def _():
            line = spot.line + 1 + at // self.pieces
            self.run("wait_recv", 1, line, piece)

            @pl.when(spot.has_below)
            def _():
                self.run("start", 1, line, piece)

            self.run("start", 2, line, piece)

    def wait_crossed(self, line):
        @pl.loop(0, self.pieces)
        def _(piece):
            self.run("wait_recv", 2, line, piece, True)

    def close(self):
        spot = self.spot

        @pl.loop(0, spot.lines * self.pieces)
        def _(at):
            line, piece = at // self.pieces, lax.rem(at, self.pieces)
            self.run("wait_send", 2, line, piece)

            @pl.when((line <= spot.line) & spot.has_above)
            def _():
                self.run("wait_send", 0, line, piece)

            @pl.when((line >= spot.line) & spot.has_below)
            def _():
                self.run("wait_send", 1, line, piece)


WINDOW = 48
SHORT = 16
FRONT = 80
PADDED = 1616
ROW_START = (0, 160, 336, 496)
USED_START = (None, None, None, 0, 128, 352, 576, 800)


def window_row(owner):
    if isinstance(owner, int):
        return owner * WINDOW if owner < 4 else 4 * WINDOW + (owner - 4) * SHORT
    return jnp.minimum(owner, 4) * WINDOW + jnp.maximum(owner - 4, 0) * SHORT


def shared_offsets(me, quarter):
    chunk = SHARED_LANES
    rows = jnp.where(me == 0, 0, jnp.where(me == 1, 160, jnp.where(me == 2, 336, 496)))
    used = (me - 4) * 224 + 128
    return (
        FRONT + 8 * rows - me * chunk + 8 * WINDOW * quarter,
        FRONT + 8 * rows - me * chunk + 8 * 32 * quarter,
        FRONT + PATCH_LANES - me * chunk + 6 * 48 * quarter,
        FRONT + PATCH_LANES + 6 * used - me * chunk + 6 * 64 * quarter,
        FRONT + PATCH_LANES + 6 * D - me * chunk,
    )


def shared_walk(me, quarter, take, phases=range(5)):
    rows, last_rows, first_used, used, norm = shared_offsets(me, quarter)
    for j in range(8):
        if 0 in phases:
            take(me < 3, 0, WINDOW, j, rows + j, 8)
        if 1 in phases:
            take((me == 3) & (quarter < 3), 0, 32, j, last_rows + j, 8)
    if 2 in phases:
        for j in range(3):
            take((me == 3) & (quarter < 3), 32, 16, j, first_used + 6 * 16 * j, 6)
    if 3 in phases:
        for j in range(4):
            take(me > 3, 0, SHORT, j, used + 6 * SHORT * j, 6)
    if 4 in phases:
        for j in range(4):
            take((me == 7) & (quarter == 0), 0, SHORT, 4 + j, norm + j, 4)


def window_pieces(kind, row):
    found = []
    if kind == 0:
        for me in range(3):
            at = row - ROW_START[me]
            if 0 <= at < 4 * WINDOW:
                found.append((me, at // WINDOW, at % WINDOW, None))
        at = row - ROW_START[3]
        if 0 <= at < 96:
            found.append((3, at // 32, at % 32, None))
    else:
        if row < 144:
            found.append((3, row // 48, 32, row % 48 // 16))
        for me in range(4, 8):
            at = row - USED_START[me]
            if 0 <= at < 256:
                found.append((me, at // 64, 0, at % 64 // 16))
    return found

SHARED_LANES = 1348
PATCH_LANES = PIN * D // 128
CHUNK_PIECES = 4


def forward_kernel(lines, q_rows, count_ref, row_ref, shared_ref, own_patch_ref,
                   weight_ref, used_ref, norm_ref,
                   embed_ref, normed1_ref, qkv_ref, attended_ref, log_ref, resid_ref, normed2_ref,
                   patches, proj, windows, own_chunk, own_sem, *rest):
    body, extra = rest[:4 + 14], rest[4 + 14:]
    corner, spot = Corner(), Lines(lines)
    barrier = pltpu.get_barrier_semaphore()
    for other in (corner.mate, corner.far):
        pl.semaphore_signal(barrier, inc=1, device_id={"tensor": other}, device_id_type=MESH)
    pl.semaphore_wait(barrier, 2 + spot.signal(barrier))
    parts = lines // 2
    chunk = weight_ref.shape[0] // (2 * lines)
    size, inputs = own_patch_ref.shape
    window = LineGather(spot, windows, corner.me * (2 * lines * WINDOW), WINDOW, 1, False, extra[0:6], SHORT)
    weights = LineGather(spot, weight_ref, 0, chunk, CHUNK_PIECES, True, extra[6:12])
    spread = Gather(corner, windows, 2 * lines, extra[12:18], SHORT)
    given = Gather(corner, patches, 1, extra[18:24])

    patches[given.part(corner.me, 0)] = own_patch_ref[...]
    given.start(0)
    base = pl.multiple_of((corner.me * 2 * lines + spot.me) * WINDOW, 16)
    windows[pl.ds(base, WINDOW)] = jnp.zeros((WINDOW, windows.shape[1]), LOW)

    def take(condition, row, rows, j, start, stride):
        @pl.when(condition)
        def _():
            windows[pl.ds(pl.multiple_of(base + row, 16), rows), j * 128 : (j + 1) * 128] = shared_ref[
                pl.ds(start, rows, stride)
            ].astype(LOW)

    shared_walk(spot.me, corner.me, take)
    window.begin()
    spread.start(spot.me)
    own = pl.multiple_of(spot.me * chunk, 16)

    @pl.when(spot.me < parts)
    def _():
        for row, rows, col, cols, at, at_col in qkv_places(1, chunk * 4 // 3, D * 3 // 4):
            for j in range(cols // 128):
                own_chunk[row : row + rows, col + j * 128 : col + (j + 1) * 128] = row_ref[
                    pl.ds(6 * at + at_col // 128 + j, rows, 6)
                ].astype(LOW)

    @pl.when(spot.me >= parts)
    def _():
        for j in range(8):
            own_chunk[:, j * 128 : (j + 1) * 128] = row_ref[pl.ds(j, chunk, 8)].astype(LOW)

    kept = pltpu.make_async_copy(own_chunk, weight_ref.at[pl.ds(own, chunk)], own_sem)
    kept.start()
    kept.wait()
    weights.begin()

    def passed(stage, act):
        if stage == 0:
            act(spot.me, None)
            act(spot.line * 2 + 1 - spot.side, spot.line)
            return
        for near in (True, False):
            for there, line in (
                (stage - 1 < spot.line, stage - 1),
                (stage - 1 < lines - 1 - spot.line, spot.line + stage),
            ):

                @pl.when(there)
                def _():
                    act(line * 2 + (spot.side if near else 1 - spot.side), None if near else line)

    def send_on(owner, line):
        if line is not None:
            window.wait_crossed(line)
        spread.start(owner)

    def relay_on(owner, line):
        spread.relay(owner)

    window.wait_crossed(spot.line)
    spread.start(spot.line * 2 + 1 - spot.side)
    window.step(0)
    passed(1, send_on)
    window.step(1)
    passed(2, send_on)
    window.step(2)
    weights.follow()
    weights.step(0)
    passed(3, send_on)
    weights.step(1)
    given.relay(0)
    passed(0, relay_on)
    weights.step(2)
    passed(1, relay_on)
    weights.step(3)
    passed(2, relay_on)
    passed(3, relay_on)
    spread.finish()
    given.finish()

    def source(me, quarter, row, rows, j):
        start = (quarter * 2 * lines + me) * WINDOW + row
        return windows[start : start + rows] if j is None else windows[start : start + rows, j * 128 : (j + 1) * 128]

    for row in range(0, proj.shape[0], 16):
        proj[row : row + 16] = sum(source(me, t, at, 16, j) for me, t, at, j in window_pieces(0, row))
    for row in range(0, used_ref.shape[0], 16):
        used_ref[row : row + 16] = sum(source(me, t, at, 16, j) for me, t, at, j in window_pieces(1, row))
    ends = source(2 * lines - 1, 0, 0, SHORT, None)[:, D // 2 :].astype(WIDE)
    norm_ref[...] = jnp.zeros_like(norm_ref)
    for row in range(8):
        norm_ref[row // 2 : row // 2 + 1, row % 2 * D // 2 : (row % 2 + 1) * D // 2] = ends[row : row + 1]

    def progress(place, at=None):
        if place == "embed":

            @pl.when(at == 2)
            def _():
                weights.step(4)

        if place == "weights":
            weights.step(5)
            weights.wait_crossed(0)
        if place == "turn":

            @pl.when(lax.rem(at, 2) == 1)
            def _():
                weights.step(6 + at // 2)

        if place == "give":

            @pl.when(at < 3)
            def _():
                weights.step(9 + at)

        if place == "out":
            weights.wait_crossed(1)

    attend_body(parts, q_rows, corner, progress, count_ref, patches, proj, norm_ref,
                weight_ref, embed_ref, normed1_ref, qkv_ref, attended_ref, log_ref, resid_ref, normed2_ref, *body)
    for line in range(2, lines):
        weights.wait_crossed(line)
    weights.close()
    window.close()


def forward(count, row_lanes, shared_lanes, own_patches, lines, collective_id):
    size, inputs = own_patches.shape
    length, width, local = 4 * size, D, D // 4
    shape = jax.ShapeDtypeStruct
    return pl.pallas_call(
        partial(forward_kernel, lines, 256),
        out_shape=(
            shape((3 * D, D), LOW),
            shape((D, 128), LOW),
            shape((8, D), WIDE),
            shape((size, width), WIDE),
            shape((length, width), LOW),
            shape((length, 3 * local), LOW),
            shape((length, local), LOW),
            shape((length, local // DH), WIDE),
            shape((size, width), WIDE),
            shape((length, width), LOW),
        ),
        in_specs=[pl.BlockSpec(memory_space=pltpu.SMEM)] + [VMEM] * 3,
        out_specs=(HBM,) + (VMEM,) * 9,
        scratch_shapes=[
            pltpu.VMEM((length, inputs), LOW),
            pltpu.VMEM((inputs, width), LOW),
            pltpu.VMEM((8 * lines * WINDOW, width), LOW),
            pltpu.VMEM((3 * D // (2 * lines), width), LOW),
            pltpu.SemaphoreType.DMA(()),
            pltpu.VMEM((width, 3 * local), LOW),
            pltpu.VMEM((size, width), WIDE),
            pltpu.VMEM((4 * local, width), LOW),
            pltpu.SemaphoreType.DMA((2,)),
        ]
        + Scatter.scratch(size, width, PIECES)
        + Gather.scratch(PIECES)
        + LineGather.scratch(lines, 1)
        + LineGather.scratch(lines, CHUNK_PIECES)
        + Gather.scratch(2 * lines)
        + Gather.scratch(1),
        compiler_params=pltpu.CompilerParams(
            collective_id=collective_id, has_side_effects=True, vmem_limit_bytes=63 * 2**20
        ),
    )(count, row_lanes, shared_lanes, own_patches)


class Moves:
    def __init__(self, sems, *pairs):
        self.copies = [pltpu.make_async_copy(src, dst, sems.at[at]) for at, (src, dst) in enumerate(pairs)]

    def start(self, *which):
        for at in which or range(len(self.copies)):
            self.copies[at].start()

    def wait(self, *which):
        for at in which or range(len(self.copies)):
            self.copies[at].wait()


def mlp_kernel(normed2_ref, weight_ref, resid1_ref, cols_ref, hidden_out, active_out, low_ref, table_ref,
               term, up_ref, down_ref, hidden_ref, active_ref, load_sem, hidden_sem, active_sem, *comm):
    first, ff = up_ref.shape[0], down_ref.shape[0]
    loads = Moves(load_sem, (weight_ref.at[pl.ds(first, first)], up_ref), (weight_ref.at[pl.ds(2 * first, ff)], down_ref))
    loads.start()
    corner = Corner()
    corner.greet()
    scatter = Scatter(corner, PIECES, *comm[:8])
    gather = Gather(corner, table_ref, PIECES, comm[8:])
    size, width = resid1_ref.shape
    loads.wait()

    def stores(step):
        here = rows_of(corner.block(step), size)
        return (
            pltpu.make_async_copy(hidden_ref.at[here], hidden_out.at[here], hidden_sem.at[step]),
            pltpu.make_async_copy(active_ref.at[here], active_out.at[here], active_sem.at[step]),
        )

    @pl.loop(0, 4)
    def _(step):
        here = rows_of(corner.block(step), size)

        def columns(cols):
            hidden = dot(normed2_ref[here], up_ref[:, cols])
            hidden_ref[here, cols] = hidden
            active_ref[here, cols] = (0.5 * hidden * (1.0 + lax.erf(hidden * ROOT_HALF))).astype(LOW)

        column_loop(up_ref.shape[1], columns)
        for copy in stores(step):
            copy.start()
        column_loop(width, lambda cols: term.__setitem__((slice(None), cols), dot(active_ref[here], down_ref[:, cols])))
        scatter.step(step, term)

    for piece in range(PIECES):
        part = scatter.part(piece)
        low_ref[part] = (resid1_ref[part] + scatter.land(piece, term)).astype(LOW)
        table_ref[gather.part(corner.me, piece)] = dot(low_ref[part], cols_ref[...]).astype(LOW)
        gather.start(piece)
    for piece in range(PIECES):
        gather.relay(piece)
    gather.finish()
    scatter.close()
    for step in range(4):
        for copy in stores(step):
            copy.wait()


def mlp(normed2, weights, resid1, used_cols, collective_id):
    length, size, width = normed2.shape[0], resid1.shape[0], resid1.shape[1]
    hidden = FF // 4
    shape = jax.ShapeDtypeStruct
    return pl.pallas_call(
        mlp_kernel,
        out_shape=(
            shape((length, hidden), WIDE),
            shape((length, hidden), LOW),
            shape((size, width), LOW),
            shape((length, used_cols.shape[1]), LOW),
        ),
        in_specs=[VMEM, HBM, VMEM, VMEM],
        out_specs=(HBM, HBM, VMEM, VMEM),
        scratch_shapes=[
            pltpu.VMEM((size, width), WIDE),
            pltpu.VMEM((width, hidden), LOW),
            pltpu.VMEM((hidden, width), LOW),
            pltpu.VMEM((length, hidden), WIDE),
            pltpu.VMEM((length, hidden), LOW),
            pltpu.SemaphoreType.DMA((2,)),
            pltpu.SemaphoreType.DMA((4,)),
            pltpu.SemaphoreType.DMA((4,)),
        ]
        + Scatter.scratch(size, width, PIECES)
        + Gather.scratch(PIECES),
        compiler_params=pltpu.CompilerParams(
            collective_id=collective_id, has_side_effects=True, vmem_limit_bytes=62 * 2**20
        ),
    )(normed2, weights, resid1, used_cols)


def mlp_back_kernel(table_ref, cols_ref, low_ref, active_in, hidden_in, normed2_in, weight_ref, resid1_ref, norm_ref, attended_ref,
                    unpatch_ref, grad_out, rounded_out, resid_grad_ref, branch_ref, gain_ref,
                    gauss, down_in, hidden_grad, term, tail, active_ref, hidden_ref, normed2_ref, up_ref, down_ref, grad_ref,
                    rounded_ref, load_sem, store_sem, *comm):
    first = up_ref.shape[0]
    loads = Moves(
        load_sem,
        (weight_ref.at[pl.ds(2 * first, down_ref.shape[0])], down_ref),
        (hidden_in, hidden_ref),
        (weight_ref.at[pl.ds(first, first)], up_ref),
        (normed2_in, normed2_ref),
        (active_in, active_ref),
    )
    loads.start()
    corner = Corner()
    corner.greet()
    small = Scatter(corner, 1, *comm[:8])
    spread = Gather(corner, gauss, 1, comm[8:14])
    scatter = Scatter(corner, PIECES, *comm[14:22])
    gather = Gather(corner, branch_ref, PIECES, comm[22:])
    size, width = resid1_ref.shape
    ff = up_ref.shape[1]

    def view(step):
        return table_ref.at[rows_of(corner.block(step), size)]

    tail[...] = view(0)[...].astype(WIDE)
    small.give(0, tail)
    tail[...] = view(1)[...].astype(WIDE)
    small.cross(tail)
    tail[...] = view(2)[...].astype(WIDE)
    small.give(1, tail)
    tail[...] = view(3)[...].astype(WIDE)
    own_gauss = small.land(0, tail).astype(LOW)
    gauss[spread.part(corner.me, 0)] = own_gauss
    spread.start(0)
    unpatch_ref[...] = dot(low_ref[...], own_gauss, TN)
    spread.relay(0)
    spread.finish()
    small.close()
    loads.wait(0, 1, 2)

    @pl.loop(0, 4)
    def _(step):
        here = rows_of(corner.block(step), size)
        term[...] = dot(gauss[here], cols_ref[...], NT)
        down_in[here] = term[...].astype(LOW)

        @pl.when(step == 3)
        def _():
            resid_grad_ref[...] = term[...]

        def columns(cols):
            active_grad = dot(down_in[here], down_ref[cols, :], NT)
            hidden = hidden_ref[here, cols]
            slope = 0.5 * (1.0 + lax.erf(hidden * ROOT_HALF)) + hidden * (jnp.exp(-0.5 * hidden * hidden) * NORMAL_PEAK)
            hidden_grad[here, cols] = (active_grad * slope).astype(LOW)

        column_loop(ff, columns)

        def back(cols):
            term[:, cols] = dot(hidden_grad[here], up_ref[cols, :], NT)

        column_loop(width, back)
        scatter.step(step, term)

    def stores(tile):
        part = pl.ds(pl.multiple_of(tile * TILE, TILE), TILE)
        return (
            pltpu.make_async_copy(grad_ref.at[part], grad_out.at[part], store_sem.at[0, tile]),
            pltpu.make_async_copy(rounded_ref.at[part], rounded_out.at[part], store_sem.at[1, tile]),
        )

    def keep(tile, value):
        part = pl.ds(pl.multiple_of(tile * TILE, TILE), TILE)
        grad_ref[part, :] = value
        rounded_ref[part, :] = value.astype(LOW)
        for copy in stores(tile):
            copy.start()

    loads.wait(3, 4)
    tiles = attended_ref.shape[1] // TILE

    @pl.loop(0, width // TILE)
    def _(tile):
        cols = pl.ds(pl.multiple_of(tile * TILE, TILE), TILE)
        keep(tiles + tile, dot(normed2_ref[:, cols], hidden_grad[...], TN))

    @pl.loop(0, ff // TILE)
    def _(tile):
        cols = pl.ds(pl.multiple_of(tile * TILE, TILE), TILE)
        keep(tiles + width // TILE + tile, dot(active_ref[:, cols], down_in[...], TN))

    gain_sum, bias_sum = jnp.zeros((1, width), WIDE), jnp.zeros((1, width), WIDE)
    for piece in range(PIECES):
        part = scatter.part(piece)
        grad = scatter.land(piece, term)
        scaled, inverse = standard(resid1_ref[part])
        total = resid_grad_ref[part] + norm_back(grad, scaled, inverse, norm_ref[2:3])
        resid_grad_ref[part] = total
        branch_ref[gather.part(corner.me, piece)] = total.astype(LOW)
        gather.start(piece)
        gain_sum += jnp.sum(grad * scaled, 0, keepdims=True)
        bias_sum += jnp.sum(grad, 0, keepdims=True)
    gain_ref[0:1] = gain_sum
    gain_ref[1:2] = bias_sum
    for piece in range(PIECES):
        gather.relay(piece)
    gather.finish()
    scatter.close()

    for tile in range(tiles):
        keep(tile, dot(attended_ref[:, tile * TILE : (tile + 1) * TILE], branch_ref[...], TN))

    @pl.loop(0, grad_ref.shape[0] // TILE)
    def _(tile):
        for copy in stores(tile):
            copy.wait()


def mlp_back(table_grad, used_cols, low, active, hidden, normed2, weights, resid1, norm, attended, collective_id):
    length, size, width = normed2.shape[0], resid1.shape[0], resid1.shape[1]
    ff, used = hidden.shape[1], used_cols.shape[1]
    total = attended.shape[1] + width + ff
    shape = jax.ShapeDtypeStruct
    return pl.pallas_call(
        mlp_back_kernel,
        out_shape=(
            shape((width, used), WIDE),
            shape((total, width), WIDE),
            shape((total, width), LOW),
            shape((size, width), WIDE),
            shape((length, width), LOW),
            shape((2, width), WIDE),
        ),
        in_specs=[VMEM] * 3 + [HBM] * 4 + [VMEM] * 3,
        out_specs=(VMEM, HBM, HBM, VMEM, VMEM, VMEM),
        scratch_shapes=[
            pltpu.VMEM((length, used), LOW),
            pltpu.VMEM((length, width), LOW),
            pltpu.VMEM((length, ff), LOW),
            pltpu.VMEM((size, width), WIDE),
            pltpu.VMEM((size, used), WIDE),
            pltpu.VMEM((length, ff), LOW),
            pltpu.VMEM((length, ff), WIDE),
            pltpu.VMEM((length, width), LOW),
            pltpu.VMEM((width, ff), LOW),
            pltpu.VMEM((ff, width), LOW),
            pltpu.VMEM((total, width), WIDE),
            pltpu.VMEM((total, width), LOW),
            pltpu.SemaphoreType.DMA((5,)),
            pltpu.SemaphoreType.DMA((2, total // TILE)),
        ]
        + Scatter.scratch(size, used, 1)
        + Gather.scratch(1)
        + Scatter.scratch(size, width, PIECES)
        + Gather.scratch(PIECES),
        compiler_params=pltpu.CompilerParams(
            collective_id=collective_id, has_side_effects=True, vmem_limit_bytes=63 * 2**20
        ),
    )(table_grad, used_cols, low, active, hidden, normed2, weights, resid1, norm, attended)


class LineSum:
    def __init__(self, spot, pieces, low, source, buffers, sems, first=0, turns=4, stored=None):
        self.spot, self.pieces, self.low, self.source = spot, pieces, low, source
        self.first, self.turns, self.stored = first, turns, stored
        self.pair_out, self.pair_in, self.part, self.line_in, self.low_out, self.low_in = buffers
        self.p_send, self.p_recv, self.l_send, self.up_recv, self.down_recv = sems
        self.count = turns * pieces
        self.rows = self.part.shape[0] // self.count

    @staticmethod
    def scratch(turns, rows, pieces, width, low, stored=False):
        half = (turns * rows, width)
        kept = half if low else (rows, width)
        kind = LOW if low else WIDE
        return [
            pltpu.VMEM((16, 128) if stored else half, LOW),
            pltpu.VMEM(half, LOW),
            pltpu.VMEM(half, WIDE),
            pltpu.VMEM(half, WIDE),
            pltpu.VMEM(half if low else (16, 128), LOW),
            pltpu.VMEM(kept, kind),
        ] + [pltpu.SemaphoreType.DMA((turns * pieces,))] * 5

    def target(self, step):
        turn = lax.rem(step, self.turns)
        if self.turns == 4:
            odd = lax.rem(turn, 2)
            return (1 - odd) * (3 - turn // 2) + odd * (turn // 2)
        if self.turns == 3:
            return self.first + 2 - 2 * jnp.minimum(turn, 1) + turn - jnp.minimum(turn, 1)
        return self.first + turn

    def stored_rows(self, step, side):
        start = ((self.target(step) - self.first) * 2 + side) * self.pieces + step // self.turns
        return pl.ds(pl.multiple_of(start * self.rows, 16), self.rows)

    def slot(self, step):
        return pl.ds(pl.multiple_of(step * self.rows, 16), self.rows)

    def pair_copy(self, step):
        slot = self.slot(step)
        if self.stored:
            sent = self.stored[1].at[self.stored_rows(step, 1 - self.spot.side)]
            return remote(sent, self.pair_in.at[slot], self.p_send.at[step], self.p_recv.at[step], self.spot.pair)
        return remote(self.pair_out.at[slot], self.pair_in.at[slot], self.p_send.at[step], self.p_recv.at[step], self.spot.pair)

    def line_copy(self, step, to, recv):
        slot = self.slot(step)
        return remote(self.part.at[slot], self.line_in.at[slot], self.l_send.at[step], recv.at[step], to)

    def low_copy(self, step, to, recv):
        slot = self.slot(step)
        return remote(self.low_out.at[slot], self.low_in.at[slot], self.l_send.at[step], recv.at[step], to)

    def last_copy(self, step):
        here = pl.ds(pl.multiple_of(step // self.turns * self.rows, 16), self.rows)
        return remote(self.part.at[self.slot(step)], self.low_in.at[here], self.l_send.at[step], self.down_recv.at[step], self.spot.below)

    def own_copy(self, step):
        own = self.stored[0].at[self.stored_rows(step, self.spot.side)]
        return pltpu.make_async_copy(own, self.part.at[self.slot(step)], self.stored[2].at[step])

    def begin(self, step):
        if self.stored:
            self.pair_copy(step).start()
            self.own_copy(step).start()
            return
        self.pair_out[self.slot(step)] = self.source(self.target(step), 1 - self.spot.side, step // self.turns).astype(LOW)
        self.pair_copy(step).start()

    def add(self, step, low):
        slot = self.slot(step)
        self.part[slot] += self.low_in[slot].astype(WIDE) if low else self.line_in[slot]

    def travel(self, step, rising):
        spot, slot = self.spot, self.slot(step)
        to, recv = (spot.above, self.up_recv) if rising else (spot.below, self.down_recv)
        last = spot.lines - 1
        from_end = spot.line == (1 if rising else last - 1)
        at_end = spot.line == (0 if rising else last)
        target = self.target(step)
        if self.low:

            @pl.when(at_end)
            def _():
                self.low_out[slot] = self.part[slot].astype(LOW)
                self.low_copy(step, to, recv).start()

            @pl.when(from_end)
            def _():
                self.low_copy(step, to, recv).wait_recv()
                self.add(step, True)

            @pl.when(jnp.logical_not(at_end | from_end))
            def _():
                self.line_copy(step, to, recv).wait_recv()
                self.add(step, False)

            @pl.when(jnp.logical_not(at_end))
            def _():
                self.line_copy(step, to, recv).start()
        else:

            @pl.when(jnp.logical_not(at_end))
            def _():
                self.line_copy(step, to, recv).wait_recv()
                self.add(step, False)

            if rising:
                self.line_copy(step, to, recv).start()
            else:

                @pl.when(target == spot.line - 1)
                def _():
                    self.last_copy(step).start()

                @pl.when(target < spot.line - 1)
                def _():
                    self.line_copy(step, to, recv).start()

    def advance(self, step):
        spot = self.spot

        @pl.when(step < self.count)
        def _():
            slot = self.slot(step)
            self.pair_copy(step).wait_recv()
            if self.stored:
                self.own_copy(step).wait()
                self.part[slot] += self.pair_in[slot].astype(WIDE)
                return
            own = self.source(self.target(step), spot.side, step // self.turns)
            self.part[slot] = own + self.pair_in[slot].astype(WIDE)

        rising = step - spot.line

        @pl.when((rising >= 0) & (rising < self.count) & (self.target(rising) > spot.line))
        def _():
            self.travel(rising, True)

        falling = step - (spot.lines - 1 - spot.line)

        @pl.when((falling >= 0) & (falling < self.count) & (self.target(falling) < spot.line))
        def _():
            self.travel(falling, False)

    def close(self, step, give):
        spot, slot = self.spot, self.slot(step)
        target = self.target(step)
        last = spot.lines - 1
        self.pair_copy(step).wait_send()

        @pl.when(target > spot.line)
        def _():
            if self.low:

                @pl.when(spot.line == 0)
                def _():
                    self.low_copy(step, spot.above, self.up_recv).wait_send()

                @pl.when(spot.line > 0)
                def _():
                    self.line_copy(step, spot.above, self.up_recv).wait_send()
            else:
                self.line_copy(step, spot.above, self.up_recv).wait_send()

        @pl.when(target < spot.line)
        def _():
            if self.low:

                @pl.when(spot.line == last)
                def _():
                    self.low_copy(step, spot.below, self.down_recv).wait_send()

                @pl.when(spot.line < last)
                def _():
                    self.line_copy(step, spot.below, self.down_recv).wait_send()
            else:
                self.line_copy(step, spot.below, self.down_recv).wait_send()

        @pl.when(target == spot.line)
        def _():
            if self.low:

                @pl.when(spot.line == 1)
                def _():
                    self.low_copy(step, spot.above, self.up_recv).wait_recv()
                    self.add(step, True)

                @pl.when(spot.line > 1)
                def _():
                    self.line_copy(step, spot.above, self.up_recv).wait_recv()
                    self.add(step, False)

                @pl.when(spot.line == last - 1)
                def _():
                    self.low_copy(step, spot.below, self.down_recv).wait_recv()
                    self.add(step, True)

                @pl.when(spot.line < last - 1)
                def _():
                    self.line_copy(step, spot.below, self.down_recv).wait_recv()
                    self.add(step, False)
            else:

                @pl.when(spot.has_below)
                def _():
                    self.line_copy(step, spot.above, self.up_recv).wait_recv()
                    self.add(step, False)

                @pl.when(spot.has_above)
                def _():
                    self.last_copy(step).wait_recv()
                    here = pl.ds(pl.multiple_of(step // self.turns * self.rows, 16), self.rows)
                    self.part[slot] += self.low_in[here]

            give(step // self.turns, self.part[slot])


def attend_back_kernel(parts, q_rows, lines, count_ref, branch_ref, weight_ref, qkv_ref, log_ref, normed1_in, embed_ref,
                       resid_grad_ref, norm_ref, *rest):
    late_in, rest = (rest[:2], rest[2:]) if lines else ((), rest)
    grad_ref, embed_grad, gain_ref = rest[:3]
    own_late, rest = (rest[3], rest[4:]) if lines else (None, rest[3:])
    qkv_proj, attended_grad, qkv_grad, key_grad, value_grad, term, held, normed1_ref, load_sem = rest[:9]
    comm, late_comm = rest[9:17], rest[17:]
    loads = Moves(load_sem, (weight_ref.at[pl.ds(0, held.shape[0])], held), (normed1_in, normed1_ref))
    loads.start()
    corner = Corner()
    size, width = embed_ref.shape
    length, local = qkv_ref.shape[0], qkv_ref.shape[1] // 3
    if lines:
        spot = Lines(lines)
        barrier = pltpu.get_barrier_semaphore()
        for other in (corner.mate, corner.far):
            pl.semaphore_signal(barrier, inc=1, device_id={"tensor": other}, device_id_type=MESH)
        pl.semaphore_wait(barrier, 2 + spot.signal(barrier))
        late = LineSum(
            spot, SUM_PIECES, True, None, late_comm[:6], late_comm[6:11], 1, lines - 1, late_in + (late_comm[11],)
        )

        @pl.loop(0, late.count)
        def _(step):
            late.begin(step)

    else:
        corner.greet()
    scatter = Scatter(corner, PIECES, *comm)
    packed_ref, out_ref = held.at[pl.ds(0, 3 * local)], held.at[pl.ds(3 * local, local)]
    loads.wait(0)
    unpack_into(qkv_proj, packed_ref, parts)

    @pl.loop(0, 4)
    def _(block):
        here = rows_of(block, size)
        attended_grad[here] = dot(branch_ref[here], out_ref[...], NT).astype(LOW)

    key_grad[...] = jnp.zeros_like(key_grad)
    value_grad[...] = jnp.zeros_like(value_grad)
    valid = lax.broadcasted_iota(jnp.int32, (1, length), 1) < count_ref[0] * VTOK
    left = lax.broadcasted_iota(jnp.int32, (1, 2 * DH), 1) < DH
    factor = jnp.array(DH ** (-0.5), LOW)

    @pl.loop(0, length // q_rows)
    def _(turn):
        here = rows_of(turn, q_rows)
        for pair in range(local // (2 * DH)):
            lanes = slice(pair * 2 * DH, (pair + 1) * 2 * DH)
            queries = qkv_ref[here, lanes] * factor
            grads = attended_grad[here, lanes]
            keyset = qkv_ref[:, local + pair * 2 * DH : local + (pair + 1) * 2 * DH]
            values = qkv_ref[:, 2 * local + pair * 2 * DH : 2 * local + (pair + 1) * 2 * DH]
            found = []
            for side in range(2):
                mine = left if side == 0 else ~left
                own_query = jnp.where(mine, queries, jnp.zeros_like(queries))
                own_grad = jnp.where(mine, grads, jnp.zeros_like(grads))
                scores = jnp.where(valid, dot(own_query, keyset, NT), masked_score)
                probs = jnp.exp(scores - log_ref[here, pair * 2 + side : pair * 2 + side + 1])
                prob_grad = dot(own_grad, values, NT)
                value_grad[:, lanes] += dot(probs.astype(LOW), own_grad, TN)
                centre = jnp.sum(probs * prob_grad, -1, keepdims=True)
                score_grad = (probs * (prob_grad - centre)).astype(LOW)
                found.append(dot(score_grad, keyset))
                key_grad[:, lanes] += dot(score_grad, own_query, TN)
            qkv_grad[here, lanes] = (jnp.where(left, found[0], found[1]) * (DH ** (-0.5))).astype(LOW)
        if lines:
            for at in range(2):
                late.advance(2 * turn + at)

    qkv_grad[:, local : 2 * local] = key_grad[...].astype(LOW)
    qkv_grad[:, 2 * local :] = value_grad[...].astype(LOW)

    @pl.loop(0, 4)
    def _(step):
        here = rows_of(corner.block(step), size)

        def columns(cols):
            term[:, cols] = dot(qkv_grad[here], qkv_proj[cols, :], NT)

        column_loop(width, columns)
        scatter.step(step, term)
        if lines:
            late.advance(12 + step)

    loads.wait(1)
    for tile in range(width // TILE):
        value = dot(normed1_ref[:, tile * TILE : (tile + 1) * TILE], qkv_grad[...], TN)
        for row, rows, col, cols, at, at_col in qkv_places(parts, width, 3 * local):
            if at // TILE == tile:
                at = at % TILE
                grad_ref[row : row + rows, col : col + cols] = value[at : at + rows, at_col : at_col + cols]
        if lines:
            late.advance(16 + tile)

    gain_sum, bias_sum = jnp.zeros((1, width), WIDE), jnp.zeros((1, width), WIDE)
    for piece in range(PIECES):
        part = scatter.part(piece)
        grad = scatter.land(piece, term)
        scaled, inverse = standard(embed_ref[part])
        embed_grad[part] = (resid_grad_ref[part] + norm_back(grad, scaled, inverse, norm_ref[0:1])).astype(LOW)
        gain_sum += jnp.sum(grad * scaled, 0, keepdims=True)
        bias_sum += jnp.sum(grad, 0, keepdims=True)
    gain_ref[0:1] = gain_sum
    gain_ref[1:2] = bias_sum
    scatter.close()
    if lines:
        for step in range(20, late.count + lines - 1):
            late.advance(step)

        def keep_rows(piece, value):
            own_late[pl.ds(pl.multiple_of(piece * late.rows, 16), late.rows)] = value

        @pl.loop(0, late.count)
        def _(step):
            late.close(step, keep_rows)


def attend_back(count, branch, weights, qkv, log_total, normed1, embed, resid_grad, norm, late, parts, lines, collective_id):
    length, local = qkv.shape[0], qkv.shape[1] // 3
    size, width = embed.shape
    shape = jax.ShapeDtypeStruct
    chunk = 3 * width // (2 * lines) if lines else 0
    return pl.pallas_call(
        partial(attend_back_kernel, parts, 256, lines),
        out_shape=(
            shape((3 * local, width), WIDE),
            shape((size, width), LOW),
            shape((2, width), WIDE),
        )
        + ((shape((chunk, width), WIDE),) if lines else ()),
        in_specs=[pl.BlockSpec(memory_space=pltpu.SMEM), VMEM, HBM, VMEM, VMEM, HBM, VMEM, VMEM, VMEM] + [HBM] * len(late),
        out_specs=(VMEM,) * (4 if lines else 3),
        scratch_shapes=[
            pltpu.VMEM((width, 3 * local), LOW),
            pltpu.VMEM((length, local), LOW),
            pltpu.VMEM((length, 3 * local), LOW),
            pltpu.VMEM((length, local), WIDE),
            pltpu.VMEM((length, local), WIDE),
            pltpu.VMEM((size, width), WIDE),
            pltpu.VMEM((4 * local, width), LOW),
            pltpu.VMEM((length, width), LOW),
            pltpu.SemaphoreType.DMA((2,)),
        ]
        + Scatter.scratch(size, width, PIECES)
        + (
            LineSum.scratch(lines - 1, chunk, SUM_PIECES, width, True, True)
            + [pltpu.SemaphoreType.DMA(((lines - 1) * SUM_PIECES,))]
            if lines
            else []
        ),
        compiler_params=pltpu.CompilerParams(
            collective_id=collective_id, has_side_effects=True, vmem_limit_bytes=63 * 2**20
        ),
    )(count, branch, weights, qkv, log_total, normed1, embed, resid_grad, norm, *late)


SUM_PIECES = 6


def share_kernel(lines, early_ref, late_ref, embed_ref, own_patch_ref, used_ref, gain_ref, loss_ref, label_ref,
                 row_ref, shared_ref, total_ref,
                 term, windows, mine, slots, rows_out, patch_ref, *comm):
    corner, spot = Corner(), Lines(lines)
    pairs, width = 2 * lines, early_ref.shape[1]
    quarters = 4
    count = pairs * quarters
    me = spot.me * quarters + corner.me
    barrier = pltpu.get_barrier_semaphore()

    def peer(step):
        other = lax.rem(me + step, count)
        return {"dp": other // quarters, "tensor": lax.rem(other, quarters)}

    @pl.loop(1, count)
    def _(step):
        pl.semaphore_signal(barrier, inc=1, device_id=peer(step), device_id_type=MESH)

    pl.semaphore_wait(barrier, count - 1)
    chunk = late_ref.shape[0]
    rows = chunk // SUM_PIECES

    def weight_term(line, side, piece):
        return early_ref[pl.ds(pl.multiple_of(side * chunk + piece * rows, 8), rows)]

    def shared_term(line, side, piece):
        return mine[pl.ds(pl.multiple_of(window_row(line * 2 + side), 16), WINDOW)]

    weights = LineSum(spot, SUM_PIECES, True, weight_term, comm[0:6], comm[6:11], 0, 1)
    shared = LineSum(spot, 1, False, shared_term, comm[11:17], comm[17:22])
    scatter = Scatter(corner, PIECES, *comm[22:30])
    gather = Gather(corner, windows, 1, comm[30:36])
    own_sem, send_sem, recv_sem = comm[36:39]

    @pl.loop(0, weights.count)
    def _(step):
        weights.begin(step)

    patch_ref[...] = dot(own_patch_ref[...], embed_ref[...], TN)

    @pl.loop(0, 4)
    def _(step):
        block = corner.block(step)
        term[...] = jnp.zeros_like(term)

        def rows_at(start, size):
            return pl.ds(pl.multiple_of(start, 16), size)

        for owner in range(3):
            at = owner * WINDOW
            term[at : at + WINDOW] = patch_ref[rows_at(ROW_START[owner] + block * WINDOW, WINDOW)]

        @pl.when(block < 3)
        def _():
            at = 3 * WINDOW
            term[at : at + 16] = patch_ref[rows_at(ROW_START[3] + block * 32, 16)]

            @pl.when(block < 2)
            def _():
                term[at + 16 : at + 32] = patch_ref[rows_at(ROW_START[3] + block * 32 + 16, 16)]

            for j in range(3):
                term[at + 32 : at + 48, j * 128 : (j + 1) * 128] = used_ref[rows_at(block * 48 + 16 * j, 16)]

        for owner in range(4, 8):
            at = window_row(owner)
            for j in range(4):

                @pl.when((block < 3) | (owner < 7) | (j < 2))
                def _():
                    term[at : at + SHORT, j * 128 : (j + 1) * 128] = used_ref[
                        rows_at(USED_START[owner] + block * 64 + SHORT * j, SHORT)
                    ]

        @pl.when(block == 0)
        def _():
            for row in range(8):
                at = window_row(7) + row
                term[at : at + 1, width // 2 :] = gain_ref[row // 2 : row // 2 + 1, row % 2 * width // 2 : (row % 2 + 1) * width // 2]

        scatter.step(step, term)

    for step in range(2):
        weights.advance(step)
    for piece in range(PIECES):
        mine[scatter.part(piece)] = scatter.land(piece, term)
    for step in range(lines):
        shared.begin(step)
    for step in range(2 * lines - 1):
        weights.advance(2 + step)
        shared.advance(step)

    def keep_window(piece, value):
        windows[gather.part(corner.me, 0)] = value

    @pl.loop(0, lines)
    def _(step):
        shared.close(step, keep_window)

    gather.start(0)

    def keep_rows(piece, value):
        rows_out[pl.ds(pl.multiple_of(piece * rows, rows), rows)] = value

    @pl.loop(0, weights.count)
    def _(step):
        weights.close(step, keep_rows)

    @pl.when(spot.line > 0)
    def _():
        rows_out[...] = late_ref[...]

    gather.relay(0)

    @pl.when(spot.me < lines // 2)
    def _():
        for row, height, col, cols, at, at_col in qkv_places(1, chunk * 4 // 3, width * 3 // 4):
            for j in range(cols // 128):
                row_ref[pl.ds(6 * at + at_col // 128 + j, height, 6)] = rows_out[
                    row : row + height, col + j * 128 : col + (j + 1) * 128
                ]

    @pl.when(spot.me >= lines // 2)
    def _():
        for j in range(8):
            row_ref[pl.ds(j, chunk, 8)] = rows_out[:, j * 128 : (j + 1) * 128]

    squares = jnp.sum(rows_out[...] * rows_out[...], 0, keepdims=True)
    gather.finish()
    shared_ref[...] = jnp.zeros_like(shared_ref)
    for phase in range(5):
        for quarter in range(4):

            def take(condition, row, height, j, start, stride):
                @pl.when(condition)
                def _():
                    at = quarter * WINDOW + row
                    shared_ref[pl.ds(start, height, stride)] = windows[at : at + height, j * 128 : (j + 1) * 128]

            shared_walk(spot.me, quarter, take, (phase,))
    kept = shared_ref[FRONT : FRONT + PADDED - FRONT]
    place = lax.broadcasted_iota(jnp.int32, kept.shape, 0)
    kept = jnp.where((place < SHARED_LANES) & (corner.me == 0), kept, 0.0)
    square = jnp.sum(jnp.sum(squares, 1, keepdims=True)) + jnp.sum(kept * kept)
    counted = jnp.sum(jnp.where(label_ref[...] < 2, 1.0, 0.0))
    line = lax.broadcasted_iota(jnp.int32, total_ref.shape, 0)
    slots[me] = jnp.where(line == 0, square, jnp.where(line == 1, loss_ref[...], jnp.where(line == 2, counted, 0.0)))

    def send(step):
        return remote(slots.at[me], slots.at[me], send_sem.at[step], recv_sem.at[step], peer(step))

    def arrive(step):
        source = lax.rem(me - step + count, count)
        return remote(slots.at[source], slots.at[source], send_sem.at[step], recv_sem.at[step], peer(step))

    @pl.loop(1, count)
    def _(step):
        send(step).start()

    @pl.loop(1, count)
    def _(step):
        arrive(step).wait_recv()

    total_ref[...] = jnp.sum(slots[...], 0)

    @pl.loop(1, count)
    def _(step):
        send(step).wait_send()

    scatter.close()


def share(early, late, embed_grad, patches, used_grad, gains, loss_tile, labels, lines, collective_id):
    width = early.shape[1]
    chunk = late.shape[0]
    packed = 4 * WINDOW + (2 * lines - 4) * SHORT
    count = 8 * lines
    shape = jax.ShapeDtypeStruct
    return pl.pallas_call(
        partial(share_kernel, lines),
        out_shape=(shape((chunk * width // 128, 128), WIDE), shape((PADDED, 128), WIDE), shape((8, 128), WIDE)),
        in_specs=[VMEM] * 8,
        out_specs=(VMEM,) * 3,
        scratch_shapes=[
            pltpu.VMEM((packed, width), WIDE),
            pltpu.VMEM((4 * WINDOW, width), WIDE),
            pltpu.VMEM((packed + WINDOW - SHORT, width), WIDE),
            pltpu.VMEM((count, 8, 128), WIDE),
            pltpu.VMEM((chunk, width), WIDE),
            pltpu.VMEM((patches.shape[1], width), WIDE),
        ]
        + LineSum.scratch(1, chunk, SUM_PIECES, width, True)
        + LineSum.scratch(lines, WINDOW, 1, width, False)
        + Scatter.scratch(packed, width, PIECES)
        + Gather.scratch(1)
        + [
            pltpu.SemaphoreType.DMA(()),
            pltpu.SemaphoreType.DMA((count,)),
            pltpu.SemaphoreType.DMA((count,)),
        ],
        compiler_params=pltpu.CompilerParams(
            collective_id=collective_id, has_side_effects=True, vmem_limit_bytes=63 * 2**20
        ),
    )(early, late, embed_grad, patches, used_grad, gains, loss_tile, labels)


def render_kernel(area, wide, block, split, table_ref, splat_ref, dist_ref, label_ref, loss_ref, grad_ref, flip, picked, hot, spread_grad):
    tokens = table_ref.shape[0]
    groups = tokens // wide
    splats, pixels = splat_ref.shape
    for j in range(groups):
        flip[j * 2 * area : (j + 1) * 2 * area] = jnp.transpose(table_ref[j * wide : (j + 1) * wide].astype(jnp.float32)).astype(jnp.bfloat16)
    spread_grad[...] = jnp.zeros_like(spread_grad)
    wide_ids = lax.broadcasted_iota(jnp.int32, (wide, block), 0).astype(jnp.float32).astype(jnp.bfloat16)
    cell_ids = lax.broadcasted_iota(jnp.int32, (area, block), 0).astype(jnp.float32)
    cell_low = cell_ids.astype(jnp.bfloat16)
    one, nil = jnp.ones((wide, block), jnp.bfloat16), jnp.zeros((wide, block), jnp.bfloat16)

    def one_block(step, loss):
        here = pl.ds(pl.multiple_of(step * block, block), block)
        opacities, spreads, lows = [], [], []
        for k in range(splats):
            index = splat_ref[k : k + 1, here]
            token = index // area
            column = (token % wide).astype(jnp.float32).astype(jnp.bfloat16)
            group = (token // wide)
            cell = (index % area).astype(jnp.float32)
            match = jnp.where(wide_ids == column, one, nil)
            hot[k] = match
            picked[...] = lax.dot_general(flip[...], match, NN, preferred_element_type=jnp.float32)
            op_sum = jnp.zeros((area, block), jnp.float32)
            sp_sum = jnp.zeros((area, block), jnp.float32)
            for j in range(groups):
                same = cell_ids == jnp.where(group == j, cell, -1.0)
                op_sum += jnp.where(same, picked[j * 2 * area : j * 2 * area + area], 0.0)
                sp_sum += jnp.where(same, picked[j * 2 * area + area : (j + 1) * 2 * area], 0.0)
            opacities.append(jnp.sum(op_sum, 0, keepdims=True))
            spreads.append(jnp.sum(sp_sum, 0, keepdims=True))
            lows.append((group, cell))
        opacity, spread = jnp.concatenate(opacities, 0), jnp.concatenate(spreads, 0)
        distance = dist_ref[:, here].astype(jnp.float32)
        labels = label_ref[:, here]
        valid = jnp.where(labels < 2, 1.0, 0.0)
        target = jnp.where(labels == 1, 1.0, 0.0)
        op_sig, sp_sig = jax.nn.sigmoid(opacity), jax.nn.sigmoid(spread)
        fade = jnp.exp(-0.25 * distance * sp_sig)
        contrib = (0.02 + 0.96 * op_sig) * fade
        keep_log = jnp.sum(jnp.log1p(-contrib), 0, keepdims=True)
        keep = jnp.exp(keep_log)
        alpha = 1.0 - keep
        alpha_log = jnp.log(alpha)
        loss = loss - valid * (target * alpha_log + (1.0 - target) * keep_log)
        keep_grad = valid * (target * keep / alpha - (1.0 - target))
        contrib_grad = -keep_grad / (1.0 - contrib)
        op_grad = contrib_grad * (0.96 * op_sig * (1.0 - op_sig)) * fade
        sp_grad = contrib_grad * contrib * (-0.25 * distance * sp_sig * (1.0 - sp_sig))
        for k in range(splats):
            group, cell = lows[k]
            parts_op, parts_sp = op_grad[k : k + 1], sp_grad[k : k + 1]
            for part in range(split):
                low_op, low_sp = parts_op.astype(jnp.bfloat16), parts_sp.astype(jnp.bfloat16)
                parts_op, parts_sp = parts_op - low_op.astype(jnp.float32), parts_sp - low_sp.astype(jnp.float32)
                pieces = []
                for j in range(groups):
                    same = cell_low == jnp.where(group == j, cell, -1.0).astype(jnp.bfloat16)
                    pieces.append(jnp.where(same, low_op, jnp.bfloat16(0)))
                    pieces.append(jnp.where(same, low_sp, jnp.bfloat16(0)))
                weighted = jnp.concatenate(pieces, 0)
                spread_grad[...] += lax.dot_general(weighted, hot[k], NT, preferred_element_type=jnp.float32)
        return loss

    loss = lax.fori_loop(0, pixels // block, one_block, jnp.zeros((1, block), jnp.float32))
    loss_ref[...] = jnp.broadcast_to(jnp.sum(loss, 1, keepdims=True), loss_ref.shape)
    for j in range(groups):
        grad_ref[j * wide : (j + 1) * wide] = jnp.transpose(spread_grad[j * 2 * area : (j + 1) * 2 * area]).astype(grad_ref.dtype)

def render(table, splats, distance, labels, area, block=512, wide=256, split=2):
    tokens = table.shape[0]
    vm = pl.BlockSpec(memory_space=pltpu.VMEM)
    groups = tokens // wide
    return pl.pallas_call(
        partial(render_kernel, area, wide, block, split),
        out_shape=(jax.ShapeDtypeStruct((8, 128), jnp.float32), jax.ShapeDtypeStruct(table.shape, jnp.bfloat16)),
        in_specs=[vm] * 4, out_specs=(vm, vm),
        scratch_shapes=[pltpu.VMEM((groups * 2 * area, wide), jnp.bfloat16), pltpu.VMEM((groups * 2 * area, block), jnp.float32),
            pltpu.VMEM((splats.shape[0], wide, block), jnp.bfloat16), pltpu.VMEM((groups * 2 * area, wide), jnp.float32)],
        compiler_params=pltpu.CompilerParams(vmem_limit_bytes=48 * 2**20),
    )(table, splats, distance, labels)


def owner_sum_kernel(lines, pieces, g_ref, o_ref, pair_out, pair_in, part, line_in, own_in, p_send, p_recv, l_send, up_recv, down_recv):
    me = lax.axis_index("dp")
    line, side = me // 2, lax.rem(me, 2)
    chunk = o_ref.shape[0]
    rows = chunk // pieces
    count = lines * pieces
    pair = {"dp": line * 2 + 1 - side}
    above = {"dp": lax.rem(line + 1, lines) * 2 + side}
    below = {"dp": lax.rem(line + lines - 1, lines) * 2 + side}
    has_below, has_above = line > 0, line < lines - 1

    def target(step):
        turn = lax.rem(step, lines)
        odd = lax.rem(turn, 2)
        return (1 - odd) * (lines - 1 - turn // 2) + odd * (turn // 2)

    def slot(step):
        return pl.ds(pl.multiple_of(step * rows, rows), rows)

    def here(step):
        return pl.ds(pl.multiple_of(step // lines * rows, rows), rows)

    def source(step, owner):
        return pl.ds(pl.multiple_of((target(step) * 2 + owner) * chunk + step // lines * rows, rows), rows)

    def copy(src, dst, send, recv, to):
        return pltpu.make_async_remote_copy(
            src_ref=src, dst_ref=dst, send_sem=send, recv_sem=recv, device_id=to, device_id_type=MESH
        )

    def pair_copy(step):
        return copy(pair_out.at[slot(step)], pair_in.at[slot(step)], p_send.at[step], p_recv.at[step], pair)

    def line_copy(step, to, recv):
        return copy(part.at[slot(step)], line_in.at[slot(step)], l_send.at[step], recv.at[step], to)

    def last_copy(step):
        return copy(part.at[slot(step)], own_in.at[here(step)], l_send.at[step], down_recv.at[step], below)

    barrier = pltpu.get_barrier_semaphore()
    pl.semaphore_signal(barrier, inc=1, device_id=pair, device_id_type=MESH)

    @pl.when(has_below)
    def _():
        pl.semaphore_signal(barrier, inc=1, device_id=below, device_id_type=MESH)

    @pl.when(has_above)
    def _():
        pl.semaphore_signal(barrier, inc=1, device_id=above, device_id_type=MESH)

    pl.semaphore_wait(barrier, 1 + jnp.minimum(line, 1) + jnp.minimum(lines - 1 - line, 1))

    @pl.loop(0, count)
    def _(step):
        pair_out[slot(step)] = g_ref[source(step, 1 - side)].astype(jnp.bfloat16)
        pair_copy(step).start()

    @pl.loop(0, count + lines - 1)
    def _(step):
        @pl.when(step < count)
        def _():
            pair_copy(step).wait_recv()
            part[slot(step)] = g_ref[source(step, side)].astype(jnp.float32) + pair_in[slot(step)].astype(jnp.float32)

        rising = step - line

        @pl.when((rising >= 0) & (rising < count) & (target(rising) > line))
        def _():
            @pl.when(has_below)
            def _():
                line_copy(rising, above, up_recv).wait_recv()
                part[slot(rising)] += line_in[slot(rising)]

            line_copy(rising, above, up_recv).start()

        falling = step - (lines - 1 - line)

        @pl.when((falling >= 0) & (falling < count) & (target(falling) < line))
        def _():
            @pl.when(has_above)
            def _():
                line_copy(falling, below, down_recv).wait_recv()
                part[slot(falling)] += line_in[slot(falling)]

            @pl.when(target(falling) == line - 1)
            def _():
                last_copy(falling).start()

            @pl.when(target(falling) < line - 1)
            def _():
                line_copy(falling, below, down_recv).start()

    @pl.loop(0, count)
    def _(step):
        pair_copy(step).wait_send()

        @pl.when(target(step) > line)
        def _():
            line_copy(step, above, up_recv).wait_send()

        @pl.when(target(step) < line)
        def _():
            line_copy(step, below, down_recv).wait_send()

        @pl.when(target(step) == line)
        def _():
            o_ref[here(step)] = part[slot(step)]

            @pl.when(has_below)
            def _():
                line_copy(step, above, up_recv).wait_recv()
                o_ref[here(step)] += line_in[slot(step)]

            @pl.when(has_above)
            def _():
                last_copy(step).wait_recv()
                o_ref[here(step)] += own_in[here(step)]


def owner_sum(grad, count_dp, collective_id, pieces):
    lines = count_dp // 2
    total, width = grad.shape
    chunk = total // count_dp
    half = (lines * chunk, width)
    vmem = pl.BlockSpec(memory_space=pltpu.VMEM)
    return pl.pallas_call(
        partial(owner_sum_kernel, lines, pieces),
        out_shape=jax.ShapeDtypeStruct((chunk, width), jnp.float32),
        in_specs=[vmem],
        out_specs=vmem,
        scratch_shapes=[
            pltpu.VMEM(half, jnp.bfloat16),
            pltpu.VMEM(half, jnp.bfloat16),
            pltpu.VMEM(half, jnp.float32),
            pltpu.VMEM(half, jnp.float32),
            pltpu.VMEM((chunk, width), jnp.float32),
        ]
        + [pltpu.SemaphoreType.DMA((lines * pieces,))] * 5,
        compiler_params=pltpu.CompilerParams(
            collective_id=collective_id, has_side_effects=True, vmem_limit_bytes=62 * 2**20
        ),
    )(grad)


def total_kernel(mine_ref, sum_ref, slots, own_sem, send_sem, recv_sem):
    first, second = lax.axis_size("dp"), lax.axis_size("tensor")
    count = first * second
    me = lax.axis_index("dp") * second + lax.axis_index("tensor")

    def peer(step):
        other = lax.rem(me + step, count)
        return {"dp": other // second, "tensor": lax.rem(other, second)}

    barrier = pltpu.get_barrier_semaphore()

    @pl.loop(1, count)
    def _(step):
        pl.semaphore_signal(barrier, inc=1, device_id=peer(step), device_id_type=MESH)

    pl.semaphore_wait(barrier, count - 1)
    own = pltpu.make_async_copy(mine_ref, slots.at[me], own_sem)
    own.start()

    def send(step):
        return pltpu.make_async_remote_copy(
            src_ref=mine_ref,
            dst_ref=slots.at[me],
            send_sem=send_sem.at[step],
            recv_sem=recv_sem.at[step],
            device_id=peer(step),
            device_id_type=MESH,
        )

    @pl.loop(1, count)
    def _(step):
        send(step).start()

    @pl.loop(1, count)
    def _(step):
        send(step).wait()

    own.wait()
    sum_ref[...] = jnp.sum(slots[...], 0)


def total_over_all(mine, collective_id):
    count = lax.axis_size("dp") * lax.axis_size("tensor")
    vmem = pl.BlockSpec(memory_space=pltpu.VMEM)
    return pl.pallas_call(
        total_kernel,
        out_shape=jax.ShapeDtypeStruct(mine.shape, jnp.float32),
        in_specs=[vmem],
        out_specs=vmem,
        scratch_shapes=[
            pltpu.VMEM((count,) + mine.shape, jnp.float32),
            pltpu.SemaphoreType.DMA(()),
            pltpu.SemaphoreType.DMA((count,)),
            pltpu.SemaphoreType.DMA((count,)),
        ],
        compiler_params=pltpu.CompilerParams(collective_id=collective_id, has_side_effects=True),
    )(mine)


def pack_qkv(matrix, parts):
    rows, cols = matrix.shape
    first = matrix[:, :512].reshape(parts, 2, rows // parts // 2, 512).transpose(0, 2, 1, 3)
    second = matrix[:, 512:].reshape(parts, 4, rows // parts // 4, 256).transpose(0, 2, 1, 3)
    return jnp.concatenate([first.reshape(parts, -1, 1024), second.reshape(parts, -1, 1024)], 1).reshape(-1, 1024)


def unpack_qkv(packed, parts):
    rows = packed.shape[0] // parts
    packed = packed.reshape(parts, rows, 1024)
    cut = rows * 2 // 3
    first = packed[:, :cut].reshape(parts, cut, 2, 512).transpose(0, 2, 1, 3).reshape(-1, 512)
    second = packed[:, cut:].reshape(parts, rows - cut, 4, 256).transpose(0, 2, 1, 3).reshape(-1, 256)
    return jnp.concatenate([first, second], 1)


def by_lanes(flat, outer):
    size = flat.size // math.prod(outer)
    return flat.reshape(outer + ((size // 128, 128) if size % 128 == 0 else (size,)))


def pad_first(array, axis, unit):
    short = -array.shape[axis] % unit
    return jnp.pad(array, [(0, short if at == axis else 0) for at in range(array.ndim)])


def sum_to_owners(stack, count_dp):
    if count_dp == 8:
        return owner_sum(stack, count_dp, 1, 9)
    return lax.psum_scatter(stack, "dp", scatter_dimension=0, tiled=True)

def adam_update(master, first_mom, second_mom, gradient, step_float):
    first_new = beta_one * first_mom + (1.0 - beta_one) * gradient
    second_new = beta_two * second_mom + (1.0 - beta_two) * gradient * gradient
    first_hat = first_new / (1.0 - jnp.power(beta_one, step_float))
    second_hat = second_new / (1.0 - jnp.power(beta_two, step_float))
    master_new = master - learn_rate * (
        first_hat / (jnp.sqrt(second_hat) + adam_eps) + decay_rate * master
    )
    return (master_new, first_new, second_new)


def adam_kernel(total_ref, count_ref, *refs):
    norm_value = jnp.sqrt(total_ref[0, 0:1]) / total_ref[2, 0:1]
    factor = clip_norm / jnp.maximum(norm_value, clip_norm) / total_ref[2, 0:1]
    step_float = jnp.full((1, 1), count_ref[0], jnp.int32).astype(WIDE)
    grad, master, first, second, ema = (ref[...] for ref in refs[:5])
    new, first_new, second_new = adam_update(master, first, second, grad * factor.reshape(1, 1), step_float)
    for ref, value in zip(refs[5:], (new, first_new, second_new, ema_rate * ema + (1.0 - ema_rate) * new, new.astype(LOW))):
        ref[...] = value


def adam(totals, step_count, grad, master, first, second, ema, block):
    size = master.shape[1]
    spec = pl.BlockSpec((1, block), lambda at: (0, at))
    return pl.pallas_call(
        adam_kernel,
        grid=(size // block,),
        out_shape=tuple(jax.ShapeDtypeStruct(master.shape, kind) for kind in (WIDE,) * 4 + (LOW,)),
        in_specs=[pl.BlockSpec((8, 128), lambda at: (0, 0)), pl.BlockSpec(memory_space=pltpu.SMEM)] + [spec] * 5,
        out_specs=(spec,) * 5,
    )(totals, step_count, grad, master, first, second, ema)


def per_device(
    patches,
    view_counts,
    splat_index,
    splat_dist,
    alpha_label,
    step_count,
    row_master,
    row_first,
    row_second,
    row_ema,
    shared_master,
    shared_first,
    shared_second,
    shared_ema,
):
    groups = lax.axis_size("tensor")
    my_dp = lax.axis_index("dp")
    count_dp = lax.axis_size("dp")
    local_width = D // groups
    qkv_parts = count_dp // 4
    share_rows = row_master.shape[1] // D
    own_patches = patches[0]
    if count_dp == 8:
        shared_lanes = jnp.pad(
            shared_master.reshape(SHARED_LANES, 128), ((FRONT, PADDED - FRONT - SHARED_LANES), (0, 0))
        )
        weights, used_cols, norm, embed, normed1, qkv, attended, log_total, resid1, normed2 = forward(
            view_counts, row_master.reshape(-1, 128), shared_lanes, own_patches, count_dp // 2, 7
        )
    else:
        own_row = row_master[0].astype(jnp.bfloat16)
        own_tiles = jnp.where(
            my_dp < qkv_parts,
            pack_qkv(own_row.reshape(-1, 3 * local_width), 1),
            own_row.reshape(share_rows, D),
        )
        weights = lax.all_gather(own_tiles, "dp", axis=0, tiled=True)
        own_flat = shared_master.astype(jnp.bfloat16)
        own_shared = by_lanes(own_flat, ())
        lead = own_shared.shape[0]
        own_shared = pad_first(own_shared, 0, 2048 // own_shared[0].size)
        shared_weights = lax.all_gather(own_shared, "dp", axis=0, tiled=False)[:, :lead].reshape(-1, 128)
        patch_rows = PIN * D // 128
        unpatch_rows = D * POUT // 128
        norm = shared_weights[patch_rows + unpatch_rows :].reshape(4, D).astype(jnp.float32)
        patch_proj = shared_weights[:patch_rows].reshape(PIN, D)
        used_cols = shared_weights[patch_rows : patch_rows + unpatch_rows].reshape(D, POUT // 128, 128)[:, 0]
        all_patches = lax.all_gather(own_patches, "tensor", axis=0, tiled=True)
        embed, normed1, qkv, attended, log_total, resid1, normed2 = attend(
            view_counts, all_patches, patch_proj, norm, weights, qkv_parts, 3
        )
    hidden, active, resid2_low, gauss_table = mlp(normed2, weights, resid1, used_cols, 4)
    loss_tile, table_grad = render(gauss_table, splat_index[0], splat_dist[0], alpha_label, PATCH * PATCH)
    loss_part = loss_tile[0, 0]
    unpatch_used, late_grad, late_low, resid_grad, branch, gain2_grad = mlp_back(
        table_grad, used_cols, resid2_low, active, hidden, normed2, weights, resid1, norm, attended, 5
    )
    early_grad, embed_grad, gain1_grad, *own_late = attend_back(
        view_counts,
        branch,
        weights,
        qkv,
        log_total,
        normed1,
        embed,
        resid_grad,
        norm,
        (late_grad, late_low) if count_dp == 8 else (),
        qkv_parts,
        count_dp // 2 if count_dp == 8 else 0,
        6,
    )
    gain_grad = jnp.concatenate([gain1_grad, gain2_grad], 0)
    if count_dp == 8:
        gains = jnp.pad(gain_grad, ((0, 4), (0, 0)))
        row_lanes, shared_kept, totals = share(
            early_grad, own_late[0], embed_grad, own_patches, unpatch_used, gains, loss_tile, alpha_label, count_dp // 2, 8
        )
        row_share = row_lanes.reshape(-1)
        shared_share = shared_kept[FRONT : FRONT + SHARED_LANES].reshape(-1)
    else:
        patch_grad = dot(own_patches, embed_grad, TN)
        unpatch_grad = jnp.concatenate(
            [unpatch_used, jnp.zeros((D, POUT - unpatch_used.shape[1]), jnp.float32)], 1
        )
        shared_grad = jnp.concatenate(
            [patch_grad.reshape(-1), unpatch_grad.reshape(-1), gain_grad.reshape(-1)]
        )
        split_grad = by_lanes(shared_grad, (count_dp, groups))
        lead = split_grad.shape[2]
        shared_stack = pad_first(split_grad, 2, 16 * D // split_grad[0, 0, 0].size).swapaxes(0, 1)
        shared_sum = lax.psum_scatter(shared_stack, "tensor", scatter_dimension=0, tiled=True)
        row_stack = jnp.concatenate([early_grad, late_grad], 0)
        stack = jnp.concatenate(
            [row_stack.reshape(count_dp, share_rows, D), shared_sum.reshape(count_dp, -1, D)], 1
        ).reshape(-1, D)
        own_share = sum_to_owners(stack, count_dp)
        own_rows = own_share[:share_rows]
        row_share = jnp.where(my_dp < qkv_parts, unpack_qkv(own_rows, 1).reshape(-1), own_rows.reshape(-1))
        shared_part = own_share[share_rows:].reshape((-1,) + split_grad.shape[3:])[:lead]
        shared_share = lax.all_gather(shared_part, "tensor", axis=0, tiled=False).reshape(-1)
        own_squares = jnp.sum(row_share * row_share) + jnp.sum(shared_part * shared_part)
        pixel_part = jnp.sum((alpha_label < 2).astype(jnp.float32))
        scalars = jnp.stack([own_squares, loss_part, pixel_part]).reshape(3, 1)
        totals = total_over_all(jnp.pad(jnp.broadcast_to(scalars, (3, 128)), ((0, 5), (0, 0))), 2)
    square_total, loss_total, pixel_total = totals[0, 0], totals[1, 0], totals[2, 0]
    norm_value = jnp.sqrt(square_total) / pixel_total
    factor = clip_norm / jnp.maximum(norm_value, clip_norm) / pixel_total
    step_float = step_count[0].astype(jnp.float32)
    row_new, row_first_new, row_second_new, row_ema_new, row_copy = adam(
        totals, step_count, row_share[None], row_master, row_first, row_second, row_ema, row_master.shape[1] // 6
    )
    shared_new, shared_first_new, shared_second_new = adam_update(
        shared_master, shared_first, shared_second, shared_share * factor, step_float
    )
    shared_ema_new = ema_rate * shared_ema + (1.0 - ema_rate) * shared_new
    return (
        norm_value.reshape(1),
        (loss_total / pixel_total).reshape(1),
        row_new,
        row_first_new,
        row_second_new,
        row_ema_new,
        row_copy,
        shared_new,
        shared_first_new,
        shared_second_new,
        shared_ema_new,
        shared_new.astype(jnp.bfloat16),
    )


def solution(mesh):
    placed = (
        P("dp", "tensor", None),
        P("dp"),
        P("dp", None, "tensor"),
        P("dp", None, "tensor"),
        P("dp", "tensor"),
        P(),
        P("tensor", "dp"),
        P("tensor", "dp"),
        P("tensor", "dp"),
        P("tensor", "dp"),
        P("dp"),
        P("dp"),
        P("dp"),
        P("dp"),
    )
    return jax.shard_map(
        per_device,
        mesh=mesh,
        in_specs=placed,
        out_specs=(
            P(),
            P(),
            P("tensor", "dp"),
            P("tensor", "dp"),
            P("tensor", "dp"),
            P("tensor", "dp"),
            P("tensor", "dp"),
            P("dp"),
            P("dp"),
            P("dp"),
            P("dp"),
            P("dp"),
        ),
        check_vma=False,
    )
```

```python
import math
from functools import partial

import jax
import jax.numpy as jnp
from jax import lax
from jax.experimental import pallas as pl
from jax.experimental.pallas import tpu as pltpu
from jax.sharding import PartitionSpec as P

D = 1024
DH = 64
FF = 4096
PATCH = 8
VTOK = 192
PIN = 576
POUT = 768
VMEM = pl.BlockSpec(memory_space=pltpu.VMEM)
HBM = pl.BlockSpec(memory_space=pl.ANY)
ROOT_HALF = 0.5**0.5
NORMAL_PEAK = (2.0 * math.pi) ** -0.5


clip_norm = 0.005
beta_one = 0.9
beta_two = 0.95
adam_eps = 1e-08
decay_rate = 0.05
learn_rate = 0.03
ema_rate = 0.9
norm_eps = 1e-05
masked_score = -1e30


MESH = pl.DeviceIdType.MESH
NN = (((1,), (0,)), ((), ()))
NT = (((1,), (1,)), ((), ()))
TN = (((0,), (0,)), ((), ()))
LOW = jnp.bfloat16
WIDE = jnp.float32
PIECES = 4
TILE = 256
UNIT = 128


def dot(left, right, dims=NN):
    return lax.dot_general(left, right, dims, preferred_element_type=WIDE)


def remote(src, dst, send, recv, to):
    return pltpu.make_async_remote_copy(
        src_ref=src, dst_ref=dst, send_sem=send, recv_sem=recv, device_id=to, device_id_type=MESH
    )


class Corner:
    def __init__(self):
        self.me = lax.axis_index("tensor")
        self.first, self.last = self.me // 2, lax.rem(self.me, 2)
        self.mate = self.first * 2 + 1 - self.last
        self.far = (1 - self.first) * 2 + self.last
        self.opposite = (1 - self.first) * 2 + 1 - self.last

    def block(self, step):
        return lax.rem(self.first + 1 - step // 2, 2) * 2 + lax.rem(self.last + 1 - lax.rem(step, 2), 2)

    def greet(self):
        barrier = pltpu.get_barrier_semaphore()
        for other in (self.mate, self.far):
            pl.semaphore_signal(barrier, inc=1, device_id={"tensor": other}, device_id_type=MESH)
        pl.semaphore_wait(barrier, 2)


class Gather:
    def __init__(self, corner, ref, pieces, sems, short=None):
        self.corner, self.ref, self.pieces, self.sems, self.short = corner, ref, pieces, sems, short
        self.size = ref.shape[0] // 4
        self.rows = self.size // pieces

    @staticmethod
    def scratch(pieces):
        return [pltpu.SemaphoreType.DMA((pieces,))] * 6

    def part(self, owner, piece, rows=None):
        return pl.ds(pl.multiple_of(owner * self.size + piece * self.rows, self.rows), rows or self.rows)

    def run(self, act, owner, piece, kind, to):
        def go(rows):
            here = self.ref.at[self.part(owner, piece, rows)]
            sems = self.sems[2 * kind].at[piece], self.sems[2 * kind + 1].at[piece]
            getattr(remote(here, here, *sems, {"tensor": to}), act)()

        by_half(self.short, piece < self.pieces // 2, self.rows, go)

    def start(self, piece):
        self.run("start", self.corner.me, piece, 1, self.corner.far)
        self.run("start", self.corner.me, piece, 0, self.corner.mate)

    def relay(self, piece):
        self.run("wait_recv", self.corner.far, piece, 1, self.corner.far)
        self.run("start", self.corner.far, piece, 2, self.corner.mate)

    def finish(self):
        corner = self.corner
        for piece in range(self.pieces):
            self.run("wait_recv", corner.mate, piece, 0, corner.mate)
            self.run("wait_recv", corner.opposite, piece, 2, corner.mate)
            self.run("wait_send", corner.me, piece, 0, corner.mate)
            self.run("wait_send", corner.me, piece, 1, corner.far)
            self.run("wait_send", corner.far, piece, 2, corner.mate)


def by_half(short, first, rows, go):
    if short is None:
        go(rows)
    elif isinstance(first, bool):
        go(rows if first else short)
    else:
        pl.when(first)(lambda: go(rows))
        pl.when(jnp.logical_not(first))(lambda: go(short))


class Scatter:
    def __init__(self, corner, pieces, mate_out, mate_in, far_out, far_in, mate_send, mate_recv, far_send, far_recv):
        self.corner, self.pieces = corner, pieces
        self.mate_out, self.mate_in, self.far_out, self.far_in = mate_out, mate_in, far_out, far_in
        self.sems = mate_send, mate_recv, far_send, far_recv
        self.rows = far_out.shape[0] // pieces

    @staticmethod
    def scratch(rows, width, pieces):
        return [
            pltpu.VMEM((2, rows, width), LOW),
            pltpu.VMEM((2, rows, width), LOW),
            pltpu.VMEM((rows, width), LOW),
            pltpu.VMEM((rows, width), LOW),
            pltpu.SemaphoreType.DMA((2, pieces)),
            pltpu.SemaphoreType.DMA((2, pieces)),
            pltpu.SemaphoreType.DMA((pieces,)),
            pltpu.SemaphoreType.DMA((pieces,)),
        ]

    def part(self, piece):
        return pl.ds(piece * self.rows, self.rows)

    def mate_copy(self, half, piece):
        part = self.part(piece)
        return remote(
            self.mate_out.at[half, part],
            self.mate_in.at[half, part],
            self.sems[0].at[half, piece],
            self.sems[1].at[half, piece],
            {"tensor": self.corner.mate},
        )

    def far_copy(self, piece):
        part = self.part(piece)
        return remote(
            self.far_out.at[part],
            self.far_in.at[part],
            self.sems[2].at[piece],
            self.sems[3].at[piece],
            {"tensor": self.corner.far},
        )

    def give(self, half, ref):
        for piece in range(self.pieces):
            part = self.part(piece)
            self.mate_out[half, part] = ref[part].astype(LOW)
            self.mate_copy(half, piece).start()

    def cross(self, ref):
        for piece in range(self.pieces):
            part = self.part(piece)
            self.mate_copy(0, piece).wait_recv()
            self.far_out[part] = (ref[part] + self.mate_in[0, part].astype(WIDE)).astype(LOW)
            self.far_copy(piece).start()

    def step(self, step, ref):
        @pl.when(step == 0)
        def _():
            self.give(0, ref)

        @pl.when(step == 1)
        def _():
            self.cross(ref)

        @pl.when(step == 2)
        def _():
            self.give(1, ref)

    def land(self, piece, ref):
        part = self.part(piece)
        self.mate_copy(1, piece).wait_recv()
        self.far_copy(piece).wait_recv()
        return ref[part] + self.mate_in[1, part].astype(WIDE) + self.far_in[part].astype(WIDE)

    def close(self):
        for piece in range(self.pieces):
            self.mate_copy(0, piece).wait_send()
            self.mate_copy(1, piece).wait_send()
            self.far_copy(piece).wait_send()


def standard(values):
    centre = values - jnp.mean(values, -1, keepdims=True)
    inverse = lax.rsqrt(jnp.mean(centre * centre, -1, keepdims=True) + norm_eps)
    return centre * inverse, inverse


def norm_back(grad_out, scaled, inverse, gain):
    grad_scaled = grad_out * gain
    return inverse * (
        grad_scaled
        - jnp.mean(grad_scaled, -1, keepdims=True)
        - scaled * jnp.mean(grad_scaled * scaled, -1, keepdims=True)
    )


def qkv_places(parts, rows, columns):
    share = rows // parts
    wide = columns * 2 // 3
    packed = share * columns // 1024
    for at in range(parts):
        for j in range(2):
            half = share // 2
            yield (at * packed, half, j * wide, wide, at * share + j * half, 0)
        for j in range(4):
            quarter = share // 4
            yield (at * packed + share // 2, quarter, j * (columns - wide), columns - wide, at * share + j * quarter, wide)


def unpack_into(full, packed, parts):
    for row, rows, col, cols, to_row, to_col in qkv_places(parts, full.shape[0], full.shape[1]):
        full[to_row : to_row + rows, to_col : to_col + cols] = packed[row : row + rows, col : col + cols]


def pack_from(packed, full, parts, base=0):
    for row, rows, col, cols, to_row, to_col in qkv_places(parts, full.shape[0], full.shape[1]):
        packed[base + row : base + row + rows, col : col + cols] = full[to_row : to_row + rows, to_col : to_col + cols]


def rows_of(block, size):
    return pl.ds(pl.multiple_of(block * size, size), size)


def column_loop(width, body):
    @pl.loop(0, width // TILE)
    def _(tile):
        body(pl.ds(pl.multiple_of(tile * TILE, TILE), TILE))


def attend_kernel(parts, q_rows, count_ref, patch_ref, proj_ref, norm_ref, weight_ref, *rest):
    corner = Corner()
    corner.greet()
    attend_body(parts, q_rows, corner, None, count_ref, patch_ref, proj_ref, norm_ref, weight_ref, *rest)


def attend_body(parts, q_rows, corner, progress, count_ref, patch_ref, proj_ref, norm_ref, weight_ref,
                embed_ref, normed1_ref, qkv_ref, attended_ref, log_ref, resid_ref, normed2_ref,
                qkv_proj, term, held, held_sem, *comm):
    progress = progress or (lambda *_: None)
    scatter = Scatter(corner, PIECES, *comm[:8])
    gather = Gather(corner, normed2_ref, PIECES, comm[8:])
    packed_rows = held.shape[0] * 3 // 4
    packed_ref, out_ref = held.at[pl.ds(0, packed_rows)], held.at[pl.ds(packed_rows, held.shape[0] - packed_rows)]

    def hold(start, target, at):
        copy = pltpu.make_async_copy(weight_ref.at[pl.ds(start, target.shape[0])], target, held_sem.at[at])
        copy.start()
        copy.wait()

    size, width = embed_ref.shape
    length = patch_ref.shape[0]
    local = attended_ref.shape[1]

    @pl.loop(0, 4)
    def _(block):
        here = rows_of(block, size)
        column_loop(width, lambda cols: term.__setitem__((slice(None), cols), dot(patch_ref[here], proj_ref[:, cols])))

        @pl.when(block == corner.me)
        def _():
            embed_ref[...] = term[...]

        scaled, inverse = standard(term[...])
        normed1_ref[here] = (scaled * norm_ref[0:1] + norm_ref[1:2]).astype(LOW)
        progress("embed", block)

    progress("weights")
    hold(0, packed_ref, 0)
    unpack_into(qkv_proj, packed_ref, parts)

    @pl.loop(0, 4)
    def _(block):
        here = rows_of(block, size)

        def columns(cols):
            qkv_ref[here, cols] = dot(normed1_ref[here], qkv_proj[:, cols]).astype(LOW)

        column_loop(3 * local, columns)

    valid = lax.broadcasted_iota(jnp.int32, (1, length), 1) < count_ref[0] * VTOK
    left = lax.broadcasted_iota(jnp.int32, (1, 2 * DH), 1) < DH
    factor = jnp.array(DH ** (-0.5), LOW)

    @pl.loop(0, length // q_rows)
    def _(turn):
        here = rows_of(turn, q_rows)
        for pair in range(local // (2 * DH)):
            lanes = slice(pair * 2 * DH, (pair + 1) * 2 * DH)
            queries = qkv_ref[here, lanes] * factor
            keyset = qkv_ref[:, local + pair * 2 * DH : local + (pair + 1) * 2 * DH]
            values = qkv_ref[:, 2 * local + pair * 2 * DH : 2 * local + (pair + 1) * 2 * DH]
            found = []
            for side in range(2):
                mine = left if side == 0 else ~left
                scores = dot(jnp.where(mine, queries, jnp.zeros_like(queries)), keyset, NT)
                scores = jnp.where(valid, scores, masked_score)
                top = jnp.max(scores, -1, keepdims=True)
                powers = jnp.exp(scores - top)
                total = jnp.sum(powers, -1, keepdims=True)
                log_ref[here, pair * 2 + side : pair * 2 + side + 1] = top + jnp.log(total)
                found.append(dot((powers * (1.0 / total)).astype(LOW), values))
            attended_ref[here, lanes] = jnp.where(left, found[0], found[1]).astype(LOW)
        progress("turn", turn)

    progress("out")
    hold(packed_rows, out_ref, 1)

    @pl.loop(0, 4)
    def _(step):
        here = rows_of(corner.block(step), size)
        column_loop(width, lambda cols: term.__setitem__((slice(None), cols), dot(attended_ref[here], out_ref[:, cols])))
        scatter.step(step, term)
        progress("give", step)

    for piece in range(PIECES):
        part = scatter.part(piece)
        resid = embed_ref[part] + scatter.land(piece, term)
        resid_ref[part] = resid
        scaled, inverse = standard(resid)
        normed2_ref[gather.part(corner.me, piece)] = (scaled * norm_ref[2:3] + norm_ref[3:4]).astype(LOW)
        gather.start(piece)
        progress("land", piece)
    for piece in range(PIECES):
        gather.relay(piece)
    gather.finish()
    scatter.close()


def attend(count, patches, patch_proj, norm, weights, parts, collective_id):
    length, size = patches.shape[0], patches.shape[0] // 4
    width, local = patch_proj.shape[1], patch_proj.shape[1] // 4
    shape = jax.ShapeDtypeStruct
    return pl.pallas_call(
        partial(attend_kernel, parts, 256),
        out_shape=(
            shape((size, width), WIDE),
            shape((length, width), LOW),
            shape((length, 3 * local), LOW),
            shape((length, local), LOW),
            shape((length, local // DH), WIDE),
            shape((size, width), WIDE),
            shape((length, width), LOW),
        ),
        in_specs=[pl.BlockSpec(memory_space=pltpu.SMEM)] + [VMEM] * 3 + [HBM],
        out_specs=(VMEM,) * 7,
        scratch_shapes=[
            pltpu.VMEM((width, 3 * local), LOW),
            pltpu.VMEM((size, width), WIDE),
            pltpu.VMEM((4 * local, width), LOW),
            pltpu.SemaphoreType.DMA((2,)),
        ]
        + Scatter.scratch(size, width, PIECES)
        + Gather.scratch(PIECES),
        compiler_params=pltpu.CompilerParams(
            collective_id=collective_id, has_side_effects=True, vmem_limit_bytes=62 * 2**20
        ),
    )(count, patches, patch_proj, norm, weights)


class Lines:
    def __init__(self, lines):
        self.lines = lines
        self.me = lax.axis_index("dp")
        self.line, self.side = self.me // 2, lax.rem(self.me, 2)
        self.pair = {"dp": self.line * 2 + 1 - self.side}
        self.above = {"dp": lax.rem(self.line + 1, lines) * 2 + self.side}
        self.below = {"dp": lax.rem(self.line + lines - 1, lines) * 2 + self.side}
        self.has_below, self.has_above = self.line > 0, self.line < lines - 1

    def signal(self, barrier):
        pl.semaphore_signal(barrier, inc=1, device_id=self.pair, device_id_type=MESH)

        @pl.when(self.has_below)
        def _():
            pl.semaphore_signal(barrier, inc=1, device_id=self.below, device_id_type=MESH)

        @pl.when(self.has_above)
        def _():
            pl.semaphore_signal(barrier, inc=1, device_id=self.above, device_id_type=MESH)

        return 1 + jnp.minimum(self.line, 1) + jnp.minimum(self.lines - 1 - self.line, 1)


class LineGather:
    def __init__(self, spot, ref, base, chunk, pieces, late_own, sems, short=None):
        self.spot, self.ref, self.base, self.chunk, self.pieces, self.late_own = spot, ref, base, chunk, pieces, late_own
        self.sems, self.short = sems, short
        self.rows = chunk // pieces
        self.steps = (spot.lines - 1) * pieces

    @staticmethod
    def scratch(lines, pieces):
        return [pltpu.SemaphoreType.DMA((lines * pieces,))] * 6

    def run(self, act, kind, line, piece, crossed=False):
        spot = self.spot
        side = 1 - spot.side if crossed else spot.side
        to = (spot.above, spot.below, spot.pair)[kind]

        def go(rows):
            start = self.base + (line * 2 + side) * self.chunk + piece * self.rows
            here = self.ref.at[pl.ds(pl.multiple_of(start, 16), rows)]
            at = line * self.pieces + piece
            getattr(remote(here, here, self.sems[2 * kind].at[at], self.sems[2 * kind + 1].at[at], to), act)()

        by_half(self.short, line < spot.lines // 2, self.rows, go)

    def own(self, kind):
        @pl.loop(0, self.pieces)
        def _(piece):
            self.run("start", kind, self.spot.line, piece)

    def begin(self):
        spot = self.spot
        if self.late_own:

            @pl.when(spot.line == 0)
            def _():
                self.own(0)

            return

        @pl.when(spot.has_above)
        def _():
            self.own(0)

        @pl.when(spot.has_below)
        def _():
            self.own(1)

        self.own(2)

    def follow(self):
        @pl.when(self.spot.has_below)
        def _():
            self.own(1)

        @pl.when(self.spot.line == 0)
        def _():
            self.own(2)

    def step(self, at):
        spot = self.spot
        piece = lax.rem(at, self.pieces)

        @pl.when(at < spot.line * self.pieces)
        def _():
            turn = at // self.pieces
            line = jnp.minimum(turn, 1) * (spot.line - turn) if self.late_own else turn
            self.run("wait_recv", 0, line, piece)

            @pl.when(spot.has_above)
            def _():
                self.run("start", 0, line, piece)

            self.run("start", 2, line, piece)

        if self.late_own:

            @pl.when((at == self.pieces - 1) & spot.has_below & spot.has_above)
            def _():
                self.own(0)

            @pl.when(at == spot.line * self.pieces - 1)
            def _():
                self.own(2)

        @pl.when(at < (spot.lines - 1 - spot.line) * self.pieces)
        def _():
            line = spot.line + 1 + at // self.pieces
            self.run("wait_recv", 1, line, piece)

            @pl.when(spot.has_below)
            def _():
                self.run("start", 1, line, piece)

            self.run("start", 2, line, piece)

    def wait_crossed(self, line):
        @pl.loop(0, self.pieces)
        def _(piece):
            self.run("wait_recv", 2, line, piece, True)

    def close(self):
        spot = self.spot

        @pl.loop(0, spot.lines * self.pieces)
        def _(at):
            line, piece = at // self.pieces, lax.rem(at, self.pieces)
            self.run("wait_send", 2, line, piece)

            @pl.when((line <= spot.line) & spot.has_above)
            def _():
                self.run("wait_send", 0, line, piece)

            @pl.when((line >= spot.line) & spot.has_below)
            def _():
                self.run("wait_send", 1, line, piece)


WINDOW = 48
SHORT = 16
FRONT = 80
PADDED = 1616
ROW_START = (0, 160, 336, 496)
USED_START = (None, None, None, 0, 128, 352, 576, 800)


def window_row(owner):
    if isinstance(owner, int):
        return owner * WINDOW if owner < 4 else 4 * WINDOW + (owner - 4) * SHORT
    return jnp.minimum(owner, 4) * WINDOW + jnp.maximum(owner - 4, 0) * SHORT


def shared_offsets(me, quarter):
    chunk = SHARED_LANES
    rows = jnp.where(me == 0, 0, jnp.where(me == 1, 160, jnp.where(me == 2, 336, 496)))
    used = (me - 4) * 224 + 128
    return (
        FRONT + 8 * rows - me * chunk + 8 * WINDOW * quarter,
        FRONT + 8 * rows - me * chunk + 8 * 32 * quarter,
        FRONT + PATCH_LANES - me * chunk + 6 * 48 * quarter,
        FRONT + PATCH_LANES + 6 * used - me * chunk + 6 * 64 * quarter,
        FRONT + PATCH_LANES + 6 * D - me * chunk,
    )


def shared_walk(me, quarter, take, phases=range(5)):
    rows, last_rows, first_used, used, norm = shared_offsets(me, quarter)
    for j in range(8):
        if 0 in phases:
            take(me < 3, 0, WINDOW, j, rows + j, 8)
        if 1 in phases:
            take((me == 3) & (quarter < 3), 0, 32, j, last_rows + j, 8)
    if 2 in phases:
        for j in range(3):
            take((me == 3) & (quarter < 3), 32, 16, j, first_used + 6 * 16 * j, 6)
    if 3 in phases:
        for j in range(4):
            take(me > 3, 0, SHORT, j, used + 6 * SHORT * j, 6)
    if 4 in phases:
        for j in range(4):
            take((me == 7) & (quarter == 0), 0, SHORT, 4 + j, norm + j, 4)


def window_pieces(kind, row):
    found = []
    if kind == 0:
        for me in range(3):
            at = row - ROW_START[me]
            if 0 <= at < 4 * WINDOW:
                found.append((me, at // WINDOW, at % WINDOW, None))
        at = row - ROW_START[3]
        if 0 <= at < 96:
            found.append((3, at // 32, at % 32, None))
    else:
        if row < 144:
            found.append((3, row // 48, 32, row % 48 // 16))
        for me in range(4, 8):
            at = row - USED_START[me]
            if 0 <= at < 256:
                found.append((me, at // 64, 0, at % 64 // 16))
    return found

SHARED_LANES = 1348
PATCH_LANES = PIN * D // 128
CHUNK_PIECES = 4


def forward_kernel(lines, q_rows, count_ref, row_ref, shared_ref, own_patch_ref,
                   weight_ref, used_ref, norm_ref,
                   embed_ref, normed1_ref, qkv_ref, attended_ref, log_ref, resid_ref, normed2_ref,
                   patches, proj, windows, own_chunk, own_sem, *rest):
    body, extra = rest[:4 + 14], rest[4 + 14:]
    corner, spot = Corner(), Lines(lines)
    barrier = pltpu.get_barrier_semaphore()
    for other in (corner.mate, corner.far):
        pl.semaphore_signal(barrier, inc=1, device_id={"tensor": other}, device_id_type=MESH)
    pl.semaphore_wait(barrier, 2 + spot.signal(barrier))
    parts = lines // 2
    chunk = weight_ref.shape[0] // (2 * lines)
    size, inputs = own_patch_ref.shape
    window = LineGather(spot, windows, corner.me * (2 * lines * WINDOW), WINDOW, 1, False, extra[0:6], SHORT)
    weights = LineGather(spot, weight_ref, 0, chunk, CHUNK_PIECES, True, extra[6:12])
    spread = Gather(corner, windows, 2 * lines, extra[12:18], SHORT)
    given = Gather(corner, patches, 1, extra[18:24])

    patches[given.part(corner.me, 0)] = own_patch_ref[...]
    given.start(0)
    base = pl.multiple_of((corner.me * 2 * lines + spot.me) * WINDOW, 16)
    windows[pl.ds(base, WINDOW)] = jnp.zeros((WINDOW, windows.shape[1]), LOW)

    def take(condition, row, rows, j, start, stride):
        @pl.when(condition)
        def _():
            windows[pl.ds(pl.multiple_of(base + row, 16), rows), j * 128 : (j + 1) * 128] = shared_ref[
                pl.ds(start, rows, stride)
            ].astype(LOW)

    shared_walk(spot.me, corner.me, take)
    window.begin()
    spread.start(spot.me)
    own = pl.multiple_of(spot.me * chunk, 16)

    @pl.when(spot.me < parts)
    def _():
        for row, rows, col, cols, at, at_col in qkv_places(1, chunk * 4 // 3, D * 3 // 4):
            for j in range(cols // 128):
                own_chunk[row : row + rows, col + j * 128 : col + (j + 1) * 128] = row_ref[
                    pl.ds(6 * at + at_col // 128 + j, rows, 6)
                ].astype(LOW)

    @pl.when(spot.me >= parts)
    def _():
        for j in range(8):
            own_chunk[:, j * 128 : (j + 1) * 128] = row_ref[pl.ds(j, chunk, 8)].astype(LOW)

    kept = pltpu.make_async_copy(own_chunk, weight_ref.at[pl.ds(own, chunk)], own_sem)
    kept.start()
    kept.wait()
    weights.begin()

    def passed(stage, act):
        if stage == 0:
            act(spot.me, None)
            act(spot.line * 2 + 1 - spot.side, spot.line)
            return
        for near in (True, False):
            for there, line in (
                (stage - 1 < spot.line, stage - 1),
                (stage - 1 < lines - 1 - spot.line, spot.line + stage),
            ):

                @pl.when(there)
                def _():
                    act(line * 2 + (spot.side if near else 1 - spot.side), None if near else line)

    def send_on(owner, line):
        if line is not None:
            window.wait_crossed(line)
        spread.start(owner)

    def relay_on(owner, line):
        spread.relay(owner)

    window.wait_crossed(spot.line)
    spread.start(spot.line * 2 + 1 - spot.side)
    window.step(0)
    passed(1, send_on)
    window.step(1)
    passed(2, send_on)
    window.step(2)
    weights.follow()
    weights.step(0)
    passed(3, send_on)
    weights.step(1)
    given.relay(0)
    passed(0, relay_on)
    weights.step(2)
    passed(1, relay_on)
    weights.step(3)
    passed(2, relay_on)
    passed(3, relay_on)
    spread.finish()
    given.finish()

    def source(me, quarter, row, rows, j):
        start = (quarter * 2 * lines + me) * WINDOW + row
        return windows[start : start + rows] if j is None else windows[start : start + rows, j * 128 : (j + 1) * 128]

    for row in range(0, proj.shape[0], 16):
        proj[row : row + 16] = sum(source(me, t, at, 16, j) for me, t, at, j in window_pieces(0, row))
    for row in range(0, used_ref.shape[0], 16):
        used_ref[row : row + 16] = sum(source(me, t, at, 16, j) for me, t, at, j in window_pieces(1, row))
    ends = source(2 * lines - 1, 0, 0, SHORT, None)[:, D // 2 :].astype(WIDE)
    norm_ref[...] = jnp.zeros_like(norm_ref)
    for row in range(8):
        norm_ref[row // 2 : row // 2 + 1, row % 2 * D // 2 : (row % 2 + 1) * D // 2] = ends[row : row + 1]

    def progress(place, at=None):
        if place == "embed":

            @pl.when(at == 2)
            def _():
                weights.step(4)

        if place == "weights":
            weights.step(5)
            weights.wait_crossed(0)
        if place == "turn":

            weights.step(6 + at)
        if place == "out":
            weights.wait_crossed(1)

    attend_body(parts, q_rows, corner, progress, count_ref, patches, proj, norm_ref,
                weight_ref, embed_ref, normed1_ref, qkv_ref, attended_ref, log_ref, resid_ref, normed2_ref, *body)
    for line in range(2, lines):
        weights.wait_crossed(line)
    weights.close()
    window.close()


def forward(count, row_lanes, shared_lanes, own_patches, lines, collective_id):
    size, inputs = own_patches.shape
    length, width, local = 4 * size, D, D // 4
    shape = jax.ShapeDtypeStruct
    return pl.pallas_call(
        partial(forward_kernel, lines, 256),
        out_shape=(
            shape((3 * D, D), LOW),
            shape((D, 128), LOW),
            shape((8, D), WIDE),
            shape((size, width), WIDE),
            shape((length, width), LOW),
            shape((length, 3 * local), LOW),
            shape((length, local), LOW),
            shape((length, local // DH), WIDE),
            shape((size, width), WIDE),
            shape((length, width), LOW),
        ),
        in_specs=[pl.BlockSpec(memory_space=pltpu.SMEM)] + [VMEM] * 3,
        out_specs=(HBM,) + (VMEM,) * 9,
        scratch_shapes=[
            pltpu.VMEM((length, inputs), LOW),
            pltpu.VMEM((inputs, width), LOW),
            pltpu.VMEM((8 * lines * WINDOW, width), LOW),
            pltpu.VMEM((3 * D // (2 * lines), width), LOW),
            pltpu.SemaphoreType.DMA(()),
            pltpu.VMEM((width, 3 * local), LOW),
            pltpu.VMEM((size, width), WIDE),
            pltpu.VMEM((4 * local, width), LOW),
            pltpu.SemaphoreType.DMA((2,)),
        ]
        + Scatter.scratch(size, width, PIECES)
        + Gather.scratch(PIECES)
        + LineGather.scratch(lines, 1)
        + LineGather.scratch(lines, CHUNK_PIECES)
        + Gather.scratch(2 * lines)
        + Gather.scratch(1),
        compiler_params=pltpu.CompilerParams(
            collective_id=collective_id, has_side_effects=True, vmem_limit_bytes=63 * 2**20
        ),
    )(count, row_lanes, shared_lanes, own_patches)


class Moves:
    def __init__(self, sems, *pairs):
        self.copies = [pltpu.make_async_copy(src, dst, sems.at[at]) for at, (src, dst) in enumerate(pairs)]

    def start(self, *which):
        for at in which or range(len(self.copies)):
            self.copies[at].start()

    def wait(self, *which):
        for at in which or range(len(self.copies)):
            self.copies[at].wait()


def mlp_kernel(normed2_ref, weight_ref, resid1_ref, cols_ref, hidden_out, active_out, low_ref, table_ref,
               term, up_ref, down_ref, hidden_ref, active_ref, load_sem, hidden_sem, active_sem, *comm):
    first, ff = up_ref.shape[0], down_ref.shape[0]
    loads = Moves(load_sem, (weight_ref.at[pl.ds(first, first)], up_ref), (weight_ref.at[pl.ds(2 * first, ff)], down_ref))
    loads.start()
    corner = Corner()
    corner.greet()
    scatter = Scatter(corner, PIECES, *comm[:8])
    gather = Gather(corner, table_ref, PIECES, comm[8:])
    size, width = resid1_ref.shape
    loads.wait()

    def stores(step):
        here = rows_of(corner.block(step), size)
        return (
            pltpu.make_async_copy(hidden_ref.at[here], hidden_out.at[here], hidden_sem.at[step]),
            pltpu.make_async_copy(active_ref.at[here], active_out.at[here], active_sem.at[step]),
        )

    @pl.loop(0, 4)
    def _(step):
        here = rows_of(corner.block(step), size)

        def columns(cols):
            hidden = dot(normed2_ref[here], up_ref[:, cols])
            hidden_ref[here, cols] = hidden
            active_ref[here, cols] = (0.5 * hidden * (1.0 + lax.erf(hidden * ROOT_HALF))).astype(LOW)

        column_loop(up_ref.shape[1], columns)
        for copy in stores(step):
            copy.start()
        column_loop(width, lambda cols: term.__setitem__((slice(None), cols), dot(active_ref[here], down_ref[:, cols])))
        scatter.step(step, term)

    for piece in range(PIECES):
        part = scatter.part(piece)
        low_ref[part] = (resid1_ref[part] + scatter.land(piece, term)).astype(LOW)
        table_ref[gather.part(corner.me, piece)] = dot(low_ref[part], cols_ref[...]).astype(LOW)
        gather.start(piece)
    for piece in range(PIECES):
        gather.relay(piece)
    gather.finish()
    scatter.close()
    for step in range(4):
        for copy in stores(step):
            copy.wait()


def mlp(normed2, weights, resid1, used_cols, collective_id):
    length, size, width = normed2.shape[0], resid1.shape[0], resid1.shape[1]
    hidden = FF // 4
    shape = jax.ShapeDtypeStruct
    return pl.pallas_call(
        mlp_kernel,
        out_shape=(
            shape((length, hidden), WIDE),
            shape((length, hidden), LOW),
            shape((size, width), LOW),
            shape((length, used_cols.shape[1]), LOW),
        ),
        in_specs=[VMEM, HBM, VMEM, VMEM],
        out_specs=(HBM, HBM, VMEM, VMEM),
        scratch_shapes=[
            pltpu.VMEM((size, width), WIDE),
            pltpu.VMEM((width, hidden), LOW),
            pltpu.VMEM((hidden, width), LOW),
            pltpu.VMEM((length, hidden), WIDE),
            pltpu.VMEM((length, hidden), LOW),
            pltpu.SemaphoreType.DMA((2,)),
            pltpu.SemaphoreType.DMA((4,)),
            pltpu.SemaphoreType.DMA((4,)),
        ]
        + Scatter.scratch(size, width, PIECES)
        + Gather.scratch(PIECES),
        compiler_params=pltpu.CompilerParams(
            collective_id=collective_id, has_side_effects=True, vmem_limit_bytes=62 * 2**20
        ),
    )(normed2, weights, resid1, used_cols)


def mlp_back_kernel(chunk, table_ref, cols_ref, low_ref, active_in, hidden_in, normed2_in, weight_ref, resid1_ref, norm_ref, attended_ref,
                    unpatch_ref, grad_out, rounded_out, resid_grad_ref, branch_ref, gain_ref,
                    gauss, down_in, hidden_grad, term, tail, active_ref, hidden_ref, normed2_ref, up_ref, down_ref, grad_ref,
                    rounded_ref, load_sem, store_sem, *comm):
    first = up_ref.shape[0]
    loads = Moves(
        load_sem,
        (weight_ref.at[pl.ds(2 * first, down_ref.shape[0])], down_ref),
        (weight_ref.at[pl.ds(first, first)], up_ref),
        (normed2_in, normed2_ref),
        (active_in, active_ref),
    )
    corner = Corner()

    def load_hidden(step):
        here = rows_of(corner.block(step), resid1_ref.shape[0])
        return pltpu.make_async_copy(hidden_in.at[here], hidden_ref.at[here], load_sem.at[4 + step])

    loads.start(0)
    load_hidden(0).start()
    loads.start(1)
    for step in range(1, 4):
        load_hidden(step).start()
    loads.start(2, 3)
    corner.greet()
    small = Scatter(corner, 1, *comm[:8])
    spread = Gather(corner, gauss, 1, comm[8:14])
    scatter = Scatter(corner, PIECES, *comm[14:22])
    gather = Gather(corner, branch_ref, PIECES, comm[22:])
    size, width = resid1_ref.shape
    ff = up_ref.shape[1]

    def view(step):
        return table_ref.at[rows_of(corner.block(step), size)]

    tail[...] = view(0)[...].astype(WIDE)
    small.give(0, tail)
    tail[...] = view(1)[...].astype(WIDE)
    small.cross(tail)
    tail[...] = view(2)[...].astype(WIDE)
    small.give(1, tail)
    tail[...] = view(3)[...].astype(WIDE)
    own_gauss = small.land(0, tail).astype(LOW)
    gauss[spread.part(corner.me, 0)] = own_gauss
    spread.start(0)
    unpatch_ref[...] = dot(low_ref[...], own_gauss, TN)
    spread.relay(0)
    spread.finish()
    small.close()
    loads.wait(0, 1)

    @pl.loop(0, 4)
    def _(step):
        here = rows_of(corner.block(step), size)
        load_hidden(step).wait()
        term[...] = dot(gauss[here], cols_ref[...], NT)
        down_in[here] = term[...].astype(LOW)

        @pl.when(step == 3)
        def _():
            resid_grad_ref[...] = term[...]

        def columns(cols):
            active_grad = dot(down_in[here], down_ref[cols, :], NT)
            hidden = hidden_ref[here, cols]
            slope = 0.5 * (1.0 + lax.erf(hidden * ROOT_HALF)) + hidden * (jnp.exp(-0.5 * hidden * hidden) * NORMAL_PEAK)
            hidden_grad[here, cols] = (active_grad * slope).astype(LOW)

        column_loop(ff, columns)

        def back(cols):
            term[:, cols] = dot(hidden_grad[here], up_ref[cols, :], NT)

        column_loop(width, back)
        scatter.step(step, term)

    side = None if chunk is None else lax.rem(lax.axis_index("dp"), 2)

    def store(at, act):
        part = pl.ds(pl.multiple_of(at * UNIT, UNIT), UNIT)

        def wide():
            getattr(pltpu.make_async_copy(grad_ref.at[part], grad_out.at[part], store_sem.at[at]), act)()

        def rounded():
            getattr(pltpu.make_async_copy(rounded_ref.at[part], rounded_out.at[part], store_sem.at[at]), act)()

        if chunk is None:
            wide()
            return
        mine = lax.rem(at * UNIT // chunk, 2) == side
        pl.when(mine)(wide)
        pl.when(jnp.logical_not(mine))(rounded)

    def keep(tile, value):
        part = pl.ds(pl.multiple_of(tile * TILE, TILE), TILE)
        grad_ref[part, :] = value
        rounded_ref[part, :] = value.astype(LOW)
        for at in range(TILE // UNIT):
            store(tile * (TILE // UNIT) + at, "start")

    loads.wait(2, 3)
    tiles = attended_ref.shape[1] // TILE

    @pl.loop(0, width // TILE)
    def _(tile):
        cols = pl.ds(pl.multiple_of(tile * TILE, TILE), TILE)
        keep(tiles + tile, dot(normed2_ref[:, cols], hidden_grad[...], TN))

    @pl.loop(0, ff // TILE)
    def _(tile):
        cols = pl.ds(pl.multiple_of(tile * TILE, TILE), TILE)
        keep(tiles + width // TILE + tile, dot(active_ref[:, cols], down_in[...], TN))

    gain_sum, bias_sum = jnp.zeros((1, width), WIDE), jnp.zeros((1, width), WIDE)
    for piece in range(PIECES):
        part = scatter.part(piece)
        grad = scatter.land(piece, term)
        scaled, inverse = standard(resid1_ref[part])
        total = resid_grad_ref[part] + norm_back(grad, scaled, inverse, norm_ref[2:3])
        resid_grad_ref[part] = total
        branch_ref[gather.part(corner.me, piece)] = total.astype(LOW)
        gather.start(piece)
        gain_sum += jnp.sum(grad * scaled, 0, keepdims=True)
        bias_sum += jnp.sum(grad, 0, keepdims=True)
    gain_ref[0:1] = gain_sum
    gain_ref[1:2] = bias_sum
    for piece in range(PIECES):
        gather.relay(piece)
    gather.finish()
    scatter.close()

    for tile in range(tiles):
        keep(tile, dot(attended_ref[:, tile * TILE : (tile + 1) * TILE], branch_ref[...], TN))

    @pl.loop(0, grad_ref.shape[0] // UNIT)
    def _(at):
        store(at, "wait")


def mlp_back(table_grad, used_cols, low, active, hidden, normed2, weights, resid1, norm, attended, chunk, collective_id):
    length, size, width = normed2.shape[0], resid1.shape[0], resid1.shape[1]
    ff, used = hidden.shape[1], used_cols.shape[1]
    total = attended.shape[1] + width + ff
    shape = jax.ShapeDtypeStruct
    return pl.pallas_call(
        partial(mlp_back_kernel, chunk),
        out_shape=(
            shape((width, used), WIDE),
            shape((total, width), WIDE),
            shape((total, width), LOW),
            shape((size, width), WIDE),
            shape((length, width), LOW),
            shape((2, width), WIDE),
        ),
        in_specs=[VMEM] * 3 + [HBM] * 4 + [VMEM] * 3,
        out_specs=(VMEM, HBM, HBM, VMEM, VMEM, VMEM),
        scratch_shapes=[
            pltpu.VMEM((length, used), LOW),
            pltpu.VMEM((length, width), LOW),
            pltpu.VMEM((length, ff), LOW),
            pltpu.VMEM((size, width), WIDE),
            pltpu.VMEM((size, used), WIDE),
            pltpu.VMEM((length, ff), LOW),
            pltpu.VMEM((length, ff), WIDE),
            pltpu.VMEM((length, width), LOW),
            pltpu.VMEM((width, ff), LOW),
            pltpu.VMEM((ff, width), LOW),
            pltpu.VMEM((total, width), WIDE),
            pltpu.VMEM((total, width), LOW),
            pltpu.SemaphoreType.DMA((8,)),
            pltpu.SemaphoreType.DMA((total // UNIT,)),
        ]
        + Scatter.scratch(size, used, 1)
        + Gather.scratch(1)
        + Scatter.scratch(size, width, PIECES)
        + Gather.scratch(PIECES),
        compiler_params=pltpu.CompilerParams(
            collective_id=collective_id, has_side_effects=True, vmem_limit_bytes=63 * 2**20
        ),
    )(table_grad, used_cols, low, active, hidden, normed2, weights, resid1, norm, attended)


class LineSum:
    def __init__(self, spot, pieces, low, source, buffers, sems, first=0, turns=4, stored=None):
        self.spot, self.pieces, self.low, self.source = spot, pieces, low, source
        self.first, self.turns, self.stored = first, turns, stored
        self.pair_out, self.pair_in, self.part, self.line_in, self.low_out, self.low_in = buffers
        self.p_send, self.p_recv, self.l_send, self.up_recv, self.down_recv = sems
        self.count = turns * pieces
        self.rows = self.part.shape[0] // self.count

    @staticmethod
    def scratch(turns, rows, pieces, width, low, stored=False):
        half = (turns * rows, width)
        kept = half if low else (rows, width)
        kind = LOW if low else WIDE
        return [
            pltpu.VMEM((16, 128) if stored else half, LOW),
            pltpu.VMEM(half, LOW),
            pltpu.VMEM(half, WIDE),
            pltpu.VMEM(half, WIDE),
            pltpu.VMEM(half if low else (16, 128), LOW),
            pltpu.VMEM(kept, kind),
        ] + [pltpu.SemaphoreType.DMA((turns * pieces,))] * 5

    def target(self, step):
        turn = lax.rem(step, self.turns)
        if self.turns == 4:
            odd = lax.rem(turn, 2)
            return (1 - odd) * (3 - turn // 2) + odd * (turn // 2)
        if self.turns == 3:
            return self.first + 2 - 2 * jnp.minimum(turn, 1) + turn - jnp.minimum(turn, 1)
        return self.first + turn

    def stored_rows(self, step, side):
        start = ((self.target(step) - self.first) * 2 + side) * self.pieces + step // self.turns
        return pl.ds(pl.multiple_of(start * self.rows, 16), self.rows)

    def slot(self, step):
        return pl.ds(pl.multiple_of(step * self.rows, 16), self.rows)

    def pair_copy(self, step):
        slot = self.slot(step)
        if self.stored:
            sent = self.stored[1].at[self.stored_rows(step, 1 - self.spot.side)]
            return remote(sent, self.pair_in.at[slot], self.p_send.at[step], self.p_recv.at[step], self.spot.pair)
        return remote(self.pair_out.at[slot], self.pair_in.at[slot], self.p_send.at[step], self.p_recv.at[step], self.spot.pair)

    def line_copy(self, step, to, recv):
        slot = self.slot(step)
        return remote(self.part.at[slot], self.line_in.at[slot], self.l_send.at[step], recv.at[step], to)

    def low_copy(self, step, to, recv):
        slot = self.slot(step)
        return remote(self.low_out.at[slot], self.low_in.at[slot], self.l_send.at[step], recv.at[step], to)

    def last_copy(self, step):
        here = pl.ds(pl.multiple_of(step // self.turns * self.rows, 16), self.rows)
        return remote(self.part.at[self.slot(step)], self.low_in.at[here], self.l_send.at[step], self.down_recv.at[step], self.spot.below)

    def own_copy(self, step):
        own = self.stored[0].at[self.stored_rows(step, self.spot.side)]
        return pltpu.make_async_copy(own, self.part.at[self.slot(step)], self.stored[2].at[step])

    def begin(self, step):
        if self.stored:
            self.pair_copy(step).start()
            self.own_copy(step).start()
            return
        self.pair_out[self.slot(step)] = self.source(self.target(step), 1 - self.spot.side, step // self.turns).astype(LOW)
        self.pair_copy(step).start()

    def add(self, step, low):
        slot = self.slot(step)
        self.part[slot] += self.low_in[slot].astype(WIDE) if low else self.line_in[slot]

    def low_hop(self, rising, target):
        line, last = self.spot.line, self.spot.lines - 1
        if rising:
            top = target == last
            return (line == 0) | ((line == 1) & top), (line == 1) | ((line == 2) & top)
        return line == last, line == last - 1

    def travel(self, step, rising):
        spot, slot = self.spot, self.slot(step)
        to, recv = (spot.above, self.up_recv) if rising else (spot.below, self.down_recv)
        last = spot.lines - 1
        at_end = spot.line == (0 if rising else last)
        target = self.target(step)
        if self.low:
            low_sent, low_taken = self.low_hop(rising, target)

            @pl.when(jnp.logical_not(at_end) & low_taken)
            def _():
                self.low_copy(step, to, recv).wait_recv()
                self.add(step, True)

            @pl.when(jnp.logical_not(at_end | low_taken))
            def _():
                self.line_copy(step, to, recv).wait_recv()
                self.add(step, False)

            @pl.when(low_sent)
            def _():
                self.low_out[slot] = self.part[slot].astype(LOW)
                self.low_copy(step, to, recv).start()

            @pl.when(jnp.logical_not(low_sent))
            def _():
                self.line_copy(step, to, recv).start()
        else:

            @pl.when(jnp.logical_not(at_end))
            def _():
                self.line_copy(step, to, recv).wait_recv()
                self.add(step, False)

            if rising:
                self.line_copy(step, to, recv).start()
            else:

                @pl.when(target == spot.line - 1)
                def _():
                    self.last_copy(step).start()

                @pl.when(target < spot.line - 1)
                def _():
                    self.line_copy(step, to, recv).start()

    def advance(self, step):
        spot = self.spot

        @pl.when(step < self.count)
        def _():
            slot = self.slot(step)
            self.pair_copy(step).wait_recv()
            if self.stored:
                self.own_copy(step).wait()
                self.part[slot] += self.pair_in[slot].astype(WIDE)
                return
            own = self.source(self.target(step), spot.side, step // self.turns)
            self.part[slot] = own + self.pair_in[slot].astype(WIDE)

        rising = step - spot.line

        @pl.when((rising >= 0) & (rising < self.count) & (self.target(rising) > spot.line))
        def _():
            self.travel(rising, True)

        falling = step - (spot.lines - 1 - spot.line)

        @pl.when((falling >= 0) & (falling < self.count) & (self.target(falling) < spot.line))
        def _():
            self.travel(falling, False)

    def close(self, step, give):
        spot, slot = self.spot, self.slot(step)
        target = self.target(step)
        last = spot.lines - 1
        self.pair_copy(step).wait_send()

        @pl.when(target > spot.line)
        def _():
            if self.low:

                low_sent, low_taken = self.low_hop(True, target)

                @pl.when(low_sent)
                def _():
                    self.low_copy(step, spot.above, self.up_recv).wait_send()

                @pl.when(jnp.logical_not(low_sent))
                def _():
                    self.line_copy(step, spot.above, self.up_recv).wait_send()
            else:
                self.line_copy(step, spot.above, self.up_recv).wait_send()

        @pl.when(target < spot.line)
        def _():
            if self.low:

                @pl.when(spot.line == last)
                def _():
                    self.low_copy(step, spot.below, self.down_recv).wait_send()

                @pl.when(spot.line < last)
                def _():
                    self.line_copy(step, spot.below, self.down_recv).wait_send()
            else:
                self.line_copy(step, spot.below, self.down_recv).wait_send()

        @pl.when(target == spot.line)
        def _():
            if self.low:

                @pl.when(spot.line == 1)
                def _():
                    self.low_copy(step, spot.above, self.up_recv).wait_recv()
                    self.add(step, True)

                @pl.when(spot.line > 1)
                def _():
                    self.line_copy(step, spot.above, self.up_recv).wait_recv()
                    self.add(step, False)

                @pl.when(spot.line == last - 1)
                def _():
                    self.low_copy(step, spot.below, self.down_recv).wait_recv()
                    self.add(step, True)

                @pl.when(spot.line < last - 1)
                def _():
                    self.line_copy(step, spot.below, self.down_recv).wait_recv()
                    self.add(step, False)
            else:

                @pl.when(spot.has_below)
                def _():
                    self.line_copy(step, spot.above, self.up_recv).wait_recv()
                    self.add(step, False)

                @pl.when(spot.has_above)
                def _():
                    self.last_copy(step).wait_recv()
                    here = pl.ds(pl.multiple_of(step // self.turns * self.rows, 16), self.rows)
                    self.part[slot] += self.low_in[here]

            give(step // self.turns, self.part[slot])


def attend_back_kernel(parts, q_rows, lines, count_ref, branch_ref, weight_ref, qkv_ref, log_ref, normed1_in, embed_ref,
                       resid_grad_ref, norm_ref, *rest):
    late_in, rest = (rest[:2], rest[2:]) if lines else ((), rest)
    grad_ref, embed_grad, gain_ref = rest[:3]
    own_late, rest = (rest[3], rest[4:]) if lines else (None, rest[3:])
    qkv_proj, attended_grad, qkv_grad, key_grad, value_grad, term, held, normed1_ref, load_sem = rest[:9]
    comm, late_comm = rest[9:17], rest[17:]
    loads = Moves(load_sem, (weight_ref.at[pl.ds(0, held.shape[0])], held), (normed1_in, normed1_ref))
    loads.start()
    corner = Corner()
    size, width = embed_ref.shape
    length, local = qkv_ref.shape[0], qkv_ref.shape[1] // 3
    if lines:
        spot = Lines(lines)
        barrier = pltpu.get_barrier_semaphore()
        for other in (corner.mate, corner.far):
            pl.semaphore_signal(barrier, inc=1, device_id={"tensor": other}, device_id_type=MESH)
        pl.semaphore_wait(barrier, 2 + spot.signal(barrier))
        late = LineSum(
            spot, SUM_PIECES, True, None, late_comm[:6], late_comm[6:11], 1, lines - 1, late_in + (late_comm[11],)
        )

        @pl.loop(0, late.count)
        def _(step):
            late.begin(step)

    else:
        corner.greet()
    scatter = Scatter(corner, PIECES, *comm)
    packed_ref, out_ref = held.at[pl.ds(0, 3 * local)], held.at[pl.ds(3 * local, local)]
    loads.wait(0)
    unpack_into(qkv_proj, packed_ref, parts)

    @pl.loop(0, 4)
    def _(block):
        here = rows_of(block, size)
        attended_grad[here] = dot(branch_ref[here], out_ref[...], NT).astype(LOW)

    key_grad[...] = jnp.zeros_like(key_grad)
    value_grad[...] = jnp.zeros_like(value_grad)
    valid = lax.broadcasted_iota(jnp.int32, (1, length), 1) < count_ref[0] * VTOK
    left = lax.broadcasted_iota(jnp.int32, (1, 2 * DH), 1) < DH
    factor = jnp.array(DH ** (-0.5), LOW)

    @pl.loop(0, length // q_rows)
    def _(turn):
        here = rows_of(turn, q_rows)
        for pair in range(local // (2 * DH)):
            lanes = slice(pair * 2 * DH, (pair + 1) * 2 * DH)
            queries = qkv_ref[here, lanes] * factor
            grads = attended_grad[here, lanes]
            keyset = qkv_ref[:, local + pair * 2 * DH : local + (pair + 1) * 2 * DH]
            values = qkv_ref[:, 2 * local + pair * 2 * DH : 2 * local + (pair + 1) * 2 * DH]
            found = []
            for side in range(2):
                mine = left if side == 0 else ~left
                own_query = jnp.where(mine, queries, jnp.zeros_like(queries))
                own_grad = jnp.where(mine, grads, jnp.zeros_like(grads))
                scores = jnp.where(valid, dot(own_query, keyset, NT), masked_score)
                probs = jnp.exp(scores - log_ref[here, pair * 2 + side : pair * 2 + side + 1])
                prob_grad = dot(own_grad, values, NT)
                value_grad[:, lanes] += dot(probs.astype(LOW), own_grad, TN)
                centre = jnp.sum(probs * prob_grad, -1, keepdims=True)
                score_grad = (probs * (prob_grad - centre)).astype(LOW)
                found.append(dot(score_grad, keyset))
                key_grad[:, lanes] += dot(score_grad, own_query, TN)
            qkv_grad[here, lanes] = (jnp.where(left, found[0], found[1]) * (DH ** (-0.5))).astype(LOW)
        if lines:

            @pl.loop(0, 2)
            def _(at):
                late.advance(2 * turn + at)

    qkv_grad[:, local : 2 * local] = key_grad[...].astype(LOW)
    qkv_grad[:, 2 * local :] = value_grad[...].astype(LOW)

    @pl.loop(0, 4)
    def _(step):
        here = rows_of(corner.block(step), size)

        def columns(cols):
            term[:, cols] = dot(qkv_grad[here], qkv_proj[cols, :], NT)

        column_loop(width, columns)
        scatter.step(step, term)
        if lines:
            late.advance(12 + step)

    loads.wait(1)
    for tile in range(width // TILE):
        value = dot(normed1_ref[:, tile * TILE : (tile + 1) * TILE], qkv_grad[...], TN)
        for row, rows, col, cols, at, at_col in qkv_places(parts, width, 3 * local):
            if at // TILE == tile:
                at = at % TILE
                grad_ref[row : row + rows, col : col + cols] = value[at : at + rows, at_col : at_col + cols]
    if lines:

        @pl.loop(16, 20)
        def _(step):
            late.advance(step)

    gain_sum, bias_sum = jnp.zeros((1, width), WIDE), jnp.zeros((1, width), WIDE)
    for piece in range(PIECES):
        part = scatter.part(piece)
        grad = scatter.land(piece, term)
        scaled, inverse = standard(embed_ref[part])
        embed_grad[part] = (resid_grad_ref[part] + norm_back(grad, scaled, inverse, norm_ref[0:1])).astype(LOW)
        gain_sum += jnp.sum(grad * scaled, 0, keepdims=True)
        bias_sum += jnp.sum(grad, 0, keepdims=True)
    gain_ref[0:1] = gain_sum
    gain_ref[1:2] = bias_sum
    scatter.close()
    if lines:

        @pl.loop(20, late.count + lines - 1)
        def _(step):
            late.advance(step)

        def keep_rows(piece, value):
            own_late[pl.ds(pl.multiple_of(piece * late.rows, 16), late.rows)] = value

        @pl.loop(0, late.count)
        def _(step):
            late.close(step, keep_rows)


def attend_back(count, branch, weights, qkv, log_total, normed1, embed, resid_grad, norm, late, parts, lines, collective_id):
    length, local = qkv.shape[0], qkv.shape[1] // 3
    size, width = embed.shape
    shape = jax.ShapeDtypeStruct
    chunk = 3 * width // (2 * lines) if lines else 0
    return pl.pallas_call(
        partial(attend_back_kernel, parts, 256, lines),
        out_shape=(
            shape((3 * local, width), WIDE),
            shape((size, width), LOW),
            shape((2, width), WIDE),
        )
        + ((shape((chunk, width), WIDE),) if lines else ()),
        in_specs=[pl.BlockSpec(memory_space=pltpu.SMEM), VMEM, HBM, VMEM, VMEM, HBM, VMEM, VMEM, VMEM] + [HBM] * len(late),
        out_specs=(VMEM,) * (4 if lines else 3),
        scratch_shapes=[
            pltpu.VMEM((width, 3 * local), LOW),
            pltpu.VMEM((length, local), LOW),
            pltpu.VMEM((length, 3 * local), LOW),
            pltpu.VMEM((length, local), WIDE),
            pltpu.VMEM((length, local), WIDE),
            pltpu.VMEM((size, width), WIDE),
            pltpu.VMEM((4 * local, width), LOW),
            pltpu.VMEM((length, width), LOW),
            pltpu.SemaphoreType.DMA((2,)),
        ]
        + Scatter.scratch(size, width, PIECES)
        + (
            LineSum.scratch(lines - 1, chunk, SUM_PIECES, width, True, True)
            + [pltpu.SemaphoreType.DMA(((lines - 1) * SUM_PIECES,))]
            if lines
            else []
        ),
        compiler_params=pltpu.CompilerParams(
            collective_id=collective_id, has_side_effects=True, vmem_limit_bytes=63 * 2**20
        ),
    )(count, branch, weights, qkv, log_total, normed1, embed, resid_grad, norm, *late)


SUM_PIECES = 6


def share_kernel(lines, early_ref, late_ref, embed_ref, own_patch_ref, used_ref, gain_ref, loss_ref, label_ref,
                 row_ref, shared_ref, total_ref,
                 term, windows, mine, slots, rows_out, patch_ref, *comm):
    corner, spot = Corner(), Lines(lines)
    pairs, width = 2 * lines, early_ref.shape[1]
    quarters = 4
    count = pairs * quarters
    me = spot.me * quarters + corner.me
    barrier = pltpu.get_barrier_semaphore()

    def peer(step):
        other = lax.rem(me + step, count)
        return {"dp": other // quarters, "tensor": lax.rem(other, quarters)}

    @pl.loop(1, count)
    def _(step):
        pl.semaphore_signal(barrier, inc=1, device_id=peer(step), device_id_type=MESH)

    pl.semaphore_wait(barrier, count - 1)
    chunk = late_ref.shape[0]
    rows = chunk // SUM_PIECES

    def weight_term(line, side, piece):
        return early_ref[pl.ds(pl.multiple_of(side * chunk + piece * rows, 8), rows)]

    def shared_term(line, side, piece):
        return mine[pl.ds(pl.multiple_of(window_row(line * 2 + side), 16), WINDOW)]

    weights = LineSum(spot, SUM_PIECES, True, weight_term, comm[0:6], comm[6:11], 0, 1)
    shared = LineSum(spot, 1, False, shared_term, comm[11:17], comm[17:22])
    scatter = Scatter(corner, PIECES, *comm[22:30])
    gather = Gather(corner, windows, 1, comm[30:36])
    own_sem, send_sem, recv_sem = comm[36:39]

    @pl.loop(0, weights.count)
    def _(step):
        weights.begin(step)

    patch_ref[...] = dot(own_patch_ref[...], embed_ref[...], TN)

    @pl.loop(0, 4)
    def _(step):
        block = corner.block(step)
        term[...] = jnp.zeros_like(term)

        def rows_at(start, size):
            return pl.ds(pl.multiple_of(start, 16), size)

        for owner in range(3):
            at = owner * WINDOW
            term[at : at + WINDOW] = patch_ref[rows_at(ROW_START[owner] + block * WINDOW, WINDOW)]

        @pl.when(block < 3)
        def _():
            at = 3 * WINDOW
            term[at : at + 16] = patch_ref[rows_at(ROW_START[3] + block * 32, 16)]

            @pl.when(block < 2)
            def _():
                term[at + 16 : at + 32] = patch_ref[rows_at(ROW_START[3] + block * 32 + 16, 16)]

            for j in range(3):
                term[at + 32 : at + 48, j * 128 : (j + 1) * 128] = used_ref[rows_at(block * 48 + 16 * j, 16)]

        for owner in range(4, 8):
            at = window_row(owner)
            for j in range(4):

                @pl.when((block < 3) | (owner < 7) | (j < 2))
                def _():
                    term[at : at + SHORT, j * 128 : (j + 1) * 128] = used_ref[
                        rows_at(USED_START[owner] + block * 64 + SHORT * j, SHORT)
                    ]

        @pl.when(block == 0)
        def _():
            for row in range(8):
                at = window_row(7) + row
                term[at : at + 1, width // 2 :] = gain_ref[row // 2 : row // 2 + 1, row % 2 * width // 2 : (row % 2 + 1) * width // 2]

        scatter.step(step, term)

    @pl.loop(0, 2)
    def _(step):
        weights.advance(step)

    for piece in range(PIECES):
        mine[scatter.part(piece)] = scatter.land(piece, term)

    @pl.loop(0, lines)
    def _(step):
        shared.begin(step)

    @pl.loop(0, 2 * lines - 1)
    def _(step):
        weights.advance(2 + step)
        shared.advance(step)

    def keep_window(piece, value):
        windows[gather.part(corner.me, 0)] = value

    @pl.loop(0, lines)
    def _(step):
        shared.close(step, keep_window)

    gather.start(0)

    def keep_rows(piece, value):
        rows_out[pl.ds(pl.multiple_of(piece * rows, rows), rows)] = value

    @pl.loop(0, weights.count)
    def _(step):
        weights.close(step, keep_rows)

    @pl.when(spot.line > 0)
    def _():
        rows_out[...] = late_ref[...]

    gather.relay(0)

    @pl.when(spot.me < lines // 2)
    def _():
        for row, height, col, cols, at, at_col in qkv_places(1, chunk * 4 // 3, width * 3 // 4):
            for j in range(cols // 128):
                row_ref[pl.ds(6 * at + at_col // 128 + j, height, 6)] = rows_out[
                    row : row + height, col + j * 128 : col + (j + 1) * 128
                ]

    @pl.when(spot.me >= lines // 2)
    def _():
        for j in range(8):
            row_ref[pl.ds(j, chunk, 8)] = rows_out[:, j * 128 : (j + 1) * 128]

    squares = jnp.sum(rows_out[...] * rows_out[...], 0, keepdims=True)
    gather.finish()
    shared_ref[...] = jnp.zeros_like(shared_ref)
    for phase in range(5):

        @pl.loop(0, 4)
        def _(quarter):
            def take(condition, row, height, j, start, stride):
                @pl.when(condition)
                def _():
                    here = pl.ds(pl.multiple_of(quarter * WINDOW + row, 16), height)
                    shared_ref[pl.ds(start, height, stride)] = windows[here, j * 128 : (j + 1) * 128]

            shared_walk(spot.me, quarter, take, (phase,))
    kept = shared_ref[FRONT : FRONT + PADDED - FRONT]
    place = lax.broadcasted_iota(jnp.int32, kept.shape, 0)
    kept = jnp.where((place < SHARED_LANES) & (corner.me == 0), kept, 0.0)
    square = jnp.sum(jnp.sum(squares, 1, keepdims=True)) + jnp.sum(kept * kept)
    counted = jnp.sum(jnp.where(label_ref[...] < 2, 1.0, 0.0))
    line = lax.broadcasted_iota(jnp.int32, total_ref.shape, 0)
    slots[me] = jnp.where(line == 0, square, jnp.where(line == 1, loss_ref[...], jnp.where(line == 2, counted, 0.0)))

    def send(step):
        return remote(slots.at[me], slots.at[me], send_sem.at[step], recv_sem.at[step], peer(step))

    def arrive(step):
        source = lax.rem(me - step + count, count)
        return remote(slots.at[source], slots.at[source], send_sem.at[step], recv_sem.at[step], peer(step))

    @pl.loop(1, count)
    def _(step):
        send(step).start()

    @pl.loop(1, count)
    def _(step):
        arrive(step).wait_recv()

    total_ref[...] = jnp.sum(slots[...], 0)

    @pl.loop(1, count)
    def _(step):
        send(step).wait_send()

    scatter.close()


def share(early, late, embed_grad, patches, used_grad, gains, loss_tile, labels, lines, collective_id):
    width = early.shape[1]
    chunk = late.shape[0]
    packed = 4 * WINDOW + (2 * lines - 4) * SHORT
    count = 8 * lines
    shape = jax.ShapeDtypeStruct
    return pl.pallas_call(
        partial(share_kernel, lines),
        out_shape=(shape((chunk * width // 128, 128), WIDE), shape((PADDED, 128), WIDE), shape((8, 128), WIDE)),
        in_specs=[VMEM] * 8,
        out_specs=(VMEM,) * 3,
        scratch_shapes=[
            pltpu.VMEM((packed, width), WIDE),
            pltpu.VMEM((4 * WINDOW, width), WIDE),
            pltpu.VMEM((packed + WINDOW - SHORT, width), WIDE),
            pltpu.VMEM((count, 8, 128), WIDE),
            pltpu.VMEM((chunk, width), WIDE),
            pltpu.VMEM((patches.shape[1], width), WIDE),
        ]
        + LineSum.scratch(1, chunk, SUM_PIECES, width, True)
        + LineSum.scratch(lines, WINDOW, 1, width, False)
        + Scatter.scratch(packed, width, PIECES)
        + Gather.scratch(1)
        + [
            pltpu.SemaphoreType.DMA(()),
            pltpu.SemaphoreType.DMA((count,)),
            pltpu.SemaphoreType.DMA((count,)),
        ],
        compiler_params=pltpu.CompilerParams(
            collective_id=collective_id, has_side_effects=True, vmem_limit_bytes=63 * 2**20
        ),
    )(early, late, embed_grad, patches, used_grad, gains, loss_tile, labels)


def render_kernel(area, wide, block, split, table_ref, splat_ref, dist_ref, label_ref, loss_ref, grad_ref, flip, picked, hot, spread_grad):
    tokens = table_ref.shape[0]
    groups = tokens // wide
    splats, pixels = splat_ref.shape
    for j in range(groups):
        flip[j * 2 * area : (j + 1) * 2 * area] = jnp.transpose(table_ref[j * wide : (j + 1) * wide].astype(jnp.float32)).astype(jnp.bfloat16)
    spread_grad[...] = jnp.zeros_like(spread_grad)
    wide_ids = lax.broadcasted_iota(jnp.int32, (wide, block), 0).astype(jnp.float32).astype(jnp.bfloat16)
    cell_ids = lax.broadcasted_iota(jnp.int32, (area, block), 0).astype(jnp.float32)
    cell_low = cell_ids.astype(jnp.bfloat16)
    one, nil = jnp.ones((wide, block), jnp.bfloat16), jnp.zeros((wide, block), jnp.bfloat16)

    def one_block(step, loss):
        here = pl.ds(pl.multiple_of(step * block, block), block)
        opacities, spreads, lows = [], [], []
        for k in range(splats):
            index = splat_ref[k : k + 1, here]
            token = index // area
            column = (token % wide).astype(jnp.float32).astype(jnp.bfloat16)
            group = (token // wide)
            cell = (index % area).astype(jnp.float32)
            match = jnp.where(wide_ids == column, one, nil)
            hot[k] = match
            picked[...] = lax.dot_general(flip[...], match, NN, preferred_element_type=jnp.float32)
            op_sum = jnp.zeros((area, block), jnp.float32)
            sp_sum = jnp.zeros((area, block), jnp.float32)
            for j in range(groups):
                same = cell_ids == jnp.where(group == j, cell, -1.0)
                op_sum += jnp.where(same, picked[j * 2 * area : j * 2 * area + area], 0.0)
                sp_sum += jnp.where(same, picked[j * 2 * area + area : (j + 1) * 2 * area], 0.0)
            opacities.append(jnp.sum(op_sum, 0, keepdims=True))
            spreads.append(jnp.sum(sp_sum, 0, keepdims=True))
            lows.append((group, cell))
        opacity, spread = jnp.concatenate(opacities, 0), jnp.concatenate(spreads, 0)
        distance = dist_ref[:, here].astype(jnp.float32)
        labels = label_ref[:, here]
        valid = jnp.where(labels < 2, 1.0, 0.0)
        target = jnp.where(labels == 1, 1.0, 0.0)
        op_sig, sp_sig = jax.nn.sigmoid(opacity), jax.nn.sigmoid(spread)
        fade = jnp.exp(-0.25 * distance * sp_sig)
        contrib = (0.02 + 0.96 * op_sig) * fade
        keep_log = jnp.sum(jnp.log1p(-contrib), 0, keepdims=True)
        keep = jnp.exp(keep_log)
        alpha = 1.0 - keep
        alpha_log = jnp.log(alpha)
        loss = loss - valid * (target * alpha_log + (1.0 - target) * keep_log)
        keep_grad = valid * (target * keep / alpha - (1.0 - target))
        contrib_grad = -keep_grad / (1.0 - contrib)
        op_grad = contrib_grad * (0.96 * op_sig * (1.0 - op_sig)) * fade
        sp_grad = contrib_grad * contrib * (-0.25 * distance * sp_sig * (1.0 - sp_sig))
        for k in range(splats):
            group, cell = lows[k]
            parts_op, parts_sp = op_grad[k : k + 1], sp_grad[k : k + 1]
            for part in range(split):
                low_op, low_sp = parts_op.astype(jnp.bfloat16), parts_sp.astype(jnp.bfloat16)
                parts_op, parts_sp = parts_op - low_op.astype(jnp.float32), parts_sp - low_sp.astype(jnp.float32)
                pieces = []
                for j in range(groups):
                    same = cell_low == jnp.where(group == j, cell, -1.0).astype(jnp.bfloat16)
                    pieces.append(jnp.where(same, low_op, jnp.bfloat16(0)))
                    pieces.append(jnp.where(same, low_sp, jnp.bfloat16(0)))
                weighted = jnp.concatenate(pieces, 0)
                spread_grad[...] += lax.dot_general(weighted, hot[k], NT, preferred_element_type=jnp.float32)
        return loss

    loss = lax.fori_loop(0, pixels // block, one_block, jnp.zeros((1, block), jnp.float32))
    loss_ref[...] = jnp.broadcast_to(jnp.sum(loss, 1, keepdims=True), loss_ref.shape)
    for j in range(groups):
        grad_ref[j * wide : (j + 1) * wide] = jnp.transpose(spread_grad[j * 2 * area : (j + 1) * 2 * area]).astype(grad_ref.dtype)

def render(table, splats, distance, labels, area, block=512, wide=256, split=2):
    tokens = table.shape[0]
    vm = pl.BlockSpec(memory_space=pltpu.VMEM)
    groups = tokens // wide
    return pl.pallas_call(
        partial(render_kernel, area, wide, block, split),
        out_shape=(jax.ShapeDtypeStruct((8, 128), jnp.float32), jax.ShapeDtypeStruct(table.shape, jnp.bfloat16)),
        in_specs=[vm] * 4, out_specs=(vm, vm),
        scratch_shapes=[pltpu.VMEM((groups * 2 * area, wide), jnp.bfloat16), pltpu.VMEM((groups * 2 * area, block), jnp.float32),
            pltpu.VMEM((splats.shape[0], wide, block), jnp.bfloat16), pltpu.VMEM((groups * 2 * area, wide), jnp.float32)],
        compiler_params=pltpu.CompilerParams(vmem_limit_bytes=48 * 2**20),
    )(table, splats, distance, labels)


def owner_sum_kernel(lines, pieces, g_ref, o_ref, pair_out, pair_in, part, line_in, own_in, p_send, p_recv, l_send, up_recv, down_recv):
    me = lax.axis_index("dp")
    line, side = me // 2, lax.rem(me, 2)
    chunk = o_ref.shape[0]
    rows = chunk // pieces
    count = lines * pieces
    pair = {"dp": line * 2 + 1 - side}
    above = {"dp": lax.rem(line + 1, lines) * 2 + side}
    below = {"dp": lax.rem(line + lines - 1, lines) * 2 + side}
    has_below, has_above = line > 0, line < lines - 1

    def target(step):
        turn = lax.rem(step, lines)
        odd = lax.rem(turn, 2)
        return (1 - odd) * (lines - 1 - turn // 2) + odd * (turn // 2)

    def slot(step):
        return pl.ds(pl.multiple_of(step * rows, rows), rows)

    def here(step):
        return pl.ds(pl.multiple_of(step // lines * rows, rows), rows)

    def source(step, owner):
        return pl.ds(pl.multiple_of((target(step) * 2 + owner) * chunk + step // lines * rows, rows), rows)

    def copy(src, dst, send, recv, to):
        return pltpu.make_async_remote_copy(
            src_ref=src, dst_ref=dst, send_sem=send, recv_sem=recv, device_id=to, device_id_type=MESH
        )

    def pair_copy(step):
        return copy(pair_out.at[slot(step)], pair_in.at[slot(step)], p_send.at[step], p_recv.at[step], pair)

    def line_copy(step, to, recv):
        return copy(part.at[slot(step)], line_in.at[slot(step)], l_send.at[step], recv.at[step], to)

    def last_copy(step):
        return copy(part.at[slot(step)], own_in.at[here(step)], l_send.at[step], down_recv.at[step], below)

    barrier = pltpu.get_barrier_semaphore()
    pl.semaphore_signal(barrier, inc=1, device_id=pair, device_id_type=MESH)

    @pl.when(has_below)
    def _():
        pl.semaphore_signal(barrier, inc=1, device_id=below, device_id_type=MESH)

    @pl.when(has_above)
    def _():
        pl.semaphore_signal(barrier, inc=1, device_id=above, device_id_type=MESH)

    pl.semaphore_wait(barrier, 1 + jnp.minimum(line, 1) + jnp.minimum(lines - 1 - line, 1))

    @pl.loop(0, count)
    def _(step):
        pair_out[slot(step)] = g_ref[source(step, 1 - side)].astype(jnp.bfloat16)
        pair_copy(step).start()

    @pl.loop(0, count + lines - 1)
    def _(step):
        @pl.when(step < count)
        def _():
            pair_copy(step).wait_recv()
            part[slot(step)] = g_ref[source(step, side)].astype(jnp.float32) + pair_in[slot(step)].astype(jnp.float32)

        rising = step - line

        @pl.when((rising >= 0) & (rising < count) & (target(rising) > line))
        def _():
            @pl.when(has_below)
            def _():
                line_copy(rising, above, up_recv).wait_recv()
                part[slot(rising)] += line_in[slot(rising)]

            line_copy(rising, above, up_recv).start()

        falling = step - (lines - 1 - line)

        @pl.when((falling >= 0) & (falling < count) & (target(falling) < line))
        def _():
            @pl.when(has_above)
            def _():
                line_copy(falling, below, down_recv).wait_recv()
                part[slot(falling)] += line_in[slot(falling)]

            @pl.when(target(falling) == line - 1)
            def _():
                last_copy(falling).start()

            @pl.when(target(falling) < line - 1)
            def _():
                line_copy(falling, below, down_recv).start()

    @pl.loop(0, count)
    def _(step):
        pair_copy(step).wait_send()

        @pl.when(target(step) > line)
        def _():
            line_copy(step, above, up_recv).wait_send()

        @pl.when(target(step) < line)
        def _():
            line_copy(step, below, down_recv).wait_send()

        @pl.when(target(step) == line)
        def _():
            o_ref[here(step)] = part[slot(step)]

            @pl.when(has_below)
            def _():
                line_copy(step, above, up_recv).wait_recv()
                o_ref[here(step)] += line_in[slot(step)]

            @pl.when(has_above)
            def _():
                last_copy(step).wait_recv()
                o_ref[here(step)] += own_in[here(step)]


def owner_sum(grad, count_dp, collective_id, pieces):
    lines = count_dp // 2
    total, width = grad.shape
    chunk = total // count_dp
    half = (lines * chunk, width)
    vmem = pl.BlockSpec(memory_space=pltpu.VMEM)
    return pl.pallas_call(
        partial(owner_sum_kernel, lines, pieces),
        out_shape=jax.ShapeDtypeStruct((chunk, width), jnp.float32),
        in_specs=[vmem],
        out_specs=vmem,
        scratch_shapes=[
            pltpu.VMEM(half, jnp.bfloat16),
            pltpu.VMEM(half, jnp.bfloat16),
            pltpu.VMEM(half, jnp.float32),
            pltpu.VMEM(half, jnp.float32),
            pltpu.VMEM((chunk, width), jnp.float32),
        ]
        + [pltpu.SemaphoreType.DMA((lines * pieces,))] * 5,
        compiler_params=pltpu.CompilerParams(
            collective_id=collective_id, has_side_effects=True, vmem_limit_bytes=62 * 2**20
        ),
    )(grad)


def total_kernel(mine_ref, sum_ref, slots, own_sem, send_sem, recv_sem):
    first, second = lax.axis_size("dp"), lax.axis_size("tensor")
    count = first * second
    me = lax.axis_index("dp") * second + lax.axis_index("tensor")

    def peer(step):
        other = lax.rem(me + step, count)
        return {"dp": other // second, "tensor": lax.rem(other, second)}

    barrier = pltpu.get_barrier_semaphore()

    @pl.loop(1, count)
    def _(step):
        pl.semaphore_signal(barrier, inc=1, device_id=peer(step), device_id_type=MESH)

    pl.semaphore_wait(barrier, count - 1)
    own = pltpu.make_async_copy(mine_ref, slots.at[me], own_sem)
    own.start()

    def send(step):
        return pltpu.make_async_remote_copy(
            src_ref=mine_ref,
            dst_ref=slots.at[me],
            send_sem=send_sem.at[step],
            recv_sem=recv_sem.at[step],
            device_id=peer(step),
            device_id_type=MESH,
        )

    @pl.loop(1, count)
    def _(step):
        send(step).start()

    @pl.loop(1, count)
    def _(step):
        send(step).wait()

    own.wait()
    sum_ref[...] = jnp.sum(slots[...], 0)


def total_over_all(mine, collective_id):
    count = lax.axis_size("dp") * lax.axis_size("tensor")
    vmem = pl.BlockSpec(memory_space=pltpu.VMEM)
    return pl.pallas_call(
        total_kernel,
        out_shape=jax.ShapeDtypeStruct(mine.shape, jnp.float32),
        in_specs=[vmem],
        out_specs=vmem,
        scratch_shapes=[
            pltpu.VMEM((count,) + mine.shape, jnp.float32),
            pltpu.SemaphoreType.DMA(()),
            pltpu.SemaphoreType.DMA((count,)),
            pltpu.SemaphoreType.DMA((count,)),
        ],
        compiler_params=pltpu.CompilerParams(collective_id=collective_id, has_side_effects=True),
    )(mine)


def pack_qkv(matrix, parts):
    rows, cols = matrix.shape
    first = matrix[:, :512].reshape(parts, 2, rows // parts // 2, 512).transpose(0, 2, 1, 3)
    second = matrix[:, 512:].reshape(parts, 4, rows // parts // 4, 256).transpose(0, 2, 1, 3)
    return jnp.concatenate([first.reshape(parts, -1, 1024), second.reshape(parts, -1, 1024)], 1).reshape(-1, 1024)


def unpack_qkv(packed, parts):
    rows = packed.shape[0] // parts
    packed = packed.reshape(parts, rows, 1024)
    cut = rows * 2 // 3
    first = packed[:, :cut].reshape(parts, cut, 2, 512).transpose(0, 2, 1, 3).reshape(-1, 512)
    second = packed[:, cut:].reshape(parts, rows - cut, 4, 256).transpose(0, 2, 1, 3).reshape(-1, 256)
    return jnp.concatenate([first, second], 1)


def by_lanes(flat, outer):
    size = flat.size // math.prod(outer)
    return flat.reshape(outer + ((size // 128, 128) if size % 128 == 0 else (size,)))


def pad_first(array, axis, unit):
    short = -array.shape[axis] % unit
    return jnp.pad(array, [(0, short if at == axis else 0) for at in range(array.ndim)])


def sum_to_owners(stack, count_dp):
    if count_dp == 8:
        return owner_sum(stack, count_dp, 1, 9)
    return lax.psum_scatter(stack, "dp", scatter_dimension=0, tiled=True)

def adam_update(master, first_mom, second_mom, gradient, step_float):
    first_new = beta_one * first_mom + (1.0 - beta_one) * gradient
    second_new = beta_two * second_mom + (1.0 - beta_two) * gradient * gradient
    first_hat = first_new / (1.0 - jnp.power(beta_one, step_float))
    second_hat = second_new / (1.0 - jnp.power(beta_two, step_float))
    master_new = master - learn_rate * (
        first_hat / (jnp.sqrt(second_hat) + adam_eps) + decay_rate * master
    )
    return (master_new, first_new, second_new)


def adam_kernel(total_ref, count_ref, *refs):
    norm_value = jnp.sqrt(total_ref[0, 0:1]) / total_ref[2, 0:1]
    factor = clip_norm / jnp.maximum(norm_value, clip_norm) / total_ref[2, 0:1]
    step_float = jnp.full((1, 1), count_ref[0], jnp.int32).astype(WIDE)
    grad, master, first, second, ema = (ref[...] for ref in refs[:5])
    new, first_new, second_new = adam_update(master, first, second, grad * factor.reshape(1, 1), step_float)
    for ref, value in zip(refs[5:], (new, first_new, second_new, ema_rate * ema + (1.0 - ema_rate) * new, new.astype(LOW))):
        ref[...] = value


def adam(totals, step_count, grad, master, first, second, ema, block):
    size = master.shape[1]
    spec = pl.BlockSpec((1, block), lambda at: (0, at))
    return pl.pallas_call(
        adam_kernel,
        grid=(size // block,),
        out_shape=tuple(jax.ShapeDtypeStruct(master.shape, kind) for kind in (WIDE,) * 4 + (LOW,)),
        in_specs=[pl.BlockSpec((8, 128), lambda at: (0, 0)), pl.BlockSpec(memory_space=pltpu.SMEM)] + [spec] * 5,
        out_specs=(spec,) * 5,
    )(totals, step_count, grad, master, first, second, ema)


def per_device(
    patches,
    view_counts,
    splat_index,
    splat_dist,
    alpha_label,
    step_count,
    row_master,
    row_first,
    row_second,
    row_ema,
    shared_master,
    shared_first,
    shared_second,
    shared_ema,
):
    groups = lax.axis_size("tensor")
    my_dp = lax.axis_index("dp")
    count_dp = lax.axis_size("dp")
    local_width = D // groups
    qkv_parts = count_dp // 4
    share_rows = row_master.shape[1] // D
    own_patches = patches[0]
    if count_dp == 8:
        shared_lanes = jnp.pad(
            shared_master.reshape(SHARED_LANES, 128), ((FRONT, PADDED - FRONT - SHARED_LANES), (0, 0))
        )
        weights, used_cols, norm, embed, normed1, qkv, attended, log_total, resid1, normed2 = forward(
            view_counts, row_master.reshape(-1, 128), shared_lanes, own_patches, count_dp // 2, 7
        )
    else:
        own_row = row_master[0].astype(jnp.bfloat16)
        own_tiles = jnp.where(
            my_dp < qkv_parts,
            pack_qkv(own_row.reshape(-1, 3 * local_width), 1),
            own_row.reshape(share_rows, D),
        )
        weights = lax.all_gather(own_tiles, "dp", axis=0, tiled=True)
        own_flat = shared_master.astype(jnp.bfloat16)
        own_shared = by_lanes(own_flat, ())
        lead = own_shared.shape[0]
        own_shared = pad_first(own_shared, 0, 2048 // own_shared[0].size)
        shared_weights = lax.all_gather(own_shared, "dp", axis=0, tiled=False)[:, :lead].reshape(-1, 128)
        patch_rows = PIN * D // 128
        unpatch_rows = D * POUT // 128
        norm = shared_weights[patch_rows + unpatch_rows :].reshape(4, D).astype(jnp.float32)
        patch_proj = shared_weights[:patch_rows].reshape(PIN, D)
        used_cols = shared_weights[patch_rows : patch_rows + unpatch_rows].reshape(D, POUT // 128, 128)[:, 0]
        all_patches = lax.all_gather(own_patches, "tensor", axis=0, tiled=True)
        embed, normed1, qkv, attended, log_total, resid1, normed2 = attend(
            view_counts, all_patches, patch_proj, norm, weights, qkv_parts, 3
        )
    hidden, active, resid2_low, gauss_table = mlp(normed2, weights, resid1, used_cols, 4)
    loss_tile, table_grad = render(gauss_table, splat_index[0], splat_dist[0], alpha_label, PATCH * PATCH)
    loss_part = loss_tile[0, 0]
    unpatch_used, late_grad, late_low, resid_grad, branch, gain2_grad = mlp_back(
        table_grad, used_cols, resid2_low, active, hidden, normed2, weights, resid1, norm, attended, share_rows if count_dp == 8 else None, 5
    )
    early_grad, embed_grad, gain1_grad, *own_late = attend_back(
        view_counts,
        branch,
        weights,
        qkv,
        log_total,
        normed1,
        embed,
        resid_grad,
        norm,
        (late_grad, late_low) if count_dp == 8 else (),
        qkv_parts,
        count_dp // 2 if count_dp == 8 else 0,
        6,
    )
    gain_grad = jnp.concatenate([gain1_grad, gain2_grad], 0)
    if count_dp == 8:
        gains = jnp.pad(gain_grad, ((0, 4), (0, 0)))
        row_lanes, shared_kept, totals = share(
            early_grad, own_late[0], embed_grad, own_patches, unpatch_used, gains, loss_tile, alpha_label, count_dp // 2, 8
        )
        row_share = row_lanes.reshape(-1)
        shared_share = shared_kept[FRONT : FRONT + SHARED_LANES].reshape(-1)
    else:
        patch_grad = dot(own_patches, embed_grad, TN)
        unpatch_grad = jnp.concatenate(
            [unpatch_used, jnp.zeros((D, POUT - unpatch_used.shape[1]), jnp.float32)], 1
        )
        shared_grad = jnp.concatenate(
            [patch_grad.reshape(-1), unpatch_grad.reshape(-1), gain_grad.reshape(-1)]
        )
        split_grad = by_lanes(shared_grad, (count_dp, groups))
        lead = split_grad.shape[2]
        shared_stack = pad_first(split_grad, 2, 16 * D // split_grad[0, 0, 0].size).swapaxes(0, 1)
        shared_sum = lax.psum_scatter(shared_stack, "tensor", scatter_dimension=0, tiled=True)
        row_stack = jnp.concatenate([early_grad, late_grad], 0)
        stack = jnp.concatenate(
            [row_stack.reshape(count_dp, share_rows, D), shared_sum.reshape(count_dp, -1, D)], 1
        ).reshape(-1, D)
        own_share = sum_to_owners(stack, count_dp)
        own_rows = own_share[:share_rows]
        row_share = jnp.where(my_dp < qkv_parts, unpack_qkv(own_rows, 1).reshape(-1), own_rows.reshape(-1))
        shared_part = own_share[share_rows:].reshape((-1,) + split_grad.shape[3:])[:lead]
        shared_share = lax.all_gather(shared_part, "tensor", axis=0, tiled=False).reshape(-1)
        own_squares = jnp.sum(row_share * row_share) + jnp.sum(shared_part * shared_part)
        pixel_part = jnp.sum((alpha_label < 2).astype(jnp.float32))
        scalars = jnp.stack([own_squares, loss_part, pixel_part]).reshape(3, 1)
        totals = total_over_all(jnp.pad(jnp.broadcast_to(scalars, (3, 128)), ((0, 5), (0, 0))), 2)
    square_total, loss_total, pixel_total = totals[0, 0], totals[1, 0], totals[2, 0]
    norm_value = jnp.sqrt(square_total) / pixel_total
    factor = clip_norm / jnp.maximum(norm_value, clip_norm) / pixel_total
    step_float = step_count[0].astype(jnp.float32)
    row_new, row_first_new, row_second_new, row_ema_new, row_copy = adam(
        totals, step_count, row_share[None], row_master, row_first, row_second, row_ema, row_master.shape[1] // 6
    )
    shared_new, shared_first_new, shared_second_new = adam_update(
        shared_master, shared_first, shared_second, shared_share * factor, step_float
    )
    shared_ema_new = ema_rate * shared_ema + (1.0 - ema_rate) * shared_new
    return (
        norm_value.reshape(1),
        (loss_total / pixel_total).reshape(1),
        row_new,
        row_first_new,
        row_second_new,
        row_ema_new,
        row_copy,
        shared_new,
        shared_first_new,
        shared_second_new,
        shared_ema_new,
        shared_new.astype(jnp.bfloat16),
    )


def solution(mesh):
    placed = (
        P("dp", "tensor", None),
        P("dp"),
        P("dp", None, "tensor"),
        P("dp", None, "tensor"),
        P("dp", "tensor"),
        P(),
        P("tensor", "dp"),
        P("tensor", "dp"),
        P("tensor", "dp"),
        P("tensor", "dp"),
        P("dp"),
        P("dp"),
        P("dp"),
        P("dp"),
    )
    return jax.shard_map(
        per_device,
        mesh=mesh,
        in_specs=placed,
        out_specs=(
            P(),
            P(),
            P("tensor", "dp"),
            P("tensor", "dp"),
            P("tensor", "dp"),
            P("tensor", "dp"),
            P("tensor", "dp"),
            P("dp"),
            P("dp"),
            P("dp"),
            P("dp"),
            P("dp"),
        ),
        check_vma=False,
    )
```

```python
import math
from functools import partial

import jax
import jax.numpy as jnp
from jax import lax
from jax.experimental import pallas as pl
from jax.experimental.pallas import tpu as pltpu
from jax.sharding import PartitionSpec as P

D = 1024
DH = 64
FF = 4096
PATCH = 8
VTOK = 192
PIN = 576
POUT = 768
VMEM = pl.BlockSpec(memory_space=pltpu.VMEM)
HBM = pl.BlockSpec(memory_space=pl.ANY)
ROOT_HALF = 0.5**0.5
NORMAL_PEAK = (2.0 * math.pi) ** -0.5


clip_norm = 0.005
beta_one = 0.9
beta_two = 0.95
adam_eps = 1e-08
decay_rate = 0.05
learn_rate = 0.03
ema_rate = 0.9
norm_eps = 1e-05
masked_score = -1e30


MESH = pl.DeviceIdType.MESH
NN = (((1,), (0,)), ((), ()))
NT = (((1,), (1,)), ((), ()))
TN = (((0,), (0,)), ((), ()))
LOW = jnp.bfloat16
WIDE = jnp.float32
PIECES = 4
TILE = 256
UNIT = 128


def dot(left, right, dims=NN):
    return lax.dot_general(left, right, dims, preferred_element_type=WIDE)


def remote(src, dst, send, recv, to):
    return pltpu.make_async_remote_copy(
        src_ref=src, dst_ref=dst, send_sem=send, recv_sem=recv, device_id=to, device_id_type=MESH
    )


class Corner:
    def __init__(self):
        self.me = lax.axis_index("tensor")
        self.first, self.last = self.me // 2, lax.rem(self.me, 2)
        self.mate = self.first * 2 + 1 - self.last
        self.far = (1 - self.first) * 2 + self.last
        self.opposite = (1 - self.first) * 2 + 1 - self.last

    def block(self, step):
        return lax.rem(self.first + 1 - step // 2, 2) * 2 + lax.rem(self.last + 1 - lax.rem(step, 2), 2)

    def greet(self):
        barrier = pltpu.get_barrier_semaphore()
        for other in (self.mate, self.far):
            pl.semaphore_signal(barrier, inc=1, device_id={"tensor": other}, device_id_type=MESH)
        pl.semaphore_wait(barrier, 2)


class Gather:
    def __init__(self, corner, ref, pieces, sems, short=None):
        self.corner, self.ref, self.pieces, self.sems, self.short = corner, ref, pieces, sems, short
        self.size = ref.shape[0] // 4
        self.rows = self.size // pieces

    @staticmethod
    def scratch(pieces):
        return [pltpu.SemaphoreType.DMA((pieces,))] * 6

    def part(self, owner, piece, rows=None):
        return pl.ds(pl.multiple_of(owner * self.size + piece * self.rows, self.rows), rows or self.rows)

    def run(self, act, owner, piece, kind, to):
        def go(rows):
            here = self.ref.at[self.part(owner, piece, rows)]
            sems = self.sems[2 * kind].at[piece], self.sems[2 * kind + 1].at[piece]
            getattr(remote(here, here, *sems, {"tensor": to}), act)()

        by_half(self.short, piece < self.pieces // 2, self.rows, go)

    def start(self, piece):
        self.run("start", self.corner.me, piece, 1, self.corner.far)
        self.run("start", self.corner.me, piece, 0, self.corner.mate)

    def relay(self, piece):
        self.run("wait_recv", self.corner.far, piece, 1, self.corner.far)
        self.run("start", self.corner.far, piece, 2, self.corner.mate)

    def finish(self):
        corner = self.corner
        for piece in range(self.pieces):
            self.run("wait_recv", corner.mate, piece, 0, corner.mate)
            self.run("wait_recv", corner.opposite, piece, 2, corner.mate)
            self.run("wait_send", corner.me, piece, 0, corner.mate)
            self.run("wait_send", corner.me, piece, 1, corner.far)
            self.run("wait_send", corner.far, piece, 2, corner.mate)


def by_half(short, first, rows, go):
    if short is None:
        go(rows)
    elif isinstance(first, bool):
        go(rows if first else short)
    else:
        pl.when(first)(lambda: go(rows))
        pl.when(jnp.logical_not(first))(lambda: go(short))


class Scatter:
    def __init__(self, corner, pieces, mate_out, mate_in, far_out, far_in, mate_send, mate_recv, far_send, far_recv):
        self.corner, self.pieces = corner, pieces
        self.mate_out, self.mate_in, self.far_out, self.far_in = mate_out, mate_in, far_out, far_in
        self.sems = mate_send, mate_recv, far_send, far_recv
        self.rows = far_out.shape[0] // pieces

    @staticmethod
    def scratch(rows, width, pieces):
        return [
            pltpu.VMEM((2, rows, width), LOW),
            pltpu.VMEM((2, rows, width), LOW),
            pltpu.VMEM((rows, width), LOW),
            pltpu.VMEM((rows, width), LOW),
            pltpu.SemaphoreType.DMA((2, pieces)),
            pltpu.SemaphoreType.DMA((2, pieces)),
            pltpu.SemaphoreType.DMA((pieces,)),
            pltpu.SemaphoreType.DMA((pieces,)),
        ]

    def part(self, piece):
        return pl.ds(piece * self.rows, self.rows)

    def mate_copy(self, half, piece):
        part = self.part(piece)
        return remote(
            self.mate_out.at[half, part],
            self.mate_in.at[half, part],
            self.sems[0].at[half, piece],
            self.sems[1].at[half, piece],
            {"tensor": self.corner.mate},
        )

    def far_copy(self, piece):
        part = self.part(piece)
        return remote(
            self.far_out.at[part],
            self.far_in.at[part],
            self.sems[2].at[piece],
            self.sems[3].at[piece],
            {"tensor": self.corner.far},
        )

    def give(self, half, ref):
        for piece in range(self.pieces):
            part = self.part(piece)
            self.mate_out[half, part] = ref[part].astype(LOW)
            self.mate_copy(half, piece).start()

    def cross(self, ref):
        for piece in range(self.pieces):
            part = self.part(piece)
            self.mate_copy(0, piece).wait_recv()
            self.far_out[part] = (ref[part] + self.mate_in[0, part].astype(WIDE)).astype(LOW)
            self.far_copy(piece).start()

    def step(self, step, ref):
        @pl.when(step == 0)
        def _():
            self.give(0, ref)

        @pl.when(step == 1)
        def _():
            self.cross(ref)

        @pl.when(step == 2)
        def _():
            self.give(1, ref)

    def land(self, piece, ref):
        part = self.part(piece)
        self.mate_copy(1, piece).wait_recv()
        self.far_copy(piece).wait_recv()
        return ref[part] + self.mate_in[1, part].astype(WIDE) + self.far_in[part].astype(WIDE)

    def close(self):
        for piece in range(self.pieces):
            self.mate_copy(0, piece).wait_send()
            self.mate_copy(1, piece).wait_send()
            self.far_copy(piece).wait_send()


def standard(values):
    centre = values - jnp.mean(values, -1, keepdims=True)
    inverse = lax.rsqrt(jnp.mean(centre * centre, -1, keepdims=True) + norm_eps)
    return centre * inverse, inverse


def norm_back(grad_out, scaled, inverse, gain):
    grad_scaled = grad_out * gain
    return inverse * (
        grad_scaled
        - jnp.mean(grad_scaled, -1, keepdims=True)
        - scaled * jnp.mean(grad_scaled * scaled, -1, keepdims=True)
    )


def qkv_places(parts, rows, columns):
    share = rows // parts
    wide = columns * 2 // 3
    packed = share * columns // 1024
    for at in range(parts):
        for j in range(2):
            half = share // 2
            yield (at * packed, half, j * wide, wide, at * share + j * half, 0)
        for j in range(4):
            quarter = share // 4
            yield (at * packed + share // 2, quarter, j * (columns - wide), columns - wide, at * share + j * quarter, wide)


def unpack_into(full, packed, parts):
    for row, rows, col, cols, to_row, to_col in qkv_places(parts, full.shape[0], full.shape[1]):
        full[to_row : to_row + rows, to_col : to_col + cols] = packed[row : row + rows, col : col + cols]


def pack_from(packed, full, parts, base=0):
    for row, rows, col, cols, to_row, to_col in qkv_places(parts, full.shape[0], full.shape[1]):
        packed[base + row : base + row + rows, col : col + cols] = full[to_row : to_row + rows, to_col : to_col + cols]


def rows_of(block, size):
    return pl.ds(pl.multiple_of(block * size, size), size)


def column_loop(width, body):
    @pl.loop(0, width // TILE)
    def _(tile):
        body(pl.ds(pl.multiple_of(tile * TILE, TILE), TILE))


def attend_kernel(parts, q_rows, count_ref, patch_ref, proj_ref, norm_ref, weight_ref, *rest):
    corner = Corner()
    corner.greet()
    attend_body(parts, q_rows, corner, None, count_ref, patch_ref, proj_ref, norm_ref, weight_ref, *rest)


def attend_body(parts, q_rows, corner, progress, count_ref, patch_ref, proj_ref, norm_ref, weight_ref,
                embed_ref, normed1_ref, qkv_ref, attended_ref, log_ref, resid_ref, normed2_ref,
                qkv_proj, term, held, held_sem, *comm):
    progress = progress or (lambda *_: None)
    scatter = Scatter(corner, PIECES, *comm[:8])
    gather = Gather(corner, normed2_ref, PIECES, comm[8:])
    packed_rows = held.shape[0] * 3 // 4
    packed_ref, out_ref = held.at[pl.ds(0, packed_rows)], held.at[pl.ds(packed_rows, held.shape[0] - packed_rows)]

    def hold(start, target, at):
        copy = pltpu.make_async_copy(weight_ref.at[pl.ds(start, target.shape[0])], target, held_sem.at[at])
        copy.start()
        copy.wait()

    size, width = embed_ref.shape
    length = patch_ref.shape[0]
    local = attended_ref.shape[1]

    @pl.loop(0, 4)
    def _(block):
        here = rows_of(block, size)
        column_loop(width, lambda cols: term.__setitem__((slice(None), cols), dot(patch_ref[here], proj_ref[:, cols])))

        @pl.when(block == corner.me)
        def _():
            embed_ref[...] = term[...]

        scaled, inverse = standard(term[...])
        normed1_ref[here] = (scaled * norm_ref[0:1] + norm_ref[1:2]).astype(LOW)
        progress("embed", block)

    progress("weights")
    hold(0, packed_ref, 0)
    unpack_into(qkv_proj, packed_ref, parts)

    @pl.loop(0, 4)
    def _(block):
        here = rows_of(block, size)

        def columns(cols):
            qkv_ref[here, cols] = dot(normed1_ref[here], qkv_proj[:, cols]).astype(LOW)

        column_loop(3 * local, columns)

    valid = lax.broadcasted_iota(jnp.int32, (1, length), 1) < count_ref[0] * VTOK
    left = lax.broadcasted_iota(jnp.int32, (1, 2 * DH), 1) < DH
    factor = jnp.array(DH ** (-0.5), LOW)

    @pl.loop(0, length // q_rows)
    def _(turn):
        here = rows_of(turn, q_rows)
        for pair in range(local // (2 * DH)):
            lanes = slice(pair * 2 * DH, (pair + 1) * 2 * DH)
            queries = qkv_ref[here, lanes] * factor
            keyset = qkv_ref[:, local + pair * 2 * DH : local + (pair + 1) * 2 * DH]
            values = qkv_ref[:, 2 * local + pair * 2 * DH : 2 * local + (pair + 1) * 2 * DH]
            found = []
            for side in range(2):
                mine = left if side == 0 else ~left
                scores = dot(jnp.where(mine, queries, jnp.zeros_like(queries)), keyset, NT)
                scores = jnp.where(valid, scores, masked_score)
                top = jnp.max(scores, -1, keepdims=True)
                powers = jnp.exp(scores - top)
                total = jnp.sum(powers, -1, keepdims=True)
                log_ref[here, pair * 2 + side : pair * 2 + side + 1] = top + jnp.log(total)
                found.append(dot((powers * (1.0 / total)).astype(LOW), values))
            attended_ref[here, lanes] = jnp.where(left, found[0], found[1]).astype(LOW)
        progress("turn", turn)

    progress("out")
    hold(packed_rows, out_ref, 1)

    @pl.loop(0, 4)
    def _(step):
        here = rows_of(corner.block(step), size)
        column_loop(width, lambda cols: term.__setitem__((slice(None), cols), dot(attended_ref[here], out_ref[:, cols])))
        scatter.step(step, term)
        progress("give", step)

    for piece in range(PIECES):
        part = scatter.part(piece)
        resid = embed_ref[part] + scatter.land(piece, term)
        resid_ref[part] = resid
        scaled, inverse = standard(resid)
        normed2_ref[gather.part(corner.me, piece)] = (scaled * norm_ref[2:3] + norm_ref[3:4]).astype(LOW)
        gather.start(piece)
        progress("land", piece)
    for piece in range(PIECES):
        gather.relay(piece)
    gather.finish()
    scatter.close()


def attend(count, patches, patch_proj, norm, weights, parts, collective_id):
    length, size = patches.shape[0], patches.shape[0] // 4
    width, local = patch_proj.shape[1], patch_proj.shape[1] // 4
    shape = jax.ShapeDtypeStruct
    return pl.pallas_call(
        partial(attend_kernel, parts, 256),
        out_shape=(
            shape((size, width), WIDE),
            shape((length, width), LOW),
            shape((length, 3 * local), LOW),
            shape((length, local), LOW),
            shape((length, local // DH), WIDE),
            shape((size, width), WIDE),
            shape((length, width), LOW),
        ),
        in_specs=[pl.BlockSpec(memory_space=pltpu.SMEM)] + [VMEM] * 3 + [HBM],
        out_specs=(VMEM,) * 7,
        scratch_shapes=[
            pltpu.VMEM((width, 3 * local), LOW),
            pltpu.VMEM((size, width), WIDE),
            pltpu.VMEM((4 * local, width), LOW),
            pltpu.SemaphoreType.DMA((2,)),
        ]
        + Scatter.scratch(size, width, PIECES)
        + Gather.scratch(PIECES),
        compiler_params=pltpu.CompilerParams(
            collective_id=collective_id, has_side_effects=True, vmem_limit_bytes=62 * 2**20
        ),
    )(count, patches, patch_proj, norm, weights)


class Lines:
    def __init__(self, lines):
        self.lines = lines
        self.me = lax.axis_index("dp")
        self.line, self.side = self.me // 2, lax.rem(self.me, 2)
        self.pair = {"dp": self.line * 2 + 1 - self.side}
        self.above = {"dp": lax.rem(self.line + 1, lines) * 2 + self.side}
        self.below = {"dp": lax.rem(self.line + lines - 1, lines) * 2 + self.side}
        self.has_below, self.has_above = self.line > 0, self.line < lines - 1

    def signal(self, barrier):
        pl.semaphore_signal(barrier, inc=1, device_id=self.pair, device_id_type=MESH)

        @pl.when(self.has_below)
        def _():
            pl.semaphore_signal(barrier, inc=1, device_id=self.below, device_id_type=MESH)

        @pl.when(self.has_above)
        def _():
            pl.semaphore_signal(barrier, inc=1, device_id=self.above, device_id_type=MESH)

        return 1 + jnp.minimum(self.line, 1) + jnp.minimum(self.lines - 1 - self.line, 1)


class LineGather:
    def __init__(self, spot, ref, base, chunk, pieces, late_own, sems, short=None):
        self.spot, self.ref, self.base, self.chunk, self.pieces, self.late_own = spot, ref, base, chunk, pieces, late_own
        self.sems, self.short = sems, short
        self.rows = chunk // pieces
        self.steps = (spot.lines - 1) * pieces

    @staticmethod
    def scratch(lines, pieces):
        return [pltpu.SemaphoreType.DMA((lines * pieces,))] * 6

    def run(self, act, kind, line, piece, crossed=False):
        spot = self.spot
        side = 1 - spot.side if crossed else spot.side
        to = (spot.above, spot.below, spot.pair)[kind]

        def go(rows):
            start = self.base + (line * 2 + side) * self.chunk + piece * self.rows
            here = self.ref.at[pl.ds(pl.multiple_of(start, 16), rows)]
            at = line * self.pieces + piece
            getattr(remote(here, here, self.sems[2 * kind].at[at], self.sems[2 * kind + 1].at[at], to), act)()

        by_half(self.short, line < spot.lines // 2, self.rows, go)

    def own(self, kind):
        @pl.loop(0, self.pieces)
        def _(piece):
            self.run("start", kind, self.spot.line, piece)

    def begin(self):
        spot = self.spot
        if self.late_own:

            @pl.when(spot.line == 0)
            def _():
                self.own(0)

            return

        @pl.when(spot.has_above)
        def _():
            self.own(0)

        @pl.when(spot.has_below)
        def _():
            self.own(1)

        self.own(2)

    def follow(self):
        @pl.when(self.spot.has_below)
        def _():
            self.own(1)

        @pl.when(self.spot.line == 0)
        def _():
            self.own(2)

    def step(self, at):
        spot = self.spot
        piece = lax.rem(at, self.pieces)

        @pl.when(at < spot.line * self.pieces)
        def _():
            turn = at // self.pieces
            line = jnp.minimum(turn, 1) * (spot.line - turn) if self.late_own else turn
            self.run("wait_recv", 0, line, piece)

            @pl.when(spot.has_above)
            def _():
                self.run("start", 0, line, piece)

            self.run("start", 2, line, piece)

        if self.late_own:

            @pl.when((at == self.pieces - 1) & spot.has_below & spot.has_above)
            def _():
                self.own(0)

            @pl.when(at == spot.line * self.pieces - 1)
            def _():
                self.own(2)

        @pl.when(at < (spot.lines - 1 - spot.line) * self.pieces)
        def _():
            line = spot.line + 1 + at // self.pieces
            self.run("wait_recv", 1, line, piece)

            @pl.when(spot.has_below)
            def _():
                self.run("start", 1, line, piece)

            self.run("start", 2, line, piece)

    def wait_crossed(self, line):
        @pl.loop(0, self.pieces)
        def _(piece):
            self.run("wait_recv", 2, line, piece, True)

    def close(self):
        spot = self.spot

        @pl.loop(0, spot.lines * self.pieces)
        def _(at):
            line, piece = at // self.pieces, lax.rem(at, self.pieces)
            self.run("wait_send", 2, line, piece)

            @pl.when((line <= spot.line) & spot.has_above)
            def _():
                self.run("wait_send", 0, line, piece)

            @pl.when((line >= spot.line) & spot.has_below)
            def _():
                self.run("wait_send", 1, line, piece)


WINDOW = 48
SHORT = 16
FRONT = 80
PADDED = 1616
ROW_START = (0, 160, 336, 496)
USED_START = (None, None, None, 0, 128, 352, 576, 800)


def window_row(owner):
    if isinstance(owner, int):
        return owner * WINDOW if owner < 4 else 4 * WINDOW + (owner - 4) * SHORT
    return jnp.minimum(owner, 4) * WINDOW + jnp.maximum(owner - 4, 0) * SHORT


def shared_offsets(me, quarter):
    chunk = SHARED_LANES
    rows = jnp.where(me == 0, 0, jnp.where(me == 1, 160, jnp.where(me == 2, 336, 496)))
    used = (me - 4) * 224 + 128
    return (
        FRONT + 8 * rows - me * chunk + 8 * WINDOW * quarter,
        FRONT + 8 * rows - me * chunk + 8 * 32 * quarter,
        FRONT + PATCH_LANES - me * chunk + 6 * 48 * quarter,
        FRONT + PATCH_LANES + 6 * used - me * chunk + 6 * 64 * quarter,
        FRONT + PATCH_LANES + 6 * D - me * chunk,
    )


def shared_walk(me, quarter, take, phases=range(5)):
    rows, last_rows, first_used, used, norm = shared_offsets(me, quarter)
    for j in range(8):
        if 0 in phases:
            take(me < 3, 0, WINDOW, j, rows + j, 8)
        if 1 in phases:
            take((me == 3) & (quarter < 3), 0, 32, j, last_rows + j, 8)
    if 2 in phases:
        for j in range(3):
            take((me == 3) & (quarter < 3), 32, 16, j, first_used + 6 * 16 * j, 6)
    if 3 in phases:
        for j in range(4):
            take(me > 3, 0, SHORT, j, used + 6 * SHORT * j, 6)
    if 4 in phases:
        for j in range(4):
            take((me == 7) & (quarter == 0), 0, SHORT, 4 + j, norm + j, 4)


def window_pieces(kind, row):
    found = []
    if kind == 0:
        for me in range(3):
            at = row - ROW_START[me]
            if 0 <= at < 4 * WINDOW:
                found.append((me, at // WINDOW, at % WINDOW, None))
        at = row - ROW_START[3]
        if 0 <= at < 96:
            found.append((3, at // 32, at % 32, None))
    else:
        if row < 144:
            found.append((3, row // 48, 32, row % 48 // 16))
        for me in range(4, 8):
            at = row - USED_START[me]
            if 0 <= at < 256:
                found.append((me, at // 64, 0, at % 64 // 16))
    return found

SHARED_LANES = 1348
PATCH_LANES = PIN * D // 128
CHUNK_PIECES = 4


def forward_kernel(lines, q_rows, count_ref, row_ref, shared_ref, own_patch_ref,
                   weight_ref, used_ref, norm_ref,
                   embed_ref, normed1_ref, qkv_ref, attended_ref, log_ref, resid_ref, normed2_ref,
                   patches, proj, windows, own_chunk, own_sem, *rest):
    body, extra = rest[:4 + 14], rest[4 + 14:]
    corner, spot = Corner(), Lines(lines)
    barrier = pltpu.get_barrier_semaphore()
    for other in (corner.mate, corner.far):
        pl.semaphore_signal(barrier, inc=1, device_id={"tensor": other}, device_id_type=MESH)
    pl.semaphore_wait(barrier, 2 + spot.signal(barrier))
    parts = lines // 2
    chunk = weight_ref.shape[0] // (2 * lines)
    size, inputs = own_patch_ref.shape
    window = LineGather(spot, windows, corner.me * (2 * lines * WINDOW), WINDOW, 1, False, extra[0:6], SHORT)
    weights = LineGather(spot, weight_ref, 0, chunk, CHUNK_PIECES, True, extra[6:12])
    spread = Gather(corner, windows, 2 * lines, extra[12:18], SHORT)
    given = Gather(corner, patches, 1, extra[18:24])

    patches[given.part(corner.me, 0)] = own_patch_ref[...]
    given.start(0)
    base = pl.multiple_of((corner.me * 2 * lines + spot.me) * WINDOW, 16)
    windows[pl.ds(base, WINDOW)] = jnp.zeros((WINDOW, windows.shape[1]), LOW)

    def take(condition, row, rows, j, start, stride):
        @pl.when(condition)
        def _():
            windows[pl.ds(pl.multiple_of(base + row, 16), rows), j * 128 : (j + 1) * 128] = shared_ref[
                pl.ds(start, rows, stride)
            ].astype(LOW)

    shared_walk(spot.me, corner.me, take)
    window.begin()
    spread.start(spot.me)
    own = pl.multiple_of(spot.me * chunk, 16)

    @pl.when(spot.me < parts)
    def _():
        for row, rows, col, cols, at, at_col in qkv_places(1, chunk * 4 // 3, D * 3 // 4):
            for j in range(cols // 128):
                own_chunk[row : row + rows, col + j * 128 : col + (j + 1) * 128] = row_ref[
                    pl.ds(6 * at + at_col // 128 + j, rows, 6)
                ].astype(LOW)

    @pl.when(spot.me >= parts)
    def _():
        for j in range(8):
            own_chunk[:, j * 128 : (j + 1) * 128] = row_ref[pl.ds(j, chunk, 8)].astype(LOW)

    kept = pltpu.make_async_copy(own_chunk, weight_ref.at[pl.ds(own, chunk)], own_sem)
    kept.start()
    kept.wait()
    weights.begin()

    def passed(stage, act):
        if stage == 0:
            act(spot.me, None)
            act(spot.line * 2 + 1 - spot.side, spot.line)
            return
        for near in (True, False):
            for there, line in (
                (stage - 1 < spot.line, stage - 1),
                (stage - 1 < lines - 1 - spot.line, spot.line + stage),
            ):

                @pl.when(there)
                def _():
                    act(line * 2 + (spot.side if near else 1 - spot.side), None if near else line)

    def send_on(owner, line):
        if line is not None:
            window.wait_crossed(line)
        spread.start(owner)

    def relay_on(owner, line):
        spread.relay(owner)

    window.wait_crossed(spot.line)
    spread.start(spot.line * 2 + 1 - spot.side)
    window.step(0)
    passed(1, send_on)
    window.step(1)
    passed(2, send_on)
    window.step(2)
    weights.follow()
    weights.step(0)
    passed(3, send_on)
    weights.step(1)
    given.relay(0)
    passed(0, relay_on)
    weights.step(2)
    passed(1, relay_on)
    weights.step(3)
    passed(2, relay_on)
    passed(3, relay_on)
    spread.finish()
    given.finish()

    def source(me, quarter, row, rows, j):
        start = (quarter * 2 * lines + me) * WINDOW + row
        return windows[start : start + rows] if j is None else windows[start : start + rows, j * 128 : (j + 1) * 128]

    for row in range(0, proj.shape[0], 16):
        proj[row : row + 16] = sum(source(me, t, at, 16, j) for me, t, at, j in window_pieces(0, row))
    for row in range(0, used_ref.shape[0], 16):
        used_ref[row : row + 16] = sum(source(me, t, at, 16, j) for me, t, at, j in window_pieces(1, row))
    ends = source(2 * lines - 1, 0, 0, SHORT, None)[:, D // 2 :].astype(WIDE)
    norm_ref[...] = jnp.zeros_like(norm_ref)
    for row in range(8):
        norm_ref[row // 2 : row // 2 + 1, row % 2 * D // 2 : (row % 2 + 1) * D // 2] = ends[row : row + 1]

    def progress(place, at=None):
        if place == "embed":

            @pl.when(at == 2)
            def _():
                weights.step(4)

        if place == "weights":
            weights.step(5)
            weights.wait_crossed(0)
        if place == "turn":

            weights.step(6 + at)
        if place == "out":
            weights.wait_crossed(1)

    attend_body(parts, q_rows, corner, progress, count_ref, patches, proj, norm_ref,
                weight_ref, embed_ref, normed1_ref, qkv_ref, attended_ref, log_ref, resid_ref, normed2_ref, *body)
    for line in range(2, lines):
        weights.wait_crossed(line)
    weights.close()
    window.close()


def forward(count, row_lanes, shared_lanes, own_patches, lines, collective_id):
    size, inputs = own_patches.shape
    length, width, local = 4 * size, D, D // 4
    shape = jax.ShapeDtypeStruct
    return pl.pallas_call(
        partial(forward_kernel, lines, 256),
        out_shape=(
            shape((3 * D, D), LOW),
            shape((D, 128), LOW),
            shape((8, D), WIDE),
            shape((size, width), WIDE),
            shape((length, width), LOW),
            shape((length, 3 * local), LOW),
            shape((length, local), LOW),
            shape((length, local // DH), WIDE),
            shape((size, width), WIDE),
            shape((length, width), LOW),
        ),
        in_specs=[pl.BlockSpec(memory_space=pltpu.SMEM)] + [VMEM] * 3,
        out_specs=(HBM,) + (VMEM,) * 9,
        scratch_shapes=[
            pltpu.VMEM((length, inputs), LOW),
            pltpu.VMEM((inputs, width), LOW),
            pltpu.VMEM((8 * lines * WINDOW, width), LOW),
            pltpu.VMEM((3 * D // (2 * lines), width), LOW),
            pltpu.SemaphoreType.DMA(()),
            pltpu.VMEM((width, 3 * local), LOW),
            pltpu.VMEM((size, width), WIDE),
            pltpu.VMEM((4 * local, width), LOW),
            pltpu.SemaphoreType.DMA((2,)),
        ]
        + Scatter.scratch(size, width, PIECES)
        + Gather.scratch(PIECES)
        + LineGather.scratch(lines, 1)
        + LineGather.scratch(lines, CHUNK_PIECES)
        + Gather.scratch(2 * lines)
        + Gather.scratch(1),
        compiler_params=pltpu.CompilerParams(
            collective_id=collective_id, has_side_effects=True, vmem_limit_bytes=63 * 2**20
        ),
    )(count, row_lanes, shared_lanes, own_patches)


class Moves:
    def __init__(self, sems, *pairs):
        self.copies = [pltpu.make_async_copy(src, dst, sems.at[at]) for at, (src, dst) in enumerate(pairs)]

    def start(self, *which):
        for at in which or range(len(self.copies)):
            self.copies[at].start()

    def wait(self, *which):
        for at in which or range(len(self.copies)):
            self.copies[at].wait()


def mlp_kernel(normed2_ref, weight_ref, resid1_ref, cols_ref, hidden_out, active_out, low_ref, table_ref,
               term, up_ref, down_ref, hidden_ref, active_ref, load_sem, hidden_sem, active_sem, *comm):
    first, ff = up_ref.shape[0], down_ref.shape[0]
    loads = Moves(load_sem, (weight_ref.at[pl.ds(first, first)], up_ref), (weight_ref.at[pl.ds(2 * first, ff)], down_ref))
    loads.start()
    corner = Corner()
    corner.greet()
    scatter = Scatter(corner, PIECES, *comm[:8])
    gather = Gather(corner, table_ref, PIECES, comm[8:])
    size, width = resid1_ref.shape
    loads.wait()

    def stores(step):
        here = rows_of(corner.block(step), size)
        return (
            pltpu.make_async_copy(hidden_ref.at[here], hidden_out.at[here], hidden_sem.at[step]),
            pltpu.make_async_copy(active_ref.at[here], active_out.at[here], active_sem.at[step]),
        )

    @pl.loop(0, 4)
    def _(step):
        here = rows_of(corner.block(step), size)

        def columns(cols):
            hidden = dot(normed2_ref[here], up_ref[:, cols])
            hidden_ref[here, cols] = hidden
            active_ref[here, cols] = (0.5 * hidden * (1.0 + lax.erf(hidden * ROOT_HALF))).astype(LOW)

        column_loop(up_ref.shape[1], columns)
        for copy in stores(step):
            copy.start()
        column_loop(width, lambda cols: term.__setitem__((slice(None), cols), dot(active_ref[here], down_ref[:, cols])))
        scatter.step(step, term)

    for piece in range(PIECES):
        part = scatter.part(piece)
        low_ref[part] = (resid1_ref[part] + scatter.land(piece, term)).astype(LOW)
        table_ref[gather.part(corner.me, piece)] = dot(low_ref[part], cols_ref[...]).astype(LOW)
        gather.start(piece)
    for piece in range(PIECES):
        gather.relay(piece)
    gather.finish()
    scatter.close()
    for step in range(4):
        for copy in stores(step):
            copy.wait()


def mlp(normed2, weights, resid1, used_cols, collective_id):
    length, size, width = normed2.shape[0], resid1.shape[0], resid1.shape[1]
    hidden = FF // 4
    shape = jax.ShapeDtypeStruct
    return pl.pallas_call(
        mlp_kernel,
        out_shape=(
            shape((length, hidden), WIDE),
            shape((length, hidden), LOW),
            shape((size, width), LOW),
            shape((length, used_cols.shape[1]), LOW),
        ),
        in_specs=[VMEM, HBM, VMEM, VMEM],
        out_specs=(HBM, HBM, VMEM, VMEM),
        scratch_shapes=[
            pltpu.VMEM((size, width), WIDE),
            pltpu.VMEM((width, hidden), LOW),
            pltpu.VMEM((hidden, width), LOW),
            pltpu.VMEM((length, hidden), WIDE),
            pltpu.VMEM((length, hidden), LOW),
            pltpu.SemaphoreType.DMA((2,)),
            pltpu.SemaphoreType.DMA((4,)),
            pltpu.SemaphoreType.DMA((4,)),
        ]
        + Scatter.scratch(size, width, PIECES)
        + Gather.scratch(PIECES),
        compiler_params=pltpu.CompilerParams(
            collective_id=collective_id, has_side_effects=True, vmem_limit_bytes=62 * 2**20
        ),
    )(normed2, weights, resid1, used_cols)


def mlp_back_kernel(chunk, table_ref, cols_ref, low_ref, active_in, hidden_in, normed2_in, weight_ref, resid1_ref, norm_ref, attended_ref,
                    unpatch_ref, grad_out, rounded_out, resid_grad_ref, branch_ref, gain_ref,
                    gauss, down_in, hidden_grad, term, tail, active_ref, hidden_ref, normed2_ref, up_ref, down_ref, grad_ref,
                    rounded_ref, load_sem, store_sem, *comm):
    first = up_ref.shape[0]
    loads = Moves(
        load_sem,
        (weight_ref.at[pl.ds(2 * first, down_ref.shape[0])], down_ref),
        (weight_ref.at[pl.ds(first, first)], up_ref),
        (normed2_in, normed2_ref),
        (active_in, active_ref),
    )
    corner = Corner()

    def load_hidden(step):
        here = rows_of(corner.block(step), resid1_ref.shape[0])
        return pltpu.make_async_copy(hidden_in.at[here], hidden_ref.at[here], load_sem.at[4 + step])

    loads.start(0)
    load_hidden(0).start()
    loads.start(1)
    for step in range(1, 4):
        load_hidden(step).start()
    loads.start(2, 3)
    corner.greet()
    small = Scatter(corner, 1, *comm[:8])
    spread = Gather(corner, gauss, 1, comm[8:14])
    scatter = Scatter(corner, PIECES, *comm[14:22])
    gather = Gather(corner, branch_ref, PIECES, comm[22:])
    size, width = resid1_ref.shape
    ff = up_ref.shape[1]

    def view(step):
        return table_ref.at[rows_of(corner.block(step), size)]

    tail[...] = view(0)[...].astype(WIDE)
    small.give(0, tail)
    tail[...] = view(1)[...].astype(WIDE)
    small.cross(tail)
    tail[...] = view(2)[...].astype(WIDE)
    small.give(1, tail)
    tail[...] = view(3)[...].astype(WIDE)
    own_gauss = small.land(0, tail).astype(LOW)
    gauss[spread.part(corner.me, 0)] = own_gauss
    spread.start(0)
    unpatch_ref[...] = dot(low_ref[...], own_gauss, TN)
    spread.relay(0)
    spread.finish()
    small.close()
    loads.wait(0, 1)

    @pl.loop(0, 4)
    def _(step):
        here = rows_of(corner.block(step), size)
        load_hidden(step).wait()
        term[...] = dot(gauss[here], cols_ref[...], NT)
        down_in[here] = term[...].astype(LOW)

        @pl.when(step == 3)
        def _():
            resid_grad_ref[...] = term[...]

        def columns(cols):
            active_grad = dot(down_in[here], down_ref[cols, :], NT)
            hidden = hidden_ref[here, cols]
            slope = 0.5 * (1.0 + lax.erf(hidden * ROOT_HALF)) + hidden * (jnp.exp(-0.5 * hidden * hidden) * NORMAL_PEAK)
            hidden_grad[here, cols] = (active_grad * slope).astype(LOW)

        column_loop(ff, columns)

        def back(cols):
            term[:, cols] = dot(hidden_grad[here], up_ref[cols, :], NT)

        column_loop(width, back)
        scatter.step(step, term)

    side = None if chunk is None else lax.rem(lax.axis_index("dp"), 2)

    def store(at, act):
        part = pl.ds(pl.multiple_of(at * UNIT, UNIT), UNIT)

        def wide():
            getattr(pltpu.make_async_copy(grad_ref.at[part], grad_out.at[part], store_sem.at[at]), act)()

        def rounded():
            getattr(pltpu.make_async_copy(rounded_ref.at[part], rounded_out.at[part], store_sem.at[at]), act)()

        if chunk is None:
            wide()
            return
        mine = lax.rem(at * UNIT // chunk, 2) == side
        pl.when(mine)(wide)
        pl.when(jnp.logical_not(mine))(rounded)

    def keep(tile, value):
        part = pl.ds(pl.multiple_of(tile * TILE, TILE), TILE)
        grad_ref[part, :] = value
        rounded_ref[part, :] = value.astype(LOW)
        for at in range(TILE // UNIT):
            store(tile * (TILE // UNIT) + at, "start")

    loads.wait(2, 3)
    tiles = attended_ref.shape[1] // TILE

    @pl.loop(0, width // TILE)
    def _(tile):
        cols = pl.ds(pl.multiple_of(tile * TILE, TILE), TILE)
        keep(tiles + tile, dot(normed2_ref[:, cols], hidden_grad[...], TN))

    @pl.loop(0, ff // TILE)
    def _(tile):
        cols = pl.ds(pl.multiple_of(tile * TILE, TILE), TILE)
        keep(tiles + width // TILE + tile, dot(active_ref[:, cols], down_in[...], TN))

    gain_sum, bias_sum = jnp.zeros((1, width), WIDE), jnp.zeros((1, width), WIDE)
    for piece in range(PIECES):
        part = scatter.part(piece)
        grad = scatter.land(piece, term)
        scaled, inverse = standard(resid1_ref[part])
        total = resid_grad_ref[part] + norm_back(grad, scaled, inverse, norm_ref[2:3])
        resid_grad_ref[part] = total
        branch_ref[gather.part(corner.me, piece)] = total.astype(LOW)
        gather.start(piece)
        gain_sum += jnp.sum(grad * scaled, 0, keepdims=True)
        bias_sum += jnp.sum(grad, 0, keepdims=True)
    gain_ref[0:1] = gain_sum
    gain_ref[1:2] = bias_sum
    for piece in range(PIECES):
        gather.relay(piece)
    gather.finish()
    scatter.close()

    for tile in range(tiles):
        keep(tile, dot(attended_ref[:, tile * TILE : (tile + 1) * TILE], branch_ref[...], TN))

    @pl.loop(0, grad_ref.shape[0] // UNIT)
    def _(at):
        store(at, "wait")


def mlp_back(table_grad, used_cols, low, active, hidden, normed2, weights, resid1, norm, attended, chunk, collective_id):
    length, size, width = normed2.shape[0], resid1.shape[0], resid1.shape[1]
    ff, used = hidden.shape[1], used_cols.shape[1]
    total = attended.shape[1] + width + ff
    shape = jax.ShapeDtypeStruct
    return pl.pallas_call(
        partial(mlp_back_kernel, chunk),
        out_shape=(
            shape((width, used), WIDE),
            shape((total, width), WIDE),
            shape((total, width), LOW),
            shape((size, width), WIDE),
            shape((length, width), LOW),
            shape((2, width), WIDE),
        ),
        in_specs=[VMEM] * 3 + [HBM] * 4 + [VMEM] * 3,
        out_specs=(VMEM, HBM, HBM, VMEM, VMEM, VMEM),
        scratch_shapes=[
            pltpu.VMEM((length, used), LOW),
            pltpu.VMEM((length, width), LOW),
            pltpu.VMEM((length, ff), LOW),
            pltpu.VMEM((size, width), WIDE),
            pltpu.VMEM((size, used), WIDE),
            pltpu.VMEM((length, ff), LOW),
            pltpu.VMEM((length, ff), WIDE),
            pltpu.VMEM((length, width), LOW),
            pltpu.VMEM((width, ff), LOW),
            pltpu.VMEM((ff, width), LOW),
            pltpu.VMEM((total, width), WIDE),
            pltpu.VMEM((total, width), LOW),
            pltpu.SemaphoreType.DMA((8,)),
            pltpu.SemaphoreType.DMA((total // UNIT,)),
        ]
        + Scatter.scratch(size, used, 1)
        + Gather.scratch(1)
        + Scatter.scratch(size, width, PIECES)
        + Gather.scratch(PIECES),
        compiler_params=pltpu.CompilerParams(
            collective_id=collective_id, has_side_effects=True, vmem_limit_bytes=63 * 2**20
        ),
    )(table_grad, used_cols, low, active, hidden, normed2, weights, resid1, norm, attended)


class LineSum:
    def __init__(self, spot, pieces, low, source, buffers, sems, first=0, turns=4, stored=None):
        self.spot, self.pieces, self.low, self.source = spot, pieces, low, source
        self.first, self.turns, self.stored = first, turns, stored
        self.pair_out, self.pair_in, self.part, self.line_in, self.low_out, self.low_in = buffers
        self.p_send, self.p_recv, self.l_send, self.up_recv, self.down_recv = sems
        self.count = turns * pieces
        self.rows = self.part.shape[0] // self.count

    @staticmethod
    def scratch(turns, rows, pieces, width, low, stored=False):
        half = (turns * rows, width)
        kept = half if low else (rows, width)
        kind = LOW if low else WIDE
        return [
            pltpu.VMEM((16, 128) if stored else half, LOW),
            pltpu.VMEM(half, LOW),
            pltpu.VMEM(half, WIDE),
            pltpu.VMEM(half, WIDE),
            pltpu.VMEM(half if low else (16, 128), LOW),
            pltpu.VMEM(kept, kind),
        ] + [pltpu.SemaphoreType.DMA((turns * pieces,))] * 5

    def target(self, step):
        turn = lax.rem(step, self.turns)
        if self.turns == 4:
            odd = lax.rem(turn, 2)
            return (1 - odd) * (3 - turn // 2) + odd * (turn // 2)
        if self.turns == 3:
            return self.first + 2 - 2 * jnp.minimum(turn, 1) + turn - jnp.minimum(turn, 1)
        return self.first + turn

    def stored_rows(self, step, side):
        start = ((self.target(step) - self.first) * 2 + side) * self.pieces + step // self.turns
        return pl.ds(pl.multiple_of(start * self.rows, 16), self.rows)

    def slot(self, step):
        return pl.ds(pl.multiple_of(step * self.rows, 16), self.rows)

    def pair_copy(self, step):
        slot = self.slot(step)
        if self.stored:
            sent = self.stored[1].at[self.stored_rows(step, 1 - self.spot.side)]
            return remote(sent, self.pair_in.at[slot], self.p_send.at[step], self.p_recv.at[step], self.spot.pair)
        return remote(self.pair_out.at[slot], self.pair_in.at[slot], self.p_send.at[step], self.p_recv.at[step], self.spot.pair)

    def line_copy(self, step, to, recv):
        slot = self.slot(step)
        return remote(self.part.at[slot], self.line_in.at[slot], self.l_send.at[step], recv.at[step], to)

    def low_copy(self, step, to, recv):
        slot = self.slot(step)
        return remote(self.low_out.at[slot], self.low_in.at[slot], self.l_send.at[step], recv.at[step], to)

    def last_copy(self, step):
        here = pl.ds(pl.multiple_of(step // self.turns * self.rows, 16), self.rows)
        return remote(self.part.at[self.slot(step)], self.low_in.at[here], self.l_send.at[step], self.down_recv.at[step], self.spot.below)

    def own_copy(self, step):
        own = self.stored[0].at[self.stored_rows(step, self.spot.side)]
        return pltpu.make_async_copy(own, self.part.at[self.slot(step)], self.stored[2].at[step])

    def begin(self, step):
        if self.stored:
            self.pair_copy(step).start()
            self.own_copy(step).start()
            return
        self.pair_out[self.slot(step)] = self.source(self.target(step), 1 - self.spot.side, step // self.turns).astype(LOW)
        self.pair_copy(step).start()

    def add(self, step, low):
        slot = self.slot(step)
        self.part[slot] += self.low_in[slot].astype(WIDE) if low else self.line_in[slot]

    def low_hop(self, rising, target):
        line, last = self.spot.line, self.spot.lines - 1
        if rising:
            top = target == last
            return (line == 0) | ((line == 1) & top), (line == 1) | ((line == 2) & top)
        return line == last, line == last - 1

    def travel(self, step, rising):
        spot, slot = self.spot, self.slot(step)
        to, recv = (spot.above, self.up_recv) if rising else (spot.below, self.down_recv)
        last = spot.lines - 1
        at_end = spot.line == (0 if rising else last)
        target = self.target(step)
        if self.low:
            low_sent, low_taken = self.low_hop(rising, target)

            @pl.when(jnp.logical_not(at_end) & low_taken)
            def _():
                self.low_copy(step, to, recv).wait_recv()
                self.add(step, True)

            @pl.when(jnp.logical_not(at_end | low_taken))
            def _():
                self.line_copy(step, to, recv).wait_recv()
                self.add(step, False)

            @pl.when(low_sent)
            def _():
                self.low_out[slot] = self.part[slot].astype(LOW)
                self.low_copy(step, to, recv).start()

            @pl.when(jnp.logical_not(low_sent))
            def _():
                self.line_copy(step, to, recv).start()
        else:

            @pl.when(jnp.logical_not(at_end))
            def _():
                self.line_copy(step, to, recv).wait_recv()
                self.add(step, False)

            if rising:
                self.line_copy(step, to, recv).start()
            else:

                @pl.when(target == spot.line - 1)
                def _():
                    self.last_copy(step).start()

                @pl.when(target < spot.line - 1)
                def _():
                    self.line_copy(step, to, recv).start()

    def advance(self, step):
        spot = self.spot

        @pl.when(step < self.count)
        def _():
            slot = self.slot(step)
            self.pair_copy(step).wait_recv()
            if self.stored:
                self.own_copy(step).wait()
                self.part[slot] += self.pair_in[slot].astype(WIDE)
                return
            own = self.source(self.target(step), spot.side, step // self.turns)
            self.part[slot] = own + self.pair_in[slot].astype(WIDE)

        rising = step - spot.line

        @pl.when((rising >= 0) & (rising < self.count) & (self.target(rising) > spot.line))
        def _():
            self.travel(rising, True)

        falling = step - (spot.lines - 1 - spot.line)

        @pl.when((falling >= 0) & (falling < self.count) & (self.target(falling) < spot.line))
        def _():
            self.travel(falling, False)

    def close(self, step, give):
        spot, slot = self.spot, self.slot(step)
        target = self.target(step)
        last = spot.lines - 1
        self.pair_copy(step).wait_send()

        @pl.when(target > spot.line)
        def _():
            if self.low:

                low_sent, low_taken = self.low_hop(True, target)

                @pl.when(low_sent)
                def _():
                    self.low_copy(step, spot.above, self.up_recv).wait_send()

                @pl.when(jnp.logical_not(low_sent))
                def _():
                    self.line_copy(step, spot.above, self.up_recv).wait_send()
            else:
                self.line_copy(step, spot.above, self.up_recv).wait_send()

        @pl.when(target < spot.line)
        def _():
            if self.low:

                @pl.when(spot.line == last)
                def _():
                    self.low_copy(step, spot.below, self.down_recv).wait_send()

                @pl.when(spot.line < last)
                def _():
                    self.line_copy(step, spot.below, self.down_recv).wait_send()
            else:
                self.line_copy(step, spot.below, self.down_recv).wait_send()

        @pl.when(target == spot.line)
        def _():
            if self.low:

                @pl.when(spot.line == 1)
                def _():
                    self.low_copy(step, spot.above, self.up_recv).wait_recv()
                    self.add(step, True)

                @pl.when(spot.line > 1)
                def _():
                    self.line_copy(step, spot.above, self.up_recv).wait_recv()
                    self.add(step, False)

                @pl.when(spot.line == last - 1)
                def _():
                    self.low_copy(step, spot.below, self.down_recv).wait_recv()
                    self.add(step, True)

                @pl.when(spot.line < last - 1)
                def _():
                    self.line_copy(step, spot.below, self.down_recv).wait_recv()
                    self.add(step, False)
            else:

                @pl.when(spot.has_below)
                def _():
                    self.line_copy(step, spot.above, self.up_recv).wait_recv()
                    self.add(step, False)

                @pl.when(spot.has_above)
                def _():
                    self.last_copy(step).wait_recv()
                    here = pl.ds(pl.multiple_of(step // self.turns * self.rows, 16), self.rows)
                    self.part[slot] += self.low_in[here]

            give(step // self.turns, self.part[slot])


def attend_back_kernel(parts, q_rows, lines, count_ref, branch_ref, weight_ref, qkv_ref, log_ref, normed1_in, embed_ref,
                       resid_grad_ref, norm_ref, *rest):
    late_in, rest = (rest[:2], rest[2:]) if lines else ((), rest)
    grad_ref, embed_grad, gain_ref = rest[:3]
    own_late, rest = (rest[3], rest[4:]) if lines else (None, rest[3:])
    qkv_proj, attended_grad, qkv_grad, key_grad, value_grad, term, held, normed1_ref, load_sem = rest[:9]
    comm, late_comm = rest[9:17], rest[17:]
    loads = Moves(load_sem, (weight_ref.at[pl.ds(0, held.shape[0])], held), (normed1_in, normed1_ref))
    loads.start()
    corner = Corner()
    size, width = embed_ref.shape
    length, local = qkv_ref.shape[0], qkv_ref.shape[1] // 3
    if lines:
        spot = Lines(lines)
        barrier = pltpu.get_barrier_semaphore()
        for other in (corner.mate, corner.far):
            pl.semaphore_signal(barrier, inc=1, device_id={"tensor": other}, device_id_type=MESH)
        pl.semaphore_wait(barrier, 2 + spot.signal(barrier))
        late = LineSum(
            spot, SUM_PIECES, True, None, late_comm[:6], late_comm[6:11], 1, lines - 1, late_in + (late_comm[11],)
        )

        @pl.loop(0, late.count)
        def _(step):
            late.begin(step)

    else:
        corner.greet()
    scatter = Scatter(corner, PIECES, *comm)
    packed_ref, out_ref = held.at[pl.ds(0, 3 * local)], held.at[pl.ds(3 * local, local)]
    loads.wait(0)
    unpack_into(qkv_proj, packed_ref, parts)

    @pl.loop(0, 4)
    def _(block):
        here = rows_of(block, size)
        attended_grad[here] = dot(branch_ref[here], out_ref[...], NT).astype(LOW)

    key_grad[...] = jnp.zeros_like(key_grad)
    value_grad[...] = jnp.zeros_like(value_grad)
    valid = lax.broadcasted_iota(jnp.int32, (1, length), 1) < count_ref[0] * VTOK
    left = lax.broadcasted_iota(jnp.int32, (1, 2 * DH), 1) < DH
    factor = jnp.array(DH ** (-0.5), LOW)

    @pl.loop(0, length // q_rows)
    def _(turn):
        here = rows_of(turn, q_rows)
        for pair in range(local // (2 * DH)):
            lanes = slice(pair * 2 * DH, (pair + 1) * 2 * DH)
            queries = qkv_ref[here, lanes] * factor
            grads = attended_grad[here, lanes]
            keyset = qkv_ref[:, local + pair * 2 * DH : local + (pair + 1) * 2 * DH]
            values = qkv_ref[:, 2 * local + pair * 2 * DH : 2 * local + (pair + 1) * 2 * DH]
            found = []
            for side in range(2):
                mine = left if side == 0 else ~left
                own_query = jnp.where(mine, queries, jnp.zeros_like(queries))
                own_grad = jnp.where(mine, grads, jnp.zeros_like(grads))
                scores = jnp.where(valid, dot(own_query, keyset, NT), masked_score)
                probs = jnp.exp(scores - log_ref[here, pair * 2 + side : pair * 2 + side + 1])
                prob_grad = dot(own_grad, values, NT)
                value_grad[:, lanes] += dot(probs.astype(LOW), own_grad, TN)
                centre = jnp.sum(probs * prob_grad, -1, keepdims=True)
                score_grad = (probs * (prob_grad - centre)).astype(LOW)
                found.append(dot(score_grad, keyset))
                key_grad[:, lanes] += dot(score_grad, own_query, TN)
            qkv_grad[here, lanes] = (jnp.where(left, found[0], found[1]) * (DH ** (-0.5))).astype(LOW)
        if lines:

            @pl.loop(0, 2)
            def _(at):
                late.advance(2 * turn + at)

    qkv_grad[:, local : 2 * local] = key_grad[...].astype(LOW)
    qkv_grad[:, 2 * local :] = value_grad[...].astype(LOW)

    @pl.loop(0, 4)
    def _(step):
        here = rows_of(corner.block(step), size)

        def columns(cols):
            term[:, cols] = dot(qkv_grad[here], qkv_proj[cols, :], NT)

        column_loop(width, columns)
        scatter.step(step, term)
        if lines:
            late.advance(12 + step)

    loads.wait(1)
    for tile in range(width // TILE):
        value = dot(normed1_ref[:, tile * TILE : (tile + 1) * TILE], qkv_grad[...], TN)
        for row, rows, col, cols, at, at_col in qkv_places(parts, width, 3 * local):
            if at // TILE == tile:
                at = at % TILE
                grad_ref[row : row + rows, col : col + cols] = value[at : at + rows, at_col : at_col + cols]
    if lines:

        @pl.loop(16, 20)
        def _(step):
            late.advance(step)

    gain_sum, bias_sum = jnp.zeros((1, width), WIDE), jnp.zeros((1, width), WIDE)
    for piece in range(PIECES):
        part = scatter.part(piece)
        grad = scatter.land(piece, term)
        scaled, inverse = standard(embed_ref[part])
        embed_grad[part] = (resid_grad_ref[part] + norm_back(grad, scaled, inverse, norm_ref[0:1])).astype(LOW)
        gain_sum += jnp.sum(grad * scaled, 0, keepdims=True)
        bias_sum += jnp.sum(grad, 0, keepdims=True)
    gain_ref[0:1] = gain_sum
    gain_ref[1:2] = bias_sum
    scatter.close()
    if lines:

        @pl.loop(20, late.count + lines - 1)
        def _(step):
            late.advance(step)

        def keep_rows(piece, value):
            own_late[pl.ds(pl.multiple_of(piece * late.rows, 16), late.rows)] = value

        @pl.loop(0, late.count)
        def _(step):
            late.close(step, keep_rows)


def attend_back(count, branch, weights, qkv, log_total, normed1, embed, resid_grad, norm, late, parts, lines, collective_id):
    length, local = qkv.shape[0], qkv.shape[1] // 3
    size, width = embed.shape
    shape = jax.ShapeDtypeStruct
    chunk = 3 * width // (2 * lines) if lines else 0
    return pl.pallas_call(
        partial(attend_back_kernel, parts, 256, lines),
        out_shape=(
            shape((3 * local, width), WIDE),
            shape((size, width), LOW),
            shape((2, width), WIDE),
        )
        + ((shape((chunk, width), WIDE),) if lines else ()),
        in_specs=[pl.BlockSpec(memory_space=pltpu.SMEM), VMEM, HBM, VMEM, VMEM, HBM, VMEM, VMEM, VMEM] + [HBM] * len(late),
        out_specs=(VMEM,) * (4 if lines else 3),
        scratch_shapes=[
            pltpu.VMEM((width, 3 * local), LOW),
            pltpu.VMEM((length, local), LOW),
            pltpu.VMEM((length, 3 * local), LOW),
            pltpu.VMEM((length, local), WIDE),
            pltpu.VMEM((length, local), WIDE),
            pltpu.VMEM((size, width), WIDE),
            pltpu.VMEM((4 * local, width), LOW),
            pltpu.VMEM((length, width), LOW),
            pltpu.SemaphoreType.DMA((2,)),
        ]
        + Scatter.scratch(size, width, PIECES)
        + (
            LineSum.scratch(lines - 1, chunk, SUM_PIECES, width, True, True)
            + [pltpu.SemaphoreType.DMA(((lines - 1) * SUM_PIECES,))]
            if lines
            else []
        ),
        compiler_params=pltpu.CompilerParams(
            collective_id=collective_id, has_side_effects=True, vmem_limit_bytes=63 * 2**20
        ),
    )(count, branch, weights, qkv, log_total, normed1, embed, resid_grad, norm, *late)


SUM_PIECES = 6


def share_kernel(lines, early_ref, late_ref, embed_ref, own_patch_ref, used_ref, gain_ref, loss_ref, label_ref,
                 row_ref, shared_ref, total_ref,
                 term, windows, mine, slots, rows_out, patch_ref, *comm):
    corner, spot = Corner(), Lines(lines)
    pairs, width = 2 * lines, early_ref.shape[1]
    quarters = 4
    count = pairs * quarters
    me = spot.me * quarters + corner.me
    barrier = pltpu.get_barrier_semaphore()

    def peer(step):
        other = lax.rem(me + step, count)
        return {"dp": other // quarters, "tensor": lax.rem(other, quarters)}

    @pl.loop(1, count)
    def _(step):
        pl.semaphore_signal(barrier, inc=1, device_id=peer(step), device_id_type=MESH)

    pl.semaphore_wait(barrier, count - 1)
    chunk = late_ref.shape[0]
    rows = chunk // SUM_PIECES

    def weight_term(line, side, piece):
        return early_ref[pl.ds(pl.multiple_of(side * chunk + piece * rows, 8), rows)]

    def shared_term(line, side, piece):
        return mine[pl.ds(pl.multiple_of(window_row(line * 2 + side), 16), WINDOW)]

    weights = LineSum(spot, SUM_PIECES, True, weight_term, comm[0:6], comm[6:11], 0, 1)
    shared = LineSum(spot, 1, False, shared_term, comm[11:17], comm[17:22])
    scatter = Scatter(corner, PIECES, *comm[22:30])
    gather = Gather(corner, windows, 1, comm[30:36])
    own_sem, send_sem, recv_sem = comm[36:39]

    @pl.loop(0, weights.count)
    def _(step):
        weights.begin(step)

    patch_ref[...] = dot(own_patch_ref[...], embed_ref[...], TN)

    @pl.loop(0, 4)
    def _(step):
        block = corner.block(step)
        term[...] = jnp.zeros_like(term)

        def rows_at(start, size):
            return pl.ds(pl.multiple_of(start, 16), size)

        for owner in range(3):
            at = owner * WINDOW
            term[at : at + WINDOW] = patch_ref[rows_at(ROW_START[owner] + block * WINDOW, WINDOW)]

        @pl.when(block < 3)
        def _():
            at = 3 * WINDOW
            term[at : at + 16] = patch_ref[rows_at(ROW_START[3] + block * 32, 16)]

            @pl.when(block < 2)
            def _():
                term[at + 16 : at + 32] = patch_ref[rows_at(ROW_START[3] + block * 32 + 16, 16)]

            for j in range(3):
                term[at + 32 : at + 48, j * 128 : (j + 1) * 128] = used_ref[rows_at(block * 48 + 16 * j, 16)]

        for owner in range(4, 8):
            at = window_row(owner)
            for j in range(4):

                @pl.when((block < 3) | (owner < 7) | (j < 2))
                def _():
                    term[at : at + SHORT, j * 128 : (j + 1) * 128] = used_ref[
                        rows_at(USED_START[owner] + block * 64 + SHORT * j, SHORT)
                    ]

        @pl.when(block == 0)
        def _():
            for row in range(8):
                at = window_row(7) + row
                term[at : at + 1, width // 2 :] = gain_ref[row // 2 : row // 2 + 1, row % 2 * width // 2 : (row % 2 + 1) * width // 2]

        scatter.step(step, term)

    @pl.loop(0, 2)
    def _(step):
        weights.advance(step)

    for piece in range(PIECES):
        mine[scatter.part(piece)] = scatter.land(piece, term)

    @pl.loop(0, lines)
    def _(step):
        shared.begin(step)

    @pl.loop(0, 2 * lines - 1)
    def _(step):
        weights.advance(2 + step)
        shared.advance(step)

    def keep_window(piece, value):
        windows[gather.part(corner.me, 0)] = value

    @pl.loop(0, lines)
    def _(step):
        shared.close(step, keep_window)

    gather.start(0)

    def keep_rows(piece, value):
        rows_out[pl.ds(pl.multiple_of(piece * rows, rows), rows)] = value

    @pl.loop(0, weights.count)
    def _(step):
        weights.close(step, keep_rows)

    @pl.when(spot.line > 0)
    def _():
        rows_out[...] = late_ref[...]

    gather.relay(0)

    @pl.when(spot.me < lines // 2)
    def _():
        for row, height, col, cols, at, at_col in qkv_places(1, chunk * 4 // 3, width * 3 // 4):
            for j in range(cols // 128):
                row_ref[pl.ds(6 * at + at_col // 128 + j, height, 6)] = rows_out[
                    row : row + height, col + j * 128 : col + (j + 1) * 128
                ]

    @pl.when(spot.me >= lines // 2)
    def _():
        for j in range(8):
            row_ref[pl.ds(j, chunk, 8)] = rows_out[:, j * 128 : (j + 1) * 128]

    squares = jnp.sum(rows_out[...] * rows_out[...], 0, keepdims=True)
    gather.finish()
    shared_ref[...] = jnp.zeros_like(shared_ref)
    for phase in range(5):

        @pl.loop(0, 4)
        def _(quarter):
            def take(condition, row, height, j, start, stride):
                @pl.when(condition)
                def _():
                    here = pl.ds(pl.multiple_of(quarter * WINDOW + row, 16), height)
                    shared_ref[pl.ds(start, height, stride)] = windows[here, j * 128 : (j + 1) * 128]

            shared_walk(spot.me, quarter, take, (phase,))
    kept = shared_ref[FRONT : FRONT + PADDED - FRONT]
    place = lax.broadcasted_iota(jnp.int32, kept.shape, 0)
    kept = jnp.where((place < SHARED_LANES) & (corner.me == 0), kept, 0.0)
    square = jnp.sum(jnp.sum(squares, 1, keepdims=True)) + jnp.sum(kept * kept)
    counted = jnp.sum(jnp.where(label_ref[...] < 2, 1.0, 0.0))
    line = lax.broadcasted_iota(jnp.int32, total_ref.shape, 0)
    slots[me] = jnp.where(line == 0, square, jnp.where(line == 1, loss_ref[...], jnp.where(line == 2, counted, 0.0)))

    def send(step):
        return remote(slots.at[me], slots.at[me], send_sem.at[step], recv_sem.at[step], peer(step))

    def arrive(step):
        source = lax.rem(me - step + count, count)
        return remote(slots.at[source], slots.at[source], send_sem.at[step], recv_sem.at[step], peer(step))

    @pl.loop(1, count)
    def _(step):
        send(step).start()

    @pl.loop(1, count)
    def _(step):
        arrive(step).wait_recv()

    total_ref[...] = jnp.sum(slots[...], 0)

    @pl.loop(1, count)
    def _(step):
        send(step).wait_send()

    scatter.close()


def share(early, late, embed_grad, patches, used_grad, gains, loss_tile, labels, lines, collective_id):
    width = early.shape[1]
    chunk = late.shape[0]
    packed = 4 * WINDOW + (2 * lines - 4) * SHORT
    count = 8 * lines
    shape = jax.ShapeDtypeStruct
    return pl.pallas_call(
        partial(share_kernel, lines),
        out_shape=(shape((chunk * width // 128, 128), WIDE), shape((PADDED, 128), WIDE), shape((8, 128), WIDE)),
        in_specs=[VMEM] * 8,
        out_specs=(VMEM,) * 3,
        scratch_shapes=[
            pltpu.VMEM((packed, width), WIDE),
            pltpu.VMEM((4 * WINDOW, width), WIDE),
            pltpu.VMEM((packed + WINDOW - SHORT, width), WIDE),
            pltpu.VMEM((count, 8, 128), WIDE),
            pltpu.VMEM((chunk, width), WIDE),
            pltpu.VMEM((patches.shape[1], width), WIDE),
        ]
        + LineSum.scratch(1, chunk, SUM_PIECES, width, True)
        + LineSum.scratch(lines, WINDOW, 1, width, False)
        + Scatter.scratch(packed, width, PIECES)
        + Gather.scratch(1)
        + [
            pltpu.SemaphoreType.DMA(()),
            pltpu.SemaphoreType.DMA((count,)),
            pltpu.SemaphoreType.DMA((count,)),
        ],
        compiler_params=pltpu.CompilerParams(
            collective_id=collective_id, has_side_effects=True, vmem_limit_bytes=63 * 2**20
        ),
    )(early, late, embed_grad, patches, used_grad, gains, loss_tile, labels)


def render_kernel(area, wide, block, split, span, table_ref, splat_ref, dist_ref, label_ref, loss_ref, grad_ref, flip, hot, weighted, spread_grad):
    tokens = table_ref.shape[0]
    groups = tokens // wide
    splats, pixels = splat_ref.shape
    for j in range(groups):
        flip[j * 2 * area : (j + 1) * 2 * area] = jnp.transpose(table_ref[j * wide : (j + 1) * wide].astype(jnp.float32)).astype(jnp.bfloat16)
    spread_grad[...] = jnp.zeros_like(spread_grad)
    wide_ids = lax.broadcasted_iota(jnp.int32, (wide, block), 0).astype(jnp.float32).astype(jnp.bfloat16)
    cell_ids = lax.broadcasted_iota(jnp.int32, (area, block), 0).astype(jnp.float32)
    cell_low = cell_ids.astype(jnp.bfloat16)
    one, nil = jnp.ones((wide, block), jnp.bfloat16), jnp.zeros((wide, block), jnp.bfloat16)

    def one_block(step, loss):
        here = pl.ds(pl.multiple_of(step * block, block), block)
        opacities, spreads, lows = [], [], []
        for k in range(splats):
            index = splat_ref[k : k + 1, here]
            token = index // area
            column = (token % wide).astype(jnp.float32).astype(jnp.bfloat16)
            lows.append((token // wide, (index % area).astype(jnp.float32)))
            hot[:, k * block : (k + 1) * block] = jnp.where(wide_ids == column, one, nil)
        for k in range(splats):
            lanes = slice(k * block, (k + 1) * block)
            group, cell = lows[k]
            op_sum = jnp.zeros((area, block), jnp.float32)
            sp_sum = jnp.zeros((area, block), jnp.float32)
            for at in range(0, groups, span):
                rows = slice(at * 2 * area, (at + span) * 2 * area)
                found = lax.dot_general(flip[rows], hot[:, lanes], NN, preferred_element_type=jnp.float32)
                for j in range(span):
                    same = cell_ids == jnp.where(group == at + j, cell, -1.0)
                    op_sum += jnp.where(same, found[j * 2 * area : j * 2 * area + area], 0.0)
                    sp_sum += jnp.where(same, found[j * 2 * area + area : (j + 1) * 2 * area], 0.0)
            opacities.append(jnp.sum(op_sum, 0, keepdims=True))
            spreads.append(jnp.sum(sp_sum, 0, keepdims=True))
        opacity, spread = jnp.concatenate(opacities, 0), jnp.concatenate(spreads, 0)
        distance = dist_ref[:, here].astype(jnp.float32)
        labels = label_ref[:, here]
        valid = jnp.where(labels < 2, 1.0, 0.0)
        target = jnp.where(labels == 1, 1.0, 0.0)
        op_sig, sp_sig = jax.nn.sigmoid(opacity), jax.nn.sigmoid(spread)
        fade = jnp.exp(-0.25 * distance * sp_sig)
        contrib = (0.02 + 0.96 * op_sig) * fade
        keep_log = jnp.sum(jnp.log1p(-contrib), 0, keepdims=True)
        keep = jnp.exp(keep_log)
        alpha = 1.0 - keep
        alpha_log = jnp.log(alpha)
        loss = loss - valid * (target * alpha_log + (1.0 - target) * keep_log)
        keep_grad = valid * (target * keep / alpha - (1.0 - target))
        contrib_grad = -keep_grad / (1.0 - contrib)
        op_grad = contrib_grad * (0.96 * op_sig * (1.0 - op_sig)) * fade
        sp_grad = contrib_grad * contrib * (-0.25 * distance * sp_sig * (1.0 - sp_sig))
        zero = jnp.zeros((area, block), jnp.bfloat16)
        op_parts, sp_parts = [], []
        for part in range(split):
            op_parts.append(op_grad.astype(jnp.bfloat16))
            sp_parts.append(sp_grad.astype(jnp.bfloat16))
            op_grad, sp_grad = op_grad - op_parts[-1].astype(jnp.float32), sp_grad - sp_parts[-1].astype(jnp.float32)
        for at in range(0, groups, span):
            rows = slice(at * 2 * area, (at + span) * 2 * area)
            for k in range(splats):
                lanes = slice(k * block, (k + 1) * block)
                group, cell = lows[k]
                for j in range(span):
                    same = cell_low == jnp.where(group == at + j, cell, -1.0).astype(jnp.bfloat16)
                    first = (at + j) * 2 * area
                    for part in range(split):
                        weighted[part, first : first + area, lanes] = jnp.where(same, op_parts[part][k : k + 1], zero)
                        weighted[part, first + area : first + 2 * area, lanes] = jnp.where(same, sp_parts[part][k : k + 1], zero)
            total = spread_grad[rows]
            for part in range(split):
                total += lax.dot_general(weighted[part, rows], hot[...], NT, preferred_element_type=jnp.float32)
            spread_grad[rows] = total
        return loss

    loss = lax.fori_loop(0, pixels // block, one_block, jnp.zeros((1, block), jnp.float32))
    loss_ref[...] = jnp.broadcast_to(jnp.sum(loss, 1, keepdims=True), loss_ref.shape)
    for j in range(groups):
        grad_ref[j * wide : (j + 1) * wide] = jnp.transpose(spread_grad[j * 2 * area : (j + 1) * 2 * area]).astype(grad_ref.dtype)

def render(table, splats, distance, labels, area, block=768, wide=256, split=2, span=3):
    tokens = table.shape[0]
    vm = pl.BlockSpec(memory_space=pltpu.VMEM)
    groups = tokens // wide
    count = splats.shape[0]
    return pl.pallas_call(
        partial(render_kernel, area, wide, block, split, span),
        out_shape=(jax.ShapeDtypeStruct((8, 128), jnp.float32), jax.ShapeDtypeStruct(table.shape, jnp.bfloat16)),
        in_specs=[vm] * 4, out_specs=(vm, vm),
        scratch_shapes=[pltpu.VMEM((groups * 2 * area, wide), jnp.bfloat16),
            pltpu.VMEM((wide, count * block), jnp.bfloat16), pltpu.VMEM((split, groups * 2 * area, count * block), jnp.bfloat16), pltpu.VMEM((groups * 2 * area, wide), jnp.float32)],
        compiler_params=pltpu.CompilerParams(vmem_limit_bytes=60 * 2**20),
    )(table, splats, distance, labels)


def owner_sum_kernel(lines, pieces, g_ref, o_ref, pair_out, pair_in, part, line_in, own_in, p_send, p_recv, l_send, up_recv, down_recv):
    me = lax.axis_index("dp")
    line, side = me // 2, lax.rem(me, 2)
    chunk = o_ref.shape[0]
    rows = chunk // pieces
    count = lines * pieces
    pair = {"dp": line * 2 + 1 - side}
    above = {"dp": lax.rem(line + 1, lines) * 2 + side}
    below = {"dp": lax.rem(line + lines - 1, lines) * 2 + side}
    has_below, has_above = line > 0, line < lines - 1

    def target(step):
        turn = lax.rem(step, lines)
        odd = lax.rem(turn, 2)
        return (1 - odd) * (lines - 1 - turn // 2) + odd * (turn // 2)

    def slot(step):
        return pl.ds(pl.multiple_of(step * rows, rows), rows)

    def here(step):
        return pl.ds(pl.multiple_of(step // lines * rows, rows), rows)

    def source(step, owner):
        return pl.ds(pl.multiple_of((target(step) * 2 + owner) * chunk + step // lines * rows, rows), rows)

    def copy(src, dst, send, recv, to):
        return pltpu.make_async_remote_copy(
            src_ref=src, dst_ref=dst, send_sem=send, recv_sem=recv, device_id=to, device_id_type=MESH
        )

    def pair_copy(step):
        return copy(pair_out.at[slot(step)], pair_in.at[slot(step)], p_send.at[step], p_recv.at[step], pair)

    def line_copy(step, to, recv):
        return copy(part.at[slot(step)], line_in.at[slot(step)], l_send.at[step], recv.at[step], to)

    def last_copy(step):
        return copy(part.at[slot(step)], own_in.at[here(step)], l_send.at[step], down_recv.at[step], below)

    barrier = pltpu.get_barrier_semaphore()
    pl.semaphore_signal(barrier, inc=1, device_id=pair, device_id_type=MESH)

    @pl.when(has_below)
    def _():
        pl.semaphore_signal(barrier, inc=1, device_id=below, device_id_type=MESH)

    @pl.when(has_above)
    def _():
        pl.semaphore_signal(barrier, inc=1, device_id=above, device_id_type=MESH)

    pl.semaphore_wait(barrier, 1 + jnp.minimum(line, 1) + jnp.minimum(lines - 1 - line, 1))

    @pl.loop(0, count)
    def _(step):
        pair_out[slot(step)] = g_ref[source(step, 1 - side)].astype(jnp.bfloat16)
        pair_copy(step).start()

    @pl.loop(0, count + lines - 1)
    def _(step):
        @pl.when(step < count)
        def _():
            pair_copy(step).wait_recv()
            part[slot(step)] = g_ref[source(step, side)].astype(jnp.float32) + pair_in[slot(step)].astype(jnp.float32)

        rising = step - line

        @pl.when((rising >= 0) & (rising < count) & (target(rising) > line))
        def _():
            @pl.when(has_below)
            def _():
                line_copy(rising, above, up_recv).wait_recv()
                part[slot(rising)] += line_in[slot(rising)]

            line_copy(rising, above, up_recv).start()

        falling = step - (lines - 1 - line)

        @pl.when((falling >= 0) & (falling < count) & (target(falling) < line))
        def _():
            @pl.when(has_above)
            def _():
                line_copy(falling, below, down_recv).wait_recv()
                part[slot(falling)] += line_in[slot(falling)]

            @pl.when(target(falling) == line - 1)
            def _():
                last_copy(falling).start()

            @pl.when(target(falling) < line - 1)
            def _():
                line_copy(falling, below, down_recv).start()

    @pl.loop(0, count)
    def _(step):
        pair_copy(step).wait_send()

        @pl.when(target(step) > line)
        def _():
            line_copy(step, above, up_recv).wait_send()

        @pl.when(target(step) < line)
        def _():
            line_copy(step, below, down_recv).wait_send()

        @pl.when(target(step) == line)
        def _():
            o_ref[here(step)] = part[slot(step)]

            @pl.when(has_below)
            def _():
                line_copy(step, above, up_recv).wait_recv()
                o_ref[here(step)] += line_in[slot(step)]

            @pl.when(has_above)
            def _():
                last_copy(step).wait_recv()
                o_ref[here(step)] += own_in[here(step)]


def owner_sum(grad, count_dp, collective_id, pieces):
    lines = count_dp // 2
    total, width = grad.shape
    chunk = total // count_dp
    half = (lines * chunk, width)
    vmem = pl.BlockSpec(memory_space=pltpu.VMEM)
    return pl.pallas_call(
        partial(owner_sum_kernel, lines, pieces),
        out_shape=jax.ShapeDtypeStruct((chunk, width), jnp.float32),
        in_specs=[vmem],
        out_specs=vmem,
        scratch_shapes=[
            pltpu.VMEM(half, jnp.bfloat16),
            pltpu.VMEM(half, jnp.bfloat16),
            pltpu.VMEM(half, jnp.float32),
            pltpu.VMEM(half, jnp.float32),
            pltpu.VMEM((chunk, width), jnp.float32),
        ]
        + [pltpu.SemaphoreType.DMA((lines * pieces,))] * 5,
        compiler_params=pltpu.CompilerParams(
            collective_id=collective_id, has_side_effects=True, vmem_limit_bytes=62 * 2**20
        ),
    )(grad)


def total_kernel(mine_ref, sum_ref, slots, own_sem, send_sem, recv_sem):
    first, second = lax.axis_size("dp"), lax.axis_size("tensor")
    count = first * second
    me = lax.axis_index("dp") * second + lax.axis_index("tensor")

    def peer(step):
        other = lax.rem(me + step, count)
        return {"dp": other // second, "tensor": lax.rem(other, second)}

    barrier = pltpu.get_barrier_semaphore()

    @pl.loop(1, count)
    def _(step):
        pl.semaphore_signal(barrier, inc=1, device_id=peer(step), device_id_type=MESH)

    pl.semaphore_wait(barrier, count - 1)
    own = pltpu.make_async_copy(mine_ref, slots.at[me], own_sem)
    own.start()

    def send(step):
        return pltpu.make_async_remote_copy(
            src_ref=mine_ref,
            dst_ref=slots.at[me],
            send_sem=send_sem.at[step],
            recv_sem=recv_sem.at[step],
            device_id=peer(step),
            device_id_type=MESH,
        )

    @pl.loop(1, count)
    def _(step):
        send(step).start()

    @pl.loop(1, count)
    def _(step):
        send(step).wait()

    own.wait()
    sum_ref[...] = jnp.sum(slots[...], 0)


def total_over_all(mine, collective_id):
    count = lax.axis_size("dp") * lax.axis_size("tensor")
    vmem = pl.BlockSpec(memory_space=pltpu.VMEM)
    return pl.pallas_call(
        total_kernel,
        out_shape=jax.ShapeDtypeStruct(mine.shape, jnp.float32),
        in_specs=[vmem],
        out_specs=vmem,
        scratch_shapes=[
            pltpu.VMEM((count,) + mine.shape, jnp.float32),
            pltpu.SemaphoreType.DMA(()),
            pltpu.SemaphoreType.DMA((count,)),
            pltpu.SemaphoreType.DMA((count,)),
        ],
        compiler_params=pltpu.CompilerParams(collective_id=collective_id, has_side_effects=True),
    )(mine)


def pack_qkv(matrix, parts):
    rows, cols = matrix.shape
    first = matrix[:, :512].reshape(parts, 2, rows // parts // 2, 512).transpose(0, 2, 1, 3)
    second = matrix[:, 512:].reshape(parts, 4, rows // parts // 4, 256).transpose(0, 2, 1, 3)
    return jnp.concatenate([first.reshape(parts, -1, 1024), second.reshape(parts, -1, 1024)], 1).reshape(-1, 1024)


def unpack_qkv(packed, parts):
    rows = packed.shape[0] // parts
    packed = packed.reshape(parts, rows, 1024)
    cut = rows * 2 // 3
    first = packed[:, :cut].reshape(parts, cut, 2, 512).transpose(0, 2, 1, 3).reshape(-1, 512)
    second = packed[:, cut:].reshape(parts, rows - cut, 4, 256).transpose(0, 2, 1, 3).reshape(-1, 256)
    return jnp.concatenate([first, second], 1)


def by_lanes(flat, outer):
    size = flat.size // math.prod(outer)
    return flat.reshape(outer + ((size // 128, 128) if size % 128 == 0 else (size,)))


def pad_first(array, axis, unit):
    short = -array.shape[axis] % unit
    return jnp.pad(array, [(0, short if at == axis else 0) for at in range(array.ndim)])


def sum_to_owners(stack, count_dp):
    if count_dp == 8:
        return owner_sum(stack, count_dp, 1, 9)
    return lax.psum_scatter(stack, "dp", scatter_dimension=0, tiled=True)

def adam_update(master, first_mom, second_mom, gradient, step_float):
    first_new = beta_one * first_mom + (1.0 - beta_one) * gradient
    second_new = beta_two * second_mom + (1.0 - beta_two) * gradient * gradient
    first_hat = first_new / (1.0 - jnp.power(beta_one, step_float))
    second_hat = second_new / (1.0 - jnp.power(beta_two, step_float))
    master_new = master - learn_rate * (
        first_hat / (jnp.sqrt(second_hat) + adam_eps) + decay_rate * master
    )
    return (master_new, first_new, second_new)


def adam_kernel(total_ref, count_ref, *refs):
    norm_value = jnp.sqrt(total_ref[0, 0:1]) / total_ref[2, 0:1]
    factor = clip_norm / jnp.maximum(norm_value, clip_norm) / total_ref[2, 0:1]
    step_float = jnp.full((1, 1), count_ref[0], jnp.int32).astype(WIDE)
    grad, master, first, second, ema = (ref[...] for ref in refs[:5])
    new, first_new, second_new = adam_update(master, first, second, grad * factor.reshape(1, 1), step_float)
    for ref, value in zip(refs[5:], (new, first_new, second_new, ema_rate * ema + (1.0 - ema_rate) * new, new.astype(LOW))):
        ref[...] = value


def adam(totals, step_count, grad, master, first, second, ema, block):
    size = master.shape[1]
    spec = pl.BlockSpec((1, block), lambda at: (0, at))
    return pl.pallas_call(
        adam_kernel,
        grid=(size // block,),
        out_shape=tuple(jax.ShapeDtypeStruct(master.shape, kind) for kind in (WIDE,) * 4 + (LOW,)),
        in_specs=[pl.BlockSpec((8, 128), lambda at: (0, 0)), pl.BlockSpec(memory_space=pltpu.SMEM)] + [spec] * 5,
        out_specs=(spec,) * 5,
    )(totals, step_count, grad, master, first, second, ema)


def per_device(
    patches,
    view_counts,
    splat_index,
    splat_dist,
    alpha_label,
    step_count,
    row_master,
    row_first,
    row_second,
    row_ema,
    shared_master,
    shared_first,
    shared_second,
    shared_ema,
):
    groups = lax.axis_size("tensor")
    my_dp = lax.axis_index("dp")
    count_dp = lax.axis_size("dp")
    local_width = D // groups
    qkv_parts = count_dp // 4
    share_rows = row_master.shape[1] // D
    own_patches = patches[0]
    if count_dp == 8:
        shared_lanes = jnp.pad(
            shared_master.reshape(SHARED_LANES, 128), ((FRONT, PADDED - FRONT - SHARED_LANES), (0, 0))
        )
        weights, used_cols, norm, embed, normed1, qkv, attended, log_total, resid1, normed2 = forward(
            view_counts, row_master.reshape(-1, 128), shared_lanes, own_patches, count_dp // 2, 7
        )
    else:
        own_row = row_master[0].astype(jnp.bfloat16)
        own_tiles = jnp.where(
            my_dp < qkv_parts,
            pack_qkv(own_row.reshape(-1, 3 * local_width), 1),
            own_row.reshape(share_rows, D),
        )
        weights = lax.all_gather(own_tiles, "dp", axis=0, tiled=True)
        own_flat = shared_master.astype(jnp.bfloat16)
        own_shared = by_lanes(own_flat, ())
        lead = own_shared.shape[0]
        own_shared = pad_first(own_shared, 0, 2048 // own_shared[0].size)
        shared_weights = lax.all_gather(own_shared, "dp", axis=0, tiled=False)[:, :lead].reshape(-1, 128)
        patch_rows = PIN * D // 128
        unpatch_rows = D * POUT // 128
        norm = shared_weights[patch_rows + unpatch_rows :].reshape(4, D).astype(jnp.float32)
        patch_proj = shared_weights[:patch_rows].reshape(PIN, D)
        used_cols = shared_weights[patch_rows : patch_rows + unpatch_rows].reshape(D, POUT // 128, 128)[:, 0]
        all_patches = lax.all_gather(own_patches, "tensor", axis=0, tiled=True)
        embed, normed1, qkv, attended, log_total, resid1, normed2 = attend(
            view_counts, all_patches, patch_proj, norm, weights, qkv_parts, 3
        )
    hidden, active, resid2_low, gauss_table = mlp(normed2, weights, resid1, used_cols, 4)
    loss_tile, table_grad = render(gauss_table, splat_index[0], splat_dist[0], alpha_label, PATCH * PATCH)
    loss_part = loss_tile[0, 0]
    unpatch_used, late_grad, late_low, resid_grad, branch, gain2_grad = mlp_back(
        table_grad, used_cols, resid2_low, active, hidden, normed2, weights, resid1, norm, attended, share_rows if count_dp == 8 else None, 5
    )
    early_grad, embed_grad, gain1_grad, *own_late = attend_back(
        view_counts,
        branch,
        weights,
        qkv,
        log_total,
        normed1,
        embed,
        resid_grad,
        norm,
        (late_grad, late_low) if count_dp == 8 else (),
        qkv_parts,
        count_dp // 2 if count_dp == 8 else 0,
        6,
    )
    gain_grad = jnp.concatenate([gain1_grad, gain2_grad], 0)
    if count_dp == 8:
        gains = jnp.pad(gain_grad, ((0, 4), (0, 0)))
        row_lanes, shared_kept, totals = share(
            early_grad, own_late[0], embed_grad, own_patches, unpatch_used, gains, loss_tile, alpha_label, count_dp // 2, 8
        )
        row_share = row_lanes.reshape(-1)
        shared_share = shared_kept[FRONT : FRONT + SHARED_LANES].reshape(-1)
    else:
        patch_grad = dot(own_patches, embed_grad, TN)
        unpatch_grad = jnp.concatenate(
            [unpatch_used, jnp.zeros((D, POUT - unpatch_used.shape[1]), jnp.float32)], 1
        )
        shared_grad = jnp.concatenate(
            [patch_grad.reshape(-1), unpatch_grad.reshape(-1), gain_grad.reshape(-1)]
        )
        split_grad = by_lanes(shared_grad, (count_dp, groups))
        lead = split_grad.shape[2]
        shared_stack = pad_first(split_grad, 2, 16 * D // split_grad[0, 0, 0].size).swapaxes(0, 1)
        shared_sum = lax.psum_scatter(shared_stack, "tensor", scatter_dimension=0, tiled=True)
        row_stack = jnp.concatenate([early_grad, late_grad], 0)
        stack = jnp.concatenate(
            [row_stack.reshape(count_dp, share_rows, D), shared_sum.reshape(count_dp, -1, D)], 1
        ).reshape(-1, D)
        own_share = sum_to_owners(stack, count_dp)
        own_rows = own_share[:share_rows]
        row_share = jnp.where(my_dp < qkv_parts, unpack_qkv(own_rows, 1).reshape(-1), own_rows.reshape(-1))
        shared_part = own_share[share_rows:].reshape((-1,) + split_grad.shape[3:])[:lead]
        shared_share = lax.all_gather(shared_part, "tensor", axis=0, tiled=False).reshape(-1)
        own_squares = jnp.sum(row_share * row_share) + jnp.sum(shared_part * shared_part)
        pixel_part = jnp.sum((alpha_label < 2).astype(jnp.float32))
        scalars = jnp.stack([own_squares, loss_part, pixel_part]).reshape(3, 1)
        totals = total_over_all(jnp.pad(jnp.broadcast_to(scalars, (3, 128)), ((0, 5), (0, 0))), 2)
    square_total, loss_total, pixel_total = totals[0, 0], totals[1, 0], totals[2, 0]
    norm_value = jnp.sqrt(square_total) / pixel_total
    factor = clip_norm / jnp.maximum(norm_value, clip_norm) / pixel_total
    step_float = step_count[0].astype(jnp.float32)
    row_new, row_first_new, row_second_new, row_ema_new, row_copy = adam(
        totals, step_count, row_share[None], row_master, row_first, row_second, row_ema, row_master.shape[1] // 6
    )
    shared_new, shared_first_new, shared_second_new = adam_update(
        shared_master, shared_first, shared_second, shared_share * factor, step_float
    )
    shared_ema_new = ema_rate * shared_ema + (1.0 - ema_rate) * shared_new
    return (
        norm_value.reshape(1),
        (loss_total / pixel_total).reshape(1),
        row_new,
        row_first_new,
        row_second_new,
        row_ema_new,
        row_copy,
        shared_new,
        shared_first_new,
        shared_second_new,
        shared_ema_new,
        shared_new.astype(jnp.bfloat16),
    )


def solution(mesh):
    placed = (
        P("dp", "tensor", None),
        P("dp"),
        P("dp", None, "tensor"),
        P("dp", None, "tensor"),
        P("dp", "tensor"),
        P(),
        P("tensor", "dp"),
        P("tensor", "dp"),
        P("tensor", "dp"),
        P("tensor", "dp"),
        P("dp"),
        P("dp"),
        P("dp"),
        P("dp"),
    )
    return jax.shard_map(
        per_device,
        mesh=mesh,
        in_specs=placed,
        out_specs=(
            P(),
            P(),
            P("tensor", "dp"),
            P("tensor", "dp"),
            P("tensor", "dp"),
            P("tensor", "dp"),
            P("tensor", "dp"),
            P("dp"),
            P("dp"),
            P("dp"),
            P("dp"),
            P("dp"),
        ),
        check_vma=False,
    )
```

```python
import math
from functools import partial

import jax
import jax.numpy as jnp
from jax import lax
from jax.experimental import pallas as pl
from jax.experimental.pallas import tpu as pltpu
from jax.sharding import PartitionSpec as P

D = 1024
DH = 64
FF = 4096
PATCH = 8
VTOK = 192
PIN = 576
POUT = 768
VMEM = pl.BlockSpec(memory_space=pltpu.VMEM)
HBM = pl.BlockSpec(memory_space=pl.ANY)
ROOT_HALF = 0.5**0.5
NORMAL_PEAK = (2.0 * math.pi) ** -0.5


clip_norm = 0.005
beta_one = 0.9
beta_two = 0.95
adam_eps = 1e-08
decay_rate = 0.05
learn_rate = 0.03
ema_rate = 0.9
norm_eps = 1e-05
masked_score = -1e30


MESH = pl.DeviceIdType.MESH
NN = (((1,), (0,)), ((), ()))
NT = (((1,), (1,)), ((), ()))
TN = (((0,), (0,)), ((), ()))
LOW = jnp.bfloat16
WIDE = jnp.float32
PIECES = 4
TILE = 256
UNIT = 128


def dot(left, right, dims=NN):
    return lax.dot_general(left, right, dims, preferred_element_type=WIDE)


def remote(src, dst, send, recv, to):
    return pltpu.make_async_remote_copy(
        src_ref=src, dst_ref=dst, send_sem=send, recv_sem=recv, device_id=to, device_id_type=MESH
    )


class Corner:
    def __init__(self):
        self.me = lax.axis_index("tensor")
        self.first, self.last = self.me // 2, lax.rem(self.me, 2)
        self.mate = self.first * 2 + 1 - self.last
        self.far = (1 - self.first) * 2 + self.last
        self.opposite = (1 - self.first) * 2 + 1 - self.last

    def block(self, step):
        return lax.rem(self.first + 1 - step // 2, 2) * 2 + lax.rem(self.last + 1 - lax.rem(step, 2), 2)

    def greet(self):
        barrier = pltpu.get_barrier_semaphore()
        for other in (self.mate, self.far):
            pl.semaphore_signal(barrier, inc=1, device_id={"tensor": other}, device_id_type=MESH)
        pl.semaphore_wait(barrier, 2)


class Gather:
    def __init__(self, corner, ref, pieces, sems, short=None):
        self.corner, self.ref, self.pieces, self.sems, self.short = corner, ref, pieces, sems, short
        self.size = ref.shape[0] // 4
        self.rows = self.size // pieces

    @staticmethod
    def scratch(pieces):
        return [pltpu.SemaphoreType.DMA((pieces,))] * 6

    def part(self, owner, piece, rows=None):
        return pl.ds(pl.multiple_of(owner * self.size + piece * self.rows, self.rows), rows or self.rows)

    def run(self, act, owner, piece, kind, to):
        def go(rows):
            here = self.ref.at[self.part(owner, piece, rows)]
            sems = self.sems[2 * kind].at[piece], self.sems[2 * kind + 1].at[piece]
            getattr(remote(here, here, *sems, {"tensor": to}), act)()

        by_half(self.short, piece < self.pieces // 2, self.rows, go)

    def start(self, piece):
        self.run("start", self.corner.me, piece, 1, self.corner.far)
        self.run("start", self.corner.me, piece, 0, self.corner.mate)

    def relay(self, piece):
        self.run("wait_recv", self.corner.far, piece, 1, self.corner.far)
        self.run("start", self.corner.far, piece, 2, self.corner.mate)

    def finish(self):
        corner = self.corner
        for piece in range(self.pieces):
            self.run("wait_recv", corner.mate, piece, 0, corner.mate)
            self.run("wait_recv", corner.opposite, piece, 2, corner.mate)
            self.run("wait_send", corner.me, piece, 0, corner.mate)
            self.run("wait_send", corner.me, piece, 1, corner.far)
            self.run("wait_send", corner.far, piece, 2, corner.mate)


def by_half(short, first, rows, go):
    if short is None:
        go(rows)
    elif isinstance(first, bool):
        go(rows if first else short)
    else:
        pl.when(first)(lambda: go(rows))
        pl.when(jnp.logical_not(first))(lambda: go(short))


class Scatter:
    def __init__(self, corner, pieces, mate_out, mate_in, far_out, far_in, mate_send, mate_recv, far_send, far_recv):
        self.corner, self.pieces = corner, pieces
        self.mate_out, self.mate_in, self.far_out, self.far_in = mate_out, mate_in, far_out, far_in
        self.sems = mate_send, mate_recv, far_send, far_recv
        self.rows = far_out.shape[0] // pieces

    @staticmethod
    def scratch(rows, width, pieces):
        return [
            pltpu.VMEM((2, rows, width), LOW),
            pltpu.VMEM((2, rows, width), LOW),
            pltpu.VMEM((rows, width), LOW),
            pltpu.VMEM((rows, width), LOW),
            pltpu.SemaphoreType.DMA((2, pieces)),
            pltpu.SemaphoreType.DMA((2, pieces)),
            pltpu.SemaphoreType.DMA((pieces,)),
            pltpu.SemaphoreType.DMA((pieces,)),
        ]

    def part(self, piece):
        return pl.ds(piece * self.rows, self.rows)

    def mate_copy(self, half, piece):
        part = self.part(piece)
        return remote(
            self.mate_out.at[half, part],
            self.mate_in.at[half, part],
            self.sems[0].at[half, piece],
            self.sems[1].at[half, piece],
            {"tensor": self.corner.mate},
        )

    def far_copy(self, piece):
        part = self.part(piece)
        return remote(
            self.far_out.at[part],
            self.far_in.at[part],
            self.sems[2].at[piece],
            self.sems[3].at[piece],
            {"tensor": self.corner.far},
        )

    def give(self, half, ref):
        for piece in range(self.pieces):
            part = self.part(piece)
            self.mate_out[half, part] = ref[part].astype(LOW)
            self.mate_copy(half, piece).start()

    def cross(self, ref):
        for piece in range(self.pieces):
            part = self.part(piece)
            self.mate_copy(0, piece).wait_recv()
            self.far_out[part] = (ref[part] + self.mate_in[0, part].astype(WIDE)).astype(LOW)
            self.far_copy(piece).start()

    def step(self, step, ref):
        @pl.when(step == 0)
        def _():
            self.give(0, ref)

        @pl.when(step == 1)
        def _():
            self.cross(ref)

        @pl.when(step == 2)
        def _():
            self.give(1, ref)

    def land(self, piece, ref):
        part = self.part(piece)
        self.mate_copy(1, piece).wait_recv()
        self.far_copy(piece).wait_recv()
        return ref[part] + self.mate_in[1, part].astype(WIDE) + self.far_in[part].astype(WIDE)

    def close(self):
        for piece in range(self.pieces):
            self.mate_copy(0, piece).wait_send()
            self.mate_copy(1, piece).wait_send()
            self.far_copy(piece).wait_send()


def standard(values):
    centre = values - jnp.mean(values, -1, keepdims=True)
    inverse = lax.rsqrt(jnp.mean(centre * centre, -1, keepdims=True) + norm_eps)
    return centre * inverse, inverse


def norm_back(grad_out, scaled, inverse, gain):
    grad_scaled = grad_out * gain
    return inverse * (
        grad_scaled
        - jnp.mean(grad_scaled, -1, keepdims=True)
        - scaled * jnp.mean(grad_scaled * scaled, -1, keepdims=True)
    )


def qkv_places(parts, rows, columns):
    share = rows // parts
    wide = columns * 2 // 3
    packed = share * columns // 1024
    for at in range(parts):
        for j in range(2):
            half = share // 2
            yield (at * packed, half, j * wide, wide, at * share + j * half, 0)
        for j in range(4):
            quarter = share // 4
            yield (at * packed + share // 2, quarter, j * (columns - wide), columns - wide, at * share + j * quarter, wide)


def unpack_into(full, packed, parts):
    for row, rows, col, cols, to_row, to_col in qkv_places(parts, full.shape[0], full.shape[1]):
        full[to_row : to_row + rows, to_col : to_col + cols] = packed[row : row + rows, col : col + cols]


def pack_from(packed, full, parts, base=0):
    for row, rows, col, cols, to_row, to_col in qkv_places(parts, full.shape[0], full.shape[1]):
        packed[base + row : base + row + rows, col : col + cols] = full[to_row : to_row + rows, to_col : to_col + cols]


def rows_of(block, size):
    return pl.ds(pl.multiple_of(block * size, size), size)


def column_loop(width, body):
    @pl.loop(0, width // TILE)
    def _(tile):
        body(pl.ds(pl.multiple_of(tile * TILE, TILE), TILE))


def attend_kernel(parts, q_rows, count_ref, patch_ref, proj_ref, norm_ref, weight_ref, *rest):
    corner = Corner()
    corner.greet()
    attend_body(parts, q_rows, corner, None, count_ref, patch_ref, proj_ref, norm_ref, weight_ref, *rest)


def attend_body(parts, q_rows, corner, progress, count_ref, patch_ref, proj_ref, norm_ref, weight_ref,
                embed_ref, normed1_ref, qkv_ref, attended_ref, log_ref, resid_ref, normed2_ref,
                qkv_proj, term, held, held_sem, *comm):
    progress = progress or (lambda *_: None)
    scatter = Scatter(corner, PIECES, *comm[:8])
    gather = Gather(corner, normed2_ref, PIECES, comm[8:])
    packed_rows = held.shape[0] * 3 // 4
    packed_ref, out_ref = held.at[pl.ds(0, packed_rows)], held.at[pl.ds(packed_rows, held.shape[0] - packed_rows)]

    def hold(start, target, at):
        copy = pltpu.make_async_copy(weight_ref.at[pl.ds(start, target.shape[0])], target, held_sem.at[at])
        copy.start()
        copy.wait()

    size, width = embed_ref.shape
    length = patch_ref.shape[0]
    local = attended_ref.shape[1]

    @pl.loop(0, 4)
    def _(block):
        here = rows_of(block, size)
        column_loop(width, lambda cols: term.__setitem__((slice(None), cols), dot(patch_ref[here], proj_ref[:, cols])))

        @pl.when(block == corner.me)
        def _():
            embed_ref[...] = term[...]

        scaled, inverse = standard(term[...])
        normed1_ref[here] = (scaled * norm_ref[0:1] + norm_ref[1:2]).astype(LOW)
        progress("embed", block)

    progress("weights")
    hold(0, packed_ref, 0)
    unpack_into(qkv_proj, packed_ref, parts)

    @pl.loop(0, 4)
    def _(block):
        here = rows_of(block, size)

        def columns(cols):
            qkv_ref[here, cols] = dot(normed1_ref[here], qkv_proj[:, cols]).astype(LOW)

        column_loop(3 * local, columns)

    valid = lax.broadcasted_iota(jnp.int32, (1, length), 1) < count_ref[0] * VTOK
    left = lax.broadcasted_iota(jnp.int32, (1, 2 * DH), 1) < DH
    factor = jnp.array(DH ** (-0.5), LOW)

    @pl.loop(0, length // q_rows)
    def _(turn):
        here = rows_of(turn, q_rows)
        for pair in range(local // (2 * DH)):
            lanes = slice(pair * 2 * DH, (pair + 1) * 2 * DH)
            queries = qkv_ref[here, lanes] * factor
            keyset = qkv_ref[:, local + pair * 2 * DH : local + (pair + 1) * 2 * DH]
            values = qkv_ref[:, 2 * local + pair * 2 * DH : 2 * local + (pair + 1) * 2 * DH]
            found = []
            for side in range(2):
                mine = left if side == 0 else ~left
                scores = dot(jnp.where(mine, queries, jnp.zeros_like(queries)), keyset, NT)
                scores = jnp.where(valid, scores, masked_score)
                top = jnp.max(scores, -1, keepdims=True)
                powers = jnp.exp(scores - top)
                total = jnp.sum(powers, -1, keepdims=True)
                log_ref[here, pair * 2 + side : pair * 2 + side + 1] = top + jnp.log(total)
                found.append(dot((powers * (1.0 / total)).astype(LOW), values))
            attended_ref[here, lanes] = jnp.where(left, found[0], found[1]).astype(LOW)
        progress("turn", turn)

    progress("out")
    hold(packed_rows, out_ref, 1)

    @pl.loop(0, 4)
    def _(step):
        here = rows_of(corner.block(step), size)
        column_loop(width, lambda cols: term.__setitem__((slice(None), cols), dot(attended_ref[here], out_ref[:, cols])))
        scatter.step(step, term)
        progress("give", step)

    for piece in range(PIECES):
        part = scatter.part(piece)
        resid = embed_ref[part] + scatter.land(piece, term)
        resid_ref[part] = resid
        scaled, inverse = standard(resid)
        normed2_ref[gather.part(corner.me, piece)] = (scaled * norm_ref[2:3] + norm_ref[3:4]).astype(LOW)
        gather.start(piece)
        progress("land", piece)
    for piece in range(PIECES):
        gather.relay(piece)
    gather.finish()
    scatter.close()


def attend(count, patches, patch_proj, norm, weights, parts, collective_id):
    length, size = patches.shape[0], patches.shape[0] // 4
    width, local = patch_proj.shape[1], patch_proj.shape[1] // 4
    shape = jax.ShapeDtypeStruct
    return pl.pallas_call(
        partial(attend_kernel, parts, 256),
        out_shape=(
            shape((size, width), WIDE),
            shape((length, width), LOW),
            shape((length, 3 * local), LOW),
            shape((length, local), LOW),
            shape((length, local // DH), WIDE),
            shape((size, width), WIDE),
            shape((length, width), LOW),
        ),
        in_specs=[pl.BlockSpec(memory_space=pltpu.SMEM)] + [VMEM] * 3 + [HBM],
        out_specs=(VMEM,) * 7,
        scratch_shapes=[
            pltpu.VMEM((width, 3 * local), LOW),
            pltpu.VMEM((size, width), WIDE),
            pltpu.VMEM((4 * local, width), LOW),
            pltpu.SemaphoreType.DMA((2,)),
        ]
        + Scatter.scratch(size, width, PIECES)
        + Gather.scratch(PIECES),
        compiler_params=pltpu.CompilerParams(
            collective_id=collective_id, has_side_effects=True, vmem_limit_bytes=62 * 2**20
        ),
    )(count, patches, patch_proj, norm, weights)


class Lines:
    def __init__(self, lines):
        self.lines = lines
        self.me = lax.axis_index("dp")
        self.line, self.side = self.me // 2, lax.rem(self.me, 2)
        self.pair = {"dp": self.line * 2 + 1 - self.side}
        self.above = {"dp": lax.rem(self.line + 1, lines) * 2 + self.side}
        self.below = {"dp": lax.rem(self.line + lines - 1, lines) * 2 + self.side}
        self.has_below, self.has_above = self.line > 0, self.line < lines - 1

    def signal(self, barrier):
        pl.semaphore_signal(barrier, inc=1, device_id=self.pair, device_id_type=MESH)

        @pl.when(self.has_below)
        def _():
            pl.semaphore_signal(barrier, inc=1, device_id=self.below, device_id_type=MESH)

        @pl.when(self.has_above)
        def _():
            pl.semaphore_signal(barrier, inc=1, device_id=self.above, device_id_type=MESH)

        return 1 + jnp.minimum(self.line, 1) + jnp.minimum(self.lines - 1 - self.line, 1)


class LineGather:
    def __init__(self, spot, ref, base, chunk, pieces, late_own, sems, short=None):
        self.spot, self.ref, self.base, self.chunk, self.pieces, self.late_own = spot, ref, base, chunk, pieces, late_own
        self.sems, self.short = sems, short
        self.rows = chunk // pieces
        self.steps = (spot.lines - 1) * pieces

    @staticmethod
    def scratch(lines, pieces):
        return [pltpu.SemaphoreType.DMA((lines * pieces,))] * 6

    def run(self, act, kind, line, piece, crossed=False):
        spot = self.spot
        side = 1 - spot.side if crossed else spot.side
        to = (spot.above, spot.below, spot.pair)[kind]

        def go(rows):
            start = self.base + (line * 2 + side) * self.chunk + piece * self.rows
            here = self.ref.at[pl.ds(pl.multiple_of(start, 16), rows)]
            at = line * self.pieces + piece
            getattr(remote(here, here, self.sems[2 * kind].at[at], self.sems[2 * kind + 1].at[at], to), act)()

        by_half(self.short, line < spot.lines // 2, self.rows, go)

    def own(self, kind):
        @pl.loop(0, self.pieces)
        def _(piece):
            self.run("start", kind, self.spot.line, piece)

    def begin(self):
        spot = self.spot
        if self.late_own:

            @pl.when(spot.line == 0)
            def _():
                self.own(0)

            return

        @pl.when(spot.has_above)
        def _():
            self.own(0)

        @pl.when(spot.has_below)
        def _():
            self.own(1)

        self.own(2)

    def follow(self):
        @pl.when(self.spot.has_below)
        def _():
            self.own(1)

        @pl.when(self.spot.line == 0)
        def _():
            self.own(2)

    def step(self, at):
        spot = self.spot
        piece = lax.rem(at, self.pieces)

        @pl.when(at < spot.line * self.pieces)
        def _():
            turn = at // self.pieces
            line = jnp.minimum(turn, 1) * (spot.line - turn) if self.late_own else turn
            self.run("wait_recv", 0, line, piece)

            @pl.when(spot.has_above)
            def _():
                self.run("start", 0, line, piece)

            self.run("start", 2, line, piece)

        if self.late_own:

            @pl.when((at == self.pieces - 1) & spot.has_below & spot.has_above)
            def _():
                self.own(0)

            @pl.when(at == spot.line * self.pieces - 1)
            def _():
                self.own(2)

        @pl.when(at < (spot.lines - 1 - spot.line) * self.pieces)
        def _():
            line = spot.line + 1 + at // self.pieces
            self.run("wait_recv", 1, line, piece)

            @pl.when(spot.has_below)
            def _():
                self.run("start", 1, line, piece)

            self.run("start", 2, line, piece)

    def wait_crossed(self, line):
        @pl.loop(0, self.pieces)
        def _(piece):
            self.run("wait_recv", 2, line, piece, True)

    def close(self):
        spot = self.spot

        @pl.loop(0, spot.lines * self.pieces)
        def _(at):
            line, piece = at // self.pieces, lax.rem(at, self.pieces)
            self.run("wait_send", 2, line, piece)

            @pl.when((line <= spot.line) & spot.has_above)
            def _():
                self.run("wait_send", 0, line, piece)

            @pl.when((line >= spot.line) & spot.has_below)
            def _():
                self.run("wait_send", 1, line, piece)


WINDOW = 48
SHORT = 16
FRONT = 80
PADDED = 1616
ROW_START = (0, 160, 336, 496)
USED_START = (None, None, None, 0, 128, 352, 576, 800)


def window_row(owner):
    if isinstance(owner, int):
        return owner * WINDOW if owner < 4 else 4 * WINDOW + (owner - 4) * SHORT
    return jnp.minimum(owner, 4) * WINDOW + jnp.maximum(owner - 4, 0) * SHORT


def window_valid(me, quarter, width):
    row = lax.broadcasted_iota(jnp.int32, (WINDOW, width), 0)
    block = lax.broadcasted_iota(jnp.int32, (WINDOW, width), 1) // 128
    start, stop = me * SHARED_LANES, (me + 1) * SHARED_LANES
    patch_row = jnp.where(me == 3, ROW_START[3] + 32 * quarter, 160 * me + 16 * (me // 2) + WINDOW * quarter) + row
    lane = 8 * patch_row + block
    patch = (me < 4) & ((me < 3) | ((quarter < 3) & (row < 32))) & (lane >= start) & (lane < stop) & (lane < PATCH_LANES)
    first = (me == 3) & (quarter < 3) & (row >= 32) & (block < 3)
    other = (me > 3) & (row < SHORT) & (block < 4)
    index = jnp.where(me == 3, 48 * quarter + 16 * block + row - 32, 224 * me - 768 + 64 * quarter + SHORT * block + row)
    lane = PATCH_LANES + 6 * index
    used = (first | other) & (index < D) & (lane >= start) & (lane < stop)
    norm = (me == 7) & (quarter == 0) & (row < 8) & (block >= 4)
    return patch | used | norm


def shared_offsets(me, quarter):
    chunk = SHARED_LANES
    rows = jnp.where(me == 0, 0, jnp.where(me == 1, 160, jnp.where(me == 2, 336, 496)))
    used = (me - 4) * 224 + 128
    return (
        FRONT + 8 * rows - me * chunk + 8 * WINDOW * quarter,
        FRONT + 8 * rows - me * chunk + 8 * 32 * quarter,
        FRONT + PATCH_LANES - me * chunk + 6 * 48 * quarter,
        FRONT + PATCH_LANES + 6 * used - me * chunk + 6 * 64 * quarter,
        FRONT + PATCH_LANES + 6 * D - me * chunk,
    )


def shared_walk(me, quarter, take, phases=range(5)):
    rows, last_rows, first_used, used, norm = shared_offsets(me, quarter)
    for j in range(8):
        if 0 in phases:
            take(me < 3, 0, WINDOW, j, rows + j, 8)
        if 1 in phases:
            take((me == 3) & (quarter < 3), 0, 32, j, last_rows + j, 8)
    if 2 in phases:
        for j in range(3):
            take((me == 3) & (quarter < 3), 32, 16, j, first_used + 6 * 16 * j, 6)
    if 3 in phases:
        for j in range(4):
            take(me > 3, 0, SHORT, j, used + 6 * SHORT * j, 6)
    if 4 in phases:
        for j in range(4):
            take((me == 7) & (quarter == 0), 0, SHORT, 4 + j, norm + j, 4)


def window_pieces(kind, row):
    found = []
    if kind == 0:
        for me in range(3):
            at = row - ROW_START[me]
            if 0 <= at < 4 * WINDOW:
                found.append((me, at // WINDOW, at % WINDOW, None))
        at = row - ROW_START[3]
        if 0 <= at < 96:
            found.append((3, at // 32, at % 32, None))
    else:
        if row < 144:
            found.append((3, row // 48, 32, row % 48 // 16))
        for me in range(4, 8):
            at = row - USED_START[me]
            if 0 <= at < 256:
                found.append((me, at // 64, 0, at % 64 // 16))
    return found

SHARED_LANES = 1348
PATCH_LANES = PIN * D // 128
CHUNK_PIECES = 4


def forward_kernel(lines, q_rows, count_ref, row_ref, lanes_ref, own_patch_ref,
                   weight_ref, used_ref, norm_ref,
                   embed_ref, normed1_ref, qkv_ref, attended_ref, log_ref, resid_ref, normed2_ref,
                   patches, proj, windows, shared_ref, own_chunk, own_sem, *rest):
    body, extra = rest[:4 + 14], rest[4 + 14:]
    corner, spot = Corner(), Lines(lines)
    barrier = pltpu.get_barrier_semaphore()
    for other in (corner.mate, corner.far):
        pl.semaphore_signal(barrier, inc=1, device_id={"tensor": other}, device_id_type=MESH)
    pl.semaphore_wait(barrier, 2 + spot.signal(barrier))
    parts = lines // 2
    chunk = weight_ref.shape[0] // (2 * lines)
    size, inputs = own_patch_ref.shape
    window = LineGather(spot, windows, corner.me * (2 * lines * WINDOW), WINDOW, 1, False, extra[0:6], SHORT)
    weights = LineGather(spot, weight_ref, 0, chunk, CHUNK_PIECES, True, extra[6:12])
    spread = Gather(corner, windows, 2 * lines, extra[12:18], SHORT)
    given = Gather(corner, patches, 1, extra[18:24])

    patches[given.part(corner.me, 0)] = own_patch_ref[...]
    given.start(0)
    base = pl.multiple_of((corner.me * 2 * lines + spot.me) * WINDOW, 16)
    windows[pl.ds(base, WINDOW)] = jnp.zeros((WINDOW, windows.shape[1]), LOW)
    shared_ref[...] = jnp.zeros_like(shared_ref)
    shared_ref[FRONT : FRONT + SHARED_LANES] = lanes_ref[...]

    def take(condition, row, rows, j, start, stride):
        @pl.when(condition)
        def _():
            windows[pl.ds(pl.multiple_of(base + row, 16), rows), j * 128 : (j + 1) * 128] = shared_ref[
                pl.ds(start, rows, stride)
            ].astype(LOW)

    shared_walk(spot.me, corner.me, take)
    window.begin()
    spread.start(spot.me)
    own = pl.multiple_of(spot.me * chunk, 16)

    @pl.when(spot.me < parts)
    def _():
        for row, rows, col, cols, at, at_col in qkv_places(1, chunk * 4 // 3, D * 3 // 4):
            for j in range(cols // 128):
                own_chunk[row : row + rows, col + j * 128 : col + (j + 1) * 128] = row_ref[
                    pl.ds(6 * at + at_col // 128 + j, rows, 6)
                ].astype(LOW)

    @pl.when(spot.me >= parts)
    def _():
        for j in range(8):
            own_chunk[:, j * 128 : (j + 1) * 128] = row_ref[pl.ds(j, chunk, 8)].astype(LOW)

    kept = pltpu.make_async_copy(own_chunk, weight_ref.at[pl.ds(own, chunk)], own_sem)
    kept.start()
    kept.wait()
    weights.begin()

    def passed(stage, act):
        if stage == 0:
            act(spot.me, None)
            act(spot.line * 2 + 1 - spot.side, spot.line)
            return
        for near in (True, False):
            for there, line in (
                (stage - 1 < spot.line, stage - 1),
                (stage - 1 < lines - 1 - spot.line, spot.line + stage),
            ):

                @pl.when(there)
                def _():
                    act(line * 2 + (spot.side if near else 1 - spot.side), None if near else line)

    def send_on(owner, line):
        if line is not None:
            window.wait_crossed(line)
        spread.start(owner)

    def relay_on(owner, line):
        spread.relay(owner)

    window.wait_crossed(spot.line)
    spread.start(spot.line * 2 + 1 - spot.side)
    window.step(0)
    passed(1, send_on)
    window.step(1)
    passed(2, send_on)
    window.step(2)
    weights.follow()
    weights.step(0)
    passed(3, send_on)
    weights.step(1)
    given.relay(0)
    passed(0, relay_on)
    weights.step(2)
    passed(1, relay_on)
    weights.step(3)
    passed(2, relay_on)
    passed(3, relay_on)
    spread.finish()
    given.finish()

    def source(me, quarter, row, rows, j):
        start = (quarter * 2 * lines + me) * WINDOW + row
        return windows[start : start + rows] if j is None else windows[start : start + rows, j * 128 : (j + 1) * 128]

    for row in range(0, proj.shape[0], 16):
        proj[row : row + 16] = sum(source(me, t, at, 16, j) for me, t, at, j in window_pieces(0, row))
    for row in range(0, used_ref.shape[0], 16):
        used_ref[row : row + 16] = sum(source(me, t, at, 16, j) for me, t, at, j in window_pieces(1, row))
    ends = source(2 * lines - 1, 0, 0, SHORT, None)[:, D // 2 :].astype(WIDE)
    norm_ref[...] = jnp.zeros_like(norm_ref)
    for row in range(8):
        norm_ref[row // 2 : row // 2 + 1, row % 2 * D // 2 : (row % 2 + 1) * D // 2] = ends[row : row + 1]

    def progress(place, at=None):
        if place == "embed":

            @pl.when(at == 2)
            def _():
                weights.step(4)

        if place == "weights":
            weights.step(5)
            weights.wait_crossed(0)
        if place == "turn":

            weights.step(6 + at)
        if place == "out":
            weights.wait_crossed(1)

    attend_body(parts, q_rows, corner, progress, count_ref, patches, proj, norm_ref,
                weight_ref, embed_ref, normed1_ref, qkv_ref, attended_ref, log_ref, resid_ref, normed2_ref, *body)
    for line in range(2, lines):
        weights.wait_crossed(line)
    weights.close()
    window.close()


def forward(count, row_lanes, shared_lanes, own_patches, lines, collective_id):
    size, inputs = own_patches.shape
    length, width, local = 4 * size, D, D // 4
    shape = jax.ShapeDtypeStruct
    return pl.pallas_call(
        partial(forward_kernel, lines, 256),
        out_shape=(
            shape((3 * D, D), LOW),
            shape((D, 128), LOW),
            shape((8, D), WIDE),
            shape((size, width), WIDE),
            shape((length, width), LOW),
            shape((length, 3 * local), LOW),
            shape((length, local), LOW),
            shape((length, local // DH), WIDE),
            shape((size, width), WIDE),
            shape((length, width), LOW),
        ),
        in_specs=[pl.BlockSpec(memory_space=pltpu.SMEM)] + [VMEM] * 3,
        out_specs=(HBM,) + (VMEM,) * 9,
        scratch_shapes=[
            pltpu.VMEM((length, inputs), LOW),
            pltpu.VMEM((inputs, width), LOW),
            pltpu.VMEM((8 * lines * WINDOW, width), LOW),
            pltpu.VMEM((PADDED, 128), WIDE),
            pltpu.VMEM((3 * D // (2 * lines), width), LOW),
            pltpu.SemaphoreType.DMA(()),
            pltpu.VMEM((width, 3 * local), LOW),
            pltpu.VMEM((size, width), WIDE),
            pltpu.VMEM((4 * local, width), LOW),
            pltpu.SemaphoreType.DMA((2,)),
        ]
        + Scatter.scratch(size, width, PIECES)
        + Gather.scratch(PIECES)
        + LineGather.scratch(lines, 1)
        + LineGather.scratch(lines, CHUNK_PIECES)
        + Gather.scratch(2 * lines)
        + Gather.scratch(1),
        compiler_params=pltpu.CompilerParams(
            collective_id=collective_id, has_side_effects=True, vmem_limit_bytes=63 * 2**20
        ),
    )(count, row_lanes, shared_lanes, own_patches)


class Moves:
    def __init__(self, sems, *pairs):
        self.copies = [pltpu.make_async_copy(src, dst, sems.at[at]) for at, (src, dst) in enumerate(pairs)]

    def start(self, *which):
        for at in which or range(len(self.copies)):
            self.copies[at].start()

    def wait(self, *which):
        for at in which or range(len(self.copies)):
            self.copies[at].wait()


def mlp_kernel(normed2_ref, weight_ref, resid1_ref, cols_ref, hidden_out, active_out, low_ref, table_ref,
               term, up_ref, down_ref, hidden_ref, active_ref, load_sem, hidden_sem, active_sem, *comm):
    first, ff = up_ref.shape[0], down_ref.shape[0]
    loads = Moves(load_sem, (weight_ref.at[pl.ds(first, first)], up_ref), (weight_ref.at[pl.ds(2 * first, ff)], down_ref))
    loads.start()
    corner = Corner()
    corner.greet()
    scatter = Scatter(corner, PIECES, *comm[:8])
    gather = Gather(corner, table_ref, PIECES, comm[8:])
    size, width = resid1_ref.shape
    loads.wait()

    def stores(step):
        here = rows_of(corner.block(step), size)
        return (
            pltpu.make_async_copy(hidden_ref.at[here], hidden_out.at[here], hidden_sem.at[step]),
            pltpu.make_async_copy(active_ref.at[here], active_out.at[here], active_sem.at[step]),
        )

    @pl.loop(0, 4)
    def _(step):
        here = rows_of(corner.block(step), size)

        def columns(cols):
            hidden = dot(normed2_ref[here], up_ref[:, cols])
            hidden_ref[here, cols] = hidden
            active_ref[here, cols] = (0.5 * hidden * (1.0 + lax.erf(hidden * ROOT_HALF))).astype(LOW)

        column_loop(up_ref.shape[1], columns)
        for copy in stores(step):
            copy.start()
        column_loop(width, lambda cols: term.__setitem__((slice(None), cols), dot(active_ref[here], down_ref[:, cols])))
        scatter.step(step, term)

    for piece in range(PIECES):
        part = scatter.part(piece)
        low_ref[part] = (resid1_ref[part] + scatter.land(piece, term)).astype(LOW)
        table_ref[gather.part(corner.me, piece)] = dot(low_ref[part], cols_ref[...]).astype(LOW)
        gather.start(piece)
    for piece in range(PIECES):
        gather.relay(piece)
    gather.finish()
    scatter.close()
    for step in range(4):
        for copy in stores(step):
            copy.wait()


def mlp(normed2, weights, resid1, used_cols, collective_id):
    length, size, width = normed2.shape[0], resid1.shape[0], resid1.shape[1]
    hidden = FF // 4
    shape = jax.ShapeDtypeStruct
    return pl.pallas_call(
        mlp_kernel,
        out_shape=(
            shape((length, hidden), WIDE),
            shape((length, hidden), LOW),
            shape((size, width), LOW),
            shape((length, used_cols.shape[1]), LOW),
        ),
        in_specs=[VMEM, HBM, VMEM, VMEM],
        out_specs=(HBM, HBM, VMEM, VMEM),
        scratch_shapes=[
            pltpu.VMEM((size, width), WIDE),
            pltpu.VMEM((width, hidden), LOW),
            pltpu.VMEM((hidden, width), LOW),
            pltpu.VMEM((length, hidden), WIDE),
            pltpu.VMEM((length, hidden), LOW),
            pltpu.SemaphoreType.DMA((2,)),
            pltpu.SemaphoreType.DMA((4,)),
            pltpu.SemaphoreType.DMA((4,)),
        ]
        + Scatter.scratch(size, width, PIECES)
        + Gather.scratch(PIECES),
        compiler_params=pltpu.CompilerParams(
            collective_id=collective_id, has_side_effects=True, vmem_limit_bytes=62 * 2**20
        ),
    )(normed2, weights, resid1, used_cols)


def mlp_back_kernel(chunk, table_ref, cols_ref, low_ref, active_in, hidden_in, normed2_in, weight_ref, resid1_ref, norm_ref, attended_ref,
                    unpatch_ref, grad_out, rounded_out, resid_grad_ref, branch_ref, gain_ref,
                    gauss, down_in, hidden_grad, term, tail, active_ref, hidden_ref, normed2_ref, up_ref, down_ref, grad_ref,
                    rounded_ref, load_sem, store_sem, *comm):
    first = up_ref.shape[0]
    loads = Moves(
        load_sem,
        (weight_ref.at[pl.ds(2 * first, down_ref.shape[0])], down_ref),
        (weight_ref.at[pl.ds(first, first)], up_ref),
        (normed2_in, normed2_ref),
        (active_in, active_ref),
    )
    corner = Corner()

    def load_hidden(step):
        here = rows_of(corner.block(step), resid1_ref.shape[0])
        return pltpu.make_async_copy(hidden_in.at[here], hidden_ref.at[here], load_sem.at[4 + step])

    loads.start(0)
    load_hidden(0).start()
    loads.start(1)
    for step in range(1, 4):
        load_hidden(step).start()
    loads.start(2, 3)
    corner.greet()
    small = Scatter(corner, 1, *comm[:8])
    spread = Gather(corner, gauss, 1, comm[8:14])
    scatter = Scatter(corner, PIECES, *comm[14:22])
    gather = Gather(corner, branch_ref, PIECES, comm[22:])
    size, width = resid1_ref.shape
    ff = up_ref.shape[1]

    def view(step):
        return table_ref.at[rows_of(corner.block(step), size)]

    tail[...] = view(0)[...].astype(WIDE)
    small.give(0, tail)
    tail[...] = view(1)[...].astype(WIDE)
    small.cross(tail)
    tail[...] = view(2)[...].astype(WIDE)
    small.give(1, tail)
    tail[...] = view(3)[...].astype(WIDE)
    own_gauss = small.land(0, tail).astype(LOW)
    gauss[spread.part(corner.me, 0)] = own_gauss
    spread.start(0)
    unpatch_ref[...] = dot(low_ref[...], own_gauss, TN)
    spread.relay(0)
    spread.finish()
    small.close()
    loads.wait(0, 1)

    @pl.loop(0, 4)
    def _(step):
        here = rows_of(corner.block(step), size)
        load_hidden(step).wait()
        term[...] = dot(gauss[here], cols_ref[...], NT)
        down_in[here] = term[...].astype(LOW)

        @pl.when(step == 3)
        def _():
            resid_grad_ref[...] = term[...]

        def columns(cols):
            active_grad = dot(down_in[here], down_ref[cols, :], NT)
            hidden = hidden_ref[here, cols]
            slope = 0.5 * (1.0 + lax.erf(hidden * ROOT_HALF)) + hidden * (jnp.exp(-0.5 * hidden * hidden) * NORMAL_PEAK)
            hidden_grad[here, cols] = (active_grad * slope).astype(LOW)

        column_loop(ff, columns)

        def back(cols):
            term[:, cols] = dot(hidden_grad[here], up_ref[cols, :], NT)

        column_loop(width, back)
        scatter.step(step, term)

    side = None if chunk is None else lax.rem(lax.axis_index("dp"), 2)

    def store(at, act):
        part = pl.ds(pl.multiple_of(at * UNIT, UNIT), UNIT)

        def wide():
            getattr(pltpu.make_async_copy(grad_ref.at[part], grad_out.at[part], store_sem.at[at]), act)()

        def rounded():
            getattr(pltpu.make_async_copy(rounded_ref.at[part], rounded_out.at[part], store_sem.at[at]), act)()

        if chunk is None:
            wide()
            return
        mine = lax.rem(at * UNIT // chunk, 2) == side
        pl.when(mine)(wide)
        pl.when(jnp.logical_not(mine))(rounded)

    def keep(tile, value):
        part = pl.ds(pl.multiple_of(tile * TILE, TILE), TILE)
        grad_ref[part, :] = value
        rounded_ref[part, :] = value.astype(LOW)
        for at in range(TILE // UNIT):
            store(tile * (TILE // UNIT) + at, "start")

    loads.wait(2, 3)
    tiles = attended_ref.shape[1] // TILE

    @pl.loop(0, width // TILE)
    def _(tile):
        cols = pl.ds(pl.multiple_of(tile * TILE, TILE), TILE)
        keep(tiles + tile, dot(normed2_ref[:, cols], hidden_grad[...], TN))

    @pl.loop(0, ff // TILE)
    def _(tile):
        cols = pl.ds(pl.multiple_of(tile * TILE, TILE), TILE)
        keep(tiles + width // TILE + tile, dot(active_ref[:, cols], down_in[...], TN))

    gain_sum, bias_sum = jnp.zeros((1, width), WIDE), jnp.zeros((1, width), WIDE)
    for piece in range(PIECES):
        part = scatter.part(piece)
        grad = scatter.land(piece, term)
        scaled, inverse = standard(resid1_ref[part])
        total = resid_grad_ref[part] + norm_back(grad, scaled, inverse, norm_ref[2:3])
        resid_grad_ref[part] = total
        branch_ref[gather.part(corner.me, piece)] = total.astype(LOW)
        gather.start(piece)
        gain_sum += jnp.sum(grad * scaled, 0, keepdims=True)
        bias_sum += jnp.sum(grad, 0, keepdims=True)
    gain_ref[0:1] = gain_sum
    gain_ref[1:2] = bias_sum
    for piece in range(PIECES):
        gather.relay(piece)
    gather.finish()
    scatter.close()

    for tile in range(tiles):
        keep(tile, dot(attended_ref[:, tile * TILE : (tile + 1) * TILE], branch_ref[...], TN))

    @pl.loop(0, grad_ref.shape[0] // UNIT)
    def _(at):
        store(at, "wait")


def mlp_back(table_grad, used_cols, low, active, hidden, normed2, weights, resid1, norm, attended, chunk, collective_id):
    length, size, width = normed2.shape[0], resid1.shape[0], resid1.shape[1]
    ff, used = hidden.shape[1], used_cols.shape[1]
    total = attended.shape[1] + width + ff
    shape = jax.ShapeDtypeStruct
    return pl.pallas_call(
        partial(mlp_back_kernel, chunk),
        out_shape=(
            shape((width, used), WIDE),
            shape((total, width), WIDE),
            shape((total, width), LOW),
            shape((size, width), WIDE),
            shape((length, width), LOW),
            shape((2, width), WIDE),
        ),
        in_specs=[VMEM] * 3 + [HBM] * 4 + [VMEM] * 3,
        out_specs=(VMEM, HBM, HBM, VMEM, VMEM, VMEM),
        scratch_shapes=[
            pltpu.VMEM((length, used), LOW),
            pltpu.VMEM((length, width), LOW),
            pltpu.VMEM((length, ff), LOW),
            pltpu.VMEM((size, width), WIDE),
            pltpu.VMEM((size, used), WIDE),
            pltpu.VMEM((length, ff), LOW),
            pltpu.VMEM((length, ff), WIDE),
            pltpu.VMEM((length, width), LOW),
            pltpu.VMEM((width, ff), LOW),
            pltpu.VMEM((ff, width), LOW),
            pltpu.VMEM((total, width), WIDE),
            pltpu.VMEM((total, width), LOW),
            pltpu.SemaphoreType.DMA((8,)),
            pltpu.SemaphoreType.DMA((total // UNIT,)),
        ]
        + Scatter.scratch(size, used, 1)
        + Gather.scratch(1)
        + Scatter.scratch(size, width, PIECES)
        + Gather.scratch(PIECES),
        compiler_params=pltpu.CompilerParams(
            collective_id=collective_id, has_side_effects=True, vmem_limit_bytes=63 * 2**20
        ),
    )(table_grad, used_cols, low, active, hidden, normed2, weights, resid1, norm, attended)


class LineSum:
    def __init__(self, spot, pieces, low, source, buffers, sems, first=0, turns=4, stored=None):
        self.spot, self.pieces, self.low, self.source = spot, pieces, low, source
        self.first, self.turns, self.stored = first, turns, stored
        self.pair_out, self.pair_in, self.part, self.line_in, self.low_out, self.low_in = buffers
        self.p_send, self.p_recv, self.l_send, self.up_recv, self.down_recv = sems
        self.count = turns * pieces
        self.rows = self.part.shape[0] // self.count

    @staticmethod
    def scratch(turns, rows, pieces, width, low, stored=False):
        half = (turns * rows, width)
        kept = half if low else (rows, width)
        kind = LOW if low else WIDE
        return [
            pltpu.VMEM((16, 128) if stored else half, LOW),
            pltpu.VMEM(half, LOW),
            pltpu.VMEM(half, WIDE),
            pltpu.VMEM(half, WIDE),
            pltpu.VMEM(half if low else (16, 128), LOW),
            pltpu.VMEM(kept, kind),
        ] + [pltpu.SemaphoreType.DMA((turns * pieces,))] * 5

    def target(self, step):
        turn = lax.rem(step, self.turns)
        if self.turns == 4:
            odd = lax.rem(turn, 2)
            return (1 - odd) * (3 - turn // 2) + odd * (turn // 2)
        if self.turns == 3:
            return self.first + 2 - 2 * jnp.minimum(turn, 1) + turn - jnp.minimum(turn, 1)
        return self.first + turn

    def stored_rows(self, step, side):
        start = ((self.target(step) - self.first) * 2 + side) * self.pieces + step // self.turns
        return pl.ds(pl.multiple_of(start * self.rows, 16), self.rows)

    def slot(self, step):
        return pl.ds(pl.multiple_of(step * self.rows, 16), self.rows)

    def pair_copy(self, step):
        slot = self.slot(step)
        if self.stored:
            sent = self.stored[1].at[self.stored_rows(step, 1 - self.spot.side)]
            return remote(sent, self.pair_in.at[slot], self.p_send.at[step], self.p_recv.at[step], self.spot.pair)
        return remote(self.pair_out.at[slot], self.pair_in.at[slot], self.p_send.at[step], self.p_recv.at[step], self.spot.pair)

    def line_copy(self, step, to, recv):
        slot = self.slot(step)
        return remote(self.part.at[slot], self.line_in.at[slot], self.l_send.at[step], recv.at[step], to)

    def low_copy(self, step, to, recv):
        slot = self.slot(step)
        return remote(self.low_out.at[slot], self.low_in.at[slot], self.l_send.at[step], recv.at[step], to)

    def last_copy(self, step):
        here = pl.ds(pl.multiple_of(step // self.turns * self.rows, 16), self.rows)
        return remote(self.part.at[self.slot(step)], self.low_in.at[here], self.l_send.at[step], self.down_recv.at[step], self.spot.below)

    def own_copy(self, step):
        own = self.stored[0].at[self.stored_rows(step, self.spot.side)]
        return pltpu.make_async_copy(own, self.part.at[self.slot(step)], self.stored[2].at[step])

    def begin(self, step):
        if self.stored:
            self.pair_copy(step).start()
            self.own_copy(step).start()
            return
        self.pair_out[self.slot(step)] = self.source(self.target(step), 1 - self.spot.side, step // self.turns).astype(LOW)
        self.pair_copy(step).start()

    def add(self, step, low):
        slot = self.slot(step)
        self.part[slot] += self.low_in[slot].astype(WIDE) if low else self.line_in[slot]

    def low_hop(self, rising, target):
        line, last = self.spot.line, self.spot.lines - 1
        if rising:
            top = target == last
            return (line == 0) | ((line == 1) & top), (line == 1) | ((line == 2) & top)
        return line == last, line == last - 1

    def travel(self, step, rising):
        spot, slot = self.spot, self.slot(step)
        to, recv = (spot.above, self.up_recv) if rising else (spot.below, self.down_recv)
        last = spot.lines - 1
        at_end = spot.line == (0 if rising else last)
        target = self.target(step)
        if self.low:
            low_sent, low_taken = self.low_hop(rising, target)

            @pl.when(jnp.logical_not(at_end) & low_taken)
            def _():
                self.low_copy(step, to, recv).wait_recv()
                self.add(step, True)

            @pl.when(jnp.logical_not(at_end | low_taken))
            def _():
                self.line_copy(step, to, recv).wait_recv()
                self.add(step, False)

            @pl.when(low_sent)
            def _():
                self.low_out[slot] = self.part[slot].astype(LOW)
                self.low_copy(step, to, recv).start()

            @pl.when(jnp.logical_not(low_sent))
            def _():
                self.line_copy(step, to, recv).start()
        else:

            @pl.when(jnp.logical_not(at_end))
            def _():
                self.line_copy(step, to, recv).wait_recv()
                self.add(step, False)

            if rising:
                self.line_copy(step, to, recv).start()
            else:

                @pl.when(target == spot.line - 1)
                def _():
                    self.last_copy(step).start()

                @pl.when(target < spot.line - 1)
                def _():
                    self.line_copy(step, to, recv).start()

    def advance(self, step):
        spot = self.spot

        @pl.when(step < self.count)
        def _():
            slot = self.slot(step)
            self.pair_copy(step).wait_recv()
            if self.stored:
                self.own_copy(step).wait()
                self.part[slot] += self.pair_in[slot].astype(WIDE)
                return
            own = self.source(self.target(step), spot.side, step // self.turns)
            self.part[slot] = own + self.pair_in[slot].astype(WIDE)

        rising = step - spot.line

        @pl.when((rising >= 0) & (rising < self.count) & (self.target(rising) > spot.line))
        def _():
            self.travel(rising, True)

        falling = step - (spot.lines - 1 - spot.line)

        @pl.when((falling >= 0) & (falling < self.count) & (self.target(falling) < spot.line))
        def _():
            self.travel(falling, False)

    def close(self, step, give):
        spot, slot = self.spot, self.slot(step)
        target = self.target(step)
        last = spot.lines - 1
        self.pair_copy(step).wait_send()

        @pl.when(target > spot.line)
        def _():
            if self.low:

                low_sent, low_taken = self.low_hop(True, target)

                @pl.when(low_sent)
                def _():
                    self.low_copy(step, spot.above, self.up_recv).wait_send()

                @pl.when(jnp.logical_not(low_sent))
                def _():
                    self.line_copy(step, spot.above, self.up_recv).wait_send()
            else:
                self.line_copy(step, spot.above, self.up_recv).wait_send()

        @pl.when(target < spot.line)
        def _():
            if self.low:

                @pl.when(spot.line == last)
                def _():
                    self.low_copy(step, spot.below, self.down_recv).wait_send()

                @pl.when(spot.line < last)
                def _():
                    self.line_copy(step, spot.below, self.down_recv).wait_send()
            else:
                self.line_copy(step, spot.below, self.down_recv).wait_send()

        @pl.when(target == spot.line)
        def _():
            if self.low:

                @pl.when(spot.line == 1)
                def _():
                    self.low_copy(step, spot.above, self.up_recv).wait_recv()
                    self.add(step, True)

                @pl.when(spot.line > 1)
                def _():
                    self.line_copy(step, spot.above, self.up_recv).wait_recv()
                    self.add(step, False)

                @pl.when(spot.line == last - 1)
                def _():
                    self.low_copy(step, spot.below, self.down_recv).wait_recv()
                    self.add(step, True)

                @pl.when(spot.line < last - 1)
                def _():
                    self.line_copy(step, spot.below, self.down_recv).wait_recv()
                    self.add(step, False)
            else:

                @pl.when(spot.has_below)
                def _():
                    self.line_copy(step, spot.above, self.up_recv).wait_recv()
                    self.add(step, False)

                @pl.when(spot.has_above)
                def _():
                    self.last_copy(step).wait_recv()
                    here = pl.ds(pl.multiple_of(step // self.turns * self.rows, 16), self.rows)
                    self.part[slot] += self.low_in[here]

            give(step // self.turns, self.part[slot])


def attend_back_kernel(parts, q_rows, lines, count_ref, branch_ref, weight_ref, qkv_ref, log_ref, normed1_in, embed_ref,
                       resid_grad_ref, norm_ref, *rest):
    late_in, rest = (rest[:2], rest[2:]) if lines else ((), rest)
    grad_ref, embed_grad, gain_ref = rest[:3]
    own_late, rest = (rest[3], rest[4:]) if lines else (None, rest[3:])
    qkv_proj, attended_grad, qkv_grad, key_grad, value_grad, term, held, normed1_ref, load_sem = rest[:9]
    comm, late_comm = rest[9:17], rest[17:]
    loads = Moves(load_sem, (weight_ref.at[pl.ds(0, held.shape[0])], held), (normed1_in, normed1_ref))
    loads.start()
    corner = Corner()
    size, width = embed_ref.shape
    length, local = qkv_ref.shape[0], qkv_ref.shape[1] // 3
    if lines:
        spot = Lines(lines)
        barrier = pltpu.get_barrier_semaphore()
        for other in (corner.mate, corner.far):
            pl.semaphore_signal(barrier, inc=1, device_id={"tensor": other}, device_id_type=MESH)
        pl.semaphore_wait(barrier, 2 + spot.signal(barrier))
        late = LineSum(
            spot, SUM_PIECES, True, None, late_comm[:6], late_comm[6:11], 1, lines - 1, late_in + (late_comm[11],)
        )

        @pl.loop(0, late.count)
        def _(step):
            late.begin(step)

    else:
        corner.greet()
    scatter = Scatter(corner, PIECES, *comm)
    packed_ref, out_ref = held.at[pl.ds(0, 3 * local)], held.at[pl.ds(3 * local, local)]
    loads.wait(0)
    unpack_into(qkv_proj, packed_ref, parts)

    @pl.loop(0, 4)
    def _(block):
        here = rows_of(block, size)
        attended_grad[here] = dot(branch_ref[here], out_ref[...], NT).astype(LOW)

    key_grad[...] = jnp.zeros_like(key_grad)
    value_grad[...] = jnp.zeros_like(value_grad)
    valid = lax.broadcasted_iota(jnp.int32, (1, length), 1) < count_ref[0] * VTOK
    left = lax.broadcasted_iota(jnp.int32, (1, 2 * DH), 1) < DH
    factor = jnp.array(DH ** (-0.5), LOW)

    @pl.loop(0, length // q_rows)
    def _(turn):
        here = rows_of(turn, q_rows)
        for pair in range(local // (2 * DH)):
            lanes = slice(pair * 2 * DH, (pair + 1) * 2 * DH)
            queries = qkv_ref[here, lanes] * factor
            grads = attended_grad[here, lanes]
            keyset = qkv_ref[:, local + pair * 2 * DH : local + (pair + 1) * 2 * DH]
            values = qkv_ref[:, 2 * local + pair * 2 * DH : 2 * local + (pair + 1) * 2 * DH]
            found = []
            for side in range(2):
                mine = left if side == 0 else ~left
                own_query = jnp.where(mine, queries, jnp.zeros_like(queries))
                own_grad = jnp.where(mine, grads, jnp.zeros_like(grads))
                scores = jnp.where(valid, dot(own_query, keyset, NT), masked_score)
                probs = jnp.exp(scores - log_ref[here, pair * 2 + side : pair * 2 + side + 1])
                prob_grad = dot(own_grad, values, NT)
                value_grad[:, lanes] += dot(probs.astype(LOW), own_grad, TN)
                centre = jnp.sum(probs * prob_grad, -1, keepdims=True)
                score_grad = (probs * (prob_grad - centre)).astype(LOW)
                found.append(dot(score_grad, keyset))
                key_grad[:, lanes] += dot(score_grad, own_query, TN)
            qkv_grad[here, lanes] = (jnp.where(left, found[0], found[1]) * (DH ** (-0.5))).astype(LOW)
        if lines:

            @pl.loop(0, 2)
            def _(at):
                late.advance(2 * turn + at)

    qkv_grad[:, local : 2 * local] = key_grad[...].astype(LOW)
    qkv_grad[:, 2 * local :] = value_grad[...].astype(LOW)

    @pl.loop(0, 4)
    def _(step):
        here = rows_of(corner.block(step), size)

        def columns(cols):
            term[:, cols] = dot(qkv_grad[here], qkv_proj[cols, :], NT)

        column_loop(width, columns)
        scatter.step(step, term)
        if lines:
            late.advance(12 + step)

    loads.wait(1)
    for tile in range(width // TILE):
        value = dot(normed1_ref[:, tile * TILE : (tile + 1) * TILE], qkv_grad[...], TN)
        for row, rows, col, cols, at, at_col in qkv_places(parts, width, 3 * local):
            if at // TILE == tile:
                at = at % TILE
                grad_ref[row : row + rows, col : col + cols] = value[at : at + rows, at_col : at_col + cols]
    if lines:

        @pl.loop(16, 20)
        def _(step):
            late.advance(step)

    gain_sum, bias_sum = jnp.zeros((1, width), WIDE), jnp.zeros((1, width), WIDE)
    for piece in range(PIECES):
        part = scatter.part(piece)
        grad = scatter.land(piece, term)
        scaled, inverse = standard(embed_ref[part])
        embed_grad[part] = (resid_grad_ref[part] + norm_back(grad, scaled, inverse, norm_ref[0:1])).astype(LOW)
        gain_sum += jnp.sum(grad * scaled, 0, keepdims=True)
        bias_sum += jnp.sum(grad, 0, keepdims=True)
    gain_ref[0:1] = gain_sum
    gain_ref[1:2] = bias_sum
    scatter.close()
    if lines:

        @pl.loop(20, late.count + lines - 1)
        def _(step):
            late.advance(step)

        def keep_rows(piece, value):
            own_late[pl.ds(pl.multiple_of(piece * late.rows, 16), late.rows)] = value

        @pl.loop(0, late.count)
        def _(step):
            late.close(step, keep_rows)


def attend_back(count, branch, weights, qkv, log_total, normed1, embed, resid_grad, norm, late, parts, lines, collective_id):
    length, local = qkv.shape[0], qkv.shape[1] // 3
    size, width = embed.shape
    shape = jax.ShapeDtypeStruct
    chunk = 3 * width // (2 * lines) if lines else 0
    return pl.pallas_call(
        partial(attend_back_kernel, parts, 256, lines),
        out_shape=(
            shape((3 * local, width), WIDE),
            shape((size, width), LOW),
            shape((2, width), WIDE),
        )
        + ((shape((chunk, width), WIDE),) if lines else ()),
        in_specs=[pl.BlockSpec(memory_space=pltpu.SMEM), VMEM, HBM, VMEM, VMEM, HBM, VMEM, VMEM, VMEM] + [HBM] * len(late),
        out_specs=(VMEM,) * (4 if lines else 3),
        scratch_shapes=[
            pltpu.VMEM((width, 3 * local), LOW),
            pltpu.VMEM((length, local), LOW),
            pltpu.VMEM((length, 3 * local), LOW),
            pltpu.VMEM((length, local), WIDE),
            pltpu.VMEM((length, local), WIDE),
            pltpu.VMEM((size, width), WIDE),
            pltpu.VMEM((4 * local, width), LOW),
            pltpu.VMEM((length, width), LOW),
            pltpu.SemaphoreType.DMA((2,)),
        ]
        + Scatter.scratch(size, width, PIECES)
        + (
            LineSum.scratch(lines - 1, chunk, SUM_PIECES, width, True, True)
            + [pltpu.SemaphoreType.DMA(((lines - 1) * SUM_PIECES,))]
            if lines
            else []
        ),
        compiler_params=pltpu.CompilerParams(
            collective_id=collective_id, has_side_effects=True, vmem_limit_bytes=63 * 2**20
        ),
    )(count, branch, weights, qkv, log_total, normed1, embed, resid_grad, norm, *late)


SUM_PIECES = 6


def share_kernel(lines, early_ref, late_ref, embed_ref, own_patch_ref, used_ref, gain_ref, loss_ref, label_ref,
                 row_ref, shared_out, total_ref,
                 term, windows, mine, slots, rows_out, patch_ref, shared_ref, *comm):
    corner, spot = Corner(), Lines(lines)
    pairs, width = 2 * lines, early_ref.shape[1]
    quarters = 4
    count = pairs * quarters
    me = spot.me * quarters + corner.me
    barrier = pltpu.get_barrier_semaphore()

    def peer(step):
        other = lax.rem(me + step, count)
        return {"dp": other // quarters, "tensor": lax.rem(other, quarters)}

    @pl.loop(1, count)
    def _(step):
        pl.semaphore_signal(barrier, inc=1, device_id=peer(step), device_id_type=MESH)

    pl.semaphore_wait(barrier, count - 1)
    chunk = late_ref.shape[0]
    rows = chunk // SUM_PIECES

    def weight_term(line, side, piece):
        return early_ref[pl.ds(pl.multiple_of(side * chunk + piece * rows, 8), rows)]

    def shared_term(line, side, piece):
        return mine[pl.ds(pl.multiple_of(window_row(line * 2 + side), 16), WINDOW)]

    weights = LineSum(spot, SUM_PIECES, True, weight_term, comm[0:6], comm[6:11], 0, 1)
    shared = LineSum(spot, 1, False, shared_term, comm[11:17], comm[17:22])
    scatter = Scatter(corner, PIECES, *comm[22:30])
    gather = Gather(corner, windows, 1, comm[30:36])
    own_sem, send_sem, recv_sem = comm[36:39]

    @pl.loop(0, weights.count)
    def _(step):
        weights.begin(step)

    patch_ref[...] = dot(own_patch_ref[...], embed_ref[...], TN)

    @pl.loop(0, 4)
    def _(step):
        block = corner.block(step)
        term[...] = jnp.zeros_like(term)

        def rows_at(start, size):
            return pl.ds(pl.multiple_of(start, 16), size)

        for owner in range(3):
            at = owner * WINDOW
            term[at : at + WINDOW] = patch_ref[rows_at(ROW_START[owner] + block * WINDOW, WINDOW)]

        @pl.when(block < 3)
        def _():
            at = 3 * WINDOW
            term[at : at + 16] = patch_ref[rows_at(ROW_START[3] + block * 32, 16)]

            @pl.when(block < 2)
            def _():
                term[at + 16 : at + 32] = patch_ref[rows_at(ROW_START[3] + block * 32 + 16, 16)]

            for j in range(3):
                term[at + 32 : at + 48, j * 128 : (j + 1) * 128] = used_ref[rows_at(block * 48 + 16 * j, 16)]

        for owner in range(4, 8):
            at = window_row(owner)
            for j in range(4):

                @pl.when((block < 3) | (owner < 7) | (j < 2))
                def _():
                    term[at : at + SHORT, j * 128 : (j + 1) * 128] = used_ref[
                        rows_at(USED_START[owner] + block * 64 + SHORT * j, SHORT)
                    ]

        @pl.when(block == 0)
        def _():
            for row in range(8):
                at = window_row(7) + row
                term[at : at + 1, width // 2 :] = gain_ref[row // 2 : row // 2 + 1, row % 2 * width // 2 : (row % 2 + 1) * width // 2]

        scatter.step(step, term)

    @pl.loop(0, 2)
    def _(step):
        weights.advance(step)

    for piece in range(PIECES):
        mine[scatter.part(piece)] = scatter.land(piece, term)

    @pl.loop(0, lines)
    def _(step):
        shared.begin(step)

    @pl.loop(0, 2 * lines - 1)
    def _(step):
        weights.advance(2 + step)
        shared.advance(step)

    def keep_window(piece, value):
        windows[gather.part(corner.me, 0)] = value

    @pl.loop(0, lines)
    def _(step):
        shared.close(step, keep_window)

    gather.start(0)

    def keep_rows(piece, value):
        rows_out[pl.ds(pl.multiple_of(piece * rows, rows), rows)] = value

    @pl.loop(0, weights.count)
    def _(step):
        weights.close(step, keep_rows)

    @pl.when(spot.line > 0)
    def _():
        rows_out[...] = late_ref[...]

    window = jnp.where(window_valid(spot.me, corner.me, width), windows[gather.part(corner.me, 0)], 0.0)
    square = jnp.sum(window * window) + jnp.sum(rows_out[...] * rows_out[...])
    counted = jnp.sum(jnp.where(label_ref[...] < 2, 1.0, 0.0))
    line = lax.broadcasted_iota(jnp.int32, total_ref.shape, 0)
    slots[me] = jnp.where(line == 0, square, jnp.where(line == 1, loss_ref[...], jnp.where(line == 2, counted, 0.0)))

    def send(step):
        return remote(slots.at[me], slots.at[me], send_sem.at[step], recv_sem.at[step], peer(step))

    def arrive(step):
        source = lax.rem(me - step + count, count)
        return remote(slots.at[source], slots.at[source], send_sem.at[step], recv_sem.at[step], peer(step))

    @pl.loop(1, count)
    def _(step):
        send(step).start()

    gather.relay(0)

    @pl.when(spot.me < lines // 2)
    def _():
        for row, height, col, cols, at, at_col in qkv_places(1, chunk * 4 // 3, width * 3 // 4):
            for j in range(cols // 128):
                row_ref[pl.ds(6 * at + at_col // 128 + j, height, 6)] = rows_out[
                    row : row + height, col + j * 128 : col + (j + 1) * 128
                ]

    @pl.when(spot.me >= lines // 2)
    def _():
        for j in range(8):
            row_ref[pl.ds(j, chunk, 8)] = rows_out[:, j * 128 : (j + 1) * 128]

    gather.finish()
    shared_ref[...] = jnp.zeros_like(shared_ref)
    for phase in range(5):

        @pl.loop(0, 4)
        def _(quarter):
            def take(condition, row, height, j, start, stride):
                @pl.when(condition)
                def _():
                    here = pl.ds(pl.multiple_of(quarter * WINDOW + row, 16), height)
                    shared_ref[pl.ds(start, height, stride)] = windows[here, j * 128 : (j + 1) * 128]

            shared_walk(spot.me, quarter, take, (phase,))

    shared_out[...] = shared_ref[FRONT : FRONT + SHARED_LANES]

    @pl.loop(1, count)
    def _(step):
        arrive(step).wait_recv()

    total_ref[...] = jnp.sum(slots[...], 0)

    @pl.loop(1, count)
    def _(step):
        send(step).wait_send()

    scatter.close()


def share(early, late, embed_grad, patches, used_grad, gains, loss_tile, labels, lines, collective_id):
    width = early.shape[1]
    chunk = late.shape[0]
    packed = 4 * WINDOW + (2 * lines - 4) * SHORT
    count = 8 * lines
    shape = jax.ShapeDtypeStruct
    return pl.pallas_call(
        partial(share_kernel, lines),
        out_shape=(shape((chunk * width // 128, 128), WIDE), shape((SHARED_LANES, 128), WIDE), shape((8, 128), WIDE)),
        in_specs=[VMEM] * 8,
        out_specs=(VMEM,) * 3,
        scratch_shapes=[
            pltpu.VMEM((packed, width), WIDE),
            pltpu.VMEM((4 * WINDOW, width), WIDE),
            pltpu.VMEM((packed + WINDOW - SHORT, width), WIDE),
            pltpu.VMEM((count, 8, 128), WIDE),
            pltpu.VMEM((chunk, width), WIDE),
            pltpu.VMEM((patches.shape[1], width), WIDE),
            pltpu.VMEM((PADDED, 128), WIDE),
        ]
        + LineSum.scratch(1, chunk, SUM_PIECES, width, True)
        + LineSum.scratch(lines, WINDOW, 1, width, False)
        + Scatter.scratch(packed, width, PIECES)
        + Gather.scratch(1)
        + [
            pltpu.SemaphoreType.DMA(()),
            pltpu.SemaphoreType.DMA((count,)),
            pltpu.SemaphoreType.DMA((count,)),
        ],
        compiler_params=pltpu.CompilerParams(
            collective_id=collective_id, has_side_effects=True, vmem_limit_bytes=63 * 2**20
        ),
    )(early, late, embed_grad, patches, used_grad, gains, loss_tile, labels)


def render_kernel(area, wide, block, split, span, table_ref, splat_ref, dist_ref, label_ref, loss_ref, grad_ref, flip, hot, weighted, spread_grad):
    tokens = table_ref.shape[0]
    groups = tokens // wide
    splats, pixels = splat_ref.shape
    for j in range(groups):
        flip[j * 2 * area : (j + 1) * 2 * area] = jnp.transpose(table_ref[j * wide : (j + 1) * wide].astype(jnp.float32)).astype(jnp.bfloat16)
    spread_grad[...] = jnp.zeros_like(spread_grad)
    wide_ids = lax.broadcasted_iota(jnp.int32, (wide, block), 0).astype(jnp.float32).astype(jnp.bfloat16)
    cell_ids = lax.broadcasted_iota(jnp.int32, (area, block), 0).astype(jnp.float32)
    cell_low = cell_ids.astype(jnp.bfloat16)
    one, nil = jnp.ones((wide, block), jnp.bfloat16), jnp.zeros((wide, block), jnp.bfloat16)

    def one_block(step, loss):
        here = pl.ds(pl.multiple_of(step * block, block), block)
        opacities, spreads, lows = [], [], []
        for k in range(splats):
            index = splat_ref[k : k + 1, here]
            token = index // area
            column = (token % wide).astype(jnp.float32).astype(jnp.bfloat16)
            lows.append((token // wide, (index % area).astype(jnp.float32)))
            hot[:, k * block : (k + 1) * block] = jnp.where(wide_ids == column, one, nil)
        for k in range(splats):
            lanes = slice(k * block, (k + 1) * block)
            group, cell = lows[k]
            op_sum = jnp.zeros((area, block), jnp.float32)
            sp_sum = jnp.zeros((area, block), jnp.float32)
            for at in range(0, groups, span):
                rows = slice(at * 2 * area, (at + span) * 2 * area)
                found = lax.dot_general(flip[rows], hot[:, lanes], NN, preferred_element_type=jnp.float32)
                for j in range(span):
                    same = cell_ids == jnp.where(group == at + j, cell, -1.0)
                    op_sum += jnp.where(same, found[j * 2 * area : j * 2 * area + area], 0.0)
                    sp_sum += jnp.where(same, found[j * 2 * area + area : (j + 1) * 2 * area], 0.0)
            opacities.append(jnp.sum(op_sum, 0, keepdims=True))
            spreads.append(jnp.sum(sp_sum, 0, keepdims=True))
        opacity, spread = jnp.concatenate(opacities, 0), jnp.concatenate(spreads, 0)
        distance = dist_ref[:, here].astype(jnp.float32)
        labels = label_ref[:, here]
        valid = jnp.where(labels < 2, 1.0, 0.0)
        target = jnp.where(labels == 1, 1.0, 0.0)
        op_sig, sp_sig = jax.nn.sigmoid(opacity), jax.nn.sigmoid(spread)
        fade = jnp.exp(-0.25 * distance * sp_sig)
        contrib = (0.02 + 0.96 * op_sig) * fade
        keep_log = jnp.sum(jnp.log1p(-contrib), 0, keepdims=True)
        keep = jnp.exp(keep_log)
        alpha = 1.0 - keep
        alpha_log = jnp.log(alpha)
        loss = loss - valid * (target * alpha_log + (1.0 - target) * keep_log)
        keep_grad = valid * (target * keep / alpha - (1.0 - target))
        contrib_grad = -keep_grad / (1.0 - contrib)
        op_grad = contrib_grad * (0.96 * op_sig * (1.0 - op_sig)) * fade
        sp_grad = contrib_grad * contrib * (-0.25 * distance * sp_sig * (1.0 - sp_sig))
        zero = jnp.zeros((area, block), jnp.bfloat16)
        op_parts, sp_parts = [], []
        for part in range(split):
            op_parts.append(op_grad.astype(jnp.bfloat16))
            sp_parts.append(sp_grad.astype(jnp.bfloat16))
            op_grad, sp_grad = op_grad - op_parts[-1].astype(jnp.float32), sp_grad - sp_parts[-1].astype(jnp.float32)
        for at in range(0, groups, span):
            rows = slice(at * 2 * area, (at + span) * 2 * area)
            for k in range(splats):
                lanes = slice(k * block, (k + 1) * block)
                group, cell = lows[k]
                for j in range(span):
                    same = cell_low == jnp.where(group == at + j, cell, -1.0).astype(jnp.bfloat16)
                    first = (at + j) * 2 * area
                    for part in range(split):
                        weighted[part, first : first + area, lanes] = jnp.where(same, op_parts[part][k : k + 1], zero)
                        weighted[part, first + area : first + 2 * area, lanes] = jnp.where(same, sp_parts[part][k : k + 1], zero)
            total = spread_grad[rows]
            for part in range(split):
                total += lax.dot_general(weighted[part, rows], hot[...], NT, preferred_element_type=jnp.float32)
            spread_grad[rows] = total
        return loss

    loss = lax.fori_loop(0, pixels // block, one_block, jnp.zeros((1, block), jnp.float32))
    loss_ref[...] = jnp.broadcast_to(jnp.sum(loss, 1, keepdims=True), loss_ref.shape)
    for j in range(groups):
        grad_ref[j * wide : (j + 1) * wide] = jnp.transpose(spread_grad[j * 2 * area : (j + 1) * 2 * area]).astype(grad_ref.dtype)

def render(table, splats, distance, labels, area, block=768, wide=256, split=2, span=3):
    tokens = table.shape[0]
    vm = pl.BlockSpec(memory_space=pltpu.VMEM)
    groups = tokens // wide
    count = splats.shape[0]
    return pl.pallas_call(
        partial(render_kernel, area, wide, block, split, span),
        out_shape=(jax.ShapeDtypeStruct((8, 128), jnp.float32), jax.ShapeDtypeStruct(table.shape, jnp.bfloat16)),
        in_specs=[vm] * 4, out_specs=(vm, vm),
        scratch_shapes=[pltpu.VMEM((groups * 2 * area, wide), jnp.bfloat16),
            pltpu.VMEM((wide, count * block), jnp.bfloat16), pltpu.VMEM((split, groups * 2 * area, count * block), jnp.bfloat16), pltpu.VMEM((groups * 2 * area, wide), jnp.float32)],
        compiler_params=pltpu.CompilerParams(vmem_limit_bytes=60 * 2**20),
    )(table, splats, distance, labels)


def owner_sum_kernel(lines, pieces, g_ref, o_ref, pair_out, pair_in, part, line_in, own_in, p_send, p_recv, l_send, up_recv, down_recv):
    me = lax.axis_index("dp")
    line, side = me // 2, lax.rem(me, 2)
    chunk = o_ref.shape[0]
    rows = chunk // pieces
    count = lines * pieces
    pair = {"dp": line * 2 + 1 - side}
    above = {"dp": lax.rem(line + 1, lines) * 2 + side}
    below = {"dp": lax.rem(line + lines - 1, lines) * 2 + side}
    has_below, has_above = line > 0, line < lines - 1

    def target(step):
        turn = lax.rem(step, lines)
        odd = lax.rem(turn, 2)
        return (1 - odd) * (lines - 1 - turn // 2) + odd * (turn // 2)

    def slot(step):
        return pl.ds(pl.multiple_of(step * rows, rows), rows)

    def here(step):
        return pl.ds(pl.multiple_of(step // lines * rows, rows), rows)

    def source(step, owner):
        return pl.ds(pl.multiple_of((target(step) * 2 + owner) * chunk + step // lines * rows, rows), rows)

    def copy(src, dst, send, recv, to):
        return pltpu.make_async_remote_copy(
            src_ref=src, dst_ref=dst, send_sem=send, recv_sem=recv, device_id=to, device_id_type=MESH
        )

    def pair_copy(step):
        return copy(pair_out.at[slot(step)], pair_in.at[slot(step)], p_send.at[step], p_recv.at[step], pair)

    def line_copy(step, to, recv):
        return copy(part.at[slot(step)], line_in.at[slot(step)], l_send.at[step], recv.at[step], to)

    def last_copy(step):
        return copy(part.at[slot(step)], own_in.at[here(step)], l_send.at[step], down_recv.at[step], below)

    barrier = pltpu.get_barrier_semaphore()
    pl.semaphore_signal(barrier, inc=1, device_id=pair, device_id_type=MESH)

    @pl.when(has_below)
    def _():
        pl.semaphore_signal(barrier, inc=1, device_id=below, device_id_type=MESH)

    @pl.when(has_above)
    def _():
        pl.semaphore_signal(barrier, inc=1, device_id=above, device_id_type=MESH)

    pl.semaphore_wait(barrier, 1 + jnp.minimum(line, 1) + jnp.minimum(lines - 1 - line, 1))

    @pl.loop(0, count)
    def _(step):
        pair_out[slot(step)] = g_ref[source(step, 1 - side)].astype(jnp.bfloat16)
        pair_copy(step).start()

    @pl.loop(0, count + lines - 1)
    def _(step):
        @pl.when(step < count)
        def _():
            pair_copy(step).wait_recv()
            part[slot(step)] = g_ref[source(step, side)].astype(jnp.float32) + pair_in[slot(step)].astype(jnp.float32)

        rising = step - line

        @pl.when((rising >= 0) & (rising < count) & (target(rising) > line))
        def _():
            @pl.when(has_below)
            def _():
                line_copy(rising, above, up_recv).wait_recv()
                part[slot(rising)] += line_in[slot(rising)]

            line_copy(rising, above, up_recv).start()

        falling = step - (lines - 1 - line)

        @pl.when((falling >= 0) & (falling < count) & (target(falling) < line))
        def _():
            @pl.when(has_above)
            def _():
                line_copy(falling, below, down_recv).wait_recv()
                part[slot(falling)] += line_in[slot(falling)]

            @pl.when(target(falling) == line - 1)
            def _():
                last_copy(falling).start()

            @pl.when(target(falling) < line - 1)
            def _():
                line_copy(falling, below, down_recv).start()

    @pl.loop(0, count)
    def _(step):
        pair_copy(step).wait_send()

        @pl.when(target(step) > line)
        def _():
            line_copy(step, above, up_recv).wait_send()

        @pl.when(target(step) < line)
        def _():
            line_copy(step, below, down_recv).wait_send()

        @pl.when(target(step) == line)
        def _():
            o_ref[here(step)] = part[slot(step)]

            @pl.when(has_below)
            def _():
                line_copy(step, above, up_recv).wait_recv()
                o_ref[here(step)] += line_in[slot(step)]

            @pl.when(has_above)
            def _():
                last_copy(step).wait_recv()
                o_ref[here(step)] += own_in[here(step)]


def owner_sum(grad, count_dp, collective_id, pieces):
    lines = count_dp // 2
    total, width = grad.shape
    chunk = total // count_dp
    half = (lines * chunk, width)
    vmem = pl.BlockSpec(memory_space=pltpu.VMEM)
    return pl.pallas_call(
        partial(owner_sum_kernel, lines, pieces),
        out_shape=jax.ShapeDtypeStruct((chunk, width), jnp.float32),
        in_specs=[vmem],
        out_specs=vmem,
        scratch_shapes=[
            pltpu.VMEM(half, jnp.bfloat16),
            pltpu.VMEM(half, jnp.bfloat16),
            pltpu.VMEM(half, jnp.float32),
            pltpu.VMEM(half, jnp.float32),
            pltpu.VMEM((chunk, width), jnp.float32),
        ]
        + [pltpu.SemaphoreType.DMA((lines * pieces,))] * 5,
        compiler_params=pltpu.CompilerParams(
            collective_id=collective_id, has_side_effects=True, vmem_limit_bytes=62 * 2**20
        ),
    )(grad)


def total_kernel(mine_ref, sum_ref, slots, own_sem, send_sem, recv_sem):
    first, second = lax.axis_size("dp"), lax.axis_size("tensor")
    count = first * second
    me = lax.axis_index("dp") * second + lax.axis_index("tensor")

    def peer(step):
        other = lax.rem(me + step, count)
        return {"dp": other // second, "tensor": lax.rem(other, second)}

    barrier = pltpu.get_barrier_semaphore()

    @pl.loop(1, count)
    def _(step):
        pl.semaphore_signal(barrier, inc=1, device_id=peer(step), device_id_type=MESH)

    pl.semaphore_wait(barrier, count - 1)
    own = pltpu.make_async_copy(mine_ref, slots.at[me], own_sem)
    own.start()

    def send(step):
        return pltpu.make_async_remote_copy(
            src_ref=mine_ref,
            dst_ref=slots.at[me],
            send_sem=send_sem.at[step],
            recv_sem=recv_sem.at[step],
            device_id=peer(step),
            device_id_type=MESH,
        )

    @pl.loop(1, count)
    def _(step):
        send(step).start()

    @pl.loop(1, count)
    def _(step):
        send(step).wait()

    own.wait()
    sum_ref[...] = jnp.sum(slots[...], 0)


def total_over_all(mine, collective_id):
    count = lax.axis_size("dp") * lax.axis_size("tensor")
    vmem = pl.BlockSpec(memory_space=pltpu.VMEM)
    return pl.pallas_call(
        total_kernel,
        out_shape=jax.ShapeDtypeStruct(mine.shape, jnp.float32),
        in_specs=[vmem],
        out_specs=vmem,
        scratch_shapes=[
            pltpu.VMEM((count,) + mine.shape, jnp.float32),
            pltpu.SemaphoreType.DMA(()),
            pltpu.SemaphoreType.DMA((count,)),
            pltpu.SemaphoreType.DMA((count,)),
        ],
        compiler_params=pltpu.CompilerParams(collective_id=collective_id, has_side_effects=True),
    )(mine)


def pack_qkv(matrix, parts):
    rows, cols = matrix.shape
    first = matrix[:, :512].reshape(parts, 2, rows // parts // 2, 512).transpose(0, 2, 1, 3)
    second = matrix[:, 512:].reshape(parts, 4, rows // parts // 4, 256).transpose(0, 2, 1, 3)
    return jnp.concatenate([first.reshape(parts, -1, 1024), second.reshape(parts, -1, 1024)], 1).reshape(-1, 1024)


def unpack_qkv(packed, parts):
    rows = packed.shape[0] // parts
    packed = packed.reshape(parts, rows, 1024)
    cut = rows * 2 // 3
    first = packed[:, :cut].reshape(parts, cut, 2, 512).transpose(0, 2, 1, 3).reshape(-1, 512)
    second = packed[:, cut:].reshape(parts, rows - cut, 4, 256).transpose(0, 2, 1, 3).reshape(-1, 256)
    return jnp.concatenate([first, second], 1)


def by_lanes(flat, outer):
    size = flat.size // math.prod(outer)
    return flat.reshape(outer + ((size // 128, 128) if size % 128 == 0 else (size,)))


def pad_first(array, axis, unit):
    short = -array.shape[axis] % unit
    return jnp.pad(array, [(0, short if at == axis else 0) for at in range(array.ndim)])


def sum_to_owners(stack, count_dp):
    if count_dp == 8:
        return owner_sum(stack, count_dp, 1, 9)
    return lax.psum_scatter(stack, "dp", scatter_dimension=0, tiled=True)

def adam_update(master, first_mom, second_mom, gradient, step_float):
    first_new = beta_one * first_mom + (1.0 - beta_one) * gradient
    second_new = beta_two * second_mom + (1.0 - beta_two) * gradient * gradient
    first_hat = first_new / (1.0 - jnp.power(beta_one, step_float))
    second_hat = second_new / (1.0 - jnp.power(beta_two, step_float))
    master_new = master - learn_rate * (
        first_hat / (jnp.sqrt(second_hat) + adam_eps) + decay_rate * master
    )
    return (master_new, first_new, second_new)


def adam_kernel(total_ref, count_ref, *refs):
    norm_value = jnp.sqrt(total_ref[0, 0:1]) / total_ref[2, 0:1]
    factor = (clip_norm / jnp.maximum(norm_value, clip_norm) / total_ref[2, 0:1]).reshape(1, 1)
    step_float = jnp.full((1, 1), count_ref[0], jnp.int32).astype(WIDE)

    def update(ins, outs):
        grad, master, first, second, ema = (ref[...] for ref in ins)
        new, first_new, second_new = adam_update(master, first, second, grad * factor, step_float)
        ema_new = ema_rate * ema + (1.0 - ema_rate) * new
        for ref, value in zip(outs, (new, first_new, second_new, ema_new, new.astype(LOW))):
            ref[...] = value

    parts = len(refs) // 10
    for part in range(parts):
        update(refs[5 * part : 5 * part + 5], refs[5 * (parts + part) : 5 * (parts + part) + 5])


def adam(totals, step_count, rows, shared, blocks):
    size = rows[1].shape[1] // blocks
    spec = pl.BlockSpec((1, size), lambda at: (0, at))
    if shared[0].shape[0] == 1:
        kept = [pl.BlockSpec(array.shape, lambda at: (0, 0)) for array in shared]
    else:
        kept = [pl.BlockSpec((-(-array.shape[0] // (8 * blocks)) * 8, 128), lambda at: (at, 0)) for array in shared]
    kinds = (WIDE,) * 4 + (LOW,)
    shapes = [jax.ShapeDtypeStruct(arrays[1].shape, kind) for arrays in (rows, shared) if arrays for kind in kinds]
    return pl.pallas_call(
        adam_kernel,
        grid=(blocks,),
        out_shape=tuple(shapes),
        in_specs=[pl.BlockSpec((8, 128), lambda at: (0, 0)), pl.BlockSpec(memory_space=pltpu.SMEM)] + [spec] * 5 + kept,
        out_specs=(spec,) * 5 + tuple(kept),
    )(totals, step_count, *rows, *shared)


def per_device(
    patches,
    view_counts,
    splat_index,
    splat_dist,
    alpha_label,
    step_count,
    row_master,
    row_first,
    row_second,
    row_ema,
    shared_master,
    shared_first,
    shared_second,
    shared_ema,
):
    groups = lax.axis_size("tensor")
    my_dp = lax.axis_index("dp")
    count_dp = lax.axis_size("dp")
    local_width = D // groups
    qkv_parts = count_dp // 4
    share_rows = row_master.shape[1] // D
    own_patches = patches[0]
    if count_dp == 8:
        shared_lanes = shared_master.reshape(SHARED_LANES, 128)
        weights, used_cols, norm, embed, normed1, qkv, attended, log_total, resid1, normed2 = forward(
            view_counts, row_master.reshape(-1, 128), shared_lanes, own_patches, count_dp // 2, 7
        )
    else:
        own_row = row_master[0].astype(jnp.bfloat16)
        own_tiles = jnp.where(
            my_dp < qkv_parts,
            pack_qkv(own_row.reshape(-1, 3 * local_width), 1),
            own_row.reshape(share_rows, D),
        )
        weights = lax.all_gather(own_tiles, "dp", axis=0, tiled=True)
        own_flat = shared_master.astype(jnp.bfloat16)
        own_shared = by_lanes(own_flat, ())
        lead = own_shared.shape[0]
        own_shared = pad_first(own_shared, 0, 2048 // own_shared[0].size)
        shared_weights = lax.all_gather(own_shared, "dp", axis=0, tiled=False)[:, :lead].reshape(-1, 128)
        patch_rows = PIN * D // 128
        unpatch_rows = D * POUT // 128
        norm = shared_weights[patch_rows + unpatch_rows :].reshape(4, D).astype(jnp.float32)
        patch_proj = shared_weights[:patch_rows].reshape(PIN, D)
        used_cols = shared_weights[patch_rows : patch_rows + unpatch_rows].reshape(D, POUT // 128, 128)[:, 0]
        all_patches = lax.all_gather(own_patches, "tensor", axis=0, tiled=True)
        embed, normed1, qkv, attended, log_total, resid1, normed2 = attend(
            view_counts, all_patches, patch_proj, norm, weights, qkv_parts, 3
        )
    hidden, active, resid2_low, gauss_table = mlp(normed2, weights, resid1, used_cols, 4)
    loss_tile, table_grad = render(gauss_table, splat_index[0], splat_dist[0], alpha_label, PATCH * PATCH)
    loss_part = loss_tile[0, 0]
    unpatch_used, late_grad, late_low, resid_grad, branch, gain2_grad = mlp_back(
        table_grad, used_cols, resid2_low, active, hidden, normed2, weights, resid1, norm, attended, share_rows if count_dp == 8 else None, 5
    )
    early_grad, embed_grad, gain1_grad, *own_late = attend_back(
        view_counts,
        branch,
        weights,
        qkv,
        log_total,
        normed1,
        embed,
        resid_grad,
        norm,
        (late_grad, late_low) if count_dp == 8 else (),
        qkv_parts,
        count_dp // 2 if count_dp == 8 else 0,
        6,
    )
    gain_grad = jnp.concatenate([gain1_grad, gain2_grad], 0)
    if count_dp == 8:
        gains = jnp.pad(gain_grad, ((0, 4), (0, 0)))
        row_lanes, shared_share, totals = share(
            early_grad, own_late[0], embed_grad, own_patches, unpatch_used, gains, loss_tile, alpha_label, count_dp // 2, 8
        )
        row_share = row_lanes.reshape(-1)
    else:
        patch_grad = dot(own_patches, embed_grad, TN)
        unpatch_grad = jnp.concatenate(
            [unpatch_used, jnp.zeros((D, POUT - unpatch_used.shape[1]), jnp.float32)], 1
        )
        shared_grad = jnp.concatenate(
            [patch_grad.reshape(-1), unpatch_grad.reshape(-1), gain_grad.reshape(-1)]
        )
        split_grad = by_lanes(shared_grad, (count_dp, groups))
        lead = split_grad.shape[2]
        shared_stack = pad_first(split_grad, 2, 16 * D // split_grad[0, 0, 0].size).swapaxes(0, 1)
        shared_sum = lax.psum_scatter(shared_stack, "tensor", scatter_dimension=0, tiled=True)
        row_stack = jnp.concatenate([early_grad, late_grad], 0)
        stack = jnp.concatenate(
            [row_stack.reshape(count_dp, share_rows, D), shared_sum.reshape(count_dp, -1, D)], 1
        ).reshape(-1, D)
        own_share = sum_to_owners(stack, count_dp)
        own_rows = own_share[:share_rows]
        row_share = jnp.where(my_dp < qkv_parts, unpack_qkv(own_rows, 1).reshape(-1), own_rows.reshape(-1))
        shared_part = own_share[share_rows:].reshape((-1,) + split_grad.shape[3:])[:lead]
        shared_share = lax.all_gather(shared_part, "tensor", axis=0, tiled=False).reshape(-1)
        own_squares = jnp.sum(row_share * row_share) + jnp.sum(shared_part * shared_part)
        pixel_part = jnp.sum((alpha_label < 2).astype(jnp.float32))
        scalars = jnp.stack([own_squares, loss_part, pixel_part]).reshape(3, 1)
        totals = total_over_all(jnp.pad(jnp.broadcast_to(scalars, (3, 128)), ((0, 5), (0, 0))), 2)
    square_total, loss_total, pixel_total = totals[0, 0], totals[1, 0], totals[2, 0]
    norm_value = jnp.sqrt(square_total) / pixel_total
    flat = shared_master.shape
    lanes = (-1, 128) if flat[0] % 128 == 0 else (1, -1)
    shared = [array.reshape(lanes) for array in (shared_share, shared_master, shared_first, shared_second, shared_ema)]
    updated = adam(totals, step_count, (row_share[None], row_master, row_first, row_second, row_ema), shared, 6)
    row_new, row_first_new, row_second_new, row_ema_new, row_copy = updated[:5]
    shared_new, shared_first_new, shared_second_new, shared_ema_new, shared_copy = (array.reshape(flat) for array in updated[5:])
    return (
        norm_value.reshape(1),
        (loss_total / pixel_total).reshape(1),
        row_new,
        row_first_new,
        row_second_new,
        row_ema_new,
        row_copy,
        shared_new,
        shared_first_new,
        shared_second_new,
        shared_ema_new,
        shared_copy,
    )


def solution(mesh):
    placed = (
        P("dp", "tensor", None),
        P("dp"),
        P("dp", None, "tensor"),
        P("dp", None, "tensor"),
        P("dp", "tensor"),
        P(),
        P("tensor", "dp"),
        P("tensor", "dp"),
        P("tensor", "dp"),
        P("tensor", "dp"),
        P("dp"),
        P("dp"),
        P("dp"),
        P("dp"),
    )
    return jax.shard_map(
        per_device,
        mesh=mesh,
        in_specs=placed,
        out_specs=(
            P(),
            P(),
            P("tensor", "dp"),
            P("tensor", "dp"),
            P("tensor", "dp"),
            P("tensor", "dp"),
            P("tensor", "dp"),
            P("dp"),
            P("dp"),
            P("dp"),
            P("dp"),
            P("dp"),
        ),
        check_vma=False,
    )
```

```python
import math
from functools import partial

import jax
import jax.numpy as jnp
from jax import lax
from jax.experimental import pallas as pl
from jax.experimental.pallas import tpu as pltpu
from jax.sharding import PartitionSpec as P

D = 1024
DH = 64
FF = 4096
PATCH = 8
VTOK = 192
PIN = 576
POUT = 768
VMEM = pl.BlockSpec(memory_space=pltpu.VMEM)
HBM = pl.BlockSpec(memory_space=pl.ANY)
ROOT_HALF = 0.5**0.5
NORMAL_PEAK = (2.0 * math.pi) ** -0.5


clip_norm = 0.005
beta_one = 0.9
beta_two = 0.95
adam_eps = 1e-08
decay_rate = 0.05
learn_rate = 0.03
ema_rate = 0.9
norm_eps = 1e-05
masked_score = -1e30


MESH = pl.DeviceIdType.MESH
NN = (((1,), (0,)), ((), ()))
NT = (((1,), (1,)), ((), ()))
TN = (((0,), (0,)), ((), ()))
LOW = jnp.bfloat16
WIDE = jnp.float32
PIECES = 4
TILE = 256
UNIT = 128


def dot(left, right, dims=NN):
    return lax.dot_general(left, right, dims, preferred_element_type=WIDE)


def remote(src, dst, send, recv, to):
    return pltpu.make_async_remote_copy(
        src_ref=src, dst_ref=dst, send_sem=send, recv_sem=recv, device_id=to, device_id_type=MESH
    )


class Corner:
    def __init__(self):
        self.me = lax.axis_index("tensor")
        self.first, self.last = self.me // 2, lax.rem(self.me, 2)
        self.mate = self.first * 2 + 1 - self.last
        self.far = (1 - self.first) * 2 + self.last
        self.opposite = (1 - self.first) * 2 + 1 - self.last

    def block(self, step):
        return lax.rem(self.first + 1 - step // 2, 2) * 2 + lax.rem(self.last + 1 - lax.rem(step, 2), 2)

    def greet(self):
        barrier = pltpu.get_barrier_semaphore()
        for other in (self.mate, self.far):
            pl.semaphore_signal(barrier, inc=1, device_id={"tensor": other}, device_id_type=MESH)
        pl.semaphore_wait(barrier, 2)


class Gather:
    def __init__(self, corner, ref, pieces, sems, short=None):
        self.corner, self.ref, self.pieces, self.sems, self.short = corner, ref, pieces, sems, short
        self.size = ref.shape[0] // 4
        self.rows = self.size // pieces

    @staticmethod
    def scratch(pieces):
        return [pltpu.SemaphoreType.DMA((pieces,))] * 6

    def part(self, owner, piece, rows=None):
        return pl.ds(pl.multiple_of(owner * self.size + piece * self.rows, self.rows), rows or self.rows)

    def run(self, act, owner, piece, kind, to):
        def go(rows):
            here = self.ref.at[self.part(owner, piece, rows)]
            sems = self.sems[2 * kind].at[piece], self.sems[2 * kind + 1].at[piece]
            getattr(remote(here, here, *sems, {"tensor": to}), act)()

        by_half(self.short, piece < self.pieces // 2, self.rows, go)

    def start(self, piece):
        self.run("start", self.corner.me, piece, 1, self.corner.far)
        self.run("start", self.corner.me, piece, 0, self.corner.mate)

    def relay(self, piece):
        self.run("wait_recv", self.corner.far, piece, 1, self.corner.far)
        self.run("start", self.corner.far, piece, 2, self.corner.mate)

    def finish(self):
        corner = self.corner
        for piece in range(self.pieces):
            self.run("wait_recv", corner.mate, piece, 0, corner.mate)
            self.run("wait_recv", corner.opposite, piece, 2, corner.mate)
            self.run("wait_send", corner.me, piece, 0, corner.mate)
            self.run("wait_send", corner.me, piece, 1, corner.far)
            self.run("wait_send", corner.far, piece, 2, corner.mate)


def by_half(short, first, rows, go):
    if short is None:
        go(rows)
    elif isinstance(first, bool):
        go(rows if first else short)
    else:
        pl.when(first)(lambda: go(rows))
        pl.when(jnp.logical_not(first))(lambda: go(short))


class Scatter:
    def __init__(self, corner, pieces, mate_out, mate_in, far_out, far_in, mate_send, mate_recv, far_send, far_recv):
        self.corner, self.pieces = corner, pieces
        self.mate_out, self.mate_in, self.far_out, self.far_in = mate_out, mate_in, far_out, far_in
        self.sems = mate_send, mate_recv, far_send, far_recv
        self.rows = far_out.shape[0] // pieces

    @staticmethod
    def scratch(rows, width, pieces):
        return [
            pltpu.VMEM((2, rows, width), LOW),
            pltpu.VMEM((2, rows, width), LOW),
            pltpu.VMEM((rows, width), LOW),
            pltpu.VMEM((rows, width), LOW),
            pltpu.SemaphoreType.DMA((2, pieces)),
            pltpu.SemaphoreType.DMA((2, pieces)),
            pltpu.SemaphoreType.DMA((pieces,)),
            pltpu.SemaphoreType.DMA((pieces,)),
        ]

    def part(self, piece):
        return pl.ds(piece * self.rows, self.rows)

    def mate_copy(self, half, piece):
        part = self.part(piece)
        return remote(
            self.mate_out.at[half, part],
            self.mate_in.at[half, part],
            self.sems[0].at[half, piece],
            self.sems[1].at[half, piece],
            {"tensor": self.corner.mate},
        )

    def far_copy(self, piece):
        part = self.part(piece)
        return remote(
            self.far_out.at[part],
            self.far_in.at[part],
            self.sems[2].at[piece],
            self.sems[3].at[piece],
            {"tensor": self.corner.far},
        )

    def give(self, half, ref):
        for piece in range(self.pieces):
            part = self.part(piece)
            self.mate_out[half, part] = ref[part].astype(LOW)
            self.mate_copy(half, piece).start()

    def cross(self, ref):
        for piece in range(self.pieces):
            part = self.part(piece)
            self.mate_copy(0, piece).wait_recv()
            self.far_out[part] = (ref[part] + self.mate_in[0, part].astype(WIDE)).astype(LOW)
            self.far_copy(piece).start()

    def step(self, step, ref):
        @pl.when(step == 0)
        def _():
            self.give(0, ref)

        @pl.when(step == 1)
        def _():
            self.cross(ref)

        @pl.when(step == 2)
        def _():
            self.give(1, ref)

    def land(self, piece, ref):
        part = self.part(piece)
        self.mate_copy(1, piece).wait_recv()
        self.far_copy(piece).wait_recv()
        return ref[part] + self.mate_in[1, part].astype(WIDE) + self.far_in[part].astype(WIDE)

    def close(self):
        for piece in range(self.pieces):
            self.mate_copy(0, piece).wait_send()
            self.mate_copy(1, piece).wait_send()
            self.far_copy(piece).wait_send()


def standard(values):
    centre = values - jnp.mean(values, -1, keepdims=True)
    inverse = lax.rsqrt(jnp.mean(centre * centre, -1, keepdims=True) + norm_eps)
    return centre * inverse, inverse


def norm_back(grad_out, scaled, inverse, gain):
    grad_scaled = grad_out * gain
    return inverse * (
        grad_scaled
        - jnp.mean(grad_scaled, -1, keepdims=True)
        - scaled * jnp.mean(grad_scaled * scaled, -1, keepdims=True)
    )


def qkv_places(parts, rows, columns):
    share = rows // parts
    wide = columns * 2 // 3
    packed = share * columns // 1024
    for at in range(parts):
        for j in range(2):
            half = share // 2
            yield (at * packed, half, j * wide, wide, at * share + j * half, 0)
        for j in range(4):
            quarter = share // 4
            yield (at * packed + share // 2, quarter, j * (columns - wide), columns - wide, at * share + j * quarter, wide)


def unpack_into(full, packed, parts):
    for row, rows, col, cols, to_row, to_col in qkv_places(parts, full.shape[0], full.shape[1]):
        full[to_row : to_row + rows, to_col : to_col + cols] = packed[row : row + rows, col : col + cols]


def pack_from(packed, full, parts, base=0):
    for row, rows, col, cols, to_row, to_col in qkv_places(parts, full.shape[0], full.shape[1]):
        packed[base + row : base + row + rows, col : col + cols] = full[to_row : to_row + rows, to_col : to_col + cols]


def rows_of(block, size):
    return pl.ds(pl.multiple_of(block * size, size), size)


def column_loop(width, body, size=TILE):
    @pl.loop(0, width // size)
    def _(tile):
        body(pl.ds(pl.multiple_of(tile * size, size), size))


def attend_kernel(parts, q_rows, count_ref, patch_ref, proj_ref, norm_ref, weight_ref, *rest):
    corner = Corner()
    corner.greet()
    attend_body(parts, q_rows, corner, None, count_ref, patch_ref, proj_ref, norm_ref, weight_ref, *rest)


def attend_body(parts, q_rows, corner, progress, count_ref, patch_ref, proj_ref, norm_ref, weight_ref,
                embed_ref, normed1_ref, qkv_ref, attended_ref, log_ref, resid_ref, normed2_ref,
                qkv_proj, term, held, held_sem, *comm):
    progress = progress or (lambda *_: None)
    scatter = Scatter(corner, PIECES, *comm[:8])
    gather = Gather(corner, normed2_ref, PIECES, comm[8:])
    packed_rows = held.shape[0] * 3 // 4
    packed_ref, out_ref = held.at[pl.ds(0, packed_rows)], held.at[pl.ds(packed_rows, held.shape[0] - packed_rows)]

    def hold(start, target, at):
        copy = pltpu.make_async_copy(weight_ref.at[pl.ds(start, target.shape[0])], target, held_sem.at[at])
        copy.start()
        copy.wait()

    size, width = embed_ref.shape
    length = patch_ref.shape[0]
    local = attended_ref.shape[1]

    @pl.loop(0, 4)
    def _(block):
        here = rows_of(block, size)
        column_loop(width, lambda cols: term.__setitem__((slice(None), cols), dot(patch_ref[here], proj_ref[:, cols])))

        @pl.when(block == corner.me)
        def _():
            embed_ref[...] = term[...]

        scaled, inverse = standard(term[...])
        normed1_ref[here] = (scaled * norm_ref[0:1] + norm_ref[1:2]).astype(LOW)
        progress("embed", block)

    progress("weights")
    hold(0, packed_ref, 0)
    unpack_into(qkv_proj, packed_ref, parts)

    @pl.loop(0, 4)
    def _(block):
        here = rows_of(block, size)

        def columns(cols):
            qkv_ref[here, cols] = dot(normed1_ref[here], qkv_proj[:, cols]).astype(LOW)

        column_loop(3 * local, columns)

    valid = lax.broadcasted_iota(jnp.int32, (1, length), 1) < count_ref[0] * VTOK
    left = lax.broadcasted_iota(jnp.int32, (1, 2 * DH), 1) < DH
    factor = jnp.array(DH ** (-0.5), LOW)

    @pl.loop(0, length // q_rows)
    def _(turn):
        here = rows_of(turn, q_rows)
        for pair in range(local // (2 * DH)):
            lanes = slice(pair * 2 * DH, (pair + 1) * 2 * DH)
            queries = qkv_ref[here, lanes] * factor
            keyset = qkv_ref[:, local + pair * 2 * DH : local + (pair + 1) * 2 * DH]
            values = qkv_ref[:, 2 * local + pair * 2 * DH : 2 * local + (pair + 1) * 2 * DH]
            found = []
            for side in range(2):
                mine = left if side == 0 else ~left
                scores = dot(jnp.where(mine, queries, jnp.zeros_like(queries)), keyset, NT)
                scores = jnp.where(valid, scores, masked_score)
                top = jnp.max(scores, -1, keepdims=True)
                powers = jnp.exp(scores - top)
                total = jnp.sum(powers, -1, keepdims=True)
                log_ref[here, pair * 2 + side : pair * 2 + side + 1] = top + jnp.log(total)
                found.append(dot((powers * (1.0 / total)).astype(LOW), values))
            attended_ref[here, lanes] = jnp.where(left, found[0], found[1]).astype(LOW)
        progress("turn", turn)

    progress("out")
    hold(packed_rows, out_ref, 1)

    @pl.loop(0, 4)
    def _(step):
        here = rows_of(corner.block(step), size)
        column_loop(width, lambda cols: term.__setitem__((slice(None), cols), dot(attended_ref[here], out_ref[:, cols])))
        scatter.step(step, term)
        progress("give", step)

    for piece in range(PIECES):
        part = scatter.part(piece)
        resid = embed_ref[part] + scatter.land(piece, term)
        resid_ref[part] = resid
        scaled, inverse = standard(resid)
        normed2_ref[gather.part(corner.me, piece)] = (scaled * norm_ref[2:3] + norm_ref[3:4]).astype(LOW)
        gather.start(piece)
        progress("land", piece)
    for piece in range(PIECES):
        gather.relay(piece)
    gather.finish()
    scatter.close()


def attend(count, patches, patch_proj, norm, weights, parts, collective_id):
    length, size = patches.shape[0], patches.shape[0] // 4
    width, local = patch_proj.shape[1], patch_proj.shape[1] // 4
    shape = jax.ShapeDtypeStruct
    return pl.pallas_call(
        partial(attend_kernel, parts, 256),
        out_shape=(
            shape((size, width), WIDE),
            shape((length, width), LOW),
            shape((length, 3 * local), LOW),
            shape((length, local), LOW),
            shape((length, local // DH), WIDE),
            shape((size, width), WIDE),
            shape((length, width), LOW),
        ),
        in_specs=[pl.BlockSpec(memory_space=pltpu.SMEM)] + [VMEM] * 3 + [HBM],
        out_specs=(VMEM,) * 7,
        scratch_shapes=[
            pltpu.VMEM((width, 3 * local), LOW),
            pltpu.VMEM((size, width), WIDE),
            pltpu.VMEM((4 * local, width), LOW),
            pltpu.SemaphoreType.DMA((2,)),
        ]
        + Scatter.scratch(size, width, PIECES)
        + Gather.scratch(PIECES),
        compiler_params=pltpu.CompilerParams(
            collective_id=collective_id, has_side_effects=True, vmem_limit_bytes=62 * 2**20
        ),
    )(count, patches, patch_proj, norm, weights)


class Lines:
    def __init__(self, lines):
        self.lines = lines
        self.me = lax.axis_index("dp")
        self.line, self.side = self.me // 2, lax.rem(self.me, 2)
        self.pair = {"dp": self.line * 2 + 1 - self.side}
        self.above = {"dp": lax.rem(self.line + 1, lines) * 2 + self.side}
        self.below = {"dp": lax.rem(self.line + lines - 1, lines) * 2 + self.side}
        self.has_below, self.has_above = self.line > 0, self.line < lines - 1

    def signal(self, barrier):
        pl.semaphore_signal(barrier, inc=1, device_id=self.pair, device_id_type=MESH)

        @pl.when(self.has_below)
        def _():
            pl.semaphore_signal(barrier, inc=1, device_id=self.below, device_id_type=MESH)

        @pl.when(self.has_above)
        def _():
            pl.semaphore_signal(barrier, inc=1, device_id=self.above, device_id_type=MESH)

        return 1 + jnp.minimum(self.line, 1) + jnp.minimum(self.lines - 1 - self.line, 1)


class LineGather:
    def __init__(self, spot, ref, base, chunk, pieces, late_own, sems, short=None):
        self.spot, self.ref, self.base, self.chunk, self.pieces, self.late_own = spot, ref, base, chunk, pieces, late_own
        self.sems, self.short = sems, short
        self.rows = chunk // pieces
        self.steps = (spot.lines - 1) * pieces

    @staticmethod
    def scratch(lines, pieces):
        return [pltpu.SemaphoreType.DMA((lines * pieces,))] * 6

    def run(self, act, kind, line, piece, crossed=False):
        spot = self.spot
        side = 1 - spot.side if crossed else spot.side
        to = (spot.above, spot.below, spot.pair)[kind]

        def go(rows):
            start = self.base + (line * 2 + side) * self.chunk + piece * self.rows
            here = self.ref.at[pl.ds(pl.multiple_of(start, 16), rows)]
            at = line * self.pieces + piece
            getattr(remote(here, here, self.sems[2 * kind].at[at], self.sems[2 * kind + 1].at[at], to), act)()

        by_half(self.short, line < spot.lines // 2, self.rows, go)

    def own(self, kind):
        @pl.loop(0, self.pieces)
        def _(piece):
            self.run("start", kind, self.spot.line, piece)

    def begin(self):
        spot = self.spot
        if self.late_own:

            @pl.when(spot.line == 0)
            def _():
                self.own(0)

            return

        @pl.when(spot.has_above)
        def _():
            self.own(0)

        @pl.when(spot.has_below)
        def _():
            self.own(1)

        self.own(2)

    def follow(self):
        @pl.when(self.spot.has_below)
        def _():
            self.own(1)

        @pl.when(self.spot.line == 0)
        def _():
            self.own(2)

    def step(self, at):
        spot = self.spot
        piece = lax.rem(at, self.pieces)

        @pl.when(at < spot.line * self.pieces)
        def _():
            turn = at // self.pieces
            line = jnp.minimum(turn, 1) * (spot.line - turn) if self.late_own else turn
            self.run("wait_recv", 0, line, piece)

            @pl.when(spot.has_above)
            def _():
                self.run("start", 0, line, piece)

            self.run("start", 2, line, piece)

        if self.late_own:

            @pl.when((at == self.pieces - 1) & spot.has_below & spot.has_above)
            def _():
                self.own(0)

            @pl.when(at == spot.line * self.pieces - 1)
            def _():
                self.own(2)

        @pl.when(at < (spot.lines - 1 - spot.line) * self.pieces)
        def _():
            line = spot.line + 1 + at // self.pieces
            self.run("wait_recv", 1, line, piece)

            @pl.when(spot.has_below)
            def _():
                self.run("start", 1, line, piece)

            self.run("start", 2, line, piece)

    def wait_crossed(self, line):
        @pl.loop(0, self.pieces)
        def _(piece):
            self.run("wait_recv", 2, line, piece, True)

    def close(self):
        spot = self.spot

        @pl.loop(0, spot.lines * self.pieces)
        def _(at):
            line, piece = at // self.pieces, lax.rem(at, self.pieces)
            self.run("wait_send", 2, line, piece)

            @pl.when((line <= spot.line) & spot.has_above)
            def _():
                self.run("wait_send", 0, line, piece)

            @pl.when((line >= spot.line) & spot.has_below)
            def _():
                self.run("wait_send", 1, line, piece)


WINDOW = 48
SHORT = 16
FRONT = 80
PADDED = 1616
ROW_START = (0, 160, 336, 496)
USED_START = (None, None, None, 0, 128, 352, 576, 800)


def window_row(owner):
    if isinstance(owner, int):
        return owner * WINDOW if owner < 4 else 4 * WINDOW + (owner - 4) * SHORT
    return jnp.minimum(owner, 4) * WINDOW + jnp.maximum(owner - 4, 0) * SHORT


def window_valid(me, quarter, width):
    row = lax.broadcasted_iota(jnp.int32, (WINDOW, width), 0)
    block = lax.broadcasted_iota(jnp.int32, (WINDOW, width), 1) // 128
    start, stop = me * SHARED_LANES, (me + 1) * SHARED_LANES
    patch_row = jnp.where(me == 3, ROW_START[3] + 32 * quarter, 160 * me + 16 * (me // 2) + WINDOW * quarter) + row
    lane = 8 * patch_row + block
    patch = (me < 4) & ((me < 3) | ((quarter < 3) & (row < 32))) & (lane >= start) & (lane < stop) & (lane < PATCH_LANES)
    first = (me == 3) & (quarter < 3) & (row >= 32) & (block < 3)
    other = (me > 3) & (row < SHORT) & (block < 4)
    index = jnp.where(me == 3, 48 * quarter + 16 * block + row - 32, 224 * me - 768 + 64 * quarter + SHORT * block + row)
    lane = PATCH_LANES + 6 * index
    used = (first | other) & (index < D) & (lane >= start) & (lane < stop)
    norm = (me == 7) & (quarter == 0) & (row < 8) & (block >= 4)
    return patch | used | norm


def shared_offsets(me, quarter):
    chunk = SHARED_LANES
    rows = jnp.where(me == 0, 0, jnp.where(me == 1, 160, jnp.where(me == 2, 336, 496)))
    used = (me - 4) * 224 + 128
    return (
        FRONT + 8 * rows - me * chunk + 8 * WINDOW * quarter,
        FRONT + 8 * rows - me * chunk + 8 * 32 * quarter,
        FRONT + PATCH_LANES - me * chunk + 6 * 48 * quarter,
        FRONT + PATCH_LANES + 6 * used - me * chunk + 6 * 64 * quarter,
        FRONT + PATCH_LANES + 6 * D - me * chunk,
    )


def shared_walk(me, quarter, take, phases=range(5)):
    rows, last_rows, first_used, used, norm = shared_offsets(me, quarter)
    for j in range(8):
        if 0 in phases:
            take(me < 3, 0, WINDOW, j, rows + j, 8)
        if 1 in phases:
            take((me == 3) & (quarter < 3), 0, 32, j, last_rows + j, 8)
    if 2 in phases:
        for j in range(3):
            take((me == 3) & (quarter < 3), 32, 16, j, first_used + 6 * 16 * j, 6)
    if 3 in phases:
        for j in range(4):
            take(me > 3, 0, SHORT, j, used + 6 * SHORT * j, 6)
    if 4 in phases:
        for j in range(4):
            take((me == 7) & (quarter == 0), 0, SHORT, 4 + j, norm + j, 4)


def window_pieces(kind, row):
    found = []
    if kind == 0:
        for me in range(3):
            at = row - ROW_START[me]
            if 0 <= at < 4 * WINDOW:
                found.append((me, at // WINDOW, at % WINDOW, None))
        at = row - ROW_START[3]
        if 0 <= at < 96:
            found.append((3, at // 32, at % 32, None))
    else:
        if row < 144:
            found.append((3, row // 48, 32, row % 48 // 16))
        for me in range(4, 8):
            at = row - USED_START[me]
            if 0 <= at < 256:
                found.append((me, at // 64, 0, at % 64 // 16))
    return found

SHARED_LANES = 1348
PATCH_LANES = PIN * D // 128
CHUNK_PIECES = 4


def forward_kernel(lines, q_rows, count_ref, row_ref, lanes_ref, own_patch_ref,
                   weight_ref, used_ref, norm_ref,
                   embed_ref, normed1_ref, qkv_ref, attended_ref, log_ref, resid_ref, normed2_ref,
                   patches, proj, windows, shared_ref, own_chunk, own_sem, *rest):
    body, extra = rest[:4 + 14], rest[4 + 14:]
    corner, spot = Corner(), Lines(lines)
    barrier = pltpu.get_barrier_semaphore()
    for other in (corner.mate, corner.far):
        pl.semaphore_signal(barrier, inc=1, device_id={"tensor": other}, device_id_type=MESH)
    pl.semaphore_wait(barrier, 2 + spot.signal(barrier))
    parts = lines // 2
    chunk = weight_ref.shape[0] // (2 * lines)
    size, inputs = own_patch_ref.shape
    window = LineGather(spot, windows, corner.me * (2 * lines * WINDOW), WINDOW, 1, False, extra[0:6], SHORT)
    weights = LineGather(spot, weight_ref, 0, chunk, CHUNK_PIECES, True, extra[6:12])
    spread = Gather(corner, windows, 2 * lines, extra[12:18], SHORT)
    given = Gather(corner, patches, 1, extra[18:24])

    patches[given.part(corner.me, 0)] = own_patch_ref[...]
    given.start(0)
    base = pl.multiple_of((corner.me * 2 * lines + spot.me) * WINDOW, 16)
    windows[pl.ds(base, WINDOW)] = jnp.zeros((WINDOW, windows.shape[1]), LOW)
    shared_ref[...] = jnp.zeros_like(shared_ref)
    shared_ref[FRONT : FRONT + SHARED_LANES] = lanes_ref[...]

    def take(condition, row, rows, j, start, stride):
        @pl.when(condition)
        def _():
            windows[pl.ds(pl.multiple_of(base + row, 16), rows), j * 128 : (j + 1) * 128] = shared_ref[
                pl.ds(start, rows, stride)
            ].astype(LOW)

    shared_walk(spot.me, corner.me, take)
    window.begin()
    spread.start(spot.me)
    own = pl.multiple_of(spot.me * chunk, 16)

    @pl.when(spot.me < parts)
    def _():
        for row, rows, col, cols, at, at_col in qkv_places(1, chunk * 4 // 3, D * 3 // 4):
            for j in range(cols // 128):
                own_chunk[row : row + rows, col + j * 128 : col + (j + 1) * 128] = row_ref[
                    pl.ds(6 * at + at_col // 128 + j, rows, 6)
                ].astype(LOW)

    @pl.when(spot.me >= parts)
    def _():
        for j in range(8):
            own_chunk[:, j * 128 : (j + 1) * 128] = row_ref[pl.ds(j, chunk, 8)].astype(LOW)

    kept = pltpu.make_async_copy(own_chunk, weight_ref.at[pl.ds(own, chunk)], own_sem)
    kept.start()
    kept.wait()
    weights.begin()

    def passed(stage, act):
        if stage == 0:
            act(spot.me, None)
            act(spot.line * 2 + 1 - spot.side, spot.line)
            return
        for near in (True, False):
            for there, line in (
                (stage - 1 < spot.line, stage - 1),
                (stage - 1 < lines - 1 - spot.line, spot.line + stage),
            ):

                @pl.when(there)
                def _():
                    act(line * 2 + (spot.side if near else 1 - spot.side), None if near else line)

    def send_on(owner, line):
        if line is not None:
            window.wait_crossed(line)
        spread.start(owner)

    def relay_on(owner, line):
        spread.relay(owner)

    window.wait_crossed(spot.line)
    spread.start(spot.line * 2 + 1 - spot.side)
    window.step(0)
    passed(1, send_on)
    window.step(1)
    passed(2, send_on)
    window.step(2)
    weights.follow()
    weights.step(0)
    passed(3, send_on)
    weights.step(1)
    given.relay(0)
    passed(0, relay_on)
    weights.step(2)
    passed(1, relay_on)
    weights.step(3)
    passed(2, relay_on)
    passed(3, relay_on)
    spread.finish()
    given.finish()

    def source(me, quarter, row, rows, j):
        start = (quarter * 2 * lines + me) * WINDOW + row
        return windows[start : start + rows] if j is None else windows[start : start + rows, j * 128 : (j + 1) * 128]

    for row in range(0, proj.shape[0], 16):
        proj[row : row + 16] = sum(source(me, t, at, 16, j) for me, t, at, j in window_pieces(0, row))
    for row in range(0, used_ref.shape[0], 16):
        used_ref[row : row + 16] = sum(source(me, t, at, 16, j) for me, t, at, j in window_pieces(1, row))
    ends = source(2 * lines - 1, 0, 0, SHORT, None)[:, D // 2 :].astype(WIDE)
    norm_ref[...] = jnp.zeros_like(norm_ref)
    for row in range(8):
        norm_ref[row // 2 : row // 2 + 1, row % 2 * D // 2 : (row % 2 + 1) * D // 2] = ends[row : row + 1]

    def progress(place, at=None):
        if place == "embed":

            @pl.when(at == 2)
            def _():
                weights.step(4)

        if place == "weights":
            weights.step(5)
            weights.wait_crossed(0)
        if place == "turn":

            weights.step(6 + at)
        if place == "out":
            weights.wait_crossed(1)

    attend_body(parts, q_rows, corner, progress, count_ref, patches, proj, norm_ref,
                weight_ref, embed_ref, normed1_ref, qkv_ref, attended_ref, log_ref, resid_ref, normed2_ref, *body)
    for line in range(2, lines):
        weights.wait_crossed(line)
    weights.close()
    window.close()


def forward(count, row_lanes, shared_lanes, own_patches, lines, collective_id):
    size, inputs = own_patches.shape
    length, width, local = 4 * size, D, D // 4
    shape = jax.ShapeDtypeStruct
    return pl.pallas_call(
        partial(forward_kernel, lines, 256),
        out_shape=(
            shape((3 * D, D), LOW),
            shape((D, 128), LOW),
            shape((8, D), WIDE),
            shape((size, width), WIDE),
            shape((length, width), LOW),
            shape((length, 3 * local), LOW),
            shape((length, local), LOW),
            shape((length, local // DH), WIDE),
            shape((size, width), WIDE),
            shape((length, width), LOW),
        ),
        in_specs=[pl.BlockSpec(memory_space=pltpu.SMEM)] + [VMEM] * 3,
        out_specs=(HBM,) + (VMEM,) * 9,
        scratch_shapes=[
            pltpu.VMEM((length, inputs), LOW),
            pltpu.VMEM((inputs, width), LOW),
            pltpu.VMEM((8 * lines * WINDOW, width), LOW),
            pltpu.VMEM((PADDED, 128), WIDE),
            pltpu.VMEM((3 * D // (2 * lines), width), LOW),
            pltpu.SemaphoreType.DMA(()),
            pltpu.VMEM((width, 3 * local), LOW),
            pltpu.VMEM((size, width), WIDE),
            pltpu.VMEM((4 * local, width), LOW),
            pltpu.SemaphoreType.DMA((2,)),
        ]
        + Scatter.scratch(size, width, PIECES)
        + Gather.scratch(PIECES)
        + LineGather.scratch(lines, 1)
        + LineGather.scratch(lines, CHUNK_PIECES)
        + Gather.scratch(2 * lines)
        + Gather.scratch(1),
        compiler_params=pltpu.CompilerParams(
            collective_id=collective_id, has_side_effects=True, vmem_limit_bytes=63 * 2**20
        ),
    )(count, row_lanes, shared_lanes, own_patches)


class Moves:
    def __init__(self, sems, *pairs):
        self.copies = [pltpu.make_async_copy(src, dst, sems.at[at]) for at, (src, dst) in enumerate(pairs)]

    def start(self, *which):
        for at in which or range(len(self.copies)):
            self.copies[at].start()

    def wait(self, *which):
        for at in which or range(len(self.copies)):
            self.copies[at].wait()


def mlp_kernel(normed2_ref, weight_ref, resid1_ref, cols_ref, hidden_out, active_out, low_ref, table_ref,
               term, up_ref, down_ref, hidden_ref, active_ref, load_sem, hidden_sem, active_sem, *comm):
    first, ff = up_ref.shape[0], down_ref.shape[0]
    loads = Moves(load_sem, (weight_ref.at[pl.ds(first, first)], up_ref), (weight_ref.at[pl.ds(2 * first, ff)], down_ref))
    loads.start()
    corner = Corner()
    corner.greet()
    scatter = Scatter(corner, PIECES, *comm[:8])
    gather = Gather(corner, table_ref, PIECES, comm[8:])
    size, width = resid1_ref.shape
    loads.wait()

    def stores(step):
        here = rows_of(corner.block(step), size)
        return (
            pltpu.make_async_copy(hidden_ref.at[here], hidden_out.at[here], hidden_sem.at[step]),
            pltpu.make_async_copy(active_ref.at[here], active_out.at[here], active_sem.at[step]),
        )

    @pl.loop(0, 4)
    def _(step):
        here = rows_of(corner.block(step), size)

        def columns(cols):
            hidden = dot(normed2_ref[here], up_ref[:, cols])
            hidden_ref[here, cols] = hidden
            active_ref[here, cols] = (0.5 * hidden * (1.0 + lax.erf(hidden * ROOT_HALF))).astype(LOW)

        column_loop(up_ref.shape[1], columns, 2 * TILE)
        for copy in stores(step):
            copy.start()
        column_loop(width, lambda cols: term.__setitem__((slice(None), cols), dot(active_ref[here], down_ref[:, cols])), 2 * TILE)
        scatter.step(step, term)

    for piece in range(PIECES):
        part = scatter.part(piece)
        low_ref[part] = (resid1_ref[part] + scatter.land(piece, term)).astype(LOW)
        table_ref[gather.part(corner.me, piece)] = dot(low_ref[part], cols_ref[...]).astype(LOW)
        gather.start(piece)
    for piece in range(PIECES):
        gather.relay(piece)
    gather.finish()
    scatter.close()
    for step in range(4):
        for copy in stores(step):
            copy.wait()


def mlp(normed2, weights, resid1, used_cols, collective_id):
    length, size, width = normed2.shape[0], resid1.shape[0], resid1.shape[1]
    hidden = FF // 4
    shape = jax.ShapeDtypeStruct
    return pl.pallas_call(
        mlp_kernel,
        out_shape=(
            shape((length, hidden), WIDE),
            shape((length, hidden), LOW),
            shape((size, width), LOW),
            shape((length, used_cols.shape[1]), LOW),
        ),
        in_specs=[VMEM, HBM, VMEM, VMEM],
        out_specs=(HBM, HBM, VMEM, VMEM),
        scratch_shapes=[
            pltpu.VMEM((size, width), WIDE),
            pltpu.VMEM((width, hidden), LOW),
            pltpu.VMEM((hidden, width), LOW),
            pltpu.VMEM((length, hidden), WIDE),
            pltpu.VMEM((length, hidden), LOW),
            pltpu.SemaphoreType.DMA((2,)),
            pltpu.SemaphoreType.DMA((4,)),
            pltpu.SemaphoreType.DMA((4,)),
        ]
        + Scatter.scratch(size, width, PIECES)
        + Gather.scratch(PIECES),
        compiler_params=pltpu.CompilerParams(
            collective_id=collective_id, has_side_effects=True, vmem_limit_bytes=62 * 2**20
        ),
    )(normed2, weights, resid1, used_cols)


def mlp_back_kernel(chunk, table_ref, cols_ref, low_ref, active_in, hidden_in, normed2_in, weight_ref, resid1_ref, norm_ref, attended_ref,
                    unpatch_ref, grad_out, rounded_out, resid_grad_ref, branch_ref, gain_ref,
                    gauss, down_in, hidden_grad, term, tail, active_ref, hidden_ref, normed2_ref, up_ref, down_ref, grad_ref,
                    rounded_ref, load_sem, store_sem, *comm):
    first = up_ref.shape[0]
    loads = Moves(
        load_sem,
        (weight_ref.at[pl.ds(2 * first, down_ref.shape[0])], down_ref),
        (weight_ref.at[pl.ds(first, first)], up_ref),
        (normed2_in, normed2_ref),
        (active_in, active_ref),
    )
    corner = Corner()

    def load_hidden(step):
        here = rows_of(corner.block(step), resid1_ref.shape[0])
        return pltpu.make_async_copy(hidden_in.at[here], hidden_ref.at[here], load_sem.at[4 + step])

    loads.start(0)
    load_hidden(0).start()
    loads.start(1)
    for step in range(1, 4):
        load_hidden(step).start()
    loads.start(2, 3)
    corner.greet()
    small = Scatter(corner, 1, *comm[:8])
    spread = Gather(corner, gauss, 1, comm[8:14])
    scatter = Scatter(corner, PIECES, *comm[14:22])
    gather = Gather(corner, branch_ref, PIECES, comm[22:])
    size, width = resid1_ref.shape
    ff = up_ref.shape[1]

    def view(step):
        return table_ref.at[rows_of(corner.block(step), size)]

    tail[...] = view(0)[...].astype(WIDE)
    small.give(0, tail)
    tail[...] = view(1)[...].astype(WIDE)
    small.cross(tail)
    tail[...] = view(2)[...].astype(WIDE)
    small.give(1, tail)
    tail[...] = view(3)[...].astype(WIDE)
    own_gauss = small.land(0, tail).astype(LOW)
    gauss[spread.part(corner.me, 0)] = own_gauss
    spread.start(0)
    unpatch_ref[...] = dot(low_ref[...], own_gauss, TN)
    spread.relay(0)
    spread.finish()
    small.close()
    loads.wait(0, 1)

    @pl.loop(0, 4)
    def _(step):
        here = rows_of(corner.block(step), size)
        load_hidden(step).wait()
        term[...] = dot(gauss[here], cols_ref[...], NT)
        down_in[here] = term[...].astype(LOW)

        @pl.when(step == 3)
        def _():
            resid_grad_ref[...] = term[...]

        def columns(cols):
            active_grad = dot(down_in[here], down_ref[cols, :], NT)
            hidden = hidden_ref[here, cols]
            slope = 0.5 * (1.0 + lax.erf(hidden * ROOT_HALF)) + hidden * (jnp.exp(-0.5 * hidden * hidden) * NORMAL_PEAK)
            hidden_grad[here, cols] = (active_grad * slope).astype(LOW)

        column_loop(ff, columns)

        def back(cols):
            term[:, cols] = dot(hidden_grad[here], up_ref[cols, :], NT)

        column_loop(width, back)
        scatter.step(step, term)

    side = None if chunk is None else lax.rem(lax.axis_index("dp"), 2)

    def store(at, act):
        part = pl.ds(pl.multiple_of(at * UNIT, UNIT), UNIT)

        def wide():
            getattr(pltpu.make_async_copy(grad_ref.at[part], grad_out.at[part], store_sem.at[at]), act)()

        def rounded():
            getattr(pltpu.make_async_copy(rounded_ref.at[part], rounded_out.at[part], store_sem.at[at]), act)()

        if chunk is None:
            wide()
            return
        mine = lax.rem(at * UNIT // chunk, 2) == side
        pl.when(mine)(wide)
        pl.when(jnp.logical_not(mine))(rounded)

    def keep(tile, value):
        part = pl.ds(pl.multiple_of(tile * TILE, TILE), TILE)
        grad_ref[part, :] = value
        rounded_ref[part, :] = value.astype(LOW)
        for at in range(TILE // UNIT):
            store(tile * (TILE // UNIT) + at, "start")

    loads.wait(2, 3)
    tiles = attended_ref.shape[1] // TILE

    @pl.loop(0, width // TILE)
    def _(tile):
        cols = pl.ds(pl.multiple_of(tile * TILE, TILE), TILE)
        keep(tiles + tile, dot(normed2_ref[:, cols], hidden_grad[...], TN))

    @pl.loop(0, ff // TILE)
    def _(tile):
        cols = pl.ds(pl.multiple_of(tile * TILE, TILE), TILE)
        keep(tiles + width // TILE + tile, dot(active_ref[:, cols], down_in[...], TN))

    gain_sum, bias_sum = jnp.zeros((1, width), WIDE), jnp.zeros((1, width), WIDE)
    for piece in range(PIECES):
        part = scatter.part(piece)
        grad = scatter.land(piece, term)
        scaled, inverse = standard(resid1_ref[part])
        total = resid_grad_ref[part] + norm_back(grad, scaled, inverse, norm_ref[2:3])
        resid_grad_ref[part] = total
        branch_ref[gather.part(corner.me, piece)] = total.astype(LOW)
        gather.start(piece)
        gain_sum += jnp.sum(grad * scaled, 0, keepdims=True)
        bias_sum += jnp.sum(grad, 0, keepdims=True)
    gain_ref[0:1] = gain_sum
    gain_ref[1:2] = bias_sum
    for piece in range(PIECES):
        gather.relay(piece)
    gather.finish()
    scatter.close()

    for tile in range(tiles):
        keep(tile, dot(attended_ref[:, tile * TILE : (tile + 1) * TILE], branch_ref[...], TN))

    @pl.loop(0, grad_ref.shape[0] // UNIT)
    def _(at):
        store(at, "wait")


def mlp_back(table_grad, used_cols, low, active, hidden, normed2, weights, resid1, norm, attended, chunk, collective_id):
    length, size, width = normed2.shape[0], resid1.shape[0], resid1.shape[1]
    ff, used = hidden.shape[1], used_cols.shape[1]
    total = attended.shape[1] + width + ff
    shape = jax.ShapeDtypeStruct
    return pl.pallas_call(
        partial(mlp_back_kernel, chunk),
        out_shape=(
            shape((width, used), WIDE),
            shape((total, width), WIDE),
            shape((total, width), LOW),
            shape((size, width), WIDE),
            shape((length, width), LOW),
            shape((2, width), WIDE),
        ),
        in_specs=[VMEM] * 3 + [HBM] * 4 + [VMEM] * 3,
        out_specs=(VMEM, HBM, HBM, VMEM, VMEM, VMEM),
        scratch_shapes=[
            pltpu.VMEM((length, used), LOW),
            pltpu.VMEM((length, width), LOW),
            pltpu.VMEM((length, ff), LOW),
            pltpu.VMEM((size, width), WIDE),
            pltpu.VMEM((size, used), WIDE),
            pltpu.VMEM((length, ff), LOW),
            pltpu.VMEM((length, ff), WIDE),
            pltpu.VMEM((length, width), LOW),
            pltpu.VMEM((width, ff), LOW),
            pltpu.VMEM((ff, width), LOW),
            pltpu.VMEM((total, width), WIDE),
            pltpu.VMEM((total, width), LOW),
            pltpu.SemaphoreType.DMA((8,)),
            pltpu.SemaphoreType.DMA((total // UNIT,)),
        ]
        + Scatter.scratch(size, used, 1)
        + Gather.scratch(1)
        + Scatter.scratch(size, width, PIECES)
        + Gather.scratch(PIECES),
        compiler_params=pltpu.CompilerParams(
            collective_id=collective_id, has_side_effects=True, vmem_limit_bytes=63 * 2**20
        ),
    )(table_grad, used_cols, low, active, hidden, normed2, weights, resid1, norm, attended)


class LineSum:
    def __init__(self, spot, pieces, low, source, buffers, sems, first=0, turns=4, stored=None):
        self.spot, self.pieces, self.low, self.source = spot, pieces, low, source
        self.first, self.turns, self.stored = first, turns, stored
        self.pair_out, self.pair_in, self.part, self.line_in, self.low_out, self.low_in = buffers
        self.p_send, self.p_recv, self.l_send, self.up_recv, self.down_recv = sems
        self.count = turns * pieces
        self.rows = self.part.shape[0] // self.count

    @staticmethod
    def scratch(turns, rows, pieces, width, low, stored=False):
        half = (turns * rows, width)
        kept = half if low else (rows, width)
        kind = LOW if low else WIDE
        return [
            pltpu.VMEM((16, 128) if stored else half, LOW),
            pltpu.VMEM(half, LOW),
            pltpu.VMEM(half, WIDE),
            pltpu.VMEM(half, WIDE),
            pltpu.VMEM(half if low else (16, 128), LOW),
            pltpu.VMEM(kept, kind),
        ] + [pltpu.SemaphoreType.DMA((turns * pieces,))] * 5

    def target(self, step):
        turn = lax.rem(step, self.turns)
        if self.turns == 4:
            odd = lax.rem(turn, 2)
            return (1 - odd) * (3 - turn // 2) + odd * (turn // 2)
        if self.turns == 3:
            return self.first + 2 - 2 * jnp.minimum(turn, 1) + turn - jnp.minimum(turn, 1)
        return self.first + turn

    def stored_rows(self, step, side):
        start = ((self.target(step) - self.first) * 2 + side) * self.pieces + step // self.turns
        return pl.ds(pl.multiple_of(start * self.rows, 16), self.rows)

    def slot(self, step):
        return pl.ds(pl.multiple_of(step * self.rows, 16), self.rows)

    def pair_copy(self, step):
        slot = self.slot(step)
        if self.stored:
            sent = self.stored[1].at[self.stored_rows(step, 1 - self.spot.side)]
            return remote(sent, self.pair_in.at[slot], self.p_send.at[step], self.p_recv.at[step], self.spot.pair)
        return remote(self.pair_out.at[slot], self.pair_in.at[slot], self.p_send.at[step], self.p_recv.at[step], self.spot.pair)

    def line_copy(self, step, to, recv):
        slot = self.slot(step)
        return remote(self.part.at[slot], self.line_in.at[slot], self.l_send.at[step], recv.at[step], to)

    def low_copy(self, step, to, recv):
        slot = self.slot(step)
        return remote(self.low_out.at[slot], self.low_in.at[slot], self.l_send.at[step], recv.at[step], to)

    def last_copy(self, step):
        here = pl.ds(pl.multiple_of(step // self.turns * self.rows, 16), self.rows)
        return remote(self.part.at[self.slot(step)], self.low_in.at[here], self.l_send.at[step], self.down_recv.at[step], self.spot.below)

    def own_copy(self, step):
        own = self.stored[0].at[self.stored_rows(step, self.spot.side)]
        return pltpu.make_async_copy(own, self.part.at[self.slot(step)], self.stored[2].at[step])

    def begin(self, step):
        if self.stored:
            self.pair_copy(step).start()
            self.own_copy(step).start()
            return
        self.pair_out[self.slot(step)] = self.source(self.target(step), 1 - self.spot.side, step // self.turns).astype(LOW)
        self.pair_copy(step).start()

    def add(self, step, low):
        slot = self.slot(step)
        self.part[slot] += self.low_in[slot].astype(WIDE) if low else self.line_in[slot]

    def low_hop(self, rising, target):
        line, last = self.spot.line, self.spot.lines - 1
        if rising:
            top = target == last
            return (line == 0) | ((line == 1) & top), (line == 1) | ((line == 2) & top)
        return line == last, line == last - 1

    def travel(self, step, rising):
        spot, slot = self.spot, self.slot(step)
        to, recv = (spot.above, self.up_recv) if rising else (spot.below, self.down_recv)
        last = spot.lines - 1
        at_end = spot.line == (0 if rising else last)
        target = self.target(step)
        if self.low:
            low_sent, low_taken = self.low_hop(rising, target)

            @pl.when(jnp.logical_not(at_end) & low_taken)
            def _():
                self.low_copy(step, to, recv).wait_recv()
                self.add(step, True)

            @pl.when(jnp.logical_not(at_end | low_taken))
            def _():
                self.line_copy(step, to, recv).wait_recv()
                self.add(step, False)

            @pl.when(low_sent)
            def _():
                self.low_out[slot] = self.part[slot].astype(LOW)
                self.low_copy(step, to, recv).start()

            @pl.when(jnp.logical_not(low_sent))
            def _():
                self.line_copy(step, to, recv).start()
        else:

            @pl.when(jnp.logical_not(at_end))
            def _():
                self.line_copy(step, to, recv).wait_recv()
                self.add(step, False)

            if rising:
                self.line_copy(step, to, recv).start()
            else:

                @pl.when(target == spot.line - 1)
                def _():
                    self.last_copy(step).start()

                @pl.when(target < spot.line - 1)
                def _():
                    self.line_copy(step, to, recv).start()

    def advance(self, step):
        spot = self.spot

        @pl.when(step < self.count)
        def _():
            slot = self.slot(step)
            self.pair_copy(step).wait_recv()
            if self.stored:
                self.own_copy(step).wait()
                self.part[slot] += self.pair_in[slot].astype(WIDE)
                return
            own = self.source(self.target(step), spot.side, step // self.turns)
            self.part[slot] = own + self.pair_in[slot].astype(WIDE)

        rising = step - spot.line

        @pl.when((rising >= 0) & (rising < self.count) & (self.target(rising) > spot.line))
        def _():
            self.travel(rising, True)

        falling = step - (spot.lines - 1 - spot.line)

        @pl.when((falling >= 0) & (falling < self.count) & (self.target(falling) < spot.line))
        def _():
            self.travel(falling, False)

    def close(self, step, give):
        spot, slot = self.spot, self.slot(step)
        target = self.target(step)
        last = spot.lines - 1
        self.pair_copy(step).wait_send()

        @pl.when(target > spot.line)
        def _():
            if self.low:

                low_sent, low_taken = self.low_hop(True, target)

                @pl.when(low_sent)
                def _():
                    self.low_copy(step, spot.above, self.up_recv).wait_send()

                @pl.when(jnp.logical_not(low_sent))
                def _():
                    self.line_copy(step, spot.above, self.up_recv).wait_send()
            else:
                self.line_copy(step, spot.above, self.up_recv).wait_send()

        @pl.when(target < spot.line)
        def _():
            if self.low:

                @pl.when(spot.line == last)
                def _():
                    self.low_copy(step, spot.below, self.down_recv).wait_send()

                @pl.when(spot.line < last)
                def _():
                    self.line_copy(step, spot.below, self.down_recv).wait_send()
            else:
                self.line_copy(step, spot.below, self.down_recv).wait_send()

        @pl.when(target == spot.line)
        def _():
            if self.low:

                @pl.when(spot.line == 1)
                def _():
                    self.low_copy(step, spot.above, self.up_recv).wait_recv()
                    self.add(step, True)

                @pl.when(spot.line > 1)
                def _():
                    self.line_copy(step, spot.above, self.up_recv).wait_recv()
                    self.add(step, False)

                @pl.when(spot.line == last - 1)
                def _():
                    self.low_copy(step, spot.below, self.down_recv).wait_recv()
                    self.add(step, True)

                @pl.when(spot.line < last - 1)
                def _():
                    self.line_copy(step, spot.below, self.down_recv).wait_recv()
                    self.add(step, False)
            else:

                @pl.when(spot.has_below)
                def _():
                    self.line_copy(step, spot.above, self.up_recv).wait_recv()
                    self.add(step, False)

                @pl.when(spot.has_above)
                def _():
                    self.last_copy(step).wait_recv()
                    here = pl.ds(pl.multiple_of(step // self.turns * self.rows, 16), self.rows)
                    self.part[slot] += self.low_in[here]

            give(step // self.turns, self.part[slot])


def attend_back_kernel(parts, q_rows, lines, count_ref, branch_ref, weight_ref, qkv_ref, log_ref, normed1_in, embed_ref,
                       resid_grad_ref, norm_ref, *rest):
    late_in, rest = (rest[:2], rest[2:]) if lines else ((), rest)
    grad_ref, embed_grad, gain_ref = rest[:3]
    own_late, rest = (rest[3], rest[4:]) if lines else (None, rest[3:])
    qkv_proj, attended_grad, qkv_grad, key_grad, value_grad, term, held, normed1_ref, load_sem = rest[:9]
    comm, late_comm = rest[9:17], rest[17:]
    loads = Moves(load_sem, (weight_ref.at[pl.ds(0, held.shape[0])], held), (normed1_in, normed1_ref))
    loads.start()
    corner = Corner()
    size, width = embed_ref.shape
    length, local = qkv_ref.shape[0], qkv_ref.shape[1] // 3
    if lines:
        spot = Lines(lines)
        barrier = pltpu.get_barrier_semaphore()
        for other in (corner.mate, corner.far):
            pl.semaphore_signal(barrier, inc=1, device_id={"tensor": other}, device_id_type=MESH)
        pl.semaphore_wait(barrier, 2 + spot.signal(barrier))
        late = LineSum(
            spot, SUM_PIECES, True, None, late_comm[:6], late_comm[6:11], 1, lines - 1, late_in + (late_comm[11],)
        )

        @pl.loop(0, late.count)
        def _(step):
            late.begin(step)

    else:
        corner.greet()
    scatter = Scatter(corner, PIECES, *comm)
    packed_ref, out_ref = held.at[pl.ds(0, 3 * local)], held.at[pl.ds(3 * local, local)]
    loads.wait(0)
    unpack_into(qkv_proj, packed_ref, parts)

    @pl.loop(0, 4)
    def _(block):
        here = rows_of(block, size)
        attended_grad[here] = dot(branch_ref[here], out_ref[...], NT).astype(LOW)

    key_grad[...] = jnp.zeros_like(key_grad)
    value_grad[...] = jnp.zeros_like(value_grad)
    valid = lax.broadcasted_iota(jnp.int32, (1, length), 1) < count_ref[0] * VTOK
    left = lax.broadcasted_iota(jnp.int32, (1, 2 * DH), 1) < DH
    factor = jnp.array(DH ** (-0.5), LOW)

    @pl.loop(0, length // q_rows)
    def _(turn):
        here = rows_of(turn, q_rows)
        for pair in range(local // (2 * DH)):
            lanes = slice(pair * 2 * DH, (pair + 1) * 2 * DH)
            queries = qkv_ref[here, lanes] * factor
            grads = attended_grad[here, lanes]
            keyset = qkv_ref[:, local + pair * 2 * DH : local + (pair + 1) * 2 * DH]
            values = qkv_ref[:, 2 * local + pair * 2 * DH : 2 * local + (pair + 1) * 2 * DH]
            found = []
            for side in range(2):
                mine = left if side == 0 else ~left
                own_query = jnp.where(mine, queries, jnp.zeros_like(queries))
                own_grad = jnp.where(mine, grads, jnp.zeros_like(grads))
                scores = jnp.where(valid, dot(own_query, keyset, NT), masked_score)
                probs = jnp.exp(scores - log_ref[here, pair * 2 + side : pair * 2 + side + 1])
                prob_grad = dot(own_grad, values, NT)
                value_grad[:, lanes] += dot(probs.astype(LOW), own_grad, TN)
                centre = jnp.sum(probs * prob_grad, -1, keepdims=True)
                score_grad = (probs * (prob_grad - centre)).astype(LOW)
                found.append(dot(score_grad, keyset))
                key_grad[:, lanes] += dot(score_grad, own_query, TN)
            qkv_grad[here, lanes] = (jnp.where(left, found[0], found[1]) * (DH ** (-0.5))).astype(LOW)
        if lines:

            @pl.loop(0, 2)
            def _(at):
                late.advance(2 * turn + at)

    qkv_grad[:, local : 2 * local] = key_grad[...].astype(LOW)
    qkv_grad[:, 2 * local :] = value_grad[...].astype(LOW)

    @pl.loop(0, 4)
    def _(step):
        here = rows_of(corner.block(step), size)

        def columns(cols):
            term[:, cols] = dot(qkv_grad[here], qkv_proj[cols, :], NT)

        column_loop(width, columns)
        scatter.step(step, term)
        if lines:
            late.advance(12 + step)

    loads.wait(1)
    for tile in range(width // TILE):
        value = dot(normed1_ref[:, tile * TILE : (tile + 1) * TILE], qkv_grad[...], TN)
        for row, rows, col, cols, at, at_col in qkv_places(parts, width, 3 * local):
            if at // TILE == tile:
                at = at % TILE
                grad_ref[row : row + rows, col : col + cols] = value[at : at + rows, at_col : at_col + cols]
    if lines:

        @pl.loop(16, 20)
        def _(step):
            late.advance(step)

    gain_sum, bias_sum = jnp.zeros((1, width), WIDE), jnp.zeros((1, width), WIDE)
    for piece in range(PIECES):
        part = scatter.part(piece)
        grad = scatter.land(piece, term)
        scaled, inverse = standard(embed_ref[part])
        embed_grad[part] = (resid_grad_ref[part] + norm_back(grad, scaled, inverse, norm_ref[0:1])).astype(LOW)
        gain_sum += jnp.sum(grad * scaled, 0, keepdims=True)
        bias_sum += jnp.sum(grad, 0, keepdims=True)
    gain_ref[0:1] = gain_sum
    gain_ref[1:2] = bias_sum
    scatter.close()
    if lines:

        @pl.loop(20, late.count + lines - 1)
        def _(step):
            late.advance(step)

        def keep_rows(piece, value):
            own_late[pl.ds(pl.multiple_of(piece * late.rows, 16), late.rows)] = value

        @pl.loop(0, late.count)
        def _(step):
            late.close(step, keep_rows)


def attend_back(count, branch, weights, qkv, log_total, normed1, embed, resid_grad, norm, late, parts, lines, collective_id):
    length, local = qkv.shape[0], qkv.shape[1] // 3
    size, width = embed.shape
    shape = jax.ShapeDtypeStruct
    chunk = 3 * width // (2 * lines) if lines else 0
    return pl.pallas_call(
        partial(attend_back_kernel, parts, 256, lines),
        out_shape=(
            shape((3 * local, width), WIDE),
            shape((size, width), LOW),
            shape((2, width), WIDE),
        )
        + ((shape((chunk, width), WIDE),) if lines else ()),
        in_specs=[pl.BlockSpec(memory_space=pltpu.SMEM), VMEM, HBM, VMEM, VMEM, HBM, VMEM, VMEM, VMEM] + [HBM] * len(late),
        out_specs=(VMEM,) * (4 if lines else 3),
        scratch_shapes=[
            pltpu.VMEM((width, 3 * local), LOW),
            pltpu.VMEM((length, local), LOW),
            pltpu.VMEM((length, 3 * local), LOW),
            pltpu.VMEM((length, local), WIDE),
            pltpu.VMEM((length, local), WIDE),
            pltpu.VMEM((size, width), WIDE),
            pltpu.VMEM((4 * local, width), LOW),
            pltpu.VMEM((length, width), LOW),
            pltpu.SemaphoreType.DMA((2,)),
        ]
        + Scatter.scratch(size, width, PIECES)
        + (
            LineSum.scratch(lines - 1, chunk, SUM_PIECES, width, True, True)
            + [pltpu.SemaphoreType.DMA(((lines - 1) * SUM_PIECES,))]
            if lines
            else []
        ),
        compiler_params=pltpu.CompilerParams(
            collective_id=collective_id, has_side_effects=True, vmem_limit_bytes=63 * 2**20
        ),
    )(count, branch, weights, qkv, log_total, normed1, embed, resid_grad, norm, *late)


SUM_PIECES = 6


def share_kernel(lines, early_ref, late_ref, embed_ref, own_patch_ref, used_ref, gain_ref, loss_ref, label_ref,
                 row_ref, shared_out, total_ref,
                 term, windows, mine, slots, rows_out, patch_ref, shared_ref, *comm):
    corner, spot = Corner(), Lines(lines)
    pairs, width = 2 * lines, early_ref.shape[1]
    quarters = 4
    count = pairs * quarters
    me = spot.me * quarters + corner.me
    barrier = pltpu.get_barrier_semaphore()

    def peer(step):
        other = lax.rem(me + step, count)
        return {"dp": other // quarters, "tensor": lax.rem(other, quarters)}

    @pl.loop(1, count)
    def _(step):
        pl.semaphore_signal(barrier, inc=1, device_id=peer(step), device_id_type=MESH)

    pl.semaphore_wait(barrier, count - 1)
    chunk = late_ref.shape[0]
    rows = chunk // SUM_PIECES

    def weight_term(line, side, piece):
        return early_ref[pl.ds(pl.multiple_of(side * chunk + piece * rows, 8), rows)]

    def shared_term(line, side, piece):
        return mine[pl.ds(pl.multiple_of(window_row(line * 2 + side), 16), WINDOW)]

    weights = LineSum(spot, SUM_PIECES, True, weight_term, comm[0:6], comm[6:11], 0, 1)
    shared = LineSum(spot, 1, False, shared_term, comm[11:17], comm[17:22])
    scatter = Scatter(corner, PIECES, *comm[22:30])
    gather = Gather(corner, windows, 1, comm[30:36])
    own_sem, send_sem, recv_sem = comm[36:39]

    @pl.loop(0, weights.count)
    def _(step):
        weights.begin(step)

    patch_ref[...] = dot(own_patch_ref[...], embed_ref[...], TN)

    @pl.loop(0, 4)
    def _(step):
        block = corner.block(step)
        term[...] = jnp.zeros_like(term)

        def rows_at(start, size):
            return pl.ds(pl.multiple_of(start, 16), size)

        for owner in range(3):
            at = owner * WINDOW
            term[at : at + WINDOW] = patch_ref[rows_at(ROW_START[owner] + block * WINDOW, WINDOW)]

        @pl.when(block < 3)
        def _():
            at = 3 * WINDOW
            term[at : at + 16] = patch_ref[rows_at(ROW_START[3] + block * 32, 16)]

            @pl.when(block < 2)
            def _():
                term[at + 16 : at + 32] = patch_ref[rows_at(ROW_START[3] + block * 32 + 16, 16)]

            for j in range(3):
                term[at + 32 : at + 48, j * 128 : (j + 1) * 128] = used_ref[rows_at(block * 48 + 16 * j, 16)]

        for owner in range(4, 8):
            at = window_row(owner)
            for j in range(4):

                @pl.when((block < 3) | (owner < 7) | (j < 2))
                def _():
                    term[at : at + SHORT, j * 128 : (j + 1) * 128] = used_ref[
                        rows_at(USED_START[owner] + block * 64 + SHORT * j, SHORT)
                    ]

        @pl.when(block == 0)
        def _():
            for row in range(8):
                at = window_row(7) + row
                term[at : at + 1, width // 2 :] = gain_ref[row // 2 : row // 2 + 1, row % 2 * width // 2 : (row % 2 + 1) * width // 2]

        scatter.step(step, term)

    @pl.loop(0, 2)
    def _(step):
        weights.advance(step)

    for piece in range(PIECES):
        mine[scatter.part(piece)] = scatter.land(piece, term)

    @pl.loop(0, lines)
    def _(step):
        shared.begin(step)

    @pl.loop(0, 2 * lines - 1)
    def _(step):
        weights.advance(2 + step)
        shared.advance(step)

    def keep_window(piece, value):
        windows[gather.part(corner.me, 0)] = value

    @pl.loop(0, lines)
    def _(step):
        shared.close(step, keep_window)

    gather.start(0)

    def keep_rows(piece, value):
        rows_out[pl.ds(pl.multiple_of(piece * rows, rows), rows)] = value

    @pl.loop(0, weights.count)
    def _(step):
        weights.close(step, keep_rows)

    @pl.when(spot.line > 0)
    def _():
        rows_out[...] = late_ref[...]

    window = jnp.where(window_valid(spot.me, corner.me, width), windows[gather.part(corner.me, 0)], 0.0)
    square = jnp.sum(window * window) + jnp.sum(rows_out[...] * rows_out[...])
    counted = jnp.sum(jnp.where(label_ref[...] < 2, 1.0, 0.0))
    line = lax.broadcasted_iota(jnp.int32, total_ref.shape, 0)
    slots[me] = jnp.where(line == 0, square, jnp.where(line == 1, loss_ref[...], jnp.where(line == 2, counted, 0.0)))

    def send(step):
        return remote(slots.at[me], slots.at[me], send_sem.at[step], recv_sem.at[step], peer(step))

    def arrive(step):
        source = lax.rem(me - step + count, count)
        return remote(slots.at[source], slots.at[source], send_sem.at[step], recv_sem.at[step], peer(step))

    @pl.loop(1, count)
    def _(step):
        send(step).start()

    gather.relay(0)

    @pl.when(spot.me < lines // 2)
    def _():
        for row, height, col, cols, at, at_col in qkv_places(1, chunk * 4 // 3, width * 3 // 4):
            for j in range(cols // 128):
                row_ref[pl.ds(6 * at + at_col // 128 + j, height, 6)] = rows_out[
                    row : row + height, col + j * 128 : col + (j + 1) * 128
                ]

    @pl.when(spot.me >= lines // 2)
    def _():
        for j in range(8):
            row_ref[pl.ds(j, chunk, 8)] = rows_out[:, j * 128 : (j + 1) * 128]

    gather.finish()
    shared_ref[...] = jnp.zeros_like(shared_ref)
    for phase in range(5):

        @pl.loop(0, 4)
        def _(quarter):
            def take(condition, row, height, j, start, stride):
                @pl.when(condition)
                def _():
                    here = pl.ds(pl.multiple_of(quarter * WINDOW + row, 16), height)
                    shared_ref[pl.ds(start, height, stride)] = windows[here, j * 128 : (j + 1) * 128]

            shared_walk(spot.me, quarter, take, (phase,))

    shared_out[...] = shared_ref[FRONT : FRONT + SHARED_LANES]

    @pl.loop(1, count)
    def _(step):
        arrive(step).wait_recv()

    total_ref[...] = jnp.sum(slots[...], 0)

    @pl.loop(1, count)
    def _(step):
        send(step).wait_send()

    scatter.close()


def share(early, late, embed_grad, patches, used_grad, gains, loss_tile, labels, lines, collective_id):
    width = early.shape[1]
    chunk = late.shape[0]
    packed = 4 * WINDOW + (2 * lines - 4) * SHORT
    count = 8 * lines
    shape = jax.ShapeDtypeStruct
    return pl.pallas_call(
        partial(share_kernel, lines),
        out_shape=(shape((chunk * width // 128, 128), WIDE), shape((SHARED_LANES, 128), WIDE), shape((8, 128), WIDE)),
        in_specs=[VMEM] * 8,
        out_specs=(VMEM,) * 3,
        scratch_shapes=[
            pltpu.VMEM((packed, width), WIDE),
            pltpu.VMEM((4 * WINDOW, width), WIDE),
            pltpu.VMEM((packed + WINDOW - SHORT, width), WIDE),
            pltpu.VMEM((count, 8, 128), WIDE),
            pltpu.VMEM((chunk, width), WIDE),
            pltpu.VMEM((patches.shape[1], width), WIDE),
            pltpu.VMEM((PADDED, 128), WIDE),
        ]
        + LineSum.scratch(1, chunk, SUM_PIECES, width, True)
        + LineSum.scratch(lines, WINDOW, 1, width, False)
        + Scatter.scratch(packed, width, PIECES)
        + Gather.scratch(1)
        + [
            pltpu.SemaphoreType.DMA(()),
            pltpu.SemaphoreType.DMA((count,)),
            pltpu.SemaphoreType.DMA((count,)),
        ],
        compiler_params=pltpu.CompilerParams(
            collective_id=collective_id, has_side_effects=True, vmem_limit_bytes=63 * 2**20
        ),
    )(early, late, embed_grad, patches, used_grad, gains, loss_tile, labels)


def render_kernel(area, wide, block, split, span, table_ref, splat_ref, dist_ref, label_ref, loss_ref, grad_ref, flip, hot, weighted, spread_grad):
    tokens = table_ref.shape[0]
    groups = tokens // wide
    splats, pixels = splat_ref.shape
    for j in range(groups):
        flip[j * 2 * area : (j + 1) * 2 * area] = jnp.transpose(table_ref[j * wide : (j + 1) * wide].astype(jnp.float32)).astype(jnp.bfloat16)
    spread_grad[...] = jnp.zeros_like(spread_grad)
    wide_ids = lax.broadcasted_iota(jnp.int32, (wide, block), 0).astype(jnp.float32).astype(jnp.bfloat16)
    cell_ids = lax.broadcasted_iota(jnp.int32, (area, block), 0).astype(jnp.float32)
    cell_low = cell_ids.astype(jnp.bfloat16)
    one, nil = jnp.ones((wide, block), jnp.bfloat16), jnp.zeros((wide, block), jnp.bfloat16)

    def one_block(step, loss):
        here = pl.ds(pl.multiple_of(step * block, block), block)
        opacities, spreads, lows = [], [], []
        for k in range(splats):
            index = splat_ref[k : k + 1, here]
            token = index // area
            column = (token % wide).astype(jnp.float32).astype(jnp.bfloat16)
            lows.append((token // wide, (index % area).astype(jnp.float32)))
            hot[:, k * block : (k + 1) * block] = jnp.where(wide_ids == column, one, nil)
        for k in range(splats):
            lanes = slice(k * block, (k + 1) * block)
            group, cell = lows[k]
            op_sum = jnp.zeros((area, block), jnp.float32)
            sp_sum = jnp.zeros((area, block), jnp.float32)
            for at in range(0, groups, span):
                rows = slice(at * 2 * area, (at + span) * 2 * area)
                found = lax.dot_general(flip[rows], hot[:, lanes], NN, preferred_element_type=jnp.float32)
                for j in range(span):
                    same = cell_ids == jnp.where(group == at + j, cell, -1.0)
                    op_sum += jnp.where(same, found[j * 2 * area : j * 2 * area + area], 0.0)
                    sp_sum += jnp.where(same, found[j * 2 * area + area : (j + 1) * 2 * area], 0.0)
            opacities.append(jnp.sum(op_sum, 0, keepdims=True))
            spreads.append(jnp.sum(sp_sum, 0, keepdims=True))
        opacity, spread = jnp.concatenate(opacities, 0), jnp.concatenate(spreads, 0)
        distance = dist_ref[:, here].astype(jnp.float32)
        labels = label_ref[:, here]
        valid = jnp.where(labels < 2, 1.0, 0.0)
        target = jnp.where(labels == 1, 1.0, 0.0)
        op_sig, sp_sig = jax.nn.sigmoid(opacity), jax.nn.sigmoid(spread)
        fade = jnp.exp(-0.25 * distance * sp_sig)
        contrib = (0.02 + 0.96 * op_sig) * fade
        keep_log = jnp.sum(jnp.log1p(-contrib), 0, keepdims=True)
        keep = jnp.exp(keep_log)
        alpha = 1.0 - keep
        alpha_log = jnp.log(alpha)
        loss = loss - valid * (target * alpha_log + (1.0 - target) * keep_log)
        keep_grad = valid * (target * keep / alpha - (1.0 - target))
        contrib_grad = -keep_grad / (1.0 - contrib)
        op_grad = contrib_grad * (0.96 * op_sig * (1.0 - op_sig)) * fade
        sp_grad = contrib_grad * contrib * (-0.25 * distance * sp_sig * (1.0 - sp_sig))
        zero = jnp.zeros((area, block), jnp.bfloat16)
        op_parts, sp_parts = [], []
        for part in range(split):
            op_parts.append(op_grad.astype(jnp.bfloat16))
            sp_parts.append(sp_grad.astype(jnp.bfloat16))
            op_grad, sp_grad = op_grad - op_parts[-1].astype(jnp.float32), sp_grad - sp_parts[-1].astype(jnp.float32)
        for at in range(0, groups, span):
            rows = slice(at * 2 * area, (at + span) * 2 * area)
            for k in range(splats):
                lanes = slice(k * block, (k + 1) * block)
                group, cell = lows[k]
                for j in range(span):
                    same = cell_low == jnp.where(group == at + j, cell, -1.0).astype(jnp.bfloat16)
                    first = (at + j) * 2 * area
                    for part in range(split):
                        weighted[part, first : first + area, lanes] = jnp.where(same, op_parts[part][k : k + 1], zero)
                        weighted[part, first + area : first + 2 * area, lanes] = jnp.where(same, sp_parts[part][k : k + 1], zero)
            total = spread_grad[rows]
            for part in range(split):
                total += lax.dot_general(weighted[part, rows], hot[...], NT, preferred_element_type=jnp.float32)
            spread_grad[rows] = total
        return loss

    loss = lax.fori_loop(0, pixels // block, one_block, jnp.zeros((1, block), jnp.float32))
    loss_ref[...] = jnp.broadcast_to(jnp.sum(loss, 1, keepdims=True), loss_ref.shape)
    for j in range(groups):
        grad_ref[j * wide : (j + 1) * wide] = jnp.transpose(spread_grad[j * 2 * area : (j + 1) * 2 * area]).astype(grad_ref.dtype)

def render(table, splats, distance, labels, area, block=768, wide=256, split=2, span=3):
    tokens = table.shape[0]
    vm = pl.BlockSpec(memory_space=pltpu.VMEM)
    groups = tokens // wide
    count = splats.shape[0]
    return pl.pallas_call(
        partial(render_kernel, area, wide, block, split, span),
        out_shape=(jax.ShapeDtypeStruct((8, 128), jnp.float32), jax.ShapeDtypeStruct(table.shape, jnp.bfloat16)),
        in_specs=[vm] * 4, out_specs=(vm, vm),
        scratch_shapes=[pltpu.VMEM((groups * 2 * area, wide), jnp.bfloat16),
            pltpu.VMEM((wide, count * block), jnp.bfloat16), pltpu.VMEM((split, groups * 2 * area, count * block), jnp.bfloat16), pltpu.VMEM((groups * 2 * area, wide), jnp.float32)],
        compiler_params=pltpu.CompilerParams(vmem_limit_bytes=60 * 2**20),
    )(table, splats, distance, labels)


def owner_sum_kernel(lines, pieces, g_ref, o_ref, pair_out, pair_in, part, line_in, own_in, p_send, p_recv, l_send, up_recv, down_recv):
    me = lax.axis_index("dp")
    line, side = me // 2, lax.rem(me, 2)
    chunk = o_ref.shape[0]
    rows = chunk // pieces
    count = lines * pieces
    pair = {"dp": line * 2 + 1 - side}
    above = {"dp": lax.rem(line + 1, lines) * 2 + side}
    below = {"dp": lax.rem(line + lines - 1, lines) * 2 + side}
    has_below, has_above = line > 0, line < lines - 1

    def target(step):
        turn = lax.rem(step, lines)
        odd = lax.rem(turn, 2)
        return (1 - odd) * (lines - 1 - turn // 2) + odd * (turn // 2)

    def slot(step):
        return pl.ds(pl.multiple_of(step * rows, rows), rows)

    def here(step):
        return pl.ds(pl.multiple_of(step // lines * rows, rows), rows)

    def source(step, owner):
        return pl.ds(pl.multiple_of((target(step) * 2 + owner) * chunk + step // lines * rows, rows), rows)

    def copy(src, dst, send, recv, to):
        return pltpu.make_async_remote_copy(
            src_ref=src, dst_ref=dst, send_sem=send, recv_sem=recv, device_id=to, device_id_type=MESH
        )

    def pair_copy(step):
        return copy(pair_out.at[slot(step)], pair_in.at[slot(step)], p_send.at[step], p_recv.at[step], pair)

    def line_copy(step, to, recv):
        return copy(part.at[slot(step)], line_in.at[slot(step)], l_send.at[step], recv.at[step], to)

    def last_copy(step):
        return copy(part.at[slot(step)], own_in.at[here(step)], l_send.at[step], down_recv.at[step], below)

    barrier = pltpu.get_barrier_semaphore()
    pl.semaphore_signal(barrier, inc=1, device_id=pair, device_id_type=MESH)

    @pl.when(has_below)
    def _():
        pl.semaphore_signal(barrier, inc=1, device_id=below, device_id_type=MESH)

    @pl.when(has_above)
    def _():
        pl.semaphore_signal(barrier, inc=1, device_id=above, device_id_type=MESH)

    pl.semaphore_wait(barrier, 1 + jnp.minimum(line, 1) + jnp.minimum(lines - 1 - line, 1))

    @pl.loop(0, count)
    def _(step):
        pair_out[slot(step)] = g_ref[source(step, 1 - side)].astype(jnp.bfloat16)
        pair_copy(step).start()

    @pl.loop(0, count + lines - 1)
    def _(step):
        @pl.when(step < count)
        def _():
            pair_copy(step).wait_recv()
            part[slot(step)] = g_ref[source(step, side)].astype(jnp.float32) + pair_in[slot(step)].astype(jnp.float32)

        rising = step - line

        @pl.when((rising >= 0) & (rising < count) & (target(rising) > line))
        def _():
            @pl.when(has_below)
            def _():
                line_copy(rising, above, up_recv).wait_recv()
                part[slot(rising)] += line_in[slot(rising)]

            line_copy(rising, above, up_recv).start()

        falling = step - (lines - 1 - line)

        @pl.when((falling >= 0) & (falling < count) & (target(falling) < line))
        def _():
            @pl.when(has_above)
            def _():
                line_copy(falling, below, down_recv).wait_recv()
                part[slot(falling)] += line_in[slot(falling)]

            @pl.when(target(falling) == line - 1)
            def _():
                last_copy(falling).start()

            @pl.when(target(falling) < line - 1)
            def _():
                line_copy(falling, below, down_recv).start()

    @pl.loop(0, count)
    def _(step):
        pair_copy(step).wait_send()

        @pl.when(target(step) > line)
        def _():
            line_copy(step, above, up_recv).wait_send()

        @pl.when(target(step) < line)
        def _():
            line_copy(step, below, down_recv).wait_send()

        @pl.when(target(step) == line)
        def _():
            o_ref[here(step)] = part[slot(step)]

            @pl.when(has_below)
            def _():
                line_copy(step, above, up_recv).wait_recv()
                o_ref[here(step)] += line_in[slot(step)]

            @pl.when(has_above)
            def _():
                last_copy(step).wait_recv()
                o_ref[here(step)] += own_in[here(step)]


def owner_sum(grad, count_dp, collective_id, pieces):
    lines = count_dp // 2
    total, width = grad.shape
    chunk = total // count_dp
    half = (lines * chunk, width)
    vmem = pl.BlockSpec(memory_space=pltpu.VMEM)
    return pl.pallas_call(
        partial(owner_sum_kernel, lines, pieces),
        out_shape=jax.ShapeDtypeStruct((chunk, width), jnp.float32),
        in_specs=[vmem],
        out_specs=vmem,
        scratch_shapes=[
            pltpu.VMEM(half, jnp.bfloat16),
            pltpu.VMEM(half, jnp.bfloat16),
            pltpu.VMEM(half, jnp.float32),
            pltpu.VMEM(half, jnp.float32),
            pltpu.VMEM((chunk, width), jnp.float32),
        ]
        + [pltpu.SemaphoreType.DMA((lines * pieces,))] * 5,
        compiler_params=pltpu.CompilerParams(
            collective_id=collective_id, has_side_effects=True, vmem_limit_bytes=62 * 2**20
        ),
    )(grad)


def total_kernel(mine_ref, sum_ref, slots, own_sem, send_sem, recv_sem):
    first, second = lax.axis_size("dp"), lax.axis_size("tensor")
    count = first * second
    me = lax.axis_index("dp") * second + lax.axis_index("tensor")

    def peer(step):
        other = lax.rem(me + step, count)
        return {"dp": other // second, "tensor": lax.rem(other, second)}

    barrier = pltpu.get_barrier_semaphore()

    @pl.loop(1, count)
    def _(step):
        pl.semaphore_signal(barrier, inc=1, device_id=peer(step), device_id_type=MESH)

    pl.semaphore_wait(barrier, count - 1)
    own = pltpu.make_async_copy(mine_ref, slots.at[me], own_sem)
    own.start()

    def send(step):
        return pltpu.make_async_remote_copy(
            src_ref=mine_ref,
            dst_ref=slots.at[me],
            send_sem=send_sem.at[step],
            recv_sem=recv_sem.at[step],
            device_id=peer(step),
            device_id_type=MESH,
        )

    @pl.loop(1, count)
    def _(step):
        send(step).start()

    @pl.loop(1, count)
    def _(step):
        send(step).wait()

    own.wait()
    sum_ref[...] = jnp.sum(slots[...], 0)


def total_over_all(mine, collective_id):
    count = lax.axis_size("dp") * lax.axis_size("tensor")
    vmem = pl.BlockSpec(memory_space=pltpu.VMEM)
    return pl.pallas_call(
        total_kernel,
        out_shape=jax.ShapeDtypeStruct(mine.shape, jnp.float32),
        in_specs=[vmem],
        out_specs=vmem,
        scratch_shapes=[
            pltpu.VMEM((count,) + mine.shape, jnp.float32),
            pltpu.SemaphoreType.DMA(()),
            pltpu.SemaphoreType.DMA((count,)),
            pltpu.SemaphoreType.DMA((count,)),
        ],
        compiler_params=pltpu.CompilerParams(collective_id=collective_id, has_side_effects=True),
    )(mine)


def pack_qkv(matrix, parts):
    rows, cols = matrix.shape
    first = matrix[:, :512].reshape(parts, 2, rows // parts // 2, 512).transpose(0, 2, 1, 3)
    second = matrix[:, 512:].reshape(parts, 4, rows // parts // 4, 256).transpose(0, 2, 1, 3)
    return jnp.concatenate([first.reshape(parts, -1, 1024), second.reshape(parts, -1, 1024)], 1).reshape(-1, 1024)


def unpack_qkv(packed, parts):
    rows = packed.shape[0] // parts
    packed = packed.reshape(parts, rows, 1024)
    cut = rows * 2 // 3
    first = packed[:, :cut].reshape(parts, cut, 2, 512).transpose(0, 2, 1, 3).reshape(-1, 512)
    second = packed[:, cut:].reshape(parts, rows - cut, 4, 256).transpose(0, 2, 1, 3).reshape(-1, 256)
    return jnp.concatenate([first, second], 1)


def by_lanes(flat, outer):
    size = flat.size // math.prod(outer)
    return flat.reshape(outer + ((size // 128, 128) if size % 128 == 0 else (size,)))


def pad_first(array, axis, unit):
    short = -array.shape[axis] % unit
    return jnp.pad(array, [(0, short if at == axis else 0) for at in range(array.ndim)])


def sum_to_owners(stack, count_dp):
    if count_dp == 8:
        return owner_sum(stack, count_dp, 1, 9)
    return lax.psum_scatter(stack, "dp", scatter_dimension=0, tiled=True)

def adam_update(master, first_mom, second_mom, gradient, step_float):
    first_new = beta_one * first_mom + (1.0 - beta_one) * gradient
    second_new = beta_two * second_mom + (1.0 - beta_two) * gradient * gradient
    first_hat = first_new / (1.0 - jnp.power(beta_one, step_float))
    second_hat = second_new / (1.0 - jnp.power(beta_two, step_float))
    master_new = master - learn_rate * (
        first_hat / (jnp.sqrt(second_hat) + adam_eps) + decay_rate * master
    )
    return (master_new, first_new, second_new)


def adam_kernel(total_ref, count_ref, *refs):
    norm_value = jnp.sqrt(total_ref[0, 0:1]) / total_ref[2, 0:1]
    factor = (clip_norm / jnp.maximum(norm_value, clip_norm) / total_ref[2, 0:1]).reshape(1, 1)
    step_float = jnp.full((1, 1), count_ref[0], jnp.int32).astype(WIDE)

    def update(ins, outs):
        grad, master, first, second, ema = (ref[...] for ref in ins)
        new, first_new, second_new = adam_update(master, first, second, grad * factor, step_float)
        ema_new = ema_rate * ema + (1.0 - ema_rate) * new
        for ref, value in zip(outs, (new, first_new, second_new, ema_new, new.astype(LOW))):
            ref[...] = value

    parts = len(refs) // 10
    for part in range(parts):
        update(refs[5 * part : 5 * part + 5], refs[5 * (parts + part) : 5 * (parts + part) + 5])


def adam(totals, step_count, rows, shared, blocks):
    size = rows[1].shape[1] // blocks
    spec = pl.BlockSpec((1, size), lambda at: (0, at))
    if shared[0].shape[0] == 1:
        kept = [pl.BlockSpec(array.shape, lambda at: (0, 0)) for array in shared]
    else:
        kept = [pl.BlockSpec((-(-array.shape[0] // (8 * blocks)) * 8, 128), lambda at: (at, 0)) for array in shared]
    kinds = (WIDE,) * 4 + (LOW,)
    shapes = [jax.ShapeDtypeStruct(arrays[1].shape, kind) for arrays in (rows, shared) if arrays for kind in kinds]
    return pl.pallas_call(
        adam_kernel,
        grid=(blocks,),
        out_shape=tuple(shapes),
        in_specs=[pl.BlockSpec((8, 128), lambda at: (0, 0)), pl.BlockSpec(memory_space=pltpu.SMEM)] + [spec] * 5 + kept,
        out_specs=(spec,) * 5 + tuple(kept),
    )(totals, step_count, *rows, *shared)


def per_device(
    patches,
    view_counts,
    splat_index,
    splat_dist,
    alpha_label,
    step_count,
    row_master,
    row_first,
    row_second,
    row_ema,
    shared_master,
    shared_first,
    shared_second,
    shared_ema,
):
    groups = lax.axis_size("tensor")
    my_dp = lax.axis_index("dp")
    count_dp = lax.axis_size("dp")
    local_width = D // groups
    qkv_parts = count_dp // 4
    share_rows = row_master.shape[1] // D
    own_patches = patches[0]
    if count_dp == 8:
        shared_lanes = shared_master.reshape(SHARED_LANES, 128)
        weights, used_cols, norm, embed, normed1, qkv, attended, log_total, resid1, normed2 = forward(
            view_counts, row_master.reshape(-1, 128), shared_lanes, own_patches, count_dp // 2, 7
        )
    else:
        own_row = row_master[0].astype(jnp.bfloat16)
        own_tiles = jnp.where(
            my_dp < qkv_parts,
            pack_qkv(own_row.reshape(-1, 3 * local_width), 1),
            own_row.reshape(share_rows, D),
        )
        weights = lax.all_gather(own_tiles, "dp", axis=0, tiled=True)
        own_flat = shared_master.astype(jnp.bfloat16)
        own_shared = by_lanes(own_flat, ())
        lead = own_shared.shape[0]
        own_shared = pad_first(own_shared, 0, 2048 // own_shared[0].size)
        shared_weights = lax.all_gather(own_shared, "dp", axis=0, tiled=False)[:, :lead].reshape(-1, 128)
        patch_rows = PIN * D // 128
        unpatch_rows = D * POUT // 128
        norm = shared_weights[patch_rows + unpatch_rows :].reshape(4, D).astype(jnp.float32)
        patch_proj = shared_weights[:patch_rows].reshape(PIN, D)
        used_cols = shared_weights[patch_rows : patch_rows + unpatch_rows].reshape(D, POUT // 128, 128)[:, 0]
        all_patches = lax.all_gather(own_patches, "tensor", axis=0, tiled=True)
        embed, normed1, qkv, attended, log_total, resid1, normed2 = attend(
            view_counts, all_patches, patch_proj, norm, weights, qkv_parts, 3
        )
    hidden, active, resid2_low, gauss_table = mlp(normed2, weights, resid1, used_cols, 4)
    loss_tile, table_grad = render(gauss_table, splat_index[0], splat_dist[0], alpha_label, PATCH * PATCH)
    loss_part = loss_tile[0, 0]
    unpatch_used, late_grad, late_low, resid_grad, branch, gain2_grad = mlp_back(
        table_grad, used_cols, resid2_low, active, hidden, normed2, weights, resid1, norm, attended, share_rows if count_dp == 8 else None, 5
    )
    early_grad, embed_grad, gain1_grad, *own_late = attend_back(
        view_counts,
        branch,
        weights,
        qkv,
        log_total,
        normed1,
        embed,
        resid_grad,
        norm,
        (late_grad, late_low) if count_dp == 8 else (),
        qkv_parts,
        count_dp // 2 if count_dp == 8 else 0,
        6,
    )
    gain_grad = jnp.concatenate([gain1_grad, gain2_grad], 0)
    if count_dp == 8:
        gains = jnp.pad(gain_grad, ((0, 4), (0, 0)))
        row_lanes, shared_share, totals = share(
            early_grad, own_late[0], embed_grad, own_patches, unpatch_used, gains, loss_tile, alpha_label, count_dp // 2, 8
        )
        row_share = row_lanes.reshape(-1)
    else:
        patch_grad = dot(own_patches, embed_grad, TN)
        unpatch_grad = jnp.concatenate(
            [unpatch_used, jnp.zeros((D, POUT - unpatch_used.shape[1]), jnp.float32)], 1
        )
        shared_grad = jnp.concatenate(
            [patch_grad.reshape(-1), unpatch_grad.reshape(-1), gain_grad.reshape(-1)]
        )
        split_grad = by_lanes(shared_grad, (count_dp, groups))
        lead = split_grad.shape[2]
        shared_stack = pad_first(split_grad, 2, 16 * D // split_grad[0, 0, 0].size).swapaxes(0, 1)
        shared_sum = lax.psum_scatter(shared_stack, "tensor", scatter_dimension=0, tiled=True)
        row_stack = jnp.concatenate([early_grad, late_grad], 0)
        stack = jnp.concatenate(
            [row_stack.reshape(count_dp, share_rows, D), shared_sum.reshape(count_dp, -1, D)], 1
        ).reshape(-1, D)
        own_share = sum_to_owners(stack, count_dp)
        own_rows = own_share[:share_rows]
        row_share = jnp.where(my_dp < qkv_parts, unpack_qkv(own_rows, 1).reshape(-1), own_rows.reshape(-1))
        shared_part = own_share[share_rows:].reshape((-1,) + split_grad.shape[3:])[:lead]
        shared_share = lax.all_gather(shared_part, "tensor", axis=0, tiled=False).reshape(-1)
        own_squares = jnp.sum(row_share * row_share) + jnp.sum(shared_part * shared_part)
        pixel_part = jnp.sum((alpha_label < 2).astype(jnp.float32))
        scalars = jnp.stack([own_squares, loss_part, pixel_part]).reshape(3, 1)
        totals = total_over_all(jnp.pad(jnp.broadcast_to(scalars, (3, 128)), ((0, 5), (0, 0))), 2)
    square_total, loss_total, pixel_total = totals[0, 0], totals[1, 0], totals[2, 0]
    norm_value = jnp.sqrt(square_total) / pixel_total
    flat = shared_master.shape
    lanes = (-1, 128) if flat[0] % 128 == 0 else (1, -1)
    shared = [array.reshape(lanes) for array in (shared_share, shared_master, shared_first, shared_second, shared_ema)]
    updated = adam(totals, step_count, (row_share[None], row_master, row_first, row_second, row_ema), shared, 6)
    row_new, row_first_new, row_second_new, row_ema_new, row_copy = updated[:5]
    shared_new, shared_first_new, shared_second_new, shared_ema_new, shared_copy = (array.reshape(flat) for array in updated[5:])
    return (
        norm_value.reshape(1),
        (loss_total / pixel_total).reshape(1),
        row_new,
        row_first_new,
        row_second_new,
        row_ema_new,
        row_copy,
        shared_new,
        shared_first_new,
        shared_second_new,
        shared_ema_new,
        shared_copy,
    )


def solution(mesh):
    placed = (
        P("dp", "tensor", None),
        P("dp"),
        P("dp", None, "tensor"),
        P("dp", None, "tensor"),
        P("dp", "tensor"),
        P(),
        P("tensor", "dp"),
        P("tensor", "dp"),
        P("tensor", "dp"),
        P("tensor", "dp"),
        P("dp"),
        P("dp"),
        P("dp"),
        P("dp"),
    )
    return jax.shard_map(
        per_device,
        mesh=mesh,
        in_specs=placed,
        out_specs=(
            P(),
            P(),
            P("tensor", "dp"),
            P("tensor", "dp"),
            P("tensor", "dp"),
            P("tensor", "dp"),
            P("tensor", "dp"),
            P("dp"),
            P("dp"),
            P("dp"),
            P("dp"),
            P("dp"),
        ),
        check_vma=False,
    )
```
